32 devices in a mesh: dp: 8 (over z, core), group: 4 (over y, x).
Axes of the slice: x: 2, y: 2, z: 4, core: 2. Of those that a mesh axis runs over, the one named last changes fastest.
Arguments:
- activations: bfloat16 [16, 1024, 1024], P('dp', 'group'), may hold values from -6 to 6
- cotangent: bfloat16 [16, 1024, 1024], P('dp', 'group'), may hold values from -6 to 6
- segments: int32 [16, 1024], P('dp'), may hold values from 0 to 2, never falling along the last dimension, each value on 1 to 800 neighbouring positions
- padding: int32 [16, 1024], P('dp'), may hold values 0 or 1
- step_count: int32 [1], replicated, may hold values from 1 to 999
- learn_rate: float32 [1], replicated, may hold values from 0.005 to 0.02
- gain_before: bfloat16 [1024], replicated, may hold values from 0.5 to 1.5
- shift_before: bfloat16 [1024], replicated, may hold values from -2 to 2
- joint_weight: bfloat16 [1024, 3072], replicated, may hold values from -0.1875 to 0.1875
- joint_bias: bfloat16 [2048], replicated, may hold values from -2 to 2
- mixer_weight: bfloat16 [1024, 1024], replicated, may hold values from -0.75 to 0.75
- mixer_bias: bfloat16 [1024], replicated, may hold values from -2 to 2
- gain_middle: bfloat16 [1024], replicated, may hold values from 0.5 to 1.5
- shift_middle: bfloat16 [1024], replicated, may hold values from -2 to 2
- expand_weight: bfloat16 [1024, 4096], replicated, may hold values from -0.1875 to 0.1875
- expand_bias: bfloat16 [4096], replicated, may hold values from -3 to 3
- reduce_weight: bfloat16 [4096, 1024], replicated, may hold values from -0.09375 to 0.09375
- reduce_bias: bfloat16 [1024], replicated, may hold values from -2 to 2
- master_weights: float32 [12595200], P(('dp', 'group')), may hold values from -0.06 to 0.06
- first_moment: float32 [12595200], P(('dp', 'group')), may hold values from -6 to 6
- second_moment: float32 [12595200], P(('dp', 'group')), may hold values from 1 to 1000
Outputs:
- output: bfloat16 [16, 1024, 1024], P('dp', 'group')
- input_gradient: bfloat16 [16, 1024, 1024], P('dp', 'group')
- updated_master: float32 [12595200], P(('dp', 'group'))
- updated_first: float32 [12595200], P(('dp', 'group'))
- updated_second: float32 [12595200], P(('dp', 'group'))
- small_gradient: float32 [12288], P(('dp', 'group'))
The draws below stay inside these ranges and needn't reach their ends.
Inputs may be any that keep to these rules, and one draw needn't show every extreme that they name: `segments`: in each sequence the numbers never fall; a document is 1 to 800 consecutive tokens, and every sequence has one of exactly 800.
All inputs are finite; a program needn't handle non-finite values. No bound on the sum of `padding` on one device may be relied on, other than what follows from the above.
Results may differ from the reference program's by a relative error of at most 0.015.
Values may be sent and summed in bfloat16 or wider, within the bound.
A program may use at most 384 MiB of HBM per device.

```python
import math
import jax
import jax.numpy as jnp
import numpy as np
from jax import lax

D = 1024
HEADS = 16
FF = 4096
DOC_MOST = 800
HEAD_DIM = 64
LENGTH = 1024
SEQS = 16
DOCS = 3
NPARAM = 12595200


def touch_ends(drawn, rng, low, high):
    longest = drawn.shape.index(max(drawn.shape))
    spots = []
    for shift in (0, 1):
        where = [jax.random.randint(jax.random.fold_in(rng, axis), (), 0, length) for axis, length in enumerate(drawn.shape)]
        where[longest] = (where[longest] + shift) % drawn.shape[longest]
        spots.append(tuple(where))
    return drawn.at[spots[0]].set(low).at[spots[1]].set(high)


def level_of(own_key, extent, shards, least, top_value):
    def one(position, parts):
        heights = jax.random.uniform(jax.random.fold_in(jax.random.fold_in(own_key, 6), position), (parts,), jnp.float32, least / len(shards), top_value / len(shards))
        return jnp.repeat(jnp.exp(heights), extent[position] // parts).reshape((-1,) + (1,) * (len(extent) - position - 1))

    level = one(*shards[0])
    for cut in shards[1:]:
        level = level * one(*cut)
    return level


def profile(amount, total, most, lean):
    portions = [(1 << 20) // math.isqrt(grade ** lean) + 1 for grade in range(2, amount + 1)]
    surplus, given = total - most - (amount - 1), [1] * (amount - 1)
    while surplus > 0:
        free = [i for i in range(amount - 1) if given[i] < most]
        pool, remaining = sum([portions[i] for i in free]), surplus
        for i in free:
            addition = min(most - given[i], max(1, remaining * portions[i] // pool), surplus)
            given[i] = given[i] + addition
            surplus = surplus - addition
    return np.array([most] + given)


def uneven_parts(own_key, amount, total, most, slope):
    if amount == 2:
        one = jax.random.randint(own_key, (), max(1, total - most), min(most, total - 1) + 1)
        return jnp.stack([one, total - one])
    lengths = jnp.asarray(profile(amount, total, most, slope), jnp.int32)
    couples = (amount - 1) // 2
    source_of, receiver = lengths[1:1 + 2 * couples:2], lengths[2:2 + 2 * couples:2]
    margin = jnp.minimum(source_of - 1, most - receiver)
    moved = jax.random.randint(jax.random.fold_in(own_key, 1), (couples,), 0, 1 << 20) % (margin + 1)
    lengths = lengths.at[1:1 + 2 * couples:2].set(source_of - moved).at[2:2 + 2 * couples:2].set(receiver + moved)
    return lengths[jax.random.permutation(jax.random.fold_in(own_key, 2), amount)]


def bell_draw(rng, shape, spread, limit, pieces=(), kind=jnp.bfloat16):
    values = jax.random.normal(rng, shape, jnp.float32) * spread
    if len(pieces) > 0:
        values = level_of(rng, shape, pieces, -0.22, 0.18) * values
    return jnp.clip(values, min=-limit, max=limit).astype(kind)


def setup_inputs(seed: int = 0) -> dict:
    streams_of = jax.random.split(jax.random.key(seed), 22)
    activations = bell_draw(streams_of[0], (SEQS, LENGTH, D), 1.0, 6.0, ((0, 8), (1, 4)))
    cotangent = bell_draw(streams_of[1], (SEQS, LENGTH, D), 1.0, 6.0, ((0, 8), (1, 4)))
    segments = jax.vmap(lambda own: jnp.searchsorted(jnp.cumsum(uneven_parts(own, DOCS, LENGTH, DOC_MOST, 1)), jnp.arange(LENGTH), side="right"))(jax.random.split(streams_of[2], SEQS)).reshape((SEQS, LENGTH)).astype(jnp.int32)
    padding = touch_ends((jax.random.randint(streams_of[3], (SEQS, LENGTH), 0, 16) < 15).astype(jnp.int32), jax.random.fold_in(streams_of[3], 1), 0, 1)
    step_count = jax.random.randint(streams_of[4], (1,), 1, 1000).astype(jnp.int32)
    learn_rate = jnp.clip(jnp.exp(jax.random.uniform(streams_of[5], (1,), jnp.float32, math.log(0.005), math.log(0.02))), 0.005, 0.02)
    gain_before = jnp.clip(1.0 + 0.1 * jax.random.normal(streams_of[6], (D,), jnp.float32), 0.5, 1.5).astype(jnp.bfloat16)
    shift_before = bell_draw(streams_of[7], (D,), 0.3, 2.0)
    joint_weight = bell_draw(streams_of[8], (D, 3 * D), D ** -0.5, 0.1875)
    joint_bias = bell_draw(streams_of[9], (2 * D,), 0.3, 2.0)
    mixer_weight = bell_draw(streams_of[10], (D, D), (D // 16) ** -0.5, 0.75)
    mixer_bias = bell_draw(streams_of[11], (D,), 0.3, 2.0)
    gain_middle = jnp.clip(1.0 + 0.1 * jax.random.normal(streams_of[12], (D,), jnp.float32), 0.5, 1.5).astype(jnp.bfloat16)
    shift_middle = bell_draw(streams_of[13], (D,), 0.3, 2.0)
    expand_weight = bell_draw(streams_of[14], (D, FF), D ** -0.5, 0.1875)
    expand_bias = bell_draw(streams_of[15], (FF,), 0.5, 3.0)
    reduce_weight = bell_draw(streams_of[16], (FF, D), FF ** -0.5, 0.09375)
    reduce_bias = bell_draw(streams_of[17], (D,), 0.3, 2.0)
    master_weights = bell_draw(streams_of[18], (NPARAM,), 0.01, 0.06, ((0, 32),), jnp.float32)
    first_moment = bell_draw(streams_of[19], (NPARAM,), 1.0, 6.0, ((0, 32),), jnp.float32)
    second_moment = jnp.clip(jnp.exp(math.log(1000.0) - 6.9077553 * jax.random.uniform(streams_of[20], (NPARAM,), jnp.float32) ** level_of(streams_of[20], (NPARAM,), ((0, 32),), -0.2, 0.2)), 1.0, 1000.0)
    return {"activations": activations, "cotangent": cotangent, "segments": segments, "padding": padding, "step_count": step_count, "learn_rate": learn_rate, "gain_before": gain_before, "shift_before": shift_before, "joint_weight": joint_weight, "joint_bias": joint_bias, "mixer_weight": mixer_weight, "mixer_bias": mixer_bias, "gain_middle": gain_middle, "shift_middle": shift_middle, "expand_weight": expand_weight, "expand_bias": expand_bias, "reduce_weight": reduce_weight, "reduce_bias": reduce_bias, "master_weights": master_weights, "first_moment": first_moment, "second_moment": second_moment}


beta_first = 0.9
beta_second = 0.95
adam_epsilon = 1e-08
weight_decay = 0.1
norm_epsilon = 1e-05
masked_score = -1e+30

@jax.custom_vjp
def low(v):
    return lax.optimization_barrier(v.astype(jnp.bfloat16)).astype(jnp.float32)

@jax.custom_vjp
def low_back(v):
    return v

def low_keep(v):
    return (low(v), None)

def low_pass(kept, grad):
    return (grad,)

def back_keep(v):
    return (v, None)

def back_low(kept, grad):
    return (low(grad),)
low.defvjp(low_keep, low_pass)
low_back.defvjp(back_keep, back_low)

def matmul(left, right):
    return jnp.einsum('nld,de->nle', left, right, precision=lax.Precision.HIGHEST)

def normalize(values, gain, shift):
    center = values - lax.optimization_barrier(jnp.mean(values, -1, keepdims=True))
    variance = lax.optimization_barrier(jnp.mean(center * center, -1, keepdims=True))
    return center * lax.rsqrt(variance + norm_epsilon) * gain + shift

def attend_one(items):
    query4, key4, value4, seg_row, pad_row = items
    places = jnp.arange(LENGTH, dtype=jnp.int32)
    distance = (places[:, None] - places[None, :]).astype(jnp.float32)
    slopes = jnp.exp2(-8.0 * (jnp.arange(HEADS, dtype=jnp.float32) + 1.0) / HEADS)
    raw = jnp.einsum('qhd,khd->hqk', query4, key4, precision=lax.Precision.HIGHEST)
    scores = low_back(raw * (1.0 / math.sqrt(HEAD_DIM)) - slopes[:, None, None] * distance[None])
    itself = places[None, :] == places[:, None]
    allowed = (seg_row[:, None] == seg_row[None, :]) & (places[None, :] <= places[:, None]) & ((pad_row[None, :] == 1) | itself)
    allowed = allowed[None]
    row_top = lax.optimization_barrier(jnp.max(jnp.where(allowed, scores, masked_score), -1, keepdims=True))
    expo = jnp.exp(jnp.where(allowed, scores - row_top, masked_score))
    probs = low(expo / lax.optimization_barrier(jnp.sum(expo, -1, keepdims=True)))
    return jnp.einsum('hqk,khd->qhd', probs, value4, precision=lax.Precision.HIGHEST)

def forward(params, inputs, seg_rows, pad_rows):
    gain_one, shift_one, joint_w, joint_b, mixer_w, mixer_b, gain_two, shift_two, expand_w, expand_b, reduce_w, reduce_b = params
    width = inputs.shape[-1]
    normed_one = low(normalize(inputs, gain_one, shift_one))
    joint = matmul(normed_one, joint_w)
    query = low(low_back(joint[..., :width] + joint_b[:width]))
    keys = low(low_back(joint[..., width:2 * width]))
    values = low(low_back(joint[..., 2 * width:] + joint_b[width:]))
    shape4 = inputs.shape[:2] + (HEADS, HEAD_DIM)
    attended = lax.map(jax.checkpoint(attend_one), (query.reshape(shape4), keys.reshape(shape4), values.reshape(shape4), seg_rows, pad_rows))
    attended = low(low_back(attended.reshape(inputs.shape)))
    resid = inputs + low_back(matmul(attended, mixer_w) + mixer_b)
    normed_two = low(normalize(resid, gain_two, shift_two))
    hidden = low_back(matmul(normed_two, expand_w) + expand_b)
    act = low(jax.nn.gelu(hidden, approximate=True))
    return resid + low_back(matmul(act, reduce_w) + reduce_b)

def reference(activations, cotangent, segments, padding, step_count, learn_rate, gain_before, shift_before, joint_weight, joint_bias, mixer_weight, mixer_bias, gain_middle, shift_middle, expand_weight, expand_bias, reduce_weight, reduce_bias, master_weights, first_moment, second_moment):
    params = tuple((param.astype(jnp.float32) for param in (gain_before, shift_before, joint_weight, joint_bias, mixer_weight, mixer_bias, gain_middle, shift_middle, expand_weight, expand_bias, reduce_weight, reduce_bias)))
    pairs = SEQS // 2
    inputs = activations.astype(jnp.float32).reshape(pairs, 2, LENGTH, D)
    cots = cotangent.astype(jnp.float32).reshape(pairs, 2, LENGTH, D)
    seg_all = segments.reshape(pairs, 2, LENGTH)
    pad_all = padding.reshape(pairs, 2, LENGTH)

    def pair_step(totals, batch):
        inputs_in, cot_in, seg_in, pad_in = batch
        result, pull = jax.vjp(lambda params_in, values_in: forward(params_in, values_in, seg_in, pad_in), params, inputs_in)
        grads, input_grad = pull(cot_in)
        totals = tuple((total + single for total, single in zip(totals, grads)))
        return (totals, (result.astype(jnp.bfloat16), input_grad.astype(jnp.bfloat16)))
    zeros = tuple((jnp.zeros_like(param) for param in params))
    totals, (results, input_grads) = lax.scan(pair_step, zeros, (inputs, cots, seg_all, pad_all))
    gradient = jnp.concatenate([total.reshape(-1) for total in totals])
    small_gradient = jnp.concatenate([totals[place].reshape(-1) for place in (0, 1, 3, 5, 6, 7, 9, 11)])
    moment_step = step_count[0].astype(jnp.float32)
    rate = learn_rate[0]
    fix_one = 1.0 - jnp.exp(moment_step * math.log(beta_first))
    fix_two = 1.0 - jnp.exp(moment_step * math.log(beta_second))
    updated_first = beta_first * first_moment + (1.0 - beta_first) * gradient
    updated_second = beta_second * second_moment + (1.0 - beta_second) * gradient * gradient
    updated_master = master_weights - rate * (updated_first / fix_one / (jnp.sqrt(updated_second / fix_two) + adam_epsilon) + weight_decay * master_weights)
    return (results.reshape(SEQS, LENGTH, D), input_grads.reshape(SEQS, LENGTH, D), updated_master, updated_first, updated_second, small_gradient)
```

```python
import functools
import math

import jax
import jax.numpy as jnp
from jax import lax
from jax.experimental import pallas as pl
from jax.experimental.pallas import tpu as pltpu
from jax.sharding import PartitionSpec as P

HEADS = 16
DOC_MOST = 800


beta_first = 0.9
beta_second = 0.95
adam_epsilon = 1e-08
weight_decay = 0.1
norm_epsilon = 1e-05
masked_score = -1e30


def shifted(block, axis, distance):
    devices = range(lax.axis_size(axis))
    route = [(i - distance, i) for i in devices if i - distance in devices]
    return lax.ppermute(block, axis, route)


def standardize(values):
    center = values - jnp.mean(values, -1, keepdims=True)
    spread = lax.rsqrt(jnp.mean(center * center, -1, keepdims=True) + norm_epsilon)
    return (center * spread, spread)


def norm_back(dnormed, normed, spread):
    return spread * (
        dnormed
        - jnp.mean(dnormed, -1, keepdims=True)
        - normed * jnp.mean(dnormed * normed, -1, keepdims=True)
    )


def window_mask(segments, padding, member, hop, block_len):
    places = jnp.arange(block_len, dtype=jnp.int32)
    source = member - hop
    query_place = member * block_len + places
    key_place = source * block_len + places
    start = jnp.maximum(source, 0) * block_len
    seg_query = lax.dynamic_slice_in_dim(segments, member * block_len, block_len, 1)
    seg_key = lax.dynamic_slice_in_dim(segments, start, block_len, 1)
    pad_key = lax.dynamic_slice_in_dim(padding, start, block_len, 1)
    earlier = key_place[None, None, :] <= query_place[None, :, None]
    itself = key_place[None, None, :] == query_place[None, :, None]
    allowed = (
        (seg_query[:, :, None] == seg_key[:, None, :])
        & earlier
        & ((pad_key[:, None, :] == 1) | itself)
        & (source >= 0)
    )
    distance = (query_place[:, None] - key_place[None, :]).astype(jnp.float32)
    return (allowed[:, None], distance)


def piece_scores(query4, key4, slopes, distance, score_scale):
    raw = jnp.einsum("sqhd,skhd->shqk", query4, key4, preferred_element_type=jnp.float32)
    return raw * score_scale - slopes[:, None, None] * distance[None]


def on_device_general(
    activations,
    cotangent,
    segments,
    padding,
    step_count,
    learn_rate,
    gain_before,
    shift_before,
    joint_weight,
    joint_bias,
    mixer_weight,
    mixer_bias,
    gain_middle,
    shift_middle,
    expand_weight,
    expand_bias,
    reduce_weight,
    reduce_bias,
    master_weights,
    first_moment,
    second_moment,
):
    seq_count, block_len, width = activations.shape
    head_size = width // HEADS
    row_count = seq_count * block_len
    shape4 = (seq_count, block_len, HEADS, head_size)
    score_scale = 1.0 / math.sqrt(head_size)
    group_size = lax.axis_size("group")
    member = lax.axis_index("group")
    reach = min((DOC_MOST + block_len - 2) // block_len, group_size - 1)
    slopes = jnp.exp2(-8.0 * (jnp.arange(HEADS, dtype=jnp.float32) + 1.0) / HEADS)
    inputs = activations.reshape(row_count, width).astype(jnp.float32)
    gain_one = gain_before.astype(jnp.float32)
    gain_two = gain_middle.astype(jnp.float32)
    normal_one, spread_one = standardize(inputs)
    normed_one = (normal_one * gain_one + shift_before.astype(jnp.float32)).astype(jnp.bfloat16)
    joint = jnp.dot(normed_one, joint_weight, preferred_element_type=jnp.float32)
    bias_joint = joint_bias.astype(jnp.float32)
    query_rows = (joint[:, :width] + bias_joint[:width]).astype(jnp.bfloat16)
    key_rows = joint[:, width : 2 * width].astype(jnp.bfloat16)
    value_rows = (joint[:, 2 * width :] + bias_joint[width:]).astype(jnp.bfloat16)
    own_piece = jnp.stack([key_rows, value_rows]).reshape(2, seq_count, block_len, width)
    query4 = query_rows.reshape(shape4)
    pieces = [own_piece]
    for hop in range(1, reach + 1):
        pieces.append(shifted(own_piece, "group", hop))
    row_top = jnp.full((seq_count, HEADS, block_len), masked_score, jnp.float32)
    row_total = jnp.zeros((seq_count, HEADS, block_len), jnp.float32)
    for hop in range(reach + 1):
        allowed, distance = window_mask(segments, padding, member, hop, block_len)
        scores = piece_scores(query4, pieces[hop][0].reshape(shape4), slopes, distance, score_scale)
        fresh = jnp.maximum(row_top, jnp.max(jnp.where(allowed, scores, masked_score), -1))
        row_total = row_total * jnp.exp(row_top - fresh) + jnp.sum(
            jnp.exp(jnp.where(allowed, scores - fresh[..., None], masked_score)), -1
        )
        row_top = fresh
    log_total = row_top + jnp.log(row_total)
    attended = jnp.zeros(shape4, jnp.float32)
    for hop in range(reach + 1):
        allowed, distance = window_mask(segments, padding, member, hop, block_len)
        scores = piece_scores(query4, pieces[hop][0].reshape(shape4), slopes, distance, score_scale)
        probs = jnp.exp(jnp.where(allowed, scores - log_total[..., None], masked_score)).astype(
            jnp.bfloat16
        )
        attended = attended + jnp.einsum(
            "shqk,skhd->sqhd",
            probs,
            pieces[hop][1].reshape(shape4),
            preferred_element_type=jnp.float32,
        )
    attended_low = attended.reshape(row_count, width).astype(jnp.bfloat16)
    resid = inputs + (
        jnp.dot(attended_low, mixer_weight, preferred_element_type=jnp.float32)
        + mixer_bias.astype(jnp.float32)
    )
    normal_two, spread_two = standardize(resid)
    normed_two = (normal_two * gain_two + shift_middle.astype(jnp.float32)).astype(jnp.bfloat16)
    hidden = jnp.dot(
        normed_two, expand_weight, preferred_element_type=jnp.float32
    ) + expand_bias.astype(jnp.float32)
    act = jax.nn.gelu(hidden, approximate=True).astype(jnp.bfloat16)
    result = resid + (
        jnp.dot(act, reduce_weight, preferred_element_type=jnp.float32)
        + reduce_bias.astype(jnp.float32)
    )
    output = result.astype(jnp.bfloat16).reshape(seq_count, block_len, width)
    cot_low = cotangent.reshape(row_count, width)
    cot_full = cot_low.astype(jnp.float32)
    reduce_grad = jnp.einsum("tf,td->fd", act, cot_low, preferred_element_type=jnp.float32)
    reduce_bias_grad = jnp.sum(cot_full, 0)
    dact = jnp.einsum("td,fd->tf", cot_low, reduce_weight, preferred_element_type=jnp.float32)
    gelu_pull = jax.vjp(lambda inner: jax.nn.gelu(inner, approximate=True), hidden)[1]
    dhidden = gelu_pull(dact)[0].astype(jnp.bfloat16)
    expand_grad = jnp.einsum("td,tf->df", normed_two, dhidden, preferred_element_type=jnp.float32)
    expand_bias_grad = jnp.sum(dhidden.astype(jnp.float32), 0)
    dnormed_two = jnp.einsum(
        "tf,df->td", dhidden, expand_weight, preferred_element_type=jnp.float32
    )
    gain_middle_grad = jnp.sum(dnormed_two * normal_two, 0)
    shift_middle_grad = jnp.sum(dnormed_two, 0)
    dresid = cot_full + norm_back(dnormed_two * gain_two, normal_two, spread_two)
    dbranch = dresid.astype(jnp.bfloat16)
    mixer_grad = jnp.einsum("td,te->de", attended_low, dbranch, preferred_element_type=jnp.float32)
    mixer_bias_grad = jnp.sum(dbranch.astype(jnp.float32), 0)
    dattended = jnp.einsum(
        "te,de->td", dbranch, mixer_weight, preferred_element_type=jnp.float32
    ).astype(jnp.bfloat16)
    dattended4 = dattended.reshape(shape4)
    row_delta = jnp.einsum("sqhd,sqhd->shq", dattended4.astype(jnp.float32), attended)
    dquery = jnp.zeros(shape4, jnp.float32)
    dkv_own = jnp.zeros((2, seq_count, block_len, width), jnp.float32)
    for hop in range(reach + 1):
        piece = pieces[hop]
        key4 = piece[0].reshape(shape4)
        value4 = piece[1].reshape(shape4)
        allowed, distance = window_mask(segments, padding, member, hop, block_len)
        scores = piece_scores(query4, key4, slopes, distance, score_scale)
        probs = jnp.exp(jnp.where(allowed, scores - log_total[..., None], masked_score))
        dvalue = jnp.einsum(
            "shqk,sqhd->skhd",
            probs.astype(jnp.bfloat16),
            dattended4,
            preferred_element_type=jnp.float32,
        )
        dprobs = jnp.einsum(
            "sqhd,skhd->shqk", dattended4, value4, preferred_element_type=jnp.float32
        )
        dscores = (probs * (dprobs - row_delta[..., None])).astype(jnp.bfloat16)
        dquery = dquery + jnp.einsum(
            "shqk,skhd->sqhd", dscores, key4, preferred_element_type=jnp.float32
        )
        dkey = (
            jnp.einsum("shqk,sqhd->skhd", dscores, query4, preferred_element_type=jnp.float32)
            * score_scale
        )
        returned = jnp.stack([dkey, dvalue]).reshape(2, seq_count, block_len, width)
        if hop == 0:
            dkv_own = returned
        else:
            dkv_own = dkv_own + shifted(returned.astype(jnp.bfloat16), "group", -hop).astype(
                returned.dtype
            )
    dquery_low = (dquery * score_scale).reshape(row_count, width).astype(jnp.bfloat16)
    dkey_low = dkv_own[0].reshape(row_count, width).astype(jnp.bfloat16)
    dvalue_low = dkv_own[1].reshape(row_count, width).astype(jnp.bfloat16)
    djoint = jnp.concatenate([dquery_low, dkey_low, dvalue_low], 1)
    joint_grad = jnp.einsum("td,te->de", normed_one, djoint, preferred_element_type=jnp.float32)
    joint_bias_grad = jnp.concatenate(
        [jnp.sum(dquery_low.astype(jnp.float32), 0), jnp.sum(dvalue_low.astype(jnp.float32), 0)]
    )
    dnormed_one = jnp.einsum("te,de->td", djoint, joint_weight, preferred_element_type=jnp.float32)
    gain_before_grad = jnp.sum(dnormed_one * normal_one, 0)
    shift_before_grad = jnp.sum(dnormed_one, 0)
    dinput = dresid + norm_back(dnormed_one * gain_one, normal_one, spread_one)
    input_gradient = dinput.astype(jnp.bfloat16).reshape(seq_count, block_len, width)
    listing = [
        gain_before_grad,
        shift_before_grad,
        joint_grad,
        joint_bias_grad,
        mixer_grad,
        mixer_bias_grad,
        gain_middle_grad,
        shift_middle_grad,
        expand_grad,
        expand_bias_grad,
        reduce_grad,
        reduce_bias_grad,
    ]
    gradient = jnp.concatenate([single.reshape(-1) for single in listing])
    small_list = [
        gain_before_grad,
        shift_before_grad,
        joint_bias_grad,
        mixer_bias_grad,
        gain_middle_grad,
        shift_middle_grad,
        expand_bias_grad,
        reduce_bias_grad,
    ]
    small_local = jnp.concatenate(small_list)
    share, small_share = (
        lax.psum_scatter(gradient, ("dp", "group"), scatter_dimension=0, tiled=True),
        lax.psum_scatter(small_local, ("dp", "group"), scatter_dimension=0, tiled=True),
    )
    moment_step = step_count[0].astype(jnp.float32)
    rate = learn_rate[0]
    fix_one = 1.0 - jnp.exp(moment_step * math.log(beta_first))
    fix_two = 1.0 - jnp.exp(moment_step * math.log(beta_second))
    updated_first = beta_first * first_moment + (1.0 - beta_first) * share
    updated_second = beta_second * second_moment + (1.0 - beta_second) * share * share
    updated_master = master_weights - rate * (
        updated_first / fix_one / (jnp.sqrt(updated_second / fix_two) + adam_epsilon)
        + weight_decay * master_weights
    )
    return (output, input_gradient, updated_master, updated_first, updated_second, small_share)


WIDTH = 1024
HIDDEN = 4096
TOKENS = 1024
LANES = 128
OWNED = 393600
OWNED_ROWS = OWNED // LANES
PIECE = 1568
HALF = PIECE // 2
JOINT_AT, MIXER_AT, EXPAND_AT, REDUCE_AT = 16, 12320, 16432, 32832
FLAT_ROWS = 49248
U_JOINT, U_JBIAS, U_MIXER, U_MBIAS, U_EXPAND, U_EBIAS, U_REDUCE, U_RBIAS = (
    2, 3074, 3076, 4100, 4103, 8199, 8203, 12299,
)


def section_shift(unit):
    return 8 if unit < U_JBIAS else 16 if unit < U_MBIAS else 20


def piece_start(owner):
    unit = OWNED_ROWS * owner // 8
    return (4 * unit + section_shift(unit)) // 16 * 16


def piece_offset(q, y, x):
    at = [piece_start(4 * q + k) // 16 for k in range(4)]
    row = (
        at[0] * (1 - y) * (1 - x) + at[1] * (1 - y) * x + at[2] * y * (1 - x) + at[3] * y * x
    )
    return pl.multiple_of(row * 16, 16)


MESH_ID = pl.DeviceIdType.MESH


def add_into(target, other):
    target[...] = (
        target[...].astype(jnp.float32) + other[...].astype(jnp.float32)
    ).astype(target.dtype)


def reduce_kernel(
    flat, small, own_out, peer_out, small_out,
    own_a, own_b, rx_a1, rx_b1, rx_a2, rx_b2, acc, rx_up, rx_dn, parting,
    small_mine, small_rx, small_z,
    load_sem, s1_send, s1_recv, s2_send, s2_recv, z_send, z_recv, last_sem, sm_send, sm_recv,
):
    dp = lax.axis_index("dp")
    me = lax.axis_index("group")
    z, c = dp // 2, dp % 2
    y, x = me // 2, me % 2
    x_near = (dp, 2 * y + (1 - x))
    y_near = (dp, 2 * (1 - y) + x)
    core_near = (2 * z + 1 - c, me)

    def z_at(d):
        return (2 * d + c, me)

    barrier = pltpu.get_barrier_semaphore()
    for near in (x_near, y_near, core_near) + tuple(z_at((z + d) % 4) for d in (1, 2, 3)):
        pl.semaphore_signal(barrier, inc=1, device_id=near, device_id_type=MESH_ID)
    pl.semaphore_wait(barrier, 6)

    def remote(src, dst, ssem, rsem, near):
        return pltpu.make_async_remote_copy(
            src_ref=src, dst_ref=dst, send_sem=ssem, recv_sem=rsem,
            device_id=near, device_id_type=MESH_ID,
        )

    order = [6, 7, 0, 1, 4, 5, 2, 3]

    def stage1(q):
        out = []
        for k in range(2):
            out.append(remote(
                flat.at[pl.ds(piece_offset(q, k, 1 - x), HALF)], rx_a1.at[q, k],
                s1_send.at[q, 0, k], s1_recv.at[q, 0, k], x_near,
            ))
            out.append(remote(
                flat.at[pl.ds(piece_offset(q, 1 - y, k) + HALF, HALF)], rx_b1.at[q, k],
                s1_send.at[q, 1, k], s1_recv.at[q, 1, k], y_near,
            ))
        return out

    def loads(q):
        out = []
        for k in range(2):
            out.append(pltpu.make_async_copy(
                flat.at[pl.ds(piece_offset(q, k, x), HALF)], own_a.at[q, k], load_sem.at[q, 0, k]
            ))
            out.append(pltpu.make_async_copy(
                flat.at[pl.ds(piece_offset(q, y, k) + HALF, HALF)], own_b.at[q, k],
                load_sem.at[q, 1, k],
            ))
        return out

    def stage2(q):
        return [
            remote(rx_a1.at[q, 1 - y], rx_a2.at[q], s2_send.at[q, 0], s2_recv.at[q, 0], y_near),
            remote(rx_b1.at[q, 1 - x], rx_b2.at[q], s2_send.at[q, 1], s2_recv.at[q, 1], x_near),
        ]

    def hop(q, up):
        return remote(
            acc.at[q], (rx_up if up else rx_dn).at[q],
            z_send.at[q, 0 if up else 1], z_recv.at[q, 0 if up else 1],
            z_at((z + 1) % 4 if up else (z + 3) % 4),
        )

    last = remote(parting, peer_out, last_sem.at[0], last_sem.at[1], core_near)

    def small_step(k):
        near = (core_near, x_near, y_near)[k]
        return remote(small_mine.at[k], small_rx.at[k], sm_send.at[k], sm_recv.at[k], near)

    def small_hop(d):
        return remote(small_mine.at[3], small_z.at[d - 1], sm_send.at[2 + d], sm_recv.at[2 + d], z_at((z + d) % 4))

    for q in order[:2]:
        for copy in stage1(q):
            copy.start()
    for q in order:
        for copy in loads(q):
            copy.start()
    small_mine[0] = small[...]
    small_step(0).start()

    for slot in range(8 + 6):
        if 2 <= slot + 2 < 8:
            for copy in stage1(order[slot]):
                copy.wait_send()
            for copy in stage1(order[slot + 2]):
                copy.start()
        elif slot < 8:
            for copy in stage1(order[slot]):
                copy.wait_send()
        if slot < 3:
            small_step(slot).wait()
            small_mine[slot + 1] = small_mine[slot] + small_rx[slot]
            if slot < 2:
                small_step(slot + 1).start()
            else:
                for d in (1, 2, 3):
                    small_hop(d).start()
        if slot == 5:
            for d in (1, 2, 3):
                small_hop(d).wait()
            pair = [small_mine[3], small_z[0], small_z[1], small_z[2]]
            even = pair[0] + pair[2]
            odd = pair[1] + pair[3]
            small_out[...] = even + odd
        if slot < 8:
            q = order[slot]
            for copy in loads(q):
                copy.wait()
            for copy in stage1(q):
                copy.wait_recv()
            add_into(rx_a1.at[q, 1 - y], own_a.at[q, 1 - y])
            add_into(rx_b1.at[q, 1 - x], own_b.at[q, 1 - x])
            for copy in stage2(q):
                copy.start()
            acc[q, 0] = (
                rx_a1[q, y].astype(jnp.float32) + own_a[q, y].astype(jnp.float32)
            ).astype(jnp.bfloat16)
            acc[q, 1] = (
                rx_b1[q, x].astype(jnp.float32) + own_b[q, x].astype(jnp.float32)
            ).astype(jnp.bfloat16)
        if 1 <= slot < 9:
            q = order[slot - 1]
            for copy in stage2(q):
                copy.wait()
            add_into(acc.at[q, 0], rx_a2.at[q])
            add_into(acc.at[q, 1], rx_b2.at[q])
        for step in range(8):
            q = order[step]
            aim = q // 2
            h = slot - (step + 1)
            if h < 0:
                continue
            if h < aim:
                @pl.when(z == h)
                def _():
                    if h > 0:
                        hop(q, True).wait_recv()
                        add_into(acc.at[q], rx_up.at[q])
                    hop(q, True).start()
            if h < 3 - aim:
                @pl.when(z == 3 - h)
                def _():
                    if h > 0:
                        hop(q, False).wait_recv()
                        add_into(acc.at[q], rx_dn.at[q])
                    hop(q, False).start()
            if h == max(aim, 3 - aim):
                @pl.when(z == aim)
                def _():
                    total = acc[q].astype(jnp.float32)
                    if aim > 0:
                        hop(q, True).wait_recv()
                        total = total + rx_up[q].astype(jnp.float32)
                    if aim < 3:
                        hop(q, False).wait_recv()
                        total = total + rx_dn[q].astype(jnp.float32)
                    total = total.reshape(PIECE, LANES)

                    @pl.when(c == q % 2)
                    def _():
                        own_out[...] = total

                    @pl.when(c != q % 2)
                    def _():
                        parting[...] = total
                        last.start()
    last.wait()
    for q in range(8):
        aim = q // 2
        for h in range(aim):
            @pl.when(z == h)
            def _():
                hop(q, True).wait_send()
        for h in range(3 - aim):
            @pl.when(z == 3 - h)
            def _():
                hop(q, False).wait_send()


def reduce_pieces(flat, small):
    bf = jnp.bfloat16
    return pl.pallas_call(
        reduce_kernel,
        out_shape=(
            jax.ShapeDtypeStruct((PIECE, LANES), jnp.float32),
            jax.ShapeDtypeStruct((PIECE, LANES), jnp.float32),
            jax.ShapeDtypeStruct(small.shape, jnp.float32),
        ),
        in_specs=[pl.BlockSpec(memory_space=pl.ANY), pl.BlockSpec(memory_space=pltpu.VMEM)],
        out_specs=[pl.BlockSpec(memory_space=pltpu.VMEM)] * 3,
        scratch_shapes=[
            pltpu.VMEM((8, 2, HALF, LANES), bf),
            pltpu.VMEM((8, 2, HALF, LANES), bf),
            pltpu.VMEM((8, 2, HALF, LANES), bf),
            pltpu.VMEM((8, 2, HALF, LANES), bf),
            pltpu.VMEM((8, HALF, LANES), bf),
            pltpu.VMEM((8, HALF, LANES), bf),
            pltpu.VMEM((8, 2, HALF, LANES), bf),
            pltpu.VMEM((8, 2, HALF, LANES), bf),
            pltpu.VMEM((8, 2, HALF, LANES), bf),
            pltpu.VMEM((PIECE, LANES), jnp.float32),
            pltpu.VMEM((4,) + small.shape, jnp.float32),
            pltpu.VMEM((3,) + small.shape, jnp.float32),
            pltpu.VMEM((3,) + small.shape, jnp.float32),
            pltpu.SemaphoreType.DMA((8, 2, 2)),
            pltpu.SemaphoreType.DMA((8, 2, 2)),
            pltpu.SemaphoreType.DMA((8, 2, 2)),
            pltpu.SemaphoreType.DMA((8, 2)),
            pltpu.SemaphoreType.DMA((8, 2)),
            pltpu.SemaphoreType.DMA((8, 2)),
            pltpu.SemaphoreType.DMA((8, 2)),
            pltpu.SemaphoreType.DMA((2,)),
            pltpu.SemaphoreType.DMA((6,)),
            pltpu.SemaphoreType.DMA((6,)),
        ],
        compiler_params=pltpu.CompilerParams(
            collective_id=0, has_side_effects=True, vmem_limit_bytes=48 << 20
        ),
    )(flat, small)


def core_swap(value):
    count = lax.axis_size("dp")
    return lax.ppermute(value, "dp", [(i, i ^ 1) for i in range(count)])


def plane_routes(dp_size, group_size):
    routes = []
    for turn in range(2):
        there = []
        for dp in range(dp_size):
            for g in range(group_size):
                k = 2 * (dp % 2) + (g + turn) % 2
                there.append((dp * group_size + g, (dp // 2 * 2 + g // 2) * group_size + k))
        routes.append(there)
    return routes


def to_chip(value, routes, group):
    came = [
        lax.ppermute(
            lax.dynamic_index_in_dim(value, (group + turn) % 2, 0, False),
            ("dp", "group"), routes[turn],
        )
        for turn in range(2)
    ]
    odd = group % 2 == 1
    return jnp.concatenate([jnp.where(odd, came[1], came[0]), jnp.where(odd, came[0], came[1])], 0)


def from_chip(value, routes, group):
    half = value.shape[0] // 2
    odd = group % 2 == 1
    first, second = value[:half], value[half:]
    sent = [jnp.where(odd, second, first), jnp.where(odd, first, second)]
    came = [
        lax.ppermute(sent[turn], ("dp", "group"), [(b, a) for a, b in routes[turn]])
        for turn in range(2)
    ]
    return jnp.stack([jnp.where(odd, came[1], came[0]), jnp.where(odd, came[0], came[1])])


def in_order(c, own, peer, axis):
    return jnp.where(
        c == 0, jnp.concatenate([own, peer], axis), jnp.concatenate([peer, own], axis)
    )


def half_columns(weight, c, block, axis=1):
    count = weight.shape[axis] // (2 * block)
    shape = weight.shape[:axis] + (count, 2, block) + weight.shape[axis + 1 :]
    taken = lax.dynamic_index_in_dim(weight.reshape(shape), c, axis + 1, False)
    return taken.reshape(weight.shape[:axis] + (count * block,) + weight.shape[axis + 1 :])


def nn(a, b):
    return lax.dot_general(a, b, (((1,), (0,)), ((), ())), preferred_element_type=jnp.float32)


def nt(a, b):
    return lax.dot_general(a, b, (((1,), (1,)), ((), ())), preferred_element_type=jnp.float32)


def tn(a, b):
    return lax.dot_general(a, b, (((0,), (0,)), ((), ())), preferred_element_type=jnp.float32)


def attention_forward(query, keys, values, last, slopes):
    q4 = query.reshape(TOKENS, 8, 64)
    k4 = keys.reshape(TOKENS, 8, 64)
    v4 = values.reshape(TOKENS, 8, 64)
    scores = jnp.einsum("qhd,khd->hqk", q4, k4, preferred_element_type=jnp.float32)
    places = jnp.arange(TOKENS, dtype=jnp.int32)
    distance = (places[:, None] - places[None, :]).astype(jnp.float32)
    allowed = (places[:, None] >= places[None, :]) & (places[:, None] <= last[None, :])
    scores = scores - slopes[:, None, None] * distance[None]
    scores = jnp.where(allowed[None], scores, masked_score)
    top = jnp.max(scores, -1, keepdims=True)
    expo = jnp.exp(scores - top)
    total = jnp.sum(expo, -1, keepdims=True)
    probs = expo / total
    out = jnp.einsum("hqk,khd->qhd", probs.astype(jnp.bfloat16), v4, preferred_element_type=jnp.float32)
    return out.reshape(TOKENS, 512).astype(jnp.bfloat16), probs


def attention_backward(query, keys, values, attended, dattended, probs):
    q4 = query.reshape(TOKENS, 8, 64)
    k4 = keys.reshape(TOKENS, 8, 64)
    v4 = values.reshape(TOKENS, 8, 64)
    d4 = dattended.reshape(TOKENS, 8, 64)
    a4 = attended.reshape(TOKENS, 8, 64)
    delta = jnp.einsum("qhd,qhd->hq", d4.astype(jnp.float32), a4.astype(jnp.float32))
    dprobs = jnp.einsum("qhd,khd->hqk", d4, v4, preferred_element_type=jnp.float32)
    ds = (probs * (dprobs - delta[..., None])).astype(jnp.bfloat16)
    dq = jnp.einsum("hqk,khd->qhd", ds, k4, preferred_element_type=jnp.float32) * 0.125
    dk = jnp.einsum("hqk,qhd->khd", ds, q4, preferred_element_type=jnp.float32)
    dv = jnp.einsum("hqk,qhd->khd", probs.astype(jnp.bfloat16), d4, preferred_element_type=jnp.float32)
    return [t.reshape(TOKENS, 512).astype(jnp.bfloat16) for t in (dq, dk, dv)]


def owned_gradient(own, peer, small, c, owner):
    first = jnp.where(c == 0, own, peer).reshape(PIECE // 4, 1, 4, LANES)
    second = jnp.where(c == 0, peer, own).reshape(PIECE // 4, 1, 4, LANES)
    rows = jnp.concatenate([first, second], 1).reshape(2 * PIECE, LANES)
    begin = OWNED_ROWS * owner
    unit = begin // 8
    shift = jnp.where(unit < U_JBIAS, 8, jnp.where(unit < U_MBIAS, 16, 20))
    start = (4 * unit + shift) // 16 * 16

    def window(moved):
        at = begin + 2 * moved - 2 * start
        padded = jnp.pad(rows, ((16, 64), (0, 0)))
        return lax.dynamic_slice_in_dim(padded, jnp.clip(at + 16, 0, 2 * PIECE + 80 - OWNED_ROWS), OWNED_ROWS, 0)

    end_unit = (begin + OWNED_ROWS - 1) // 8
    shift_end = jnp.where(end_unit < U_JBIAS, 8, jnp.where(end_unit < U_MBIAS, 16, 20))
    flat_row = begin + jnp.arange(OWNED_ROWS, dtype=jnp.int32)
    u = flat_row // 8
    moved_row = jnp.where(u < U_JBIAS, 8, jnp.where(u < U_MBIAS, 16, 20))
    big = jnp.where((moved_row == shift)[:, None], window(shift), window(shift_end))
    places = ((0, 2, 0), (3074, 3076, 16), (4100, 4103, 32), (8199, 8203, 56), (12299, 12300, 88))
    result = big
    for first_unit, end, at in places:
        inside = (u >= first_unit) & (u < end)
        shift_small = at + begin - 8 * first_unit
        padded = jnp.pad(small, ((OWNED_ROWS, OWNED_ROWS), (0, 0)))
        part = lax.dynamic_slice_in_dim(
            padded, jnp.clip(OWNED_ROWS + shift_small, 0, OWNED_ROWS + 96), OWNED_ROWS, 0
        )
        result = jnp.where(inside[:, None], part, result)
    return result


def on_device_chip(
    dp_size, group_size,
    activations, cotangent, segments, padding, step_count, learn_rate,
    gain_before, shift_before, joint_weight, joint_bias, mixer_weight, mixer_bias,
    gain_middle, shift_middle, expand_weight, expand_bias, reduce_weight, reduce_bias,
    master_weights, first_moment, second_moment,
):
    f32, bf16 = jnp.float32, jnp.bfloat16
    dp = lax.axis_index("dp")
    group = lax.axis_index("group")
    c = dp % 2
    routes = plane_routes(dp_size, group_size)
    x_own = to_chip(activations, routes, group)
    cot_own = to_chip(cotangent, routes, group)
    x_all = in_order(c, x_own, core_swap(x_own), 0)
    cot_all = in_order(c, cot_own, core_swap(cot_own), 0)
    marks = jnp.stack([segments, padding])
    marks = jnp.where(c == group // 2, marks, core_swap(marks))
    marks = lax.dynamic_index_in_dim(marks, group % 2, 1, False)
    seg, pad = marks[0], marks[1]
    places = jnp.arange(TOKENS, dtype=jnp.int32)
    last = jnp.sum((seg[:, None] <= seg[None, :]).astype(jnp.int32), 0) - 1
    last = jnp.where(pad == 1, last, places)
    slopes = jnp.exp2(-8.0 * (jnp.arange(8, dtype=f32) + 8.0 * c.astype(f32) + 1.0) / HEADS)

    joint_half = half_columns(joint_weight, c, 512)
    expand_half = half_columns(expand_weight, c, 512)
    reduce_half = half_columns(reduce_weight, c, 512, 0)
    gain_one, gain_two = gain_before.astype(f32), gain_middle.astype(f32)
    bias = half_columns(joint_bias[None], c, 512)[0].astype(f32)

    normal_one, _ = standardize(x_all.astype(f32))
    normed_one = (normal_one * gain_one + shift_before.astype(f32)).astype(bf16)
    joint = nn(normed_one, joint_half)
    query = ((joint[:, :512] + bias[:512]) * 0.125).astype(bf16)
    keys = joint[:, 512:1024].astype(bf16)
    values = (joint[:, 1024:] + bias[512:]).astype(bf16)
    attended, probs = attention_forward(query, keys, values, last, slopes)
    attended_all = in_order(c, attended, core_swap(attended), 1)
    attended_own = lax.dynamic_slice_in_dim(attended_all, 512 * c, 512, 0)
    inputs = x_own.astype(f32)
    resid = inputs + (nn(attended_own, mixer_weight) + mixer_bias.astype(f32))
    normal_two, spread_two = standardize(resid)
    normed_two = (normal_two * gain_two + shift_middle.astype(f32)).astype(bf16)
    normed_two_all = in_order(c, normed_two, core_swap(normed_two), 0)
    hidden = nn(normed_two_all, expand_half) + half_columns(expand_bias[None], c, 512)[0].astype(f32)
    act_full, gelu_pull = jax.vjp(lambda inner: jax.nn.gelu(inner, approximate=True), hidden)
    act = act_full.astype(bf16)
    partial = nn(act, reduce_half)
    mine = lax.dynamic_slice_in_dim(partial, 512 * c, 512, 0)
    other = lax.dynamic_slice_in_dim(partial, 512 * (1 - c), 512, 0)
    result = resid + ((mine + core_swap(other)) + reduce_bias.astype(f32))
    output = from_chip(result.astype(bf16), routes, group)

    dact = nt(cot_all, reduce_half)
    dhidden = gelu_pull(dact)[0].astype(bf16)
    act_all = jnp.where(
        c == 0,
        jnp.stack([act.reshape(TOKENS, 4, 512), core_swap(act).reshape(TOKENS, 4, 512)], 2),
        jnp.stack([core_swap(act).reshape(TOKENS, 4, 512), act.reshape(TOKENS, 4, 512)], 2),
    ).reshape(TOKENS, HIDDEN)
    cot_cols = lax.dynamic_slice_in_dim(cot_all, 512 * c, 512, 1)
    reduce_grad = tn(act_all, cot_cols)
    expand_grad = tn(normed_two_all, dhidden)
    partial = nt(dhidden, expand_half)
    mine = lax.dynamic_slice_in_dim(partial, 512 * c, 512, 0)
    other = lax.dynamic_slice_in_dim(partial, 512 * (1 - c), 512, 0)
    dnormed_two = mine + core_swap(other)
    cot_full = cot_own.astype(f32)
    dresid = cot_full + norm_back(dnormed_two * gain_two, normal_two, spread_two)
    dbranch = dresid.astype(bf16)
    dbranch_all = in_order(c, dbranch, core_swap(dbranch), 0)
    mixer_rows = lax.dynamic_slice_in_dim(mixer_weight, 512 * c, 512, 0)
    dattended = nt(dbranch_all, mixer_rows).astype(bf16)
    mixer_grad = tn(attended_all, lax.dynamic_slice_in_dim(dbranch_all, 512 * c, 512, 1))
    dq, dk, dv = attention_backward(query, keys, values, attended, dattended, probs)
    djoint = jnp.concatenate([dq, dk, dv], 1)
    joint_grad = tn(normed_one, djoint)
    partial = nt(djoint, joint_half)
    mine = lax.dynamic_slice_in_dim(partial, 512 * c, 512, 0)
    other = lax.dynamic_slice_in_dim(partial, 512 * (1 - c), 512, 0)
    dnormed_one = mine + core_swap(other)
    normal_own, spread_own = standardize(inputs)
    dinput = dresid + norm_back(dnormed_one * gain_one, normal_own, spread_own)
    input_gradient = from_chip(dinput.astype(bf16), routes, group)

    def placed(half):
        count = half.shape[0] // 512
        return jnp.where(
            c == 0,
            jnp.stack([half.reshape(count, 512), jnp.zeros((count, 512), f32)], 1),
            jnp.stack([jnp.zeros((count, 512), f32), half.reshape(count, 512)], 1),
        ).reshape(-1)

    small = jnp.concatenate([
        jnp.sum(dnormed_one * normal_own, 0), jnp.sum(dnormed_one, 0),
        placed(jnp.sum(dq.astype(f32), 0)), placed(jnp.sum(dv.astype(f32), 0)),
        jnp.sum(dbranch.astype(f32), 0),
        jnp.sum(dnormed_two * normal_two, 0), jnp.sum(dnormed_two, 0),
        placed(jnp.sum(dhidden.astype(f32), 0)),
        jnp.sum(cot_full, 0),
    ]).reshape(96, LANES)

    def rows_of(grad):
        return grad.astype(bf16).reshape(-1, LANES)

    def gap(count):
        return jnp.zeros((count, LANES), bf16)

    flat = jnp.concatenate([
        gap(JOINT_AT), rows_of(joint_grad),
        gap(MIXER_AT - JOINT_AT - 12288), rows_of(mixer_grad),
        gap(EXPAND_AT - MIXER_AT - 4096), rows_of(expand_grad),
        gap(REDUCE_AT - EXPAND_AT - 16384), rows_of(reduce_grad),
        gap(FLAT_ROWS - REDUCE_AT - 16384),
    ], 0)
    own, peer, small_sum = reduce_pieces(flat, small)
    owner = dp * group_size + group
    share = owned_gradient(own, peer, small_sum, c, owner).reshape(-1)
    small_share = lax.dynamic_slice_in_dim(small_sum, 3 * owner, 3, 0).reshape(-1)

    moment_step = step_count[0].astype(f32)
    rate = learn_rate[0]
    fix_one = 1.0 - jnp.exp(moment_step * math.log(beta_first))
    fix_two = 1.0 - jnp.exp(moment_step * math.log(beta_second))
    updated_first = beta_first * first_moment + (1.0 - beta_first) * share
    updated_second = beta_second * second_moment + (1.0 - beta_second) * share * share
    updated_master = master_weights - rate * (
        updated_first / fix_one / (jnp.sqrt(updated_second / fix_two) + adam_epsilon)
        + weight_decay * master_weights
    )
    return (output, input_gradient, updated_master, updated_first, updated_second, small_share)


def on_device(dp_size, group_size, activations, *rest):
    if (dp_size, group_size) == (8, 4) and activations.shape == (2, 256, WIDTH):
        return on_device_chip(dp_size, group_size, activations, *rest)
    return on_device_general(activations, *rest)


def solution(mesh):
    in_specs = (
        P("dp", "group", None),
        P("dp", "group", None),
        P("dp", None),
        P("dp", None),
        P(),
        P(),
        P(),
        P(),
        P(),
        P(),
        P(),
        P(),
        P(),
        P(),
        P(),
        P(),
        P(),
        P(),
        P(("dp", "group")),
        P(("dp", "group")),
        P(("dp", "group")),
    )
    out_specs = (
        P("dp", "group", None),
        P("dp", "group", None),
        P(("dp", "group")),
        P(("dp", "group")),
        P(("dp", "group")),
        P(("dp", "group")),
    )
    return jax.shard_map(
        functools.partial(on_device, mesh.shape["dp"], mesh.shape["group"]), mesh=mesh, in_specs=in_specs, out_specs=out_specs, check_vma=False
    )
```

```python
import functools
import math

import jax
import jax.numpy as jnp
from jax import lax
from jax.experimental import pallas as pl
from jax.experimental.pallas import tpu as pltpu
from jax.sharding import PartitionSpec as P

HEADS = 16
DOC_MOST = 800


beta_first = 0.9
beta_second = 0.95
adam_epsilon = 1e-08
weight_decay = 0.1
norm_epsilon = 1e-05
masked_score = -1e30


def shifted(block, axis, distance):
    devices = range(lax.axis_size(axis))
    route = [(i - distance, i) for i in devices if i - distance in devices]
    return lax.ppermute(block, axis, route)


def standardize(values):
    center = values - jnp.mean(values, -1, keepdims=True)
    spread = lax.rsqrt(jnp.mean(center * center, -1, keepdims=True) + norm_epsilon)
    return (center * spread, spread)


def norm_back(dnormed, normed, spread):
    return spread * (
        dnormed
        - jnp.mean(dnormed, -1, keepdims=True)
        - normed * jnp.mean(dnormed * normed, -1, keepdims=True)
    )


def window_mask(segments, padding, member, hop, block_len):
    places = jnp.arange(block_len, dtype=jnp.int32)
    source = member - hop
    query_place = member * block_len + places
    key_place = source * block_len + places
    start = jnp.maximum(source, 0) * block_len
    seg_query = lax.dynamic_slice_in_dim(segments, member * block_len, block_len, 1)
    seg_key = lax.dynamic_slice_in_dim(segments, start, block_len, 1)
    pad_key = lax.dynamic_slice_in_dim(padding, start, block_len, 1)
    earlier = key_place[None, None, :] <= query_place[None, :, None]
    itself = key_place[None, None, :] == query_place[None, :, None]
    allowed = (
        (seg_query[:, :, None] == seg_key[:, None, :])
        & earlier
        & ((pad_key[:, None, :] == 1) | itself)
        & (source >= 0)
    )
    distance = (query_place[:, None] - key_place[None, :]).astype(jnp.float32)
    return (allowed[:, None], distance)


def piece_scores(query4, key4, slopes, distance, score_scale):
    raw = jnp.einsum("sqhd,skhd->shqk", query4, key4, preferred_element_type=jnp.float32)
    return raw * score_scale - slopes[:, None, None] * distance[None]


def on_device_general(
    activations,
    cotangent,
    segments,
    padding,
    step_count,
    learn_rate,
    gain_before,
    shift_before,
    joint_weight,
    joint_bias,
    mixer_weight,
    mixer_bias,
    gain_middle,
    shift_middle,
    expand_weight,
    expand_bias,
    reduce_weight,
    reduce_bias,
    master_weights,
    first_moment,
    second_moment,
):
    seq_count, block_len, width = activations.shape
    head_size = width // HEADS
    row_count = seq_count * block_len
    shape4 = (seq_count, block_len, HEADS, head_size)
    score_scale = 1.0 / math.sqrt(head_size)
    group_size = lax.axis_size("group")
    member = lax.axis_index("group")
    reach = min((DOC_MOST + block_len - 2) // block_len, group_size - 1)
    slopes = jnp.exp2(-8.0 * (jnp.arange(HEADS, dtype=jnp.float32) + 1.0) / HEADS)
    inputs = activations.reshape(row_count, width).astype(jnp.float32)
    gain_one = gain_before.astype(jnp.float32)
    gain_two = gain_middle.astype(jnp.float32)
    normal_one, spread_one = standardize(inputs)
    normed_one = (normal_one * gain_one + shift_before.astype(jnp.float32)).astype(jnp.bfloat16)
    joint = jnp.dot(normed_one, joint_weight, preferred_element_type=jnp.float32)
    bias_joint = joint_bias.astype(jnp.float32)
    query_rows = (joint[:, :width] + bias_joint[:width]).astype(jnp.bfloat16)
    key_rows = joint[:, width : 2 * width].astype(jnp.bfloat16)
    value_rows = (joint[:, 2 * width :] + bias_joint[width:]).astype(jnp.bfloat16)
    own_piece = jnp.stack([key_rows, value_rows]).reshape(2, seq_count, block_len, width)
    query4 = query_rows.reshape(shape4)
    pieces = [own_piece]
    for hop in range(1, reach + 1):
        pieces.append(shifted(own_piece, "group", hop))
    row_top = jnp.full((seq_count, HEADS, block_len), masked_score, jnp.float32)
    row_total = jnp.zeros((seq_count, HEADS, block_len), jnp.float32)
    for hop in range(reach + 1):
        allowed, distance = window_mask(segments, padding, member, hop, block_len)
        scores = piece_scores(query4, pieces[hop][0].reshape(shape4), slopes, distance, score_scale)
        fresh = jnp.maximum(row_top, jnp.max(jnp.where(allowed, scores, masked_score), -1))
        row_total = row_total * jnp.exp(row_top - fresh) + jnp.sum(
            jnp.exp(jnp.where(allowed, scores - fresh[..., None], masked_score)), -1
        )
        row_top = fresh
    log_total = row_top + jnp.log(row_total)
    attended = jnp.zeros(shape4, jnp.float32)
    for hop in range(reach + 1):
        allowed, distance = window_mask(segments, padding, member, hop, block_len)
        scores = piece_scores(query4, pieces[hop][0].reshape(shape4), slopes, distance, score_scale)
        probs = jnp.exp(jnp.where(allowed, scores - log_total[..., None], masked_score)).astype(
            jnp.bfloat16
        )
        attended = attended + jnp.einsum(
            "shqk,skhd->sqhd",
            probs,
            pieces[hop][1].reshape(shape4),
            preferred_element_type=jnp.float32,
        )
    attended_low = attended.reshape(row_count, width).astype(jnp.bfloat16)
    resid = inputs + (
        jnp.dot(attended_low, mixer_weight, preferred_element_type=jnp.float32)
        + mixer_bias.astype(jnp.float32)
    )
    normal_two, spread_two = standardize(resid)
    normed_two = (normal_two * gain_two + shift_middle.astype(jnp.float32)).astype(jnp.bfloat16)
    hidden = jnp.dot(
        normed_two, expand_weight, preferred_element_type=jnp.float32
    ) + expand_bias.astype(jnp.float32)
    act = jax.nn.gelu(hidden, approximate=True).astype(jnp.bfloat16)
    result = resid + (
        jnp.dot(act, reduce_weight, preferred_element_type=jnp.float32)
        + reduce_bias.astype(jnp.float32)
    )
    output = result.astype(jnp.bfloat16).reshape(seq_count, block_len, width)
    cot_low = cotangent.reshape(row_count, width)
    cot_full = cot_low.astype(jnp.float32)
    reduce_grad = jnp.einsum("tf,td->fd", act, cot_low, preferred_element_type=jnp.float32)
    reduce_bias_grad = jnp.sum(cot_full, 0)
    dact = jnp.einsum("td,fd->tf", cot_low, reduce_weight, preferred_element_type=jnp.float32)
    gelu_pull = jax.vjp(lambda inner: jax.nn.gelu(inner, approximate=True), hidden)[1]
    dhidden = gelu_pull(dact)[0].astype(jnp.bfloat16)
    expand_grad = jnp.einsum("td,tf->df", normed_two, dhidden, preferred_element_type=jnp.float32)
    expand_bias_grad = jnp.sum(dhidden.astype(jnp.float32), 0)
    dnormed_two = jnp.einsum(
        "tf,df->td", dhidden, expand_weight, preferred_element_type=jnp.float32
    )
    gain_middle_grad = jnp.sum(dnormed_two * normal_two, 0)
    shift_middle_grad = jnp.sum(dnormed_two, 0)
    dresid = cot_full + norm_back(dnormed_two * gain_two, normal_two, spread_two)
    dbranch = dresid.astype(jnp.bfloat16)
    mixer_grad = jnp.einsum("td,te->de", attended_low, dbranch, preferred_element_type=jnp.float32)
    mixer_bias_grad = jnp.sum(dbranch.astype(jnp.float32), 0)
    dattended = jnp.einsum(
        "te,de->td", dbranch, mixer_weight, preferred_element_type=jnp.float32
    ).astype(jnp.bfloat16)
    dattended4 = dattended.reshape(shape4)
    row_delta = jnp.einsum("sqhd,sqhd->shq", dattended4.astype(jnp.float32), attended)
    dquery = jnp.zeros(shape4, jnp.float32)
    dkv_own = jnp.zeros((2, seq_count, block_len, width), jnp.float32)
    for hop in range(reach + 1):
        piece = pieces[hop]
        key4 = piece[0].reshape(shape4)
        value4 = piece[1].reshape(shape4)
        allowed, distance = window_mask(segments, padding, member, hop, block_len)
        scores = piece_scores(query4, key4, slopes, distance, score_scale)
        probs = jnp.exp(jnp.where(allowed, scores - log_total[..., None], masked_score))
        dvalue = jnp.einsum(
            "shqk,sqhd->skhd",
            probs.astype(jnp.bfloat16),
            dattended4,
            preferred_element_type=jnp.float32,
        )
        dprobs = jnp.einsum(
            "sqhd,skhd->shqk", dattended4, value4, preferred_element_type=jnp.float32
        )
        dscores = (probs * (dprobs - row_delta[..., None])).astype(jnp.bfloat16)
        dquery = dquery + jnp.einsum(
            "shqk,skhd->sqhd", dscores, key4, preferred_element_type=jnp.float32
        )
        dkey = (
            jnp.einsum("shqk,sqhd->skhd", dscores, query4, preferred_element_type=jnp.float32)
            * score_scale
        )
        returned = jnp.stack([dkey, dvalue]).reshape(2, seq_count, block_len, width)
        if hop == 0:
            dkv_own = returned
        else:
            dkv_own = dkv_own + shifted(returned.astype(jnp.bfloat16), "group", -hop).astype(
                returned.dtype
            )
    dquery_low = (dquery * score_scale).reshape(row_count, width).astype(jnp.bfloat16)
    dkey_low = dkv_own[0].reshape(row_count, width).astype(jnp.bfloat16)
    dvalue_low = dkv_own[1].reshape(row_count, width).astype(jnp.bfloat16)
    djoint = jnp.concatenate([dquery_low, dkey_low, dvalue_low], 1)
    joint_grad = jnp.einsum("td,te->de", normed_one, djoint, preferred_element_type=jnp.float32)
    joint_bias_grad = jnp.concatenate(
        [jnp.sum(dquery_low.astype(jnp.float32), 0), jnp.sum(dvalue_low.astype(jnp.float32), 0)]
    )
    dnormed_one = jnp.einsum("te,de->td", djoint, joint_weight, preferred_element_type=jnp.float32)
    gain_before_grad = jnp.sum(dnormed_one * normal_one, 0)
    shift_before_grad = jnp.sum(dnormed_one, 0)
    dinput = dresid + norm_back(dnormed_one * gain_one, normal_one, spread_one)
    input_gradient = dinput.astype(jnp.bfloat16).reshape(seq_count, block_len, width)
    listing = [
        gain_before_grad,
        shift_before_grad,
        joint_grad,
        joint_bias_grad,
        mixer_grad,
        mixer_bias_grad,
        gain_middle_grad,
        shift_middle_grad,
        expand_grad,
        expand_bias_grad,
        reduce_grad,
        reduce_bias_grad,
    ]
    gradient = jnp.concatenate([single.reshape(-1) for single in listing])
    small_list = [
        gain_before_grad,
        shift_before_grad,
        joint_bias_grad,
        mixer_bias_grad,
        gain_middle_grad,
        shift_middle_grad,
        expand_bias_grad,
        reduce_bias_grad,
    ]
    small_local = jnp.concatenate(small_list)
    share, small_share = (
        lax.psum_scatter(gradient, ("dp", "group"), scatter_dimension=0, tiled=True),
        lax.psum_scatter(small_local, ("dp", "group"), scatter_dimension=0, tiled=True),
    )
    moment_step = step_count[0].astype(jnp.float32)
    rate = learn_rate[0]
    fix_one = 1.0 - jnp.exp(moment_step * math.log(beta_first))
    fix_two = 1.0 - jnp.exp(moment_step * math.log(beta_second))
    updated_first = beta_first * first_moment + (1.0 - beta_first) * share
    updated_second = beta_second * second_moment + (1.0 - beta_second) * share * share
    updated_master = master_weights - rate * (
        updated_first / fix_one / (jnp.sqrt(updated_second / fix_two) + adam_epsilon)
        + weight_decay * master_weights
    )
    return (output, input_gradient, updated_master, updated_first, updated_second, small_share)


WIDTH = 1024
HIDDEN = 4096
TOKENS = 1024
LANES = 128
OWNED = 393600
OWNED_ROWS = OWNED // LANES
PIECE = 1568
HALF = PIECE // 2
JOINT_AT, MIXER_AT, EXPAND_AT, REDUCE_AT = 16, 12320, 16432, 32832
FLAT_ROWS = 49248
U_JOINT, U_JBIAS, U_MIXER, U_MBIAS, U_EXPAND, U_EBIAS, U_REDUCE, U_RBIAS = (
    2, 3074, 3076, 4100, 4103, 8199, 8203, 12299,
)


def section_shift(unit):
    return 8 if unit < U_JBIAS else 16 if unit < U_MBIAS else 20


def piece_start(owner):
    unit = OWNED_ROWS * owner // 8
    return (4 * unit + section_shift(unit)) // 16 * 16


def piece_offset(q, y, x):
    at = [piece_start(4 * q + k) // 16 for k in range(4)]
    row = (
        at[0] * (1 - y) * (1 - x) + at[1] * (1 - y) * x + at[2] * y * (1 - x) + at[3] * y * x
    )
    return pl.multiple_of(row * 16, 16)


MESH_ID = pl.DeviceIdType.MESH


def add_into(target, other):
    target[...] = (
        target[...].astype(jnp.float32) + other[...].astype(jnp.float32)
    ).astype(target.dtype)


EARLY = (3, 4, 5, 6, 7)


def reduce_kernel(
    flat, early_a, early_b, small, own_out, peer_out, small_out,
    own_a, own_b, rx_a1, rx_b1, rx_a2, rx_b2, acc, rx_up, rx_dn, parting,
    small_mine, small_rx, small_z,
    load_sem, s1_send, s1_recv, s2_send, s2_recv, z_send, z_recv, last_sem, sm_send, sm_recv,
):
    dp = lax.axis_index("dp")
    me = lax.axis_index("group")
    z, c = dp // 2, dp % 2
    y, x = me // 2, me % 2
    x_near = (dp, 2 * y + (1 - x))
    y_near = (dp, 2 * (1 - y) + x)
    core_near = (2 * z + 1 - c, me)

    def z_at(d):
        return (2 * d + c, me)

    barrier = pltpu.get_barrier_semaphore()
    for near in (x_near, y_near, core_near) + tuple(z_at((z + d) % 4) for d in (1, 2, 3)):
        pl.semaphore_signal(barrier, inc=1, device_id=near, device_id_type=MESH_ID)
    pl.semaphore_wait(barrier, 6)

    def remote(src, dst, ssem, rsem, near):
        return pltpu.make_async_remote_copy(
            src_ref=src, dst_ref=dst, send_sem=ssem, recv_sem=rsem,
            device_id=near, device_id_type=MESH_ID,
        )

    order = [6, 7, 0, 1, 4, 5, 2, 3]
    late = [0, 1, 2]

    def stage1(q):
        out = []
        for k in range(2):
            out.append(remote(
                flat.at[pl.ds(piece_offset(q, k, 1 - x), HALF)], rx_a1.at[q, k],
                s1_send.at[q, 0, k], s1_recv.at[q, 0, k], x_near,
            ))
            out.append(remote(
                flat.at[pl.ds(piece_offset(q, 1 - y, k) + HALF, HALF)], rx_b1.at[q, k],
                s1_send.at[q, 1, k], s1_recv.at[q, 1, k], y_near,
            ))
        return out

    def loads(q):
        out = []
        for k in range(2):
            out.append(pltpu.make_async_copy(
                flat.at[pl.ds(piece_offset(q, k, x), HALF)], own_a.at[q, k], load_sem.at[q, 0, k]
            ))
            out.append(pltpu.make_async_copy(
                flat.at[pl.ds(piece_offset(q, y, k) + HALF, HALF)], own_b.at[q, k],
                load_sem.at[q, 1, k],
            ))
            if q in EARLY:
                out.append(pltpu.make_async_copy(
                    early_a.at[q - 3, k], rx_a1.at[q, k], load_sem.at[q, 2, k]
                ))
                out.append(pltpu.make_async_copy(
                    early_b.at[q - 3, k], rx_b1.at[q, k], load_sem.at[q, 3, k]
                ))
        return out

    def stage2(q):
        return [
            remote(rx_a1.at[q, 1 - y], rx_a2.at[q], s2_send.at[q, 0], s2_recv.at[q, 0], y_near),
            remote(rx_b1.at[q, 1 - x], rx_b2.at[q], s2_send.at[q, 1], s2_recv.at[q, 1], x_near),
        ]

    def hop(q, up):
        return remote(
            acc.at[q], (rx_up if up else rx_dn).at[q],
            z_send.at[q, 0 if up else 1], z_recv.at[q, 0 if up else 1],
            z_at((z + 1) % 4 if up else (z + 3) % 4),
        )

    last = remote(parting, peer_out, last_sem.at[0], last_sem.at[1], core_near)

    def small_step(k):
        near = (core_near, x_near, y_near)[k]
        return remote(small_mine.at[k], small_rx.at[k], sm_send.at[k], sm_recv.at[k], near)

    def small_hop(d):
        return remote(small_mine.at[3], small_z.at[d - 1], sm_send.at[2 + d], sm_recv.at[2 + d], z_at((z + d) % 4))

    for q in late[:2]:
        for copy in stage1(q):
            copy.start()
    for q in order:
        for copy in loads(q):
            copy.start()
    small_mine[0] = small[...]
    small_step(0).start()

    for slot in range(8 + 6):
        if slot == 3:
            for copy in stage1(late[2]):
                copy.start()
        if slot < 3:
            small_step(slot).wait()
            small_mine[slot + 1] = small_mine[slot] + small_rx[slot]
            if slot < 2:
                small_step(slot + 1).start()
            else:
                for d in (1, 2, 3):
                    small_hop(d).start()
        if slot == 5:
            for d in (1, 2, 3):
                small_hop(d).wait()
            pair = [small_mine[3], small_z[0], small_z[1], small_z[2]]
            even = pair[0] + pair[2]
            odd = pair[1] + pair[3]
            small_out[...] = even + odd
        if slot < 8:
            q = order[slot]
            for copy in loads(q):
                copy.wait()
            if q in late:
                for copy in stage1(q):
                    copy.wait_recv()
            add_into(rx_a1.at[q, 1 - y], own_a.at[q, 1 - y])
            add_into(rx_b1.at[q, 1 - x], own_b.at[q, 1 - x])
            for copy in stage2(q):
                copy.start()
            acc[q, 0] = (
                rx_a1[q, y].astype(jnp.float32) + own_a[q, y].astype(jnp.float32)
            ).astype(jnp.bfloat16)
            acc[q, 1] = (
                rx_b1[q, x].astype(jnp.float32) + own_b[q, x].astype(jnp.float32)
            ).astype(jnp.bfloat16)
        if 1 <= slot < 9:
            q = order[slot - 1]
            for copy in stage2(q):
                copy.wait()
            add_into(acc.at[q, 0], rx_a2.at[q])
            add_into(acc.at[q, 1], rx_b2.at[q])
        for step in range(8):
            q = order[step]
            aim = q // 2
            h = slot - (step + 1)
            if h < 0:
                continue
            if h < aim:
                @pl.when(z == h)
                def _():
                    if h > 0:
                        hop(q, True).wait_recv()
                        add_into(acc.at[q], rx_up.at[q])
                    hop(q, True).start()
            if h < 3 - aim:
                @pl.when(z == 3 - h)
                def _():
                    if h > 0:
                        hop(q, False).wait_recv()
                        add_into(acc.at[q], rx_dn.at[q])
                    hop(q, False).start()
            if h == max(aim, 3 - aim):
                @pl.when(z == aim)
                def _():
                    total = acc[q].astype(jnp.float32)
                    if aim > 0:
                        hop(q, True).wait_recv()
                        total = total + rx_up[q].astype(jnp.float32)
                    if aim < 3:
                        hop(q, False).wait_recv()
                        total = total + rx_dn[q].astype(jnp.float32)
                    total = total.reshape(PIECE, LANES)

                    @pl.when(c == q % 2)
                    def _():
                        own_out[...] = total

                    @pl.when(c != q % 2)
                    def _():
                        parting[...] = total
                        last.start()
    last.wait()
    for q in late:
        for copy in stage1(q):
            copy.wait_send()
    for q in range(8):
        aim = q // 2
        for h in range(aim):
            @pl.when(z == h)
            def _():
                hop(q, True).wait_send()
        for h in range(3 - aim):
            @pl.when(z == 3 - h)
            def _():
                hop(q, False).wait_send()


def reduce_pieces(flat, early_a, early_b, small):
    bf = jnp.bfloat16
    return pl.pallas_call(
        reduce_kernel,
        out_shape=(
            jax.ShapeDtypeStruct((PIECE, LANES), jnp.float32),
            jax.ShapeDtypeStruct((PIECE, LANES), jnp.float32),
            jax.ShapeDtypeStruct(small.shape, jnp.float32),
        ),
        in_specs=[pl.BlockSpec(memory_space=pl.ANY)] * 3 + [pl.BlockSpec(memory_space=pltpu.VMEM)],
        out_specs=[pl.BlockSpec(memory_space=pltpu.VMEM)] * 3,
        scratch_shapes=[
            pltpu.VMEM((8, 2, HALF, LANES), bf),
            pltpu.VMEM((8, 2, HALF, LANES), bf),
            pltpu.VMEM((8, 2, HALF, LANES), bf),
            pltpu.VMEM((8, 2, HALF, LANES), bf),
            pltpu.VMEM((8, HALF, LANES), bf),
            pltpu.VMEM((8, HALF, LANES), bf),
            pltpu.VMEM((8, 2, HALF, LANES), bf),
            pltpu.VMEM((8, 2, HALF, LANES), bf),
            pltpu.VMEM((8, 2, HALF, LANES), bf),
            pltpu.VMEM((PIECE, LANES), jnp.float32),
            pltpu.VMEM((4,) + small.shape, jnp.float32),
            pltpu.VMEM((3,) + small.shape, jnp.float32),
            pltpu.VMEM((3,) + small.shape, jnp.float32),
            pltpu.SemaphoreType.DMA((8, 4, 2)),
            pltpu.SemaphoreType.DMA((8, 2, 2)),
            pltpu.SemaphoreType.DMA((8, 2, 2)),
            pltpu.SemaphoreType.DMA((8, 2)),
            pltpu.SemaphoreType.DMA((8, 2)),
            pltpu.SemaphoreType.DMA((8, 2)),
            pltpu.SemaphoreType.DMA((8, 2)),
            pltpu.SemaphoreType.DMA((2,)),
            pltpu.SemaphoreType.DMA((6,)),
            pltpu.SemaphoreType.DMA((6,)),
        ],
        compiler_params=pltpu.CompilerParams(
            collective_id=0, has_side_effects=True, vmem_limit_bytes=48 << 20
        ),
    )(flat, early_a, early_b, small)


def early_kernel(flat, out_a, out_b, sem):
    me = lax.axis_index("group")
    y, x = me // 2, me % 2
    copies = []
    for q in EARLY:
        for k in range(2):
            copies.append(pltpu.make_async_copy(
                flat.at[pl.ds(piece_offset(q, k, 1 - x), HALF)], out_a.at[q - 3, k],
                sem.at[q - 3, 0, k],
            ))
            copies.append(pltpu.make_async_copy(
                flat.at[pl.ds(piece_offset(q, 1 - y, k) + HALF, HALF)], out_b.at[q - 3, k],
                sem.at[q - 3, 1, k],
            ))
    for copy in copies:
        copy.start()
    for copy in copies:
        copy.wait()


def early_pieces(flat):
    shape = jax.ShapeDtypeStruct((5, 2, HALF, LANES), jnp.bfloat16)
    return pl.pallas_call(
        early_kernel,
        out_shape=(shape, shape),
        in_specs=[pl.BlockSpec(memory_space=pl.ANY)],
        out_specs=[pl.BlockSpec(memory_space=pltpu.VMEM)] * 2,
        scratch_shapes=[pltpu.SemaphoreType.DMA((5, 2, 2))],
        cost_estimate=pl.CostEstimate(flops=0, bytes_accessed=8 << 20, transcendentals=0),
    )(flat)


def core_swap(value):
    count = lax.axis_size("dp")
    return lax.ppermute(value, "dp", [(i, i ^ 1) for i in range(count)])


def plane_routes(dp_size, group_size):
    routes = []
    for turn in range(2):
        there = []
        for dp in range(dp_size):
            for g in range(group_size):
                k = 2 * (dp % 2) + (g + turn) % 2
                there.append((dp * group_size + g, (dp // 2 * 2 + g // 2) * group_size + k))
        routes.append(there)
    return routes


def to_chip(value, routes, group):
    came = [
        lax.ppermute(
            lax.dynamic_index_in_dim(value, (group + turn) % 2, 0, False),
            ("dp", "group"), routes[turn],
        )
        for turn in range(2)
    ]
    odd = group % 2 == 1
    return jnp.concatenate([jnp.where(odd, came[1], came[0]), jnp.where(odd, came[0], came[1])], 0)


def from_chip(value, routes, group):
    half = value.shape[0] // 2
    odd = group % 2 == 1
    first, second = value[:half], value[half:]
    sent = [jnp.where(odd, second, first), jnp.where(odd, first, second)]
    came = [
        lax.ppermute(sent[turn], ("dp", "group"), [(b, a) for a, b in routes[turn]])
        for turn in range(2)
    ]
    return jnp.stack([jnp.where(odd, came[1], came[0]), jnp.where(odd, came[0], came[1])])


def in_order(c, own, peer, axis):
    return jnp.where(
        c == 0, jnp.concatenate([own, peer], axis), jnp.concatenate([peer, own], axis)
    )


def half_columns(weight, c, axis=1):
    count = weight.shape[axis] // 1024
    return jnp.concatenate(
        [lax.dynamic_slice_in_dim(weight, 1024 * k + 512 * c, 512, axis) for k in range(count)],
        axis,
    )


def nn(a, b):
    return lax.dot_general(a, b, (((1,), (0,)), ((), ())), preferred_element_type=jnp.float32)


def nt(a, b):
    return lax.dot_general(a, b, (((1,), (1,)), ((), ())), preferred_element_type=jnp.float32)


def tn(a, b):
    return lax.dot_general(a, b, (((0,), (0,)), ((), ())), preferred_element_type=jnp.float32)


def head_lanes(value, h):
    lane = lax.broadcasted_iota(jnp.int32, (1, LANES), 1)
    return jnp.where(lane // 64 == h, value, jnp.zeros_like(value))


def forward_kernel(slopes, q_ref, k_ref, v_ref, dist_ref, out_ref, lse_ref, s_ref, p_ref, vt_ref, ot_ref):
    pair = pl.program_id(0)
    vt_ref[...] = v_ref[...].astype(jnp.float32).T.astype(jnp.bfloat16)

    def head(h, carry):
        slope = slopes[2 * pair + h]
        for qb in range(4):
            cols = pl.ds(qb * 256, 256)
            queries = head_lanes(q_ref[cols, :], h)
            top = None
            for kb in range(qb + 1):
                rows = pl.ds(kb * 256, 256)
                s = nt(k_ref[rows, :], queries) - slope * dist_ref[rows, cols]
                s_ref[rows, :] = s
                high = jnp.max(s, 0, keepdims=True)
                top = high if top is None else jnp.maximum(top, high)
            total = None
            for kb in range(qb + 1):
                rows = pl.ds(kb * 256, 256)
                p = jnp.exp(s_ref[rows, :] - top)
                more = jnp.sum(p, 0, keepdims=True)
                total = more if total is None else total + more
                p_ref[rows, :] = p.astype(jnp.bfloat16)
            span = pl.ds(0, 256 * (qb + 1))
            out = nn(vt_ref[:, span], p_ref[span, :]) / total
            row = lax.broadcasted_iota(jnp.int32, (LANES, 1), 0)
            ot_ref[:, cols] = jnp.where(row // 64 == h, out, ot_ref[:, cols])
            lse_ref[0, pl.ds(h, 1), cols] = top + jnp.log(total)
        return carry

    ot_ref[...] = jnp.zeros_like(ot_ref)
    lax.fori_loop(0, 2, head, 0)
    out_ref[...] = ot_ref[...].T.astype(jnp.bfloat16)


def joint_sides():
    return [
        pl.BlockSpec((TOKENS, LANES), lambda i, *_: (0, i)),
        pl.BlockSpec((TOKENS, LANES), lambda i, *_: (0, 4 + i)),
        pl.BlockSpec((TOKENS, LANES), lambda i, *_: (0, 8 + i)),
    ]


def attention_forward(joint, dist, slopes):
    sides = joint_sides()
    side = pl.BlockSpec((TOKENS, LANES), lambda i, *_: (0, i))
    return pl.pallas_call(
        forward_kernel,
        out_shape=(
            jax.ShapeDtypeStruct((TOKENS, 512), jnp.bfloat16),
            jax.ShapeDtypeStruct((4, 2, TOKENS), jnp.float32),
        ),
        grid_spec=pltpu.PrefetchScalarGridSpec(
            num_scalar_prefetch=1,
            grid=(4,),
            in_specs=sides + [pl.BlockSpec((TOKENS, TOKENS), lambda i, *_: (0, 0))],
            out_specs=[side, pl.BlockSpec((1, 2, TOKENS), lambda i, *_: (i, 0, 0))],
            scratch_shapes=[
                pltpu.VMEM((TOKENS, 256), jnp.float32),
                pltpu.VMEM((TOKENS, 256), jnp.bfloat16),
                pltpu.VMEM((LANES, TOKENS), jnp.bfloat16),
                pltpu.VMEM((LANES, TOKENS), jnp.float32),
            ],
        ),
        compiler_params=pltpu.CompilerParams(vmem_limit_bytes=48 << 20),
        cost_estimate=pl.CostEstimate(
            flops=4 * 8 * 655360 * 64, bytes_accessed=8 << 20, transcendentals=8 * 655360
        ),
    )(slopes, joint, joint, joint, dist)


def backward_kernel(
    slopes, q_ref, k_ref, v_ref, o_ref, do_ref, dist_ref, lse_ref,
    d_ref, p_ref, ds_ref, kt_ref, dqt_ref, dk_acc, dv_acc, delta_ref,
):
    pair = pl.program_id(0)
    kt_ref[...] = k_ref[...].astype(jnp.float32).T.astype(jnp.bfloat16)
    product = (o_ref[...].astype(jnp.float32) * do_ref[...].astype(jnp.float32)).T
    delta_ref[0:1, :] = jnp.sum(product[:64], 0, keepdims=True)
    delta_ref[1:2, :] = jnp.sum(product[64:], 0, keepdims=True)
    dk_acc[...] = jnp.zeros_like(dk_acc)
    dv_acc[...] = jnp.zeros_like(dv_acc)
    dqt_ref[...] = jnp.zeros_like(dqt_ref)

    def head(h, carry):
        slope = slopes[2 * pair + h]
        for qb in range(4):
            cols = pl.ds(qb * 256, 256)
            queries = head_lanes(q_ref[cols, :], h)
            grads = head_lanes(do_ref[cols, :], h)
            lse = lse_ref[0, pl.ds(h, 1), cols]
            delta = delta_ref[pl.ds(h, 1), cols]
            for kb in range(qb + 1):
                rows = pl.ds(kb * 256, 256)
                s = nt(k_ref[rows, :], queries) - slope * dist_ref[rows, cols]
                p = jnp.exp(s - lse)
                p_ref[rows, :] = p.astype(jnp.bfloat16)
                dp = nt(v_ref[rows, :], grads)
                ds_ref[rows, :] = (p * (dp - delta)).astype(jnp.bfloat16)
            span = pl.ds(0, 256 * (qb + 1))
            dv_acc[span, :] += nn(p_ref[span, :], grads)
            dk_acc[span, :] += nn(ds_ref[span, :], queries)
            dq = nn(kt_ref[:, span], ds_ref[span, :])
            row = lax.broadcasted_iota(jnp.int32, (LANES, 1), 0)
            dqt_ref[:, cols] = jnp.where(row // 64 == h, dq, dqt_ref[:, cols])
        return carry

    lax.fori_loop(0, 2, head, 0)
    d_ref[0] = (dqt_ref[...] * 0.125).T.astype(jnp.bfloat16)
    d_ref[1] = dk_acc[...].astype(jnp.bfloat16)
    d_ref[2] = dv_acc[...].astype(jnp.bfloat16)


def attention_backward(joint, attended, dattended, dist, lse, slopes):
    side = pl.BlockSpec((TOKENS, LANES), lambda i, *_: (0, i))
    return pl.pallas_call(
        backward_kernel,
        out_shape=jax.ShapeDtypeStruct((3, TOKENS, 512), jnp.bfloat16),
        grid_spec=pltpu.PrefetchScalarGridSpec(
            num_scalar_prefetch=1,
            grid=(4,),
            in_specs=joint_sides() + [side] * 2 + [
                pl.BlockSpec((TOKENS, TOKENS), lambda i, *_: (0, 0)),
                pl.BlockSpec((1, 2, TOKENS), lambda i, *_: (i, 0, 0)),
            ],
            out_specs=pl.BlockSpec((3, TOKENS, LANES), lambda i, *_: (0, 0, i)),
            scratch_shapes=[
                pltpu.VMEM((TOKENS, 256), jnp.bfloat16),
                pltpu.VMEM((TOKENS, 256), jnp.bfloat16),
                pltpu.VMEM((LANES, TOKENS), jnp.bfloat16),
                pltpu.VMEM((LANES, TOKENS), jnp.float32),
                pltpu.VMEM((TOKENS, LANES), jnp.float32),
                pltpu.VMEM((TOKENS, LANES), jnp.float32),
                pltpu.VMEM((8, TOKENS), jnp.float32),
            ],
        ),
        compiler_params=pltpu.CompilerParams(vmem_limit_bytes=48 << 20),
        cost_estimate=pl.CostEstimate(
            flops=1 << 20, bytes_accessed=1 << 20, transcendentals=0
        ),
    )(slopes, joint, joint, joint, attended, dattended, dist, lse)


def gradient_kernel(marks, left, right, *flats):
    flat = flats[-1]
    if len(right.shape) == 3:
        blocks = [tn(left[...], right[p]).astype(jnp.bfloat16) for p in range(right.shape[0])]
        block = jnp.concatenate(blocks, 1)
    else:
        block = tn(left[...], right[...]).astype(jnp.bfloat16)
    flat[...] = block.reshape(flat.shape)


def gradient_rows(left, right, marks, flat, at, tall, step):
    tokens, wide = left.shape
    if right.ndim == 3:
        parts, _, columns = right.shape
        right_spec = pl.BlockSpec((parts, tokens, columns), lambda i, m: (0, 0, 0))
        columns = parts * columns
    else:
        columns = 512 if step == 2 or right.shape[1] == 1024 else right.shape[1]
        right_spec = pl.BlockSpec((tokens, columns), lambda i, m: (0, m[0]))
    count = tall * columns // LANES
    return pl.pallas_call(
        gradient_kernel,
        out_shape=jax.ShapeDtypeStruct((FLAT_ROWS, LANES), jnp.bfloat16),
        grid_spec=pltpu.PrefetchScalarGridSpec(
            num_scalar_prefetch=1,
            grid=(wide // tall,),
            in_specs=[
                pl.BlockSpec((tokens, tall), lambda i, m: (0, i)),
                right_spec,
            ] + ([] if flat is None else [pl.BlockSpec(memory_space=pl.ANY)]),
            out_specs=pl.BlockSpec(
                (pl.Element(count), pl.Element(LANES)),
                lambda i, m: (pl.multiple_of(at + (step * i + m[1]) * count, 16), 0),
            ),
        ),
        input_output_aliases={} if flat is None else {3: 0},
        compiler_params=pltpu.CompilerParams(vmem_limit_bytes=48 << 20),
        cost_estimate=pl.CostEstimate(
            flops=1 << 20, bytes_accessed=1 << 20, transcendentals=0
        ),
    )(*((marks, left, right) + (() if flat is None else (flat,))))


def middle_kernel(
    attended, x_own, cot, vectors, expand_bias, mixer_hbm, expand_hbm, reduce_hbm,
    result, dresid, dattended, sums, expand_sums, flat,
    mixer, expand, reduce, att_rx, resid, normal, spread, normed, act, act_rx, dhidden,
    dn_own, dn_part, dn_rx, out_part, out_rx, dbranch, blocks,
    weight_sem, block_sem, send_sem, recv_sem, act_send, act_recv,
):
    f32, bf16 = jnp.float32, jnp.bfloat16
    dp = lax.axis_index("dp")
    me = lax.axis_index("group")
    c = dp % 2
    near = (dp + 1 - 2 * c, me)
    own = pl.ds(pl.multiple_of(512 * c, 512), 512)
    other = pl.ds(pl.multiple_of(512 * (1 - c), 512), 512)

    weights = [pltpu.make_async_copy(mixer_hbm, mixer, weight_sem.at[0])]
    for k in range(4):
        part = pl.ds(pl.multiple_of(512 * (2 * k + c), 512), 512)
        weights.append(pltpu.make_async_copy(
            expand_hbm.at[:, part], expand.at[:, pl.ds(512 * k, 512)], weight_sem.at[1 + k]
        ))
    for k in range(4):
        part = pl.ds(pl.multiple_of(512 * (2 * k + c), 512), 512)
        weights.append(pltpu.make_async_copy(
            reduce_hbm.at[part], reduce.at[pl.ds(512 * k, 512)], weight_sem.at[5 + k]
        ))
    for copy in weights:
        copy.start()

    barrier = pltpu.get_barrier_semaphore()
    pl.semaphore_signal(barrier, inc=1, device_id=near, device_id_type=MESH_ID)
    pl.semaphore_wait(barrier, 1)

    def swap(i, src, dst):
        return pltpu.make_async_remote_copy(
            src_ref=src, dst_ref=dst, send_sem=send_sem.at[i], recv_sem=recv_sem.at[i],
            device_id=near, device_id_type=MESH_ID,
        )

    att_swap = swap(0, attended, att_rx)
    normed_swap = swap(1, normed.at[own], normed.at[own])
    dn_swap = swap(2, dn_part, dn_rx)
    out_swap = swap(3, out_part, out_rx)
    branch_swap = swap(4, dbranch.at[own], dbranch.at[own])
    att_swap.start()

    mixer_bias, gain, shift, reduce_bias = (vectors[k : k + 1, :] for k in range(4))

    weights[0].wait()
    resid[...] = nn(attended[own, :], mixer[own, :]) + (x_own[...].astype(f32) + mixer_bias)
    att_swap.wait_recv()
    resid[...] += nn(att_rx[own, :], mixer[other, :])

    def norm_rows(i, carry):
        rows = pl.ds(pl.multiple_of(128 * i, 128), 128)
        here = pl.ds(pl.multiple_of(512 * c + 128 * i, 128), 128)
        values = resid[rows, :]
        center = values - jnp.mean(values, -1, keepdims=True)
        factor = lax.rsqrt(jnp.mean(center * center, -1, keepdims=True) + norm_epsilon)
        unit = center * factor
        normal[rows, :] = unit
        spread[rows, :] = jnp.broadcast_to(factor, (128, LANES))
        normed[here, :] = (unit * gain + shift).astype(bf16)
        return carry

    lax.fori_loop(0, 4, norm_rows, 0)
    normed_swap.start()

    def act_swap(half, k):
        rows = pl.ds(pl.multiple_of(512 * half, 512), 512)
        cols = pl.ds(512 * k, 512)
        return pltpu.make_async_remote_copy(
            src_ref=act.at[rows, cols], dst_ref=act_rx.at[rows, cols],
            send_sem=act_send.at[half, k], recv_sem=act_recv.at[half, k],
            device_id=near, device_id_type=MESH_ID,
        )

    root = math.sqrt(2.0 / math.pi)

    def hidden_block(half, k, first):
        rows = pl.ds(pl.multiple_of(512 * half, 512), 512)
        cols = pl.ds(512 * k, 512)
        u = nn(normed[rows, :], expand[:, cols]) + expand_bias[k : k + 1, :]
        dact = nt(cot[rows, :], reduce[cols, :])
        square = u * u
        t = jnp.tanh(u * (root + (root * 0.044715) * square))
        up = 0.5 + 0.5 * t
        act[rows, cols] = (u * up).astype(bf16)
        slope = up + (0.5 * u) * (1.0 - t * t) * (root + (3.0 * root * 0.044715) * square)
        dh = (dact * slope).astype(bf16)
        dhidden[rows, cols] = dh
        total = jnp.sum(dh.astype(f32), 0, keepdims=True)
        if first:
            expand_sums[k : k + 1, :] = total
        else:
            expand_sums[k : k + 1, :] += total
        act_swap(half, k).start()

    for k in range(4):
        weights[1 + k].wait()
        weights[5 + k].wait()
        hidden_block(c, k, True)
    normed_swap.wait_recv()
    for k in range(4):
        hidden_block(1 - c, k, False)

    dn_part[...] = nt(dhidden[other, :], expand[...])
    dn_swap.start()
    out_part[...] = nn(act[other, :], reduce[...]).astype(bf16)
    out_swap.start()

    def out_copy(slot, part, at):
        return pltpu.make_async_copy(
            blocks.at[slot, pl.ds(2048 * part, 2048)], flat.at[pl.ds(pl.multiple_of(at, 16), 2048)],
            block_sem.at[slot, part],
        )

    right = pl.ds(pl.multiple_of(512 * c, 512), 512)
    sent = []

    def emit(block, places):
        slot = len(sent) % 2
        if len(sent) >= 2:
            for part, at in enumerate(sent[-2]):
                out_copy(slot, part, at).wait()
        blocks[slot, : 2048 * len(places)] = block.astype(bf16).reshape(2048 * len(places), LANES)
        for part, at in enumerate(places):
            out_copy(slot, part, at).start()
        sent.append(places)

    for pair in range(2):
        emit(
            tn(act[:, 1024 * pair : 1024 * pair + 1024], cot[:, right]),
            [REDUCE_AT + 2048 * (2 * k + c) for k in (2 * pair, 2 * pair + 1)],
        )
    for i in range(4):
        emit(
            tn(normed[:, 256 * i : 256 * i + 256], dhidden[...]),
            [EXPAND_AT + 4096 * i, EXPAND_AT + 4096 * i + 2048],
        )
    for half in range(2):
        for k in range(4):
            act_swap(half, k).wait()
    for pair in range(2):
        emit(
            tn(act_rx[:, 1024 * pair : 1024 * pair + 1024], cot[:, right]),
            [REDUCE_AT + 2048 * (2 * k + 1 - c) for k in (2 * pair, 2 * pair + 1)],
        )

    dn_own[...] = nt(dhidden[own, :], expand[...])
    dn_swap.wait()
    sums[...] = jnp.zeros_like(sums)

    def back_rows(i, carry):
        rows = pl.ds(pl.multiple_of(128 * i, 128), 128)
        here = pl.ds(pl.multiple_of(512 * c + 128 * i, 128), 128)
        dn = dn_own[rows, :] + dn_rx[rows, :]
        unit = normal[rows, :]
        grad = cot[here, :].astype(f32)
        e = dn * gain
        down = grad + spread[rows, 0:1] * (
            e - jnp.mean(e, -1, keepdims=True) - unit * jnp.mean(e * unit, -1, keepdims=True)
        )
        dresid[rows, :] = down
        low = down.astype(bf16)
        dbranch[here, :] = low
        sums[0:1, :] += jnp.sum(low.astype(f32), 0, keepdims=True)
        sums[1:2, :] += jnp.sum(dn * unit, 0, keepdims=True)
        sums[2:3, :] += jnp.sum(dn, 0, keepdims=True)
        sums[3:4, :] += jnp.sum(grad, 0, keepdims=True)
        return carry

    lax.fori_loop(0, 4, back_rows, 0)
    branch_swap.start()
    dattended[own, :] = nt(dbranch[own, :], mixer[own, :]).astype(bf16)
    resid[...] += nn(act[own, :], reduce[...])
    out_swap.wait()
    result[...] = (resid[...] + (out_rx[...].astype(f32) + reduce_bias)).astype(bf16)
    branch_swap.wait()
    dattended[other, :] = nt(dbranch[other, :], mixer[own, :]).astype(bf16)
    emit(tn(attended[...], dbranch[:, right]), [MIXER_AT + 2048 * c])
    emit(tn(att_rx[...], dbranch[:, right]), [MIXER_AT + 2048 * (1 - c)])
    for back in (2, 1):
        for part, at in enumerate(sent[-back]):
            out_copy((len(sent) - back) % 2, part, at).wait()
    att_swap.wait_send()
    normed_swap.wait_send()


def middle(attended, x_own, cot, vectors, expand_bias, mixer, expand, reduce):
    f32, bf16 = jnp.float32, jnp.bfloat16
    vmem = pl.BlockSpec(memory_space=pltpu.VMEM)
    hbm = pl.BlockSpec(memory_space=pl.ANY)
    return pl.pallas_call(
        middle_kernel,
        out_shape=(
            jax.ShapeDtypeStruct((512, WIDTH), bf16),
            jax.ShapeDtypeStruct((512, WIDTH), f32),
            jax.ShapeDtypeStruct((TOKENS, 512), bf16),
            jax.ShapeDtypeStruct((8, WIDTH), f32),
            jax.ShapeDtypeStruct((4, 512), f32),
            jax.ShapeDtypeStruct((FLAT_ROWS, LANES), bf16),
        ),
        in_specs=[vmem] * 5 + [hbm] * 3,
        out_specs=[vmem] * 5 + [hbm],
        scratch_shapes=[
            pltpu.VMEM((WIDTH, WIDTH), bf16),
            pltpu.VMEM((WIDTH, 2048), bf16),
            pltpu.VMEM((2048, WIDTH), bf16),
            pltpu.VMEM((TOKENS, 512), bf16),
            pltpu.VMEM((512, WIDTH), f32),
            pltpu.VMEM((512, WIDTH), f32),
            pltpu.VMEM((512, LANES), f32),
            pltpu.VMEM((TOKENS, WIDTH), bf16),
            pltpu.VMEM((TOKENS, 2048), bf16),
            pltpu.VMEM((TOKENS, 2048), bf16),
            pltpu.VMEM((TOKENS, 2048), bf16),
            pltpu.VMEM((512, WIDTH), f32),
            pltpu.VMEM((512, WIDTH), f32),
            pltpu.VMEM((512, WIDTH), f32),
            pltpu.VMEM((512, WIDTH), bf16),
            pltpu.VMEM((512, WIDTH), bf16),
            pltpu.VMEM((TOKENS, WIDTH), bf16),
            pltpu.VMEM((2, 4096, LANES), bf16),
            pltpu.SemaphoreType.DMA((9,)),
            pltpu.SemaphoreType.DMA((2, 2)),
            pltpu.SemaphoreType.DMA((5,)),
            pltpu.SemaphoreType.DMA((5,)),
            pltpu.SemaphoreType.DMA((2, 4)),
            pltpu.SemaphoreType.DMA((2, 4)),
        ],
        compiler_params=pltpu.CompilerParams(
            collective_id=1, has_side_effects=True, vmem_limit_bytes=62 << 20
        ),
        cost_estimate=pl.CostEstimate(flops=30 << 30, bytes_accessed=40 << 20, transcendentals=0),
    )(attended, x_own, cot, vectors, expand_bias, mixer, expand, reduce)


def owned_gradient(own, peer, small, c, owner):
    first = jnp.where(c == 0, own, peer).reshape(PIECE // 4, 1, 4, LANES)
    second = jnp.where(c == 0, peer, own).reshape(PIECE // 4, 1, 4, LANES)
    rows = jnp.concatenate([first, second], 1).reshape(2 * PIECE, LANES)
    begin = OWNED_ROWS * owner
    unit = begin // 8
    shift = jnp.where(unit < U_JBIAS, 8, jnp.where(unit < U_MBIAS, 16, 20))
    start = (4 * unit + shift) // 16 * 16

    def window(moved):
        at = begin + 2 * moved - 2 * start
        padded = jnp.pad(rows, ((16, 64), (0, 0)))
        return lax.dynamic_slice_in_dim(padded, jnp.clip(at + 16, 0, 2 * PIECE + 80 - OWNED_ROWS), OWNED_ROWS, 0)

    end_unit = (begin + OWNED_ROWS - 1) // 8
    shift_end = jnp.where(end_unit < U_JBIAS, 8, jnp.where(end_unit < U_MBIAS, 16, 20))
    flat_row = begin + jnp.arange(OWNED_ROWS, dtype=jnp.int32)
    u = flat_row // 8
    moved_row = jnp.where(u < U_JBIAS, 8, jnp.where(u < U_MBIAS, 16, 20))
    big = jnp.where((moved_row == shift)[:, None], window(shift), window(shift_end))
    places = ((0, 2, 0), (3074, 3076, 16), (4100, 4103, 32), (8199, 8203, 56), (12299, 12300, 88))
    result = big
    for first_unit, end, at in places:
        inside = (u >= first_unit) & (u < end)
        shift_small = at + begin - 8 * first_unit
        padded = jnp.pad(small, ((OWNED_ROWS, OWNED_ROWS), (0, 0)))
        part = lax.dynamic_slice_in_dim(
            padded, jnp.clip(OWNED_ROWS + shift_small, 0, OWNED_ROWS + 96), OWNED_ROWS, 0
        )
        result = jnp.where(inside[:, None], part, result)
    return result


def on_device_chip(
    dp_size, group_size,
    activations, cotangent, segments, padding, step_count, learn_rate,
    gain_before, shift_before, joint_weight, joint_bias, mixer_weight, mixer_bias,
    gain_middle, shift_middle, expand_weight, expand_bias, reduce_weight, reduce_bias,
    master_weights, first_moment, second_moment,
):
    f32, bf16 = jnp.float32, jnp.bfloat16
    dp = lax.axis_index("dp")
    group = lax.axis_index("group")
    c = dp % 2
    routes = plane_routes(dp_size, group_size)
    joint_half = half_columns(joint_weight, c)
    x_own = to_chip(activations, routes, group)
    x_own, cotangent, joint_half = lax.optimization_barrier((x_own, cotangent, joint_half))
    cot_own = to_chip(cotangent, routes, group)
    x_all = in_order(c, x_own, core_swap(x_own), 0)
    marks = jnp.stack([segments, padding])
    marks = jnp.where(c == group // 2, marks, core_swap(marks))
    marks = lax.dynamic_index_in_dim(marks, group % 2, 1, False)
    seg, pad = marks[0], marks[1]
    places = jnp.arange(TOKENS, dtype=jnp.int32)
    last = jnp.sum((seg[:, None] <= seg[None, :]).astype(jnp.int32), 0) - 1
    last = jnp.where(pad == 1, last, places)
    allowed = (places[None, :] >= places[:, None]) & (places[None, :] <= last[:, None])
    dist = jnp.where(allowed, (places[None, :] - places[:, None]).astype(f32), -masked_score)
    slopes = jnp.exp2(-8.0 * (jnp.arange(8, dtype=f32) + 8.0 * c.astype(f32) + 1.0) / HEADS)

    gain_one = gain_before.astype(f32)
    bias = half_columns(joint_bias[None], c)[0].astype(f32)
    joint_shift = jnp.concatenate([bias[:512], jnp.zeros((512,), f32), bias[512:]])
    joint_scale = jnp.concatenate([jnp.full((512,), 0.125, f32), jnp.ones((1024,), f32)])

    normal_one, _ = standardize(x_all.astype(f32))
    normed_one = (normal_one * gain_one + shift_before.astype(f32)).astype(bf16)
    joint = ((nn(normed_one, joint_half) + joint_shift) * joint_scale).astype(bf16)
    joint, cot_own = lax.optimization_barrier((joint, cot_own))
    attended, lse = attention_forward(joint, dist, slopes)
    cot_all = in_order(c, cot_own, core_swap(cot_own), 0)
    vectors = jnp.stack(
        [mixer_bias, gain_middle, shift_middle, reduce_bias, *[mixer_bias] * 4]
    ).astype(f32)
    expand_shift = half_columns(expand_bias[None], c).reshape(4, 512).astype(f32)
    result, dresid, dattended, middle_sums, expand_sums, flat = middle(
        attended, x_own, cot_all, vectors, expand_shift, mixer_weight, expand_weight, reduce_weight
    )
    output = from_chip(result, routes, group)
    early_a, early_b = early_pieces(flat)
    dattended, early_a, early_b, output = lax.optimization_barrier(
        (dattended, early_a, early_b, output)
    )
    early_a = lax.ppermute(early_a, "group", [(i, i ^ 1) for i in range(4)])
    early_b = lax.ppermute(early_b, "group", [(i, i ^ 2) for i in range(4)])
    inputs = x_own.astype(f32)

    def own_and_other(whole):
        return (
            lax.dynamic_slice_in_dim(whole, 512 * c, 512, 0),
            lax.dynamic_slice_in_dim(whole, 512 * (1 - c), 512, 0),
        )

    first = jnp.zeros((2,), jnp.int32)
    djoint = attention_backward(joint, attended, dattended, dist, lse, slopes)
    flat = gradient_rows(normed_one, djoint, first, flat, JOINT_AT, 256, 1)
    partial = (
        nt(djoint[0], joint_half[:, :512])
        + nt(djoint[1], joint_half[:, 512:1024])
        + nt(djoint[2], joint_half[:, 1024:])
    )
    mine, other = own_and_other(partial)
    dnormed_one = mine + core_swap(other)
    normal_own, spread_own = standardize(inputs)
    dinput = dresid + norm_back(dnormed_one * gain_one, normal_own, spread_own)
    input_gradient = from_chip(dinput.astype(bf16), routes, group)

    def placed(half):
        count = half.shape[0] // 512
        half, zeros = half.reshape(count, 512), jnp.zeros((count, 512), f32)
        return jnp.where(
            c == 0, jnp.stack([half, zeros], 1), jnp.stack([zeros, half], 1)
        ).reshape(-1)

    small = jnp.concatenate([
        jnp.sum(dnormed_one * normal_own, 0), jnp.sum(dnormed_one, 0),
        placed(jnp.sum(djoint[0].astype(f32), 0)), placed(jnp.sum(djoint[2].astype(f32), 0)),
        middle_sums[0], middle_sums[1], middle_sums[2],
        placed(expand_sums.reshape(-1)),
        middle_sums[3],
    ]).reshape(96, LANES)

    own, peer, small_sum = reduce_pieces(flat, early_a, early_b, small)
    owner = dp * group_size + group
    share = owned_gradient(own, peer, small_sum, c, owner).reshape(-1)
    small_share = lax.dynamic_slice_in_dim(small_sum, 3 * owner, 3, 0).reshape(-1)

    moment_step = step_count[0].astype(f32)
    rate = learn_rate[0]
    fix_one = 1.0 - jnp.exp(moment_step * math.log(beta_first))
    fix_two = 1.0 - jnp.exp(moment_step * math.log(beta_second))
    updated_first = beta_first * first_moment + (1.0 - beta_first) * share
    updated_second = beta_second * second_moment + (1.0 - beta_second) * share * share
    updated_master = master_weights - rate * (
        updated_first / fix_one / (jnp.sqrt(updated_second / fix_two) + adam_epsilon)
        + weight_decay * master_weights
    )
    return (output, input_gradient, updated_master, updated_first, updated_second, small_share)


def on_device(dp_size, group_size, activations, *rest):
    if (dp_size, group_size) == (8, 4) and activations.shape == (2, 256, WIDTH):
        return on_device_chip(dp_size, group_size, activations, *rest)
    return on_device_general(activations, *rest)


def solution(mesh):
    in_specs = (
        P("dp", "group", None),
        P("dp", "group", None),
        P("dp", None),
        P("dp", None),
        P(),
        P(),
        P(),
        P(),
        P(),
        P(),
        P(),
        P(),
        P(),
        P(),
        P(),
        P(),
        P(),
        P(),
        P(("dp", "group")),
        P(("dp", "group")),
        P(("dp", "group")),
    )
    out_specs = (
        P("dp", "group", None),
        P("dp", "group", None),
        P(("dp", "group")),
        P(("dp", "group")),
        P(("dp", "group")),
        P(("dp", "group")),
    )
    return jax.shard_map(
        functools.partial(on_device, mesh.shape["dp"], mesh.shape["group"]), mesh=mesh, in_specs=in_specs, out_specs=out_specs, check_vma=False
    )
```

```python
import functools
import math

import jax
import jax.numpy as jnp
from jax import lax
from jax.experimental import pallas as pl
from jax.experimental.pallas import tpu as pltpu
from jax.sharding import PartitionSpec as P

HEADS = 16
DOC_MOST = 800


beta_first = 0.9
beta_second = 0.95
adam_epsilon = 1e-08
weight_decay = 0.1
norm_epsilon = 1e-05
masked_score = -1e30


def shifted(block, axis, distance):
    devices = range(lax.axis_size(axis))
    route = [(i - distance, i) for i in devices if i - distance in devices]
    return lax.ppermute(block, axis, route)


def standardize(values):
    center = values - jnp.mean(values, -1, keepdims=True)
    spread = lax.rsqrt(jnp.mean(center * center, -1, keepdims=True) + norm_epsilon)
    return (center * spread, spread)


def norm_back(dnormed, normed, spread):
    return spread * (
        dnormed
        - jnp.mean(dnormed, -1, keepdims=True)
        - normed * jnp.mean(dnormed * normed, -1, keepdims=True)
    )


def window_mask(segments, padding, member, hop, block_len):
    places = jnp.arange(block_len, dtype=jnp.int32)
    source = member - hop
    query_place = member * block_len + places
    key_place = source * block_len + places
    start = jnp.maximum(source, 0) * block_len
    seg_query = lax.dynamic_slice_in_dim(segments, member * block_len, block_len, 1)
    seg_key = lax.dynamic_slice_in_dim(segments, start, block_len, 1)
    pad_key = lax.dynamic_slice_in_dim(padding, start, block_len, 1)
    earlier = key_place[None, None, :] <= query_place[None, :, None]
    itself = key_place[None, None, :] == query_place[None, :, None]
    allowed = (
        (seg_query[:, :, None] == seg_key[:, None, :])
        & earlier
        & ((pad_key[:, None, :] == 1) | itself)
        & (source >= 0)
    )
    distance = (query_place[:, None] - key_place[None, :]).astype(jnp.float32)
    return (allowed[:, None], distance)


def piece_scores(query4, key4, slopes, distance, score_scale):
    raw = jnp.einsum("sqhd,skhd->shqk", query4, key4, preferred_element_type=jnp.float32)
    return raw * score_scale - slopes[:, None, None] * distance[None]


def on_device_general(
    activations,
    cotangent,
    segments,
    padding,
    step_count,
    learn_rate,
    gain_before,
    shift_before,
    joint_weight,
    joint_bias,
    mixer_weight,
    mixer_bias,
    gain_middle,
    shift_middle,
    expand_weight,
    expand_bias,
    reduce_weight,
    reduce_bias,
    master_weights,
    first_moment,
    second_moment,
):
    seq_count, block_len, width = activations.shape
    head_size = width // HEADS
    row_count = seq_count * block_len
    shape4 = (seq_count, block_len, HEADS, head_size)
    score_scale = 1.0 / math.sqrt(head_size)
    group_size = lax.axis_size("group")
    member = lax.axis_index("group")
    reach = min((DOC_MOST + block_len - 2) // block_len, group_size - 1)
    slopes = jnp.exp2(-8.0 * (jnp.arange(HEADS, dtype=jnp.float32) + 1.0) / HEADS)
    inputs = activations.reshape(row_count, width).astype(jnp.float32)
    gain_one = gain_before.astype(jnp.float32)
    gain_two = gain_middle.astype(jnp.float32)
    normal_one, spread_one = standardize(inputs)
    normed_one = (normal_one * gain_one + shift_before.astype(jnp.float32)).astype(jnp.bfloat16)
    joint = jnp.dot(normed_one, joint_weight, preferred_element_type=jnp.float32)
    bias_joint = joint_bias.astype(jnp.float32)
    query_rows = (joint[:, :width] + bias_joint[:width]).astype(jnp.bfloat16)
    key_rows = joint[:, width : 2 * width].astype(jnp.bfloat16)
    value_rows = (joint[:, 2 * width :] + bias_joint[width:]).astype(jnp.bfloat16)
    own_piece = jnp.stack([key_rows, value_rows]).reshape(2, seq_count, block_len, width)
    query4 = query_rows.reshape(shape4)
    pieces = [own_piece]
    for hop in range(1, reach + 1):
        pieces.append(shifted(own_piece, "group", hop))
    row_top = jnp.full((seq_count, HEADS, block_len), masked_score, jnp.float32)
    row_total = jnp.zeros((seq_count, HEADS, block_len), jnp.float32)
    for hop in range(reach + 1):
        allowed, distance = window_mask(segments, padding, member, hop, block_len)
        scores = piece_scores(query4, pieces[hop][0].reshape(shape4), slopes, distance, score_scale)
        fresh = jnp.maximum(row_top, jnp.max(jnp.where(allowed, scores, masked_score), -1))
        row_total = row_total * jnp.exp(row_top - fresh) + jnp.sum(
            jnp.exp(jnp.where(allowed, scores - fresh[..., None], masked_score)), -1
        )
        row_top = fresh
    log_total = row_top + jnp.log(row_total)
    attended = jnp.zeros(shape4, jnp.float32)
    for hop in range(reach + 1):
        allowed, distance = window_mask(segments, padding, member, hop, block_len)
        scores = piece_scores(query4, pieces[hop][0].reshape(shape4), slopes, distance, score_scale)
        probs = jnp.exp(jnp.where(allowed, scores - log_total[..., None], masked_score)).astype(
            jnp.bfloat16
        )
        attended = attended + jnp.einsum(
            "shqk,skhd->sqhd",
            probs,
            pieces[hop][1].reshape(shape4),
            preferred_element_type=jnp.float32,
        )
    attended_low = attended.reshape(row_count, width).astype(jnp.bfloat16)
    resid = inputs + (
        jnp.dot(attended_low, mixer_weight, preferred_element_type=jnp.float32)
        + mixer_bias.astype(jnp.float32)
    )
    normal_two, spread_two = standardize(resid)
    normed_two = (normal_two * gain_two + shift_middle.astype(jnp.float32)).astype(jnp.bfloat16)
    hidden = jnp.dot(
        normed_two, expand_weight, preferred_element_type=jnp.float32
    ) + expand_bias.astype(jnp.float32)
    act = jax.nn.gelu(hidden, approximate=True).astype(jnp.bfloat16)
    result = resid + (
        jnp.dot(act, reduce_weight, preferred_element_type=jnp.float32)
        + reduce_bias.astype(jnp.float32)
    )
    output = result.astype(jnp.bfloat16).reshape(seq_count, block_len, width)
    cot_low = cotangent.reshape(row_count, width)
    cot_full = cot_low.astype(jnp.float32)
    reduce_grad = jnp.einsum("tf,td->fd", act, cot_low, preferred_element_type=jnp.float32)
    reduce_bias_grad = jnp.sum(cot_full, 0)
    dact = jnp.einsum("td,fd->tf", cot_low, reduce_weight, preferred_element_type=jnp.float32)
    gelu_pull = jax.vjp(lambda inner: jax.nn.gelu(inner, approximate=True), hidden)[1]
    dhidden = gelu_pull(dact)[0].astype(jnp.bfloat16)
    expand_grad = jnp.einsum("td,tf->df", normed_two, dhidden, preferred_element_type=jnp.float32)
    expand_bias_grad = jnp.sum(dhidden.astype(jnp.float32), 0)
    dnormed_two = jnp.einsum(
        "tf,df->td", dhidden, expand_weight, preferred_element_type=jnp.float32
    )
    gain_middle_grad = jnp.sum(dnormed_two * normal_two, 0)
    shift_middle_grad = jnp.sum(dnormed_two, 0)
    dresid = cot_full + norm_back(dnormed_two * gain_two, normal_two, spread_two)
    dbranch = dresid.astype(jnp.bfloat16)
    mixer_grad = jnp.einsum("td,te->de", attended_low, dbranch, preferred_element_type=jnp.float32)
    mixer_bias_grad = jnp.sum(dbranch.astype(jnp.float32), 0)
    dattended = jnp.einsum(
        "te,de->td", dbranch, mixer_weight, preferred_element_type=jnp.float32
    ).astype(jnp.bfloat16)
    dattended4 = dattended.reshape(shape4)
    row_delta = jnp.einsum("sqhd,sqhd->shq", dattended4.astype(jnp.float32), attended)
    dquery = jnp.zeros(shape4, jnp.float32)
    dkv_own = jnp.zeros((2, seq_count, block_len, width), jnp.float32)
    for hop in range(reach + 1):
        piece = pieces[hop]
        key4 = piece[0].reshape(shape4)
        value4 = piece[1].reshape(shape4)
        allowed, distance = window_mask(segments, padding, member, hop, block_len)
        scores = piece_scores(query4, key4, slopes, distance, score_scale)
        probs = jnp.exp(jnp.where(allowed, scores - log_total[..., None], masked_score))
        dvalue = jnp.einsum(
            "shqk,sqhd->skhd",
            probs.astype(jnp.bfloat16),
            dattended4,
            preferred_element_type=jnp.float32,
        )
        dprobs = jnp.einsum(
            "sqhd,skhd->shqk", dattended4, value4, preferred_element_type=jnp.float32
        )
        dscores = (probs * (dprobs - row_delta[..., None])).astype(jnp.bfloat16)
        dquery = dquery + jnp.einsum(
            "shqk,skhd->sqhd", dscores, key4, preferred_element_type=jnp.float32
        )
        dkey = (
            jnp.einsum("shqk,sqhd->skhd", dscores, query4, preferred_element_type=jnp.float32)
            * score_scale
        )
        returned = jnp.stack([dkey, dvalue]).reshape(2, seq_count, block_len, width)
        if hop == 0:
            dkv_own = returned
        else:
            dkv_own = dkv_own + shifted(returned.astype(jnp.bfloat16), "group", -hop).astype(
                returned.dtype
            )
    dquery_low = (dquery * score_scale).reshape(row_count, width).astype(jnp.bfloat16)
    dkey_low = dkv_own[0].reshape(row_count, width).astype(jnp.bfloat16)
    dvalue_low = dkv_own[1].reshape(row_count, width).astype(jnp.bfloat16)
    djoint = jnp.concatenate([dquery_low, dkey_low, dvalue_low], 1)
    joint_grad = jnp.einsum("td,te->de", normed_one, djoint, preferred_element_type=jnp.float32)
    joint_bias_grad = jnp.concatenate(
        [jnp.sum(dquery_low.astype(jnp.float32), 0), jnp.sum(dvalue_low.astype(jnp.float32), 0)]
    )
    dnormed_one = jnp.einsum("te,de->td", djoint, joint_weight, preferred_element_type=jnp.float32)
    gain_before_grad = jnp.sum(dnormed_one * normal_one, 0)
    shift_before_grad = jnp.sum(dnormed_one, 0)
    dinput = dresid + norm_back(dnormed_one * gain_one, normal_one, spread_one)
    input_gradient = dinput.astype(jnp.bfloat16).reshape(seq_count, block_len, width)
    listing = [
        gain_before_grad,
        shift_before_grad,
        joint_grad,
        joint_bias_grad,
        mixer_grad,
        mixer_bias_grad,
        gain_middle_grad,
        shift_middle_grad,
        expand_grad,
        expand_bias_grad,
        reduce_grad,
        reduce_bias_grad,
    ]
    gradient = jnp.concatenate([single.reshape(-1) for single in listing])
    small_list = [
        gain_before_grad,
        shift_before_grad,
        joint_bias_grad,
        mixer_bias_grad,
        gain_middle_grad,
        shift_middle_grad,
        expand_bias_grad,
        reduce_bias_grad,
    ]
    small_local = jnp.concatenate(small_list)
    share, small_share = (
        lax.psum_scatter(gradient, ("dp", "group"), scatter_dimension=0, tiled=True),
        lax.psum_scatter(small_local, ("dp", "group"), scatter_dimension=0, tiled=True),
    )
    moment_step = step_count[0].astype(jnp.float32)
    rate = learn_rate[0]
    fix_one = 1.0 - jnp.exp(moment_step * math.log(beta_first))
    fix_two = 1.0 - jnp.exp(moment_step * math.log(beta_second))
    updated_first = beta_first * first_moment + (1.0 - beta_first) * share
    updated_second = beta_second * second_moment + (1.0 - beta_second) * share * share
    updated_master = master_weights - rate * (
        updated_first / fix_one / (jnp.sqrt(updated_second / fix_two) + adam_epsilon)
        + weight_decay * master_weights
    )
    return (output, input_gradient, updated_master, updated_first, updated_second, small_share)


WIDTH = 1024
HIDDEN = 4096
TOKENS = 1024
LANES = 128
OWNED = 393600
OWNED_ROWS = OWNED // LANES
PIECE = 1568
HALF = PIECE // 2
JOINT_AT, MIXER_AT, EXPAND_AT, REDUCE_AT = 16, 12320, 16432, 32832
FLAT_ROWS = 49248
U_JOINT, U_JBIAS, U_MIXER, U_MBIAS, U_EXPAND, U_EBIAS, U_REDUCE, U_RBIAS = (
    2, 3074, 3076, 4100, 4103, 8199, 8203, 12299,
)


def section_shift(unit):
    return 8 if unit < U_JBIAS else 16 if unit < U_MBIAS else 20


def piece_start(owner):
    unit = OWNED_ROWS * owner // 8
    return (4 * unit + section_shift(unit)) // 16 * 16


def piece_offset(q, y, x):
    at = [piece_start(4 * q + k) // 16 for k in range(4)]
    row = (
        at[0] * (1 - y) * (1 - x) + at[1] * (1 - y) * x + at[2] * y * (1 - x) + at[3] * y * x
    )
    return pl.multiple_of(row * 16, 16)


MESH_ID = pl.DeviceIdType.MESH


def by_rows(step):
    def one(i, carry):
        step(pl.ds(pl.multiple_of(112 * i, 16), 112))
        return carry

    lax.fori_loop(0, HALF // 112, one, 0)


class Pieces:
    def __init__(self, dp, me, flat, own_a, own_b, rx_a1, rx_b1, rx_a2, rx_b2, acc, load_sem, s2_send, s2_recv):
        self.y, self.x = me // 2, me % 2
        self.x_near = (dp, 2 * self.y + (1 - self.x))
        self.y_near = (dp, 2 * (1 - self.y) + self.x)
        self.flat, self.own_a, self.own_b = flat, own_a, own_b
        self.rx_a1, self.rx_b1, self.rx_a2, self.rx_b2, self.acc = rx_a1, rx_b1, rx_a2, rx_b2, acc
        self.load_sem, self.s2_send, self.s2_recv = load_sem, s2_send, s2_recv

    def loads(self, q, own_slot, ready=None):
        slot = q
        out = []
        for k in range(2):
            for way, (row, own) in enumerate((
                (piece_offset(q, k, self.x), self.own_a),
                (piece_offset(q, self.y, k) + HALF, self.own_b),
            )):
                out.append(pltpu.make_async_copy(
                    self.flat.at[pl.ds(row, HALF)], own.at[own_slot, k], self.load_sem.at[slot, way, k]
                ))
            if ready is not None:
                ready_a, ready_b, at = ready
                for way, (src, dst) in enumerate(((ready_a, self.rx_a1), (ready_b, self.rx_b1))):
                    out.append(pltpu.make_async_copy(
                        src.at[at, k], dst.at[slot, k], self.load_sem.at[slot, 2 + way, k]
                    ))
        return out

    def second(self, slot):
        y, x = self.y, self.x
        return [
            pltpu.make_async_remote_copy(
                src_ref=src, dst_ref=dst.at[slot], send_sem=self.s2_send.at[slot, way],
                recv_sem=self.s2_recv.at[slot, way], device_id=near, device_id_type=MESH_ID,
            )
            for way, (src, dst, near) in enumerate((
                (self.rx_a1.at[slot, 1 - y], self.rx_a2, self.y_near),
                (self.rx_b1.at[slot, 1 - x], self.rx_b2, self.x_near),
            ))
        ]

    def meet(self, slot, own_slot):
        y, x = self.y, self.x
        rx_a1, rx_b1, own_a, own_b, acc = self.rx_a1, self.rx_b1, self.own_a, self.own_b, self.acc

        def away(rows):
            rx_a1[slot, 1 - y, rows] = rx_a1[slot, 1 - y, rows] + own_a[own_slot, 1 - y, rows]
            rx_b1[slot, 1 - x, rows] = rx_b1[slot, 1 - x, rows] + own_b[own_slot, 1 - x, rows]

        by_rows(away)
        for copy in self.second(slot):
            copy.start()

        def kept(rows):
            acc[slot, 0, rows] = rx_a1[slot, y, rows] + own_a[own_slot, y, rows]
            acc[slot, 1, rows] = rx_b1[slot, x, rows] + own_b[own_slot, x, rows]

        by_rows(kept)

    def join(self, slot):
        for copy in self.second(slot):
            copy.wait_recv()
        acc, rx_a2, rx_b2 = self.acc, self.rx_a2, self.rx_b2

        def add(rows):
            acc[slot, 0, rows] = acc[slot, 0, rows] + rx_a2[slot, rows]
            acc[slot, 1, rows] = acc[slot, 1, rows] + rx_b2[slot, rows]

        by_rows(add)


MIDDLE_EARLY = (4, 5)


def core_swap(value):
    count = lax.axis_size("dp")
    return lax.ppermute(value, "dp", [(i, i ^ 1) for i in range(count)])


def plane_routes(dp_size, group_size):
    routes = []
    for turn in range(2):
        there = []
        for dp in range(dp_size):
            for g in range(group_size):
                k = 2 * (dp % 2) + (g + turn) % 2
                there.append((dp * group_size + g, (dp // 2 * 2 + g // 2) * group_size + k))
        routes.append(there)
    return routes


def to_chip(value, routes, group):
    came = [
        lax.ppermute(
            lax.dynamic_index_in_dim(value, (group + turn) % 2, 0, False),
            ("dp", "group"), routes[turn],
        )
        for turn in range(2)
    ]
    odd = group % 2 == 1
    return jnp.concatenate([jnp.where(odd, came[1], came[0]), jnp.where(odd, came[0], came[1])], 0)


def from_chip(value, routes, group):
    half = value.shape[0] // 2
    odd = group % 2 == 1
    first, second = value[:half], value[half:]
    sent = [jnp.where(odd, second, first), jnp.where(odd, first, second)]
    came = [
        lax.ppermute(sent[turn], ("dp", "group"), [(b, a) for a, b in routes[turn]])
        for turn in range(2)
    ]
    return jnp.stack([jnp.where(odd, came[1], came[0]), jnp.where(odd, came[0], came[1])])


def in_order(c, own, peer, axis):
    return jnp.where(
        c == 0, jnp.concatenate([own, peer], axis), jnp.concatenate([peer, own], axis)
    )


def half_columns(weight, c, axis=1):
    count = weight.shape[axis] // 1024
    return jnp.concatenate(
        [lax.dynamic_slice_in_dim(weight, 1024 * k + 512 * c, 512, axis) for k in range(count)],
        axis,
    )


def nn(a, b):
    return lax.dot_general(a, b, (((1,), (0,)), ((), ())), preferred_element_type=jnp.float32)


def nt(a, b):
    return lax.dot_general(a, b, (((1,), (1,)), ((), ())), preferred_element_type=jnp.float32)


def tn(a, b):
    return lax.dot_general(a, b, (((0,), (0,)), ((), ())), preferred_element_type=jnp.float32)


def head_lanes(value, h):
    lane = lax.broadcasted_iota(jnp.int32, (1, LANES), 1)
    return jnp.where(lane // 64 == h, value, jnp.zeros_like(value))


def forward_kernel(slopes, q_ref, k_ref, v_ref, dist_ref, out_ref, lse_ref, s_ref, p_ref, vt_ref, ot_ref):
    pair = pl.program_id(0)
    vt_ref[...] = v_ref[...].astype(jnp.float32).T.astype(jnp.bfloat16)

    def head(h, carry):
        slope = slopes[2 * pair + h]
        for qb in range(4):
            cols = pl.ds(qb * 256, 256)
            queries = head_lanes(q_ref[cols, :], h)
            top = None
            for kb in range(qb + 1):
                rows = pl.ds(kb * 256, 256)
                s = nt(k_ref[rows, :], queries) - slope * dist_ref[rows, cols]
                s_ref[rows, :] = s
                high = jnp.max(s, 0, keepdims=True)
                top = high if top is None else jnp.maximum(top, high)
            total = None
            for kb in range(qb + 1):
                rows = pl.ds(kb * 256, 256)
                p = jnp.exp(s_ref[rows, :] - top)
                more = jnp.sum(p, 0, keepdims=True)
                total = more if total is None else total + more
                p_ref[rows, :] = p.astype(jnp.bfloat16)
            span = pl.ds(0, 256 * (qb + 1))
            out = nn(vt_ref[:, span], p_ref[span, :]) / total
            row = lax.broadcasted_iota(jnp.int32, (LANES, 1), 0)
            ot_ref[:, cols] = jnp.where(row // 64 == h, out, ot_ref[:, cols])
            lse_ref[0, pl.ds(h, 1), cols] = top + jnp.log(total)
        return carry

    ot_ref[...] = jnp.zeros_like(ot_ref)
    lax.fori_loop(0, 2, head, 0)
    out_ref[...] = ot_ref[...].T.astype(jnp.bfloat16)


def joint_sides():
    return [
        pl.BlockSpec((TOKENS, LANES), lambda i, *_: (0, i)),
        pl.BlockSpec((TOKENS, LANES), lambda i, *_: (0, 4 + i)),
        pl.BlockSpec((TOKENS, LANES), lambda i, *_: (0, 8 + i)),
    ]


def attention_forward(joint, dist, slopes):
    sides = joint_sides()
    side = pl.BlockSpec((TOKENS, LANES), lambda i, *_: (0, i))
    return pl.pallas_call(
        forward_kernel,
        out_shape=(
            jax.ShapeDtypeStruct((TOKENS, 512), jnp.bfloat16),
            jax.ShapeDtypeStruct((4, 2, TOKENS), jnp.float32),
        ),
        grid_spec=pltpu.PrefetchScalarGridSpec(
            num_scalar_prefetch=1,
            grid=(4,),
            in_specs=sides + [pl.BlockSpec((TOKENS, TOKENS), lambda i, *_: (0, 0))],
            out_specs=[side, pl.BlockSpec((1, 2, TOKENS), lambda i, *_: (i, 0, 0))],
            scratch_shapes=[
                pltpu.VMEM((TOKENS, 256), jnp.float32),
                pltpu.VMEM((TOKENS, 256), jnp.bfloat16),
                pltpu.VMEM((LANES, TOKENS), jnp.bfloat16),
                pltpu.VMEM((LANES, TOKENS), jnp.float32),
            ],
        ),
        compiler_params=pltpu.CompilerParams(vmem_limit_bytes=48 << 20),
        cost_estimate=pl.CostEstimate(
            flops=4 * 8 * 655360 * 64, bytes_accessed=8 << 20, transcendentals=8 * 655360
        ),
    )(slopes, joint, joint, joint, dist)


def plane_devices(dp, me):
    z, c = dp // 2, dp % 2
    near = [(2 * z + 1 - c, me)]
    for d in (1, 2, 3):
        near += [(2 * z, (me + d) % 4), (2 * z + 1, (me + d) % 4)]
    return near


def greet(devices):
    barrier = pltpu.get_barrier_semaphore()
    for near in devices:
        pl.semaphore_signal(barrier, inc=1, device_id=near, device_id_type=MESH_ID)
    pl.semaphore_wait(barrier, len(devices))


class Home:
    def __init__(self, rows, out, dp, me, send_sem, recv_sem):
        z, c = dp // 2, dp % 2
        self.here = c == me // 2
        self.turns = []
        for turn in range(2):
            src = rows.at[pl.ds(256 * turn, 256)]
            dst = out.at[me % 2]
            away = pltpu.make_async_remote_copy(
                src_ref=src, dst_ref=dst, send_sem=send_sem.at[turn], recv_sem=recv_sem.at[me % 2],
                device_id=(2 * z + me // 2, 2 * c + turn), device_id_type=MESH_ID,
            )
            near = pltpu.make_async_copy(src, dst, send_sem.at[turn])
            came = pltpu.make_async_remote_copy(
                src_ref=src, dst_ref=out.at[turn], send_sem=send_sem.at[turn],
                recv_sem=recv_sem.at[turn], device_id=(2 * z + me // 2, 2 * c + turn),
                device_id_type=MESH_ID,
            )
            self.turns.append((away, near, came, self.here & (me % 2 == turn)))

    def start(self):
        for away, near, _, stays in self.turns:
            @pl.when(stays)
            def _():
                near.start()

            @pl.when(jnp.logical_not(stays))
            def _():
                away.start()

    def wait(self):
        for away, near, came, stays in self.turns:
            @pl.when(stays)
            def _():
                near.wait()

            @pl.when(jnp.logical_not(stays))
            def _():
                away.wait_send()
                came.wait_recv()


def first_stage(q, flat, rx_a, rx_b, at, send_sem, recv_sem, dp, me):
    y, x = me // 2, me % 2
    x_near = (dp, 2 * y + (1 - x))
    y_near = (dp, 2 * (1 - y) + x)
    out = []
    for k in range(2):
        for way, (row, rx, near) in enumerate((
            (piece_offset(q, k, 1 - x), rx_a, x_near),
            (piece_offset(q, 1 - y, k) + HALF, rx_b, y_near),
        )):
            out.append(pltpu.make_async_remote_copy(
                src_ref=flat.at[pl.ds(row, HALF)], dst_ref=rx.at[at, k],
                send_sem=send_sem.at[at, way, k], recv_sem=recv_sem.at[at, way, k],
                device_id=near, device_id_type=MESH_ID,
            ))
    return out


def rear_kernel(
    slopes, joint, attended, dattended, dist_hbm, lse, normed, weight, x_own, dresid, gain, result,
    mid_sums, expand_sums, mid_a, mid_b, flat_in,
    flat, own_out, peer_out, small_out, output, input_gradient,
    dist, p_ref, ds_ref, kt_ref, dqt_ref, dk_acc, dv_acc, delta_ref, djoint, dn_rx, dinput, blocks,
    own_a, own_b, rx_a1, rx_b1, rx_a2, rx_b2, acc, rx_up, rx_dn, parting,
    small_mine, small_rx, small_z,
    dist_sem, block_sem, swap_sem, load_sem, s1_send, s1_recv, s2_send, s2_recv, z_send, z_recv,
    last_sem, sm_send, sm_recv, out_send, out_recv, in_send, in_recv,
):
    f32, bf16 = jnp.float32, jnp.bfloat16
    dp = lax.axis_index("dp")
    me = lax.axis_index("group")
    z, c = dp // 2, dp % 2
    y, x = me // 2, me % 2
    x_near = (dp, 2 * y + (1 - x))
    y_near = (dp, 2 * (1 - y) + x)
    core_near = (2 * z + 1 - c, me)
    own = pl.ds(pl.multiple_of(512 * c, 512), 512)
    other = pl.ds(pl.multiple_of(512 * (1 - c), 512), 512)

    def z_at(d):
        return (2 * d + c, me)

    pieces = Pieces(
        dp, me, flat, own_a, own_b, rx_a1, rx_b1, rx_a2, rx_b2, acc, load_sem, s2_send, s2_recv
    )
    own_slot = {4: 0, 5: 1, 6: 2, 7: 3, 0: 0, 1: 1, 3: 2, 2: 3}

    def loads(q):
        ready = (mid_a, mid_b, MIDDLE_EARLY.index(q)) if q in MIDDLE_EARLY else None
        return pieces.loads(q, own_slot[q], ready)

    def start(copies):
        for copy in copies:
            copy.start()

    def stage1(q):
        return first_stage(q, flat, rx_a1, rx_b1, q, s1_send, s1_recv, dp, me)

    def hop(q, up):
        return pltpu.make_async_remote_copy(
            src_ref=acc.at[q], dst_ref=rx_up.at[q - 2] if up else rx_dn.at[q],
            send_sem=z_send.at[q, 0 if up else 1], recv_sem=z_recv.at[q, 0 if up else 1],
            device_id=z_at((z + 1) % 4 if up else (z + 3) % 4), device_id_type=MESH_ID,
        )

    def meet(q):
        for copy in loads(q):
            copy.wait()
        if q not in MIDDLE_EARLY:
            for copy in stage1(q):
                copy.wait_recv()
        pieces.meet(q, own_slot[q])

    def add_came(q, rx, at):
        def add(rows):
            for k in range(2):
                acc[q, k, rows] = acc[q, k, rows] + rx[at, k, rows]

        by_rows(add)

    def pass_on(q, h):
        aim = q // 2
        if h < aim:
            @pl.when(z == h)
            def _():
                if h > 0:
                    hop(q, True).wait_recv()
                    add_came(q, rx_up, q - 2)
                hop(q, True).start()
        if h < 3 - aim:
            @pl.when(z == 3 - h)
            def _():
                if h > 0:
                    hop(q, False).wait_recv()
                    add_came(q, rx_dn, q)
                hop(q, False).start()

    last = pltpu.make_async_remote_copy(
        src_ref=parting, dst_ref=peer_out, send_sem=last_sem.at[0], recv_sem=last_sem.at[1],
        device_id=core_near, device_id_type=MESH_ID,
    )

    def finish(q):
        aim = q // 2

        @pl.when(z == aim)
        def _():
            if aim > 0:
                hop(q, True).wait_recv()
            if aim < 3:
                hop(q, False).wait_recv()
            mine = c == q % 2
            for k in range(2):
                def add(i, carry):
                    rows = pl.ds(pl.multiple_of(112 * i, 16), 112)
                    place = pl.ds(pl.multiple_of(HALF * k + 112 * i, 16), 112)
                    total = acc[q, k, rows].astype(f32)
                    if aim > 0:
                        total = total + rx_up[q - 2, k, rows].astype(f32)
                    if aim < 3:
                        total = total + rx_dn[q, k, rows].astype(f32)

                    @pl.when(mine)
                    def _():
                        own_out[place] = total

                    @pl.when(jnp.logical_not(mine))
                    def _():
                        parting[place] = total

                    return carry

                lax.fori_loop(0, HALF // 112, add, 0)

            @pl.when(jnp.logical_not(mine))
            def _():
                last.start()

    def small_step(k):
        near = (core_near, x_near, y_near)[k]
        return pltpu.make_async_remote_copy(
            src_ref=small_mine.at[k], dst_ref=small_rx.at[k], send_sem=sm_send.at[k],
            recv_sem=sm_recv.at[k], device_id=near, device_id_type=MESH_ID,
        )

    def small_next(k):
        small_step(k).wait()
        small_mine[k + 1] = small_mine[k] + small_rx[k]
        if k < 2:
            small_step(k + 1).start()

    def small_hop(d):
        return pltpu.make_async_remote_copy(
            src_ref=small_mine.at[3], dst_ref=small_z.at[d - 1], send_sem=sm_send.at[2 + d],
            recv_sem=sm_recv.at[2 + d], device_id=z_at((z + d) % 4), device_id_type=MESH_ID,
        )

    dist_load = pltpu.make_async_copy(dist_hbm, dist, dist_sem)
    for q in (4, 5, 6, 7):
        start(loads(q))
    dist_load.start()
    greet(plane_devices(dp, me) + [z_at((z + d) % 4) for d in (1, 2, 3)])
    way_out = Home(result, output, dp, me, out_send, out_recv)
    way_in = Home(dinput, input_gradient, dp, me, in_send, in_recv)
    start(stage1(6))
    meet(4)
    meet(5)

    def go_on(pair):
        @pl.when(pair == 1)
        def _():
            start(stage1(7))

        @pl.when(pair == 2)
        def _():
            start(stage1(3))

    dist_load.wait()

    def pair_step(pair, carry):
        def lanes(block):
            return pl.ds(pl.multiple_of(512 * block + LANES * pair, LANES), LANES)

        here = lanes(0)
        kt_ref[...] = joint[:, lanes(1)].astype(f32).T.astype(bf16)
        product = (attended[:, here].astype(f32) * dattended[:, here].astype(f32)).T
        delta_ref[0:1, :] = jnp.sum(product[:64], 0, keepdims=True)
        delta_ref[1:2, :] = jnp.sum(product[64:], 0, keepdims=True)
        dk_acc[...] = jnp.zeros_like(dk_acc)
        dv_acc[...] = jnp.zeros_like(dv_acc)
        dqt_ref[...] = jnp.zeros_like(dqt_ref)

        def head(h, carry):
            slope = slopes[2 * pair + h]
            for qb in range(4):
                cols = pl.ds(qb * 256, 256)
                queries = head_lanes(joint[cols, here], h)
                grads = head_lanes(dattended[cols, here], h)
                top = lse[pair, pl.ds(h, 1), cols]
                delta = delta_ref[pl.ds(h, 1), cols]
                for kb in range(qb + 1):
                    rows = pl.ds(kb * 256, 256)
                    s = nt(joint[rows, lanes(1)], queries) - slope * dist[rows, cols]
                    p = jnp.exp(s - top)
                    p_ref[rows, :] = p.astype(bf16)
                    dprobs = nt(joint[rows, lanes(2)], grads)
                    ds_ref[rows, :] = (p * (dprobs - delta)).astype(bf16)
                span = pl.ds(0, 256 * (qb + 1))
                dv_acc[span, :] += nn(p_ref[span, :], grads)
                dk_acc[span, :] += nn(ds_ref[span, :], queries)
                dq = nn(kt_ref[:, span], ds_ref[span, :])
                row = lax.broadcasted_iota(jnp.int32, (LANES, 1), 0)
                dqt_ref[:, cols] = jnp.where(row // 64 == h, dq, dqt_ref[:, cols])
            return carry

        lax.fori_loop(0, 2, head, 0)
        djoint[:, lanes(0)] = (dqt_ref[...] * 0.125).T.astype(bf16)
        djoint[:, lanes(1)] = dk_acc[...].astype(bf16)
        djoint[:, lanes(2)] = dv_acc[...].astype(bf16)
        go_on(pair)
        return carry

    lax.fori_loop(0, 4, pair_step, 0)
    for q in (4, 5):
        pieces.join(q)
        pass_on(q, 0)

    def block_copy(slot, i):
        return pltpu.make_async_copy(
            blocks.at[slot], flat.at[pl.ds(JOINT_AT + 3072 * i, 3072)], block_sem.at[slot]
        )

    for i in range(4):
        if i >= 2:
            block_copy(i % 2, i - 2).wait()
        block = tn(normed[:, 256 * i : 256 * i + 256], djoint[...]).astype(bf16)
        blocks[i % 2] = block.reshape(3072, LANES)
        block_copy(i % 2, i).start()
    for i in (2, 3):
        block_copy(i % 2, i).wait()
    start(stage1(0))
    start(stage1(1))
    for q in (0, 1):
        start(loads(q))

    dn_own, dn_part = dist.at[pl.ds(0, 512)], dist.at[pl.ds(512, 512)]
    dn_part[...] = nt(djoint[other, :], weight[...])
    dn_swap = pltpu.make_async_remote_copy(
        src_ref=dn_part, dst_ref=dn_rx, send_sem=swap_sem.at[0], recv_sem=swap_sem.at[1],
        device_id=core_near, device_id_type=MESH_ID,
    )
    dn_swap.start()
    meet(6)
    start(loads(3))
    meet(7)
    start(loads(2))
    for q in (4, 5):
        pass_on(q, 1)
    dn_own[...] = nt(djoint[own, :], weight[...])
    bias_sums = nn(jnp.ones((8, TOKENS), bf16), djoint[...])
    half = pl.ds(pl.multiple_of(512 * c, 512), 512)
    small_mine[0] = jnp.zeros(small_mine.shape[1:], f32)
    small_mine[0, 2:3, half] = bias_sums[0:1, :512]
    small_mine[0, 3:4, half] = bias_sums[0:1, 1024:]
    small_mine[0, 4:8, :] = mid_sums[0:4, :]
    small_mine[0, 8:12, half] = expand_sums[...]
    dn_swap.wait()

    def back_rows(i, carry):
        rows = pl.ds(pl.multiple_of(128 * i, 128), 128)
        values = x_own[rows, :].astype(f32)
        center = values - jnp.mean(values, -1, keepdims=True)
        factor = lax.rsqrt(jnp.mean(center * center, -1, keepdims=True) + norm_epsilon)
        unit = center * factor
        dn = dn_own[rows, :] + dn_rx[rows, :]
        e = dn * gain[0:1, :]
        down = dresid[rows, :] + factor * (
            e - jnp.mean(e, -1, keepdims=True) - unit * jnp.mean(e * unit, -1, keepdims=True)
        )
        dinput[rows, :] = down.astype(bf16)
        small_mine[0, 0:1, :] += jnp.sum(dn * unit, 0, keepdims=True)
        small_mine[0, 1:2, :] += jnp.sum(dn, 0, keepdims=True)
        return carry

    lax.fori_loop(0, 4, back_rows, 0)
    small_step(0).start()
    for q in (6, 7):
        pieces.join(q)
        pass_on(q, 0)
    small_next(0)
    meet(0)
    meet(1)
    start(stage1(2))
    small_next(1)
    meet(3)
    for q in (0, 1):
        pieces.join(q)
        pass_on(q, 0)
    small_next(2)
    for d in (1, 2, 3):
        small_hop(d).start()
    for q in (4, 5):
        finish(q)
    for q in (6, 7):
        pass_on(q, 1)
    way_out.start()
    pieces.join(3)
    pass_on(3, 0)
    meet(2)
    way_in.start()
    for q in (0, 1):
        pass_on(q, 1)
    for q in (6, 7):
        pass_on(q, 2)
    pieces.join(2)
    pass_on(2, 0)
    pass_on(3, 1)
    for q in (0, 1):
        pass_on(q, 2)
    pass_on(2, 1)
    for d in (1, 2, 3):
        small_hop(d).wait()
    small_out[...] = (small_mine[3] + small_z[1]) + (small_z[0] + small_z[2])
    for q in (6, 7, 0, 1, 3, 2):
        finish(q)

    last.wait()
    way_out.wait()
    way_in.wait()
    for q in (0, 1, 2, 3, 6, 7):
        for copy in stage1(q):
            copy.wait_send()
    for q in range(8):
        for copy in pieces.second(q):
            copy.wait_send()
        aim = q // 2
        for h in range(3):
            if h < aim:
                @pl.when(z == h)
                def _():
                    hop(q, True).wait_send()
            if h < 3 - aim:
                @pl.when(z == 3 - h)
                def _():
                    hop(q, False).wait_send()


def rear(
    slopes, joint, attended, dattended, dist, lse, normed, weight, x_own, dresid, gain, result,
    mid_sums, expand_sums, mid_a, mid_b, flat,
):
    f32, bf16 = jnp.float32, jnp.bfloat16
    vmem = pl.BlockSpec(memory_space=pltpu.VMEM)
    hbm = pl.BlockSpec(memory_space=pl.ANY)
    home = jax.ShapeDtypeStruct((2, 256, WIDTH), bf16)
    piece = jax.ShapeDtypeStruct((PIECE, LANES), f32)
    return pl.pallas_call(
        rear_kernel,
        out_shape=(
            jax.ShapeDtypeStruct((FLAT_ROWS, LANES), bf16),
            piece,
            piece,
            jax.ShapeDtypeStruct((16, WIDTH), f32),
            home,
            home,
        ),
        in_specs=[pl.BlockSpec(memory_space=pltpu.SMEM)] + [vmem] * 3 + [hbm] + [vmem] * 6
        + [hbm] + [vmem] * 2 + [hbm] * 3,
        out_specs=[hbm] + [vmem] * 3 + [hbm] * 2,
        scratch_shapes=[
            pltpu.VMEM((TOKENS, TOKENS), f32),
            pltpu.VMEM((TOKENS, 256), bf16),
            pltpu.VMEM((TOKENS, 256), bf16),
            pltpu.VMEM((LANES, TOKENS), bf16),
            pltpu.VMEM((LANES, TOKENS), f32),
            pltpu.VMEM((TOKENS, LANES), f32),
            pltpu.VMEM((TOKENS, LANES), f32),
            pltpu.VMEM((8, TOKENS), f32),
            pltpu.VMEM((TOKENS, 1536), bf16),
            pltpu.VMEM((512, WIDTH), f32),
            pltpu.VMEM((512, WIDTH), bf16),
            pltpu.VMEM((2, 3072, LANES), bf16),
            pltpu.VMEM((4, 2, HALF, LANES), bf16),
            pltpu.VMEM((4, 2, HALF, LANES), bf16),
            pltpu.VMEM((8, 2, HALF, LANES), bf16),
            pltpu.VMEM((8, 2, HALF, LANES), bf16),
            pltpu.VMEM((8, HALF, LANES), bf16),
            pltpu.VMEM((8, HALF, LANES), bf16),
            pltpu.VMEM((8, 2, HALF, LANES), bf16),
            pltpu.VMEM((6, 2, HALF, LANES), bf16),
            pltpu.VMEM((6, 2, HALF, LANES), bf16),
            pltpu.VMEM((PIECE, LANES), f32),
            pltpu.VMEM((4, 16, WIDTH), f32),
            pltpu.VMEM((3, 16, WIDTH), f32),
            pltpu.VMEM((3, 16, WIDTH), f32),
            pltpu.SemaphoreType.DMA,
            pltpu.SemaphoreType.DMA((2,)),
            pltpu.SemaphoreType.DMA((2,)),
            pltpu.SemaphoreType.DMA((8, 4, 2)),
            pltpu.SemaphoreType.DMA((8, 2, 2)),
            pltpu.SemaphoreType.DMA((8, 2, 2)),
            pltpu.SemaphoreType.DMA((8, 2)),
            pltpu.SemaphoreType.DMA((8, 2)),
            pltpu.SemaphoreType.DMA((8, 2)),
            pltpu.SemaphoreType.DMA((8, 2)),
            pltpu.SemaphoreType.DMA((2,)),
            pltpu.SemaphoreType.DMA((6,)),
            pltpu.SemaphoreType.DMA((6,)),
            pltpu.SemaphoreType.DMA((2,)),
            pltpu.SemaphoreType.DMA((2,)),
            pltpu.SemaphoreType.DMA((2,)),
            pltpu.SemaphoreType.DMA((2,)),
        ],
        input_output_aliases={16: 0},
        compiler_params=pltpu.CompilerParams(
            collective_id=2, has_side_effects=True, vmem_limit_bytes=62 << 20
        ),
        cost_estimate=pl.CostEstimate(flops=30 << 30, bytes_accessed=30 << 20, transcendentals=0),
    )(
        slopes, joint, attended, dattended, dist, lse, normed, weight, x_own, dresid, gain, result,
        mid_sums, expand_sums, mid_a, mid_b, flat,
    )


def middle_kernel(
    attended, x_own, cot, vectors, expand_bias, mixer_hbm, expand_hbm, reduce_hbm,
    result, dresid, dattended, sums, expand_sums, flat, rx_a, rx_b,
    mixer, expand, reduce, att_rx, resid, normal, spread, normed, act, act_rx, dhidden,
    dn_own, dn_part, dn_rx, out_part, out_rx, dbranch, blocks,
    weight_sem, block_sem, send_sem, recv_sem, act_send, act_recv, s1_send, s1_recv,
):
    f32, bf16 = jnp.float32, jnp.bfloat16
    dp = lax.axis_index("dp")
    me = lax.axis_index("group")
    c = dp % 2
    near = (dp + 1 - 2 * c, me)
    own = pl.ds(pl.multiple_of(512 * c, 512), 512)
    other = pl.ds(pl.multiple_of(512 * (1 - c), 512), 512)

    weights = [pltpu.make_async_copy(mixer_hbm, mixer, weight_sem.at[0])]
    for k in range(4):
        part = pl.ds(pl.multiple_of(512 * (2 * k + c), 512), 512)
        weights.append(pltpu.make_async_copy(
            expand_hbm.at[:, part], expand.at[:, pl.ds(512 * k, 512)], weight_sem.at[1 + k]
        ))
    for k in range(4):
        part = pl.ds(pl.multiple_of(512 * (2 * k + c), 512), 512)
        weights.append(pltpu.make_async_copy(
            reduce_hbm.at[part], reduce.at[pl.ds(512 * k, 512)], weight_sem.at[5 + k]
        ))
    for copy in weights:
        copy.start()

    y, x = me // 2, me % 2
    greet([near, (dp, 2 * y + 1 - x), (dp, 2 * (1 - y) + x)])

    def swap(i, src, dst):
        return pltpu.make_async_remote_copy(
            src_ref=src, dst_ref=dst, send_sem=send_sem.at[i], recv_sem=recv_sem.at[i],
            device_id=near, device_id_type=MESH_ID,
        )

    att_swap = swap(0, attended, att_rx)
    normed_swap = swap(1, normed.at[own], normed.at[own])
    dn_swap = swap(2, dn_part, dn_rx)
    out_swap = swap(3, out_part, out_rx)
    branch_swap = swap(4, dbranch.at[own], dbranch.at[own])
    att_swap.start()

    mixer_bias, gain, shift, reduce_bias = (vectors[k : k + 1, :] for k in range(4))

    weights[0].wait()
    resid[...] = nn(attended[own, :], mixer[own, :]) + (x_own[...].astype(f32) + mixer_bias)
    att_swap.wait_recv()
    resid[...] += nn(att_rx[own, :], mixer[other, :])

    def norm_rows(i, carry):
        rows = pl.ds(pl.multiple_of(128 * i, 128), 128)
        here = pl.ds(pl.multiple_of(512 * c + 128 * i, 128), 128)
        values = resid[rows, :]
        center = values - jnp.mean(values, -1, keepdims=True)
        factor = lax.rsqrt(jnp.mean(center * center, -1, keepdims=True) + norm_epsilon)
        unit = center * factor
        normal[rows, :] = unit
        spread[rows, :] = jnp.broadcast_to(factor, (128, LANES))
        normed[here, :] = (unit * gain + shift).astype(bf16)
        return carry

    lax.fori_loop(0, 4, norm_rows, 0)
    normed_swap.start()

    def act_swap(half, k):
        rows = pl.ds(pl.multiple_of(512 * half, 512), 512)
        cols = pl.ds(512 * k, 512)
        return pltpu.make_async_remote_copy(
            src_ref=act.at[rows, cols], dst_ref=act_rx.at[rows, cols],
            send_sem=act_send.at[half, k], recv_sem=act_recv.at[half, k],
            device_id=near, device_id_type=MESH_ID,
        )

    root = math.sqrt(2.0 / math.pi)

    def hidden_block(half, k, first):
        rows = pl.ds(pl.multiple_of(512 * half, 512), 512)
        cols = pl.ds(512 * k, 512)
        u = nn(normed[rows, :], expand[:, cols]) + expand_bias[k : k + 1, :]
        dact = nt(cot[rows, :], reduce[cols, :])
        square = u * u
        t = jnp.tanh(u * (root + (root * 0.044715) * square))
        up = 0.5 + 0.5 * t
        act[rows, cols] = (u * up).astype(bf16)
        slope = up + (0.5 * u) * (1.0 - t * t) * (root + (3.0 * root * 0.044715) * square)
        dh = (dact * slope).astype(bf16)
        dhidden[rows, cols] = dh
        total = jnp.sum(dh.astype(f32), 0, keepdims=True)
        if first:
            expand_sums[k : k + 1, :] = total
        else:
            expand_sums[k : k + 1, :] += total
        act_swap(half, k).start()

    for k in range(4):
        weights[1 + k].wait()
        weights[5 + k].wait()
        hidden_block(c, k, True)
    normed_swap.wait_recv()
    for k in range(4):
        hidden_block(1 - c, k, False)

    def out_copy(slot, part, at):
        return pltpu.make_async_copy(
            blocks.at[slot, pl.ds(2048 * part, 2048)], flat.at[pl.ds(pl.multiple_of(at, 16), 2048)],
            block_sem.at[slot, part],
        )

    right = pl.ds(pl.multiple_of(512 * c, 512), 512)
    sent = []

    def emit(block, places):
        slot = len(sent) % 2
        if len(sent) >= 2:
            for part, at in enumerate(sent[-2]):
                out_copy(slot, part, at).wait()
        blocks[slot, : 2048 * len(places)] = block.astype(bf16).reshape(2048 * len(places), LANES)
        for part, at in enumerate(places):
            out_copy(slot, part, at).start()
        sent.append(places)

    for i in range(4):
        emit(
            tn(normed[:, 256 * i : 256 * i + 256], dhidden[...]),
            [EXPAND_AT + 4096 * i, EXPAND_AT + 4096 * i + 2048],
        )
    for source, parity in ((act, c), (act_rx, 1 - c)):
        if source is act_rx:
            for half in range(2):
                for k in range(4):
                    act_swap(half, k).wait()
        for pair in range(2):
            emit(
                tn(source[:, 1024 * pair : 1024 * pair + 1024], cot[:, right]),
                [REDUCE_AT + 2048 * (2 * k + parity) for k in (2 * pair, 2 * pair + 1)],
            )
    for part, at in list(enumerate(sent[-2])):
        out_copy((len(sent) - 2) % 2, part, at).wait()
    for part, at in list(enumerate(sent[-1])):
        out_copy((len(sent) - 1) % 2, part, at).wait()
    sent.clear()
    stages = []
    for at, q in enumerate(MIDDLE_EARLY):
        stages += first_stage(q, flat, rx_a, rx_b, at, s1_send, s1_recv, dp, me)
    for copy in stages:
        copy.start()

    dn_part[...] = nt(dhidden[other, :], expand[...])
    dn_swap.start()
    out_part[...] = nn(act[other, :], reduce[...]).astype(bf16)
    out_swap.start()

    dn_own[...] = nt(dhidden[own, :], expand[...])
    dn_swap.wait()
    sums[...] = jnp.zeros_like(sums)

    def back_rows(i, carry):
        rows = pl.ds(pl.multiple_of(128 * i, 128), 128)
        here = pl.ds(pl.multiple_of(512 * c + 128 * i, 128), 128)
        dn = dn_own[rows, :] + dn_rx[rows, :]
        unit = normal[rows, :]
        grad = cot[here, :].astype(f32)
        e = dn * gain
        down = grad + spread[rows, 0:1] * (
            e - jnp.mean(e, -1, keepdims=True) - unit * jnp.mean(e * unit, -1, keepdims=True)
        )
        dresid[rows, :] = down
        low = down.astype(bf16)
        dbranch[here, :] = low
        sums[0:1, :] += jnp.sum(low.astype(f32), 0, keepdims=True)
        sums[1:2, :] += jnp.sum(dn * unit, 0, keepdims=True)
        sums[2:3, :] += jnp.sum(dn, 0, keepdims=True)
        sums[3:4, :] += jnp.sum(grad, 0, keepdims=True)
        return carry

    lax.fori_loop(0, 4, back_rows, 0)
    branch_swap.start()
    dattended[own, :] = nt(dbranch[own, :], mixer[own, :]).astype(bf16)
    resid[...] += nn(act[own, :], reduce[...])
    out_swap.wait()
    result[...] = (resid[...] + (out_rx[...].astype(f32) + reduce_bias)).astype(bf16)
    branch_swap.wait()
    dattended[other, :] = nt(dbranch[other, :], mixer[own, :]).astype(bf16)
    emit(tn(attended[...], dbranch[:, right]), [MIXER_AT + 2048 * c])
    emit(tn(att_rx[...], dbranch[:, right]), [MIXER_AT + 2048 * (1 - c)])
    for back in (2, 1):
        for part, at in enumerate(sent[-back]):
            out_copy((len(sent) - back) % 2, part, at).wait()
    att_swap.wait_send()
    normed_swap.wait_send()
    for copy in stages:
        copy.wait()


def middle(attended, x_own, cot, vectors, expand_bias, mixer, expand, reduce):
    f32, bf16 = jnp.float32, jnp.bfloat16
    vmem = pl.BlockSpec(memory_space=pltpu.VMEM)
    hbm = pl.BlockSpec(memory_space=pl.ANY)
    count = len(MIDDLE_EARLY)
    early = jax.ShapeDtypeStruct((count, 2, HALF, LANES), bf16)
    return pl.pallas_call(
        middle_kernel,
        out_shape=(
            jax.ShapeDtypeStruct((512, WIDTH), bf16),
            jax.ShapeDtypeStruct((512, WIDTH), f32),
            jax.ShapeDtypeStruct((TOKENS, 512), bf16),
            jax.ShapeDtypeStruct((8, WIDTH), f32),
            jax.ShapeDtypeStruct((4, 512), f32),
            jax.ShapeDtypeStruct((FLAT_ROWS, LANES), bf16),
            early,
            early,
        ),
        in_specs=[vmem] * 5 + [hbm] * 3,
        out_specs=[vmem] * 5 + [hbm] * 3,
        scratch_shapes=[
            pltpu.VMEM((WIDTH, WIDTH), bf16),
            pltpu.VMEM((WIDTH, 2048), bf16),
            pltpu.VMEM((2048, WIDTH), bf16),
            pltpu.VMEM((TOKENS, 512), bf16),
            pltpu.VMEM((512, WIDTH), f32),
            pltpu.VMEM((512, WIDTH), f32),
            pltpu.VMEM((512, LANES), f32),
            pltpu.VMEM((TOKENS, WIDTH), bf16),
            pltpu.VMEM((TOKENS, 2048), bf16),
            pltpu.VMEM((TOKENS, 2048), bf16),
            pltpu.VMEM((TOKENS, 2048), bf16),
            pltpu.VMEM((512, WIDTH), f32),
            pltpu.VMEM((512, WIDTH), f32),
            pltpu.VMEM((512, WIDTH), f32),
            pltpu.VMEM((512, WIDTH), bf16),
            pltpu.VMEM((512, WIDTH), bf16),
            pltpu.VMEM((TOKENS, WIDTH), bf16),
            pltpu.VMEM((2, 4096, LANES), bf16),
            pltpu.SemaphoreType.DMA((9,)),
            pltpu.SemaphoreType.DMA((2, 2)),
            pltpu.SemaphoreType.DMA((5,)),
            pltpu.SemaphoreType.DMA((5,)),
            pltpu.SemaphoreType.DMA((2, 4)),
            pltpu.SemaphoreType.DMA((2, 4)),
            pltpu.SemaphoreType.DMA((count, 2, 2)),
            pltpu.SemaphoreType.DMA((count, 2, 2)),
        ],
        compiler_params=pltpu.CompilerParams(
            collective_id=1, has_side_effects=True, vmem_limit_bytes=62 << 20
        ),
        cost_estimate=pl.CostEstimate(flops=30 << 30, bytes_accessed=40 << 20, transcendentals=0),
    )(attended, x_own, cot, vectors, expand_bias, mixer, expand, reduce)


def owned_gradient(own, peer, small, c, owner):
    first = jnp.where(c == 0, own, peer).reshape(PIECE // 4, 1, 4, LANES)
    second = jnp.where(c == 0, peer, own).reshape(PIECE // 4, 1, 4, LANES)
    rows = jnp.concatenate([first, second], 1).reshape(2 * PIECE, LANES)
    begin = OWNED_ROWS * owner
    unit = begin // 8
    shift = jnp.where(unit < U_JBIAS, 8, jnp.where(unit < U_MBIAS, 16, 20))
    start = (4 * unit + shift) // 16 * 16

    def window(moved):
        at = begin + 2 * moved - 2 * start
        padded = jnp.pad(rows, ((16, 64), (0, 0)))
        return lax.dynamic_slice_in_dim(padded, jnp.clip(at + 16, 0, 2 * PIECE + 80 - OWNED_ROWS), OWNED_ROWS, 0)

    end_unit = (begin + OWNED_ROWS - 1) // 8
    shift_end = jnp.where(end_unit < U_JBIAS, 8, jnp.where(end_unit < U_MBIAS, 16, 20))
    flat_row = begin + jnp.arange(OWNED_ROWS, dtype=jnp.int32)
    u = flat_row // 8
    moved_row = jnp.where(u < U_JBIAS, 8, jnp.where(u < U_MBIAS, 16, 20))
    big = jnp.where((moved_row == shift)[:, None], window(shift), window(shift_end))
    places = ((0, 2, 0), (3074, 3076, 16), (4100, 4103, 32), (8199, 8203, 56), (12299, 12300, 88))
    result = big
    for first_unit, end, at in places:
        inside = (u >= first_unit) & (u < end)
        shift_small = at + begin - 8 * first_unit
        padded = jnp.pad(small, ((OWNED_ROWS, OWNED_ROWS), (0, 0)))
        part = lax.dynamic_slice_in_dim(
            padded, jnp.clip(OWNED_ROWS + shift_small, 0, OWNED_ROWS + 96), OWNED_ROWS, 0
        )
        result = jnp.where(inside[:, None], part, result)
    return result


def on_device_chip(
    dp_size, group_size,
    activations, cotangent, segments, padding, step_count, learn_rate,
    gain_before, shift_before, joint_weight, joint_bias, mixer_weight, mixer_bias,
    gain_middle, shift_middle, expand_weight, expand_bias, reduce_weight, reduce_bias,
    master_weights, first_moment, second_moment,
):
    f32, bf16 = jnp.float32, jnp.bfloat16
    dp = lax.axis_index("dp")
    group = lax.axis_index("group")
    c = dp % 2
    routes = plane_routes(dp_size, group_size)
    joint_half = half_columns(joint_weight, c)
    x_own = to_chip(activations, routes, group)
    x_own, cotangent, joint_half = lax.optimization_barrier((x_own, cotangent, joint_half))
    cot_own = to_chip(cotangent, routes, group)
    x_all = in_order(c, x_own, core_swap(x_own), 0)
    marks = jnp.stack([segments, padding])
    marks = jnp.where(c == group // 2, marks, core_swap(marks))
    marks = lax.dynamic_index_in_dim(marks, group % 2, 1, False)
    seg, pad = marks[0], marks[1]
    places = jnp.arange(TOKENS, dtype=jnp.int32)
    last = jnp.sum((seg[:, None] <= seg[None, :]).astype(jnp.int32), 0) - 1
    last = jnp.where(pad == 1, last, places)
    allowed = (places[None, :] >= places[:, None]) & (places[None, :] <= last[:, None])
    dist = jnp.where(allowed, (places[None, :] - places[:, None]).astype(f32), -masked_score)
    slopes = jnp.exp2(-8.0 * (jnp.arange(8, dtype=f32) + 8.0 * c.astype(f32) + 1.0) / HEADS)

    gain_one = gain_before.astype(f32)
    bias = half_columns(joint_bias[None], c)[0].astype(f32)
    joint_shift = jnp.concatenate([bias[:512], jnp.zeros((512,), f32), bias[512:]])
    joint_scale = jnp.concatenate([jnp.full((512,), 0.125, f32), jnp.ones((1024,), f32)])

    normal_one, _ = standardize(x_all.astype(f32))
    normed_one = (normal_one * gain_one + shift_before.astype(f32)).astype(bf16)
    joint = ((nn(normed_one, joint_half) + joint_shift) * joint_scale).astype(bf16)
    joint, cot_own = lax.optimization_barrier((joint, cot_own))
    attended, lse = attention_forward(joint, dist, slopes)
    cot_all = in_order(c, cot_own, core_swap(cot_own), 0)
    vectors = jnp.stack(
        [mixer_bias, gain_middle, shift_middle, reduce_bias, *[mixer_bias] * 4]
    ).astype(f32)
    expand_shift = half_columns(expand_bias[None], c).reshape(4, 512).astype(f32)
    result, dresid, dattended, middle_sums, expand_sums, flat, mid_a, mid_b = middle(
        attended, x_own, cot_all, vectors, expand_shift, mixer_weight, expand_weight, reduce_weight
    )
    gain = jnp.broadcast_to(gain_one[None], (8, WIDTH))
    _, own, peer, sums, output, input_gradient = rear(
        slopes, joint, attended, dattended, dist, lse, normed_one, joint_half, x_own, dresid, gain,
        result, middle_sums, expand_sums, mid_a, mid_b, flat,
    )
    small_sum = jnp.concatenate([sums[:7], sums[8:12], sums[7:8]]).reshape(96, LANES)
    owner = dp * group_size + group
    share = owned_gradient(own, peer, small_sum, c, owner).reshape(-1)
    small_share = lax.dynamic_slice_in_dim(small_sum, 3 * owner, 3, 0).reshape(-1)

    moment_step = step_count[0].astype(f32)
    rate = learn_rate[0]
    fix_one = 1.0 - jnp.exp(moment_step * math.log(beta_first))
    fix_two = 1.0 - jnp.exp(moment_step * math.log(beta_second))
    updated_first = beta_first * first_moment + (1.0 - beta_first) * share
    updated_second = beta_second * second_moment + (1.0 - beta_second) * share * share
    updated_master = master_weights - rate * (
        updated_first / fix_one / (jnp.sqrt(updated_second / fix_two) + adam_epsilon)
        + weight_decay * master_weights
    )
    return (output, input_gradient, updated_master, updated_first, updated_second, small_share)


def on_device(dp_size, group_size, activations, *rest):
    if (dp_size, group_size) == (8, 4) and activations.shape == (2, 256, WIDTH):
        return on_device_chip(dp_size, group_size, activations, *rest)
    return on_device_general(activations, *rest)


def solution(mesh):
    in_specs = (
        P("dp", "group", None),
        P("dp", "group", None),
        P("dp", None),
        P("dp", None),
        P(),
        P(),
        P(),
        P(),
        P(),
        P(),
        P(),
        P(),
        P(),
        P(),
        P(),
        P(),
        P(),
        P(),
        P(("dp", "group")),
        P(("dp", "group")),
        P(("dp", "group")),
    )
    out_specs = (
        P("dp", "group", None),
        P("dp", "group", None),
        P(("dp", "group")),
        P(("dp", "group")),
        P(("dp", "group")),
        P(("dp", "group")),
    )
    return jax.shard_map(
        functools.partial(on_device, mesh.shape["dp"], mesh.shape["group"]), mesh=mesh, in_specs=in_specs, out_specs=out_specs, check_vma=False
    )
```

```python
import functools
import math

import jax
import jax.numpy as jnp
from jax import lax
from jax.experimental import pallas as pl
from jax.experimental.pallas import tpu as pltpu
from jax.sharding import PartitionSpec as P

HEADS = 16
DOC_MOST = 800


beta_first = 0.9
beta_second = 0.95
adam_epsilon = 1e-08
weight_decay = 0.1
norm_epsilon = 1e-05
masked_score = -1e30


def shifted(block, axis, distance):
    devices = range(lax.axis_size(axis))
    route = [(i - distance, i) for i in devices if i - distance in devices]
    return lax.ppermute(block, axis, route)


def standardize(values):
    center = values - jnp.mean(values, -1, keepdims=True)
    spread = lax.rsqrt(jnp.mean(center * center, -1, keepdims=True) + norm_epsilon)
    return (center * spread, spread)


def norm_back(dnormed, normed, spread):
    return spread * (
        dnormed
        - jnp.mean(dnormed, -1, keepdims=True)
        - normed * jnp.mean(dnormed * normed, -1, keepdims=True)
    )


def window_mask(segments, padding, member, hop, block_len):
    places = jnp.arange(block_len, dtype=jnp.int32)
    source = member - hop
    query_place = member * block_len + places
    key_place = source * block_len + places
    start = jnp.maximum(source, 0) * block_len
    seg_query = lax.dynamic_slice_in_dim(segments, member * block_len, block_len, 1)
    seg_key = lax.dynamic_slice_in_dim(segments, start, block_len, 1)
    pad_key = lax.dynamic_slice_in_dim(padding, start, block_len, 1)
    earlier = key_place[None, None, :] <= query_place[None, :, None]
    itself = key_place[None, None, :] == query_place[None, :, None]
    allowed = (
        (seg_query[:, :, None] == seg_key[:, None, :])
        & earlier
        & ((pad_key[:, None, :] == 1) | itself)
        & (source >= 0)
    )
    distance = (query_place[:, None] - key_place[None, :]).astype(jnp.float32)
    return (allowed[:, None], distance)


def piece_scores(query4, key4, slopes, distance, score_scale):
    raw = jnp.einsum("sqhd,skhd->shqk", query4, key4, preferred_element_type=jnp.float32)
    return raw * score_scale - slopes[:, None, None] * distance[None]


def on_device_general(
    activations,
    cotangent,
    segments,
    padding,
    step_count,
    learn_rate,
    gain_before,
    shift_before,
    joint_weight,
    joint_bias,
    mixer_weight,
    mixer_bias,
    gain_middle,
    shift_middle,
    expand_weight,
    expand_bias,
    reduce_weight,
    reduce_bias,
    master_weights,
    first_moment,
    second_moment,
):
    seq_count, block_len, width = activations.shape
    head_size = width // HEADS
    row_count = seq_count * block_len
    shape4 = (seq_count, block_len, HEADS, head_size)
    score_scale = 1.0 / math.sqrt(head_size)
    group_size = lax.axis_size("group")
    member = lax.axis_index("group")
    reach = min((DOC_MOST + block_len - 2) // block_len, group_size - 1)
    slopes = jnp.exp2(-8.0 * (jnp.arange(HEADS, dtype=jnp.float32) + 1.0) / HEADS)
    inputs = activations.reshape(row_count, width).astype(jnp.float32)
    gain_one = gain_before.astype(jnp.float32)
    gain_two = gain_middle.astype(jnp.float32)
    normal_one, spread_one = standardize(inputs)
    normed_one = (normal_one * gain_one + shift_before.astype(jnp.float32)).astype(jnp.bfloat16)
    joint = jnp.dot(normed_one, joint_weight, preferred_element_type=jnp.float32)
    bias_joint = joint_bias.astype(jnp.float32)
    query_rows = (joint[:, :width] + bias_joint[:width]).astype(jnp.bfloat16)
    key_rows = joint[:, width : 2 * width].astype(jnp.bfloat16)
    value_rows = (joint[:, 2 * width :] + bias_joint[width:]).astype(jnp.bfloat16)
    own_piece = jnp.stack([key_rows, value_rows]).reshape(2, seq_count, block_len, width)
    query4 = query_rows.reshape(shape4)
    pieces = [own_piece]
    for hop in range(1, reach + 1):
        pieces.append(shifted(own_piece, "group", hop))
    row_top = jnp.full((seq_count, HEADS, block_len), masked_score, jnp.float32)
    row_total = jnp.zeros((seq_count, HEADS, block_len), jnp.float32)
    for hop in range(reach + 1):
        allowed, distance = window_mask(segments, padding, member, hop, block_len)
        scores = piece_scores(query4, pieces[hop][0].reshape(shape4), slopes, distance, score_scale)
        fresh = jnp.maximum(row_top, jnp.max(jnp.where(allowed, scores, masked_score), -1))
        row_total = row_total * jnp.exp(row_top - fresh) + jnp.sum(
            jnp.exp(jnp.where(allowed, scores - fresh[..., None], masked_score)), -1
        )
        row_top = fresh
    log_total = row_top + jnp.log(row_total)
    attended = jnp.zeros(shape4, jnp.float32)
    for hop in range(reach + 1):
        allowed, distance = window_mask(segments, padding, member, hop, block_len)
        scores = piece_scores(query4, pieces[hop][0].reshape(shape4), slopes, distance, score_scale)
        probs = jnp.exp(jnp.where(allowed, scores - log_total[..., None], masked_score)).astype(
            jnp.bfloat16
        )
        attended = attended + jnp.einsum(
            "shqk,skhd->sqhd",
            probs,
            pieces[hop][1].reshape(shape4),
            preferred_element_type=jnp.float32,
        )
    attended_low = attended.reshape(row_count, width).astype(jnp.bfloat16)
    resid = inputs + (
        jnp.dot(attended_low, mixer_weight, preferred_element_type=jnp.float32)
        + mixer_bias.astype(jnp.float32)
    )
    normal_two, spread_two = standardize(resid)
    normed_two = (normal_two * gain_two + shift_middle.astype(jnp.float32)).astype(jnp.bfloat16)
    hidden = jnp.dot(
        normed_two, expand_weight, preferred_element_type=jnp.float32
    ) + expand_bias.astype(jnp.float32)
    act = jax.nn.gelu(hidden, approximate=True).astype(jnp.bfloat16)
    result = resid + (
        jnp.dot(act, reduce_weight, preferred_element_type=jnp.float32)
        + reduce_bias.astype(jnp.float32)
    )
    output = result.astype(jnp.bfloat16).reshape(seq_count, block_len, width)
    cot_low = cotangent.reshape(row_count, width)
    cot_full = cot_low.astype(jnp.float32)
    reduce_grad = jnp.einsum("tf,td->fd", act, cot_low, preferred_element_type=jnp.float32)
    reduce_bias_grad = jnp.sum(cot_full, 0)
    dact = jnp.einsum("td,fd->tf", cot_low, reduce_weight, preferred_element_type=jnp.float32)
    gelu_pull = jax.vjp(lambda inner: jax.nn.gelu(inner, approximate=True), hidden)[1]
    dhidden = gelu_pull(dact)[0].astype(jnp.bfloat16)
    expand_grad = jnp.einsum("td,tf->df", normed_two, dhidden, preferred_element_type=jnp.float32)
    expand_bias_grad = jnp.sum(dhidden.astype(jnp.float32), 0)
    dnormed_two = jnp.einsum(
        "tf,df->td", dhidden, expand_weight, preferred_element_type=jnp.float32
    )
    gain_middle_grad = jnp.sum(dnormed_two * normal_two, 0)
    shift_middle_grad = jnp.sum(dnormed_two, 0)
    dresid = cot_full + norm_back(dnormed_two * gain_two, normal_two, spread_two)
    dbranch = dresid.astype(jnp.bfloat16)
    mixer_grad = jnp.einsum("td,te->de", attended_low, dbranch, preferred_element_type=jnp.float32)
    mixer_bias_grad = jnp.sum(dbranch.astype(jnp.float32), 0)
    dattended = jnp.einsum(
        "te,de->td", dbranch, mixer_weight, preferred_element_type=jnp.float32
    ).astype(jnp.bfloat16)
    dattended4 = dattended.reshape(shape4)
    row_delta = jnp.einsum("sqhd,sqhd->shq", dattended4.astype(jnp.float32), attended)
    dquery = jnp.zeros(shape4, jnp.float32)
    dkv_own = jnp.zeros((2, seq_count, block_len, width), jnp.float32)
    for hop in range(reach + 1):
        piece = pieces[hop]
        key4 = piece[0].reshape(shape4)
        value4 = piece[1].reshape(shape4)
        allowed, distance = window_mask(segments, padding, member, hop, block_len)
        scores = piece_scores(query4, key4, slopes, distance, score_scale)
        probs = jnp.exp(jnp.where(allowed, scores - log_total[..., None], masked_score))
        dvalue = jnp.einsum(
            "shqk,sqhd->skhd",
            probs.astype(jnp.bfloat16),
            dattended4,
            preferred_element_type=jnp.float32,
        )
        dprobs = jnp.einsum(
            "sqhd,skhd->shqk", dattended4, value4, preferred_element_type=jnp.float32
        )
        dscores = (probs * (dprobs - row_delta[..., None])).astype(jnp.bfloat16)
        dquery = dquery + jnp.einsum(
            "shqk,skhd->sqhd", dscores, key4, preferred_element_type=jnp.float32
        )
        dkey = (
            jnp.einsum("shqk,sqhd->skhd", dscores, query4, preferred_element_type=jnp.float32)
            * score_scale
        )
        returned = jnp.stack([dkey, dvalue]).reshape(2, seq_count, block_len, width)
        if hop == 0:
            dkv_own = returned
        else:
            dkv_own = dkv_own + shifted(returned.astype(jnp.bfloat16), "group", -hop).astype(
                returned.dtype
            )
    dquery_low = (dquery * score_scale).reshape(row_count, width).astype(jnp.bfloat16)
    dkey_low = dkv_own[0].reshape(row_count, width).astype(jnp.bfloat16)
    dvalue_low = dkv_own[1].reshape(row_count, width).astype(jnp.bfloat16)
    djoint = jnp.concatenate([dquery_low, dkey_low, dvalue_low], 1)
    joint_grad = jnp.einsum("td,te->de", normed_one, djoint, preferred_element_type=jnp.float32)
    joint_bias_grad = jnp.concatenate(
        [jnp.sum(dquery_low.astype(jnp.float32), 0), jnp.sum(dvalue_low.astype(jnp.float32), 0)]
    )
    dnormed_one = jnp.einsum("te,de->td", djoint, joint_weight, preferred_element_type=jnp.float32)
    gain_before_grad = jnp.sum(dnormed_one * normal_one, 0)
    shift_before_grad = jnp.sum(dnormed_one, 0)
    dinput = dresid + norm_back(dnormed_one * gain_one, normal_one, spread_one)
    input_gradient = dinput.astype(jnp.bfloat16).reshape(seq_count, block_len, width)
    listing = [
        gain_before_grad,
        shift_before_grad,
        joint_grad,
        joint_bias_grad,
        mixer_grad,
        mixer_bias_grad,
        gain_middle_grad,
        shift_middle_grad,
        expand_grad,
        expand_bias_grad,
        reduce_grad,
        reduce_bias_grad,
    ]
    gradient = jnp.concatenate([single.reshape(-1) for single in listing])
    small_list = [
        gain_before_grad,
        shift_before_grad,
        joint_bias_grad,
        mixer_bias_grad,
        gain_middle_grad,
        shift_middle_grad,
        expand_bias_grad,
        reduce_bias_grad,
    ]
    small_local = jnp.concatenate(small_list)
    share, small_share = (
        lax.psum_scatter(gradient, ("dp", "group"), scatter_dimension=0, tiled=True),
        lax.psum_scatter(small_local, ("dp", "group"), scatter_dimension=0, tiled=True),
    )
    moment_step = step_count[0].astype(jnp.float32)
    rate = learn_rate[0]
    fix_one = 1.0 - jnp.exp(moment_step * math.log(beta_first))
    fix_two = 1.0 - jnp.exp(moment_step * math.log(beta_second))
    updated_first = beta_first * first_moment + (1.0 - beta_first) * share
    updated_second = beta_second * second_moment + (1.0 - beta_second) * share * share
    updated_master = master_weights - rate * (
        updated_first / fix_one / (jnp.sqrt(updated_second / fix_two) + adam_epsilon)
        + weight_decay * master_weights
    )
    return (output, input_gradient, updated_master, updated_first, updated_second, small_share)


WIDTH = 1024
HIDDEN = 4096
TOKENS = 1024
LANES = 128
OWNED = 393600
OWNED_ROWS = OWNED // LANES
PIECE = 1568
HALF = PIECE // 2
JOINT_AT, MIXER_AT, EXPAND_AT, REDUCE_AT = 16, 12320, 16432, 32832
FLAT_ROWS = 49248
U_JOINT, U_JBIAS, U_MIXER, U_MBIAS, U_EXPAND, U_EBIAS, U_REDUCE, U_RBIAS = (
    2, 3074, 3076, 4100, 4103, 8199, 8203, 12299,
)


def section_shift(unit):
    return 8 if unit < U_JBIAS else 16 if unit < U_MBIAS else 20


def piece_start(owner):
    unit = OWNED_ROWS * owner // 8
    return (4 * unit + section_shift(unit)) // 16 * 16


def piece_offset(q, y, x):
    at = [piece_start(4 * q + k) // 16 for k in range(4)]
    row = (
        at[0] * (1 - y) * (1 - x) + at[1] * (1 - y) * x + at[2] * y * (1 - x) + at[3] * y * x
    )
    return pl.multiple_of(row * 16, 16)


MESH_ID = pl.DeviceIdType.MESH


def by_rows(step):
    def one(i, carry):
        step(pl.ds(pl.multiple_of(112 * i, 16), 112))
        return carry

    lax.fori_loop(0, HALF // 112, one, 0)


class Pieces:
    def __init__(self, dp, me, flat, own_a, own_b, rx_a1, rx_b1, rx_a2, rx_b2, acc, load_sem, s2_send, s2_recv):
        self.y, self.x = me // 2, me % 2
        self.x_near = (dp, 2 * self.y + (1 - self.x))
        self.y_near = (dp, 2 * (1 - self.y) + self.x)
        self.flat, self.own_a, self.own_b = flat, own_a, own_b
        self.rx_a1, self.rx_b1, self.rx_a2, self.rx_b2, self.acc = rx_a1, rx_b1, rx_a2, rx_b2, acc
        self.load_sem, self.s2_send, self.s2_recv = load_sem, s2_send, s2_recv

    def loads(self, q, own_slot, ready=None):
        slot = q
        out = []
        for k in range(2):
            for way, (row, own) in enumerate((
                (piece_offset(q, k, self.x), self.own_a),
                (piece_offset(q, self.y, k) + HALF, self.own_b),
            )):
                out.append(pltpu.make_async_copy(
                    self.flat.at[pl.ds(row, HALF)], own.at[own_slot, k], self.load_sem.at[slot, way, k]
                ))
            if ready is not None:
                ready_a, ready_b, at = ready
                for way, (src, dst) in enumerate(((ready_a, self.rx_a1), (ready_b, self.rx_b1))):
                    out.append(pltpu.make_async_copy(
                        src.at[at, k], dst.at[slot, k], self.load_sem.at[slot, 2 + way, k]
                    ))
        return out

    def second(self, slot):
        y, x = self.y, self.x
        return [
            pltpu.make_async_remote_copy(
                src_ref=src, dst_ref=dst.at[slot], send_sem=self.s2_send.at[slot, way],
                recv_sem=self.s2_recv.at[slot, way], device_id=near, device_id_type=MESH_ID,
            )
            for way, (src, dst, near) in enumerate((
                (self.rx_a1.at[slot, 1 - y], self.rx_a2, self.y_near),
                (self.rx_b1.at[slot, 1 - x], self.rx_b2, self.x_near),
            ))
        ]

    def meet(self, slot, own_slot):
        y, x = self.y, self.x
        rx_a1, rx_b1, own_a, own_b, acc = self.rx_a1, self.rx_b1, self.own_a, self.own_b, self.acc

        def away(rows):
            rx_a1[slot, 1 - y, rows] = rx_a1[slot, 1 - y, rows] + own_a[own_slot, 1 - y, rows]
            rx_b1[slot, 1 - x, rows] = rx_b1[slot, 1 - x, rows] + own_b[own_slot, 1 - x, rows]

        by_rows(away)
        for copy in self.second(slot):
            copy.start()

        def kept(rows):
            acc[slot, 0, rows] = rx_a1[slot, y, rows] + own_a[own_slot, y, rows]
            acc[slot, 1, rows] = rx_b1[slot, x, rows] + own_b[own_slot, x, rows]

        by_rows(kept)

    def join(self, slot):
        for copy in self.second(slot):
            copy.wait_recv()
        acc, rx_a2, rx_b2 = self.acc, self.rx_a2, self.rx_b2

        def add(rows):
            acc[slot, 0, rows] = acc[slot, 0, rows] + rx_a2[slot, rows]
            acc[slot, 1, rows] = acc[slot, 1, rows] + rx_b2[slot, rows]

        by_rows(add)


MIDDLE_EARLY = (4, 5)


def half_columns(weight, c, axis=1):
    count = weight.shape[axis] // 1024
    return jnp.concatenate(
        [lax.dynamic_slice_in_dim(weight, 1024 * k + 512 * c, 512, axis) for k in range(count)],
        axis,
    )


def nn(a, b):
    return lax.dot_general(a, b, (((1,), (0,)), ((), ())), preferred_element_type=jnp.float32)


def nt(a, b):
    return lax.dot_general(a, b, (((1,), (1,)), ((), ())), preferred_element_type=jnp.float32)


def tn(a, b):
    return lax.dot_general(a, b, (((0,), (0,)), ((), ())), preferred_element_type=jnp.float32)


def head_lanes(value, h):
    lane = lax.broadcasted_iota(jnp.int32, (1, LANES), 1)
    return jnp.where(lane // 64 == h, value, jnp.zeros_like(value))


def plane_devices(dp, me):
    z, c = dp // 2, dp % 2
    near = [(2 * z + 1 - c, me)]
    for d in (1, 2, 3):
        near += [(2 * z, (me + d) % 4), (2 * z + 1, (me + d) % 4)]
    return near


def greet(devices):
    barrier = pltpu.get_barrier_semaphore()
    for near in devices:
        pl.semaphore_signal(barrier, inc=1, device_id=near, device_id_type=MESH_ID)
    pl.semaphore_wait(barrier, len(devices))


class Home:
    def __init__(self, rows, out, dp, me, send_sem, recv_sem):
        z, c = dp // 2, dp % 2
        self.here = c == me // 2
        self.turns = []
        for turn in range(2):
            src = rows.at[pl.ds(256 * turn, 256)]
            dst = out.at[me % 2]
            away = pltpu.make_async_remote_copy(
                src_ref=src, dst_ref=dst, send_sem=send_sem.at[turn], recv_sem=recv_sem.at[me % 2],
                device_id=(2 * z + me // 2, 2 * c + turn), device_id_type=MESH_ID,
            )
            near = pltpu.make_async_copy(src, dst, send_sem.at[turn])
            came = pltpu.make_async_remote_copy(
                src_ref=src, dst_ref=out.at[turn], send_sem=send_sem.at[turn],
                recv_sem=recv_sem.at[turn], device_id=(2 * z + me // 2, 2 * c + turn),
                device_id_type=MESH_ID,
            )
            self.turns.append((away, near, came, self.here & (me % 2 == turn)))

    def start(self):
        for away, near, _, stays in self.turns:
            @pl.when(stays)
            def _():
                near.start()

            @pl.when(jnp.logical_not(stays))
            def _():
                away.start()

    def wait(self):
        for away, near, came, stays in self.turns:
            @pl.when(stays)
            def _():
                near.wait()

            @pl.when(jnp.logical_not(stays))
            def _():
                away.wait_send()
                came.wait_recv()


def first_stage(q, flat, rx_a, rx_b, at, send_sem, recv_sem, dp, me):
    y, x = me // 2, me % 2
    x_near = (dp, 2 * y + (1 - x))
    y_near = (dp, 2 * (1 - y) + x)
    out = []
    for k in range(2):
        for way, (row, rx, near) in enumerate((
            (piece_offset(q, k, 1 - x), rx_a, x_near),
            (piece_offset(q, 1 - y, k) + HALF, rx_b, y_near),
        )):
            out.append(pltpu.make_async_remote_copy(
                src_ref=flat.at[pl.ds(row, HALF)], dst_ref=rx.at[at, k],
                send_sem=send_sem.at[at, way, k], recv_sem=recv_sem.at[at, way, k],
                device_id=near, device_id_type=MESH_ID,
            ))
    return out


class Spread:
    def __init__(self, blocks, rows, dp, me, send_sem, recv_sem):
        z, c = dp // 2, dp % 2
        here = c == me // 2
        self.turns = []
        for turn in range(2):
            src = blocks.at[turn]
            dst = rows.at[pl.ds(pl.multiple_of(256 * me, 256), 256)]
            away = pltpu.make_async_remote_copy(
                src_ref=src, dst_ref=dst, send_sem=send_sem.at[turn], recv_sem=recv_sem.at[me % 2],
                device_id=(2 * z + me // 2, 2 * c + turn), device_id_type=MESH_ID,
            )
            near = pltpu.make_async_copy(src, dst, send_sem.at[turn])
            came = pltpu.make_async_remote_copy(
                src_ref=src, dst_ref=rows.at[pl.ds(pl.multiple_of(512 * c + 256 * turn, 256), 256)],
                send_sem=send_sem.at[turn], recv_sem=recv_sem.at[turn],
                device_id=(2 * z + me // 2, 2 * c + turn), device_id_type=MESH_ID,
            )
            self.turns.append((away, near, came, here & (me % 2 == turn)))

    def start(self):
        for away, near, _, stays in self.turns:
            @pl.when(stays)
            def _():
                near.start()

            @pl.when(jnp.logical_not(stays))
            def _():
                away.start()

    def wait_came(self, turn):
        _, near, came, stays = self.turns[turn]

        @pl.when(stays)
        def _():
            near.wait()

        @pl.when(jnp.logical_not(stays))
        def _():
            came.wait_recv()

    def wait_sent(self):
        for away, _, _, stays in self.turns:
            @pl.when(jnp.logical_not(stays))
            def _():
                away.wait_send()


def front_kernel(
    slopes, blocks, cot_blocks, marks, vectors, joint_vectors, weight_hbm,
    x_out, cot_out, normed_out, joint_out, dist_out, att_out, lse_out,
    x_all, cot_all, normed, joint, weight, dist, att, lse, marks_rx, columns, s_ref, p_ref, vt_ref, ot_ref,
    weight_sem, out_sem, mark_sem, x_send, x_recv, cot_send, cot_recv, pass_send, pass_recv,
):
    f32, bf16 = jnp.float32, jnp.bfloat16
    dp = lax.axis_index("dp")
    me = lax.axis_index("group")
    c = dp % 2
    core_near = (dp + 1 - 2 * c, me)
    own = pl.ds(pl.multiple_of(512 * c, 512), 512)
    other = pl.ds(pl.multiple_of(512 * (1 - c), 512), 512)

    weights = [
        pltpu.make_async_copy(
            weight_hbm.at[:, pl.ds(pl.multiple_of(1024 * p + 512 * c, 512), 512)],
            weight.at[:, pl.ds(512 * p, 512)], weight_sem.at[p],
        )
        for p in range(3)
    ]
    greet(plane_devices(dp, me))
    x_way = Spread(blocks, x_all, dp, me, x_send, x_recv)
    cot_way = Spread(cot_blocks, cot_all, dp, me, cot_send, cot_recv)
    x_way.start()
    mark_swap = pltpu.make_async_remote_copy(
        src_ref=marks, dst_ref=marks_rx, send_sem=mark_sem.at[0], recv_sem=mark_sem.at[1],
        device_id=core_near, device_id_type=MESH_ID,
    )
    mark_swap.start()
    for copy in weights:
        copy.start()

    def hand_over(rows, way, turn):
        at = pl.ds(pl.multiple_of(512 * c + 256 * turn, 256), 256)
        return pltpu.make_async_remote_copy(
            src_ref=rows.at[at], dst_ref=rows.at[at], send_sem=pass_send.at[way, turn],
            recv_sem=pass_recv.at[way, turn], device_id=core_near, device_id_type=MESH_ID,
        )

    mark_swap.wait()
    held = jnp.where(c == me // 2, marks[...], marks_rx[...]).astype(f32)
    odd = me % 2 == 1
    seg = jnp.where(odd, held[1:2], held[0:1])
    pad = jnp.where(odd, held[3:4], held[2:3])
    kind = lax.broadcasted_iota(jnp.int32, (8, TOKENS), 0)
    columns[...] = jnp.broadcast_to(
        jnp.where(kind == 0, seg, pad).T[:, :8].reshape(TOKENS, 8), (TOKENS, 8)
    )

    def dist_rows(i, carry):
        rows = pl.ds(pl.multiple_of(128 * i, 128), 128)
        key_seg, key_pad = columns[rows, 0:1], columns[rows, 1:2]
        key = (lax.broadcasted_iota(jnp.int32, (128, 1), 0) + 128 * i).astype(f32)
        query = lax.broadcasted_iota(jnp.int32, (128, TOKENS), 1).astype(f32)
        last = jnp.sum(jnp.where(seg <= key_seg, 1.0, 0.0), 1, keepdims=True) - 1.0
        last = jnp.where(key_pad == 1.0, last, key)
        dist[rows, :] = jnp.where((query >= key) & (query <= last), query - key, -masked_score)
        return carry

    lax.fori_loop(0, 8, dist_rows, 0)
    outs = []

    def put(src, dst):
        copy = pltpu.make_async_copy(src, dst, out_sem.at[len(outs)])
        copy.start()
        outs.append(copy)

    put(dist, dist_out)
    gain, shift = vectors[0:1, :], vectors[1:2, :]

    def norm_rows(half):
        def one(i, carry):
            rows = pl.ds(pl.multiple_of(512 * half + 128 * i, 128), 128)
            values = x_all[rows, :].astype(f32)
            center = values - jnp.mean(values, -1, keepdims=True)
            factor = lax.rsqrt(jnp.mean(center * center, -1, keepdims=True) + norm_epsilon)
            normed[rows, :] = (center * factor * gain + shift).astype(bf16)
            return carry

        lax.fori_loop(0, 4, one, 0)
        rows = pl.ds(pl.multiple_of(512 * half, 512), 512)
        joint[rows, :] = (
            (nn(normed[rows, :], weight[...]) + joint_vectors[0:1, :]) * joint_vectors[1:2, :]
        ).astype(bf16)

    for turn in range(2):
        x_way.wait_came(turn)
        hand_over(x_all, 0, turn).start()
    x_way.wait_sent()
    cot_way.start()
    put(x_all.at[own], x_out)
    for copy in weights:
        copy.wait()
    norm_rows(c)
    for turn in range(2):
        hand_over(x_all, 0, turn).wait_recv()
    norm_rows(1 - c)
    put(normed, normed_out)
    put(joint, joint_out)

    def pair_step(pair, carry):
        def lanes(block):
            return pl.ds(pl.multiple_of(512 * block + LANES * pair, LANES), LANES)

        vt_ref[...] = joint[:, lanes(2)].astype(f32).T.astype(bf16)
        ot_ref[...] = jnp.zeros_like(ot_ref)

        def head(h, carry):
            slope = slopes[2 * pair + h]
            for qb in range(4):
                cols = pl.ds(qb * 256, 256)
                queries = head_lanes(joint[cols, lanes(0)], h)
                top = None
                for kb in range(qb + 1):
                    rows = pl.ds(kb * 256, 256)
                    s = nt(joint[rows, lanes(1)], queries) - slope * dist[rows, cols]
                    s_ref[rows, :] = s
                    high = jnp.max(s, 0, keepdims=True)
                    top = high if top is None else jnp.maximum(top, high)
                total = None
                for kb in range(qb + 1):
                    rows = pl.ds(kb * 256, 256)
                    p = jnp.exp(s_ref[rows, :] - top)
                    more = jnp.sum(p, 0, keepdims=True)
                    total = more if total is None else total + more
                    p_ref[rows, :] = p.astype(bf16)
                span = pl.ds(0, 256 * (qb + 1))
                out = nn(vt_ref[:, span], p_ref[span, :]) / total
                row = lax.broadcasted_iota(jnp.int32, (LANES, 1), 0)
                ot_ref[:, cols] = jnp.where(row // 64 == h, out, ot_ref[:, cols])
                lse[pair, pl.ds(h, 1), cols] = top + jnp.log(total)
            return carry

        lax.fori_loop(0, 2, head, 0)
        att[:, lanes(0)] = ot_ref[...].T.astype(bf16)

        @pl.when(pair == 2)
        def _():
            for turn in range(2):
                cot_way.wait_came(turn)
                hand_over(cot_all, 1, turn).start()

        return carry

    lax.fori_loop(0, 4, pair_step, 0)
    put(att, att_out)
    put(lse, lse_out)
    for turn in range(2):
        hand_over(cot_all, 1, turn).wait()
        hand_over(x_all, 0, turn).wait_send()
    put(cot_all, cot_out)
    cot_way.wait_sent()
    for copy in outs:
        copy.wait()


def front(slopes, blocks, cot_blocks, marks, vectors, joint_vectors, weight):
    f32, bf16 = jnp.float32, jnp.bfloat16
    vmem = pl.BlockSpec(memory_space=pltpu.VMEM)
    hbm = pl.BlockSpec(memory_space=pl.ANY)
    return pl.pallas_call(
        front_kernel,
        out_shape=(
            jax.ShapeDtypeStruct((512, WIDTH), bf16),
            jax.ShapeDtypeStruct((TOKENS, WIDTH), bf16),
            jax.ShapeDtypeStruct((TOKENS, WIDTH), bf16),
            jax.ShapeDtypeStruct((TOKENS, 1536), bf16),
            jax.ShapeDtypeStruct((TOKENS, TOKENS), f32),
            jax.ShapeDtypeStruct((TOKENS, 512), bf16),
            jax.ShapeDtypeStruct((4, 2, TOKENS), f32),
        ),
        in_specs=[pl.BlockSpec(memory_space=pltpu.SMEM)] + [hbm] * 2 + [vmem] * 3 + [hbm],
        out_specs=[hbm] * 7,
        scratch_shapes=[
            pltpu.VMEM((TOKENS, WIDTH), bf16),
            pltpu.VMEM((TOKENS, WIDTH), bf16),
            pltpu.VMEM((TOKENS, WIDTH), bf16),
            pltpu.VMEM((TOKENS, 1536), bf16),
            pltpu.VMEM((WIDTH, 1536), bf16),
            pltpu.VMEM((TOKENS, TOKENS), f32),
            pltpu.VMEM((TOKENS, 512), bf16),
            pltpu.VMEM((4, 2, TOKENS), f32),
            pltpu.VMEM((8, TOKENS), jnp.int32),
            pltpu.VMEM((TOKENS, 8), f32),
            pltpu.VMEM((TOKENS, 256), f32),
            pltpu.VMEM((TOKENS, 256), bf16),
            pltpu.VMEM((LANES, TOKENS), bf16),
            pltpu.VMEM((LANES, TOKENS), f32),
            pltpu.SemaphoreType.DMA((3,)),
            pltpu.SemaphoreType.DMA((7,)),
            pltpu.SemaphoreType.DMA((2,)),
            pltpu.SemaphoreType.DMA((2,)),
            pltpu.SemaphoreType.DMA((2,)),
            pltpu.SemaphoreType.DMA((2,)),
            pltpu.SemaphoreType.DMA((2,)),
            pltpu.SemaphoreType.DMA((2, 2)),
            pltpu.SemaphoreType.DMA((2, 2)),
        ],
        compiler_params=pltpu.CompilerParams(
            collective_id=0, has_side_effects=True, vmem_limit_bytes=56 << 20
        ),
        cost_estimate=pl.CostEstimate(flops=10 << 30, bytes_accessed=20 << 20, transcendentals=0),
    )(slopes, blocks, cot_blocks, marks, vectors, joint_vectors, weight)


def rear_kernel(
    slopes, joint_hbm, att_hbm, datt_hbm, dist_hbm, lse, normed_hbm, weight_hbm, x_hbm, dresid_hbm, gain,
    result, mid_sums, expand_sums, mid_a, mid_b, flat_in,
    flat, own_out, peer_out, small_out, output, input_gradient,
    joint, attended, dattended, normed, weight, x_own, dresid,
    dist, p_ref, ds_ref, kt_ref, dqt_ref, dk_acc, dv_acc, delta_ref, djoint, dn_rx, dinput, blocks,
    own_a, own_b, rx_a1, rx_b1, rx_a2, rx_b2, acc, rx_up, rx_dn, parting,
    small_mine, small_rx, small_z,
    dist_sem, block_sem, swap_sem, load_sem, s1_send, s1_recv, s2_send, s2_recv, z_send, z_recv,
    last_sem, sm_send, sm_recv, out_send, out_recv, in_send, in_recv,
):
    f32, bf16 = jnp.float32, jnp.bfloat16
    dp = lax.axis_index("dp")
    me = lax.axis_index("group")
    z, c = dp // 2, dp % 2
    y, x = me // 2, me % 2
    x_near = (dp, 2 * y + (1 - x))
    y_near = (dp, 2 * (1 - y) + x)
    core_near = (2 * z + 1 - c, me)
    own = pl.ds(pl.multiple_of(512 * c, 512), 512)
    other = pl.ds(pl.multiple_of(512 * (1 - c), 512), 512)

    def z_at(d):
        return (2 * d + c, me)

    pieces = Pieces(
        dp, me, flat, own_a, own_b, rx_a1, rx_b1, rx_a2, rx_b2, acc, load_sem, s2_send, s2_recv
    )
    own_slot = {4: 0, 5: 1, 6: 2, 7: 3, 0: 0, 1: 1, 3: 2, 2: 3}

    def loads(q):
        ready = (mid_a, mid_b, MIDDLE_EARLY.index(q)) if q in MIDDLE_EARLY else None
        return pieces.loads(q, own_slot[q], ready)

    def start(copies):
        for copy in copies:
            copy.start()

    def stage1(q):
        return first_stage(q, flat, rx_a1, rx_b1, q, s1_send, s1_recv, dp, me)

    def hop(q, up):
        return pltpu.make_async_remote_copy(
            src_ref=acc.at[q], dst_ref=rx_up.at[q - 2] if up else rx_dn.at[q],
            send_sem=z_send.at[q, 0 if up else 1], recv_sem=z_recv.at[q, 0 if up else 1],
            device_id=z_at((z + 1) % 4 if up else (z + 3) % 4), device_id_type=MESH_ID,
        )

    def meet(q):
        for copy in loads(q):
            copy.wait()
        if q not in MIDDLE_EARLY:
            for copy in stage1(q):
                copy.wait_recv()
        pieces.meet(q, own_slot[q])

    def add_came(q, rx, at):
        def add(rows):
            for k in range(2):
                acc[q, k, rows] = acc[q, k, rows] + rx[at, k, rows]

        by_rows(add)

    def pass_on(q, h):
        aim = q // 2
        if h < aim:
            @pl.when(z == h)
            def _():
                if h > 0:
                    hop(q, True).wait_recv()
                    add_came(q, rx_up, q - 2)
                hop(q, True).start()
        if h < 3 - aim:
            @pl.when(z == 3 - h)
            def _():
                if h > 0:
                    hop(q, False).wait_recv()
                    add_came(q, rx_dn, q)
                hop(q, False).start()

    last = pltpu.make_async_remote_copy(
        src_ref=parting, dst_ref=peer_out, send_sem=last_sem.at[0], recv_sem=last_sem.at[1],
        device_id=core_near, device_id_type=MESH_ID,
    )

    def finish(q):
        aim = q // 2

        @pl.when(z == aim)
        def _():
            if aim > 0:
                hop(q, True).wait_recv()
            if aim < 3:
                hop(q, False).wait_recv()
            mine = c == q % 2
            for k in range(2):
                def add(i, carry):
                    rows = pl.ds(pl.multiple_of(112 * i, 16), 112)
                    place = pl.ds(pl.multiple_of(HALF * k + 112 * i, 16), 112)
                    total = acc[q, k, rows].astype(f32)
                    if aim > 0:
                        total = total + rx_up[q - 2, k, rows].astype(f32)
                    if aim < 3:
                        total = total + rx_dn[q, k, rows].astype(f32)

                    @pl.when(mine)
                    def _():
                        own_out[place] = total

                    @pl.when(jnp.logical_not(mine))
                    def _():
                        parting[place] = total

                    return carry

                lax.fori_loop(0, HALF // 112, add, 0)

            @pl.when(jnp.logical_not(mine))
            def _():
                last.start()

    def small_step(k):
        near = (core_near, x_near, y_near)[k]
        return pltpu.make_async_remote_copy(
            src_ref=small_mine.at[k], dst_ref=small_rx.at[k], send_sem=sm_send.at[k],
            recv_sem=sm_recv.at[k], device_id=near, device_id_type=MESH_ID,
        )

    def small_next(k):
        small_step(k).wait()
        small_mine[k + 1] = small_mine[k] + small_rx[k]
        if k < 2:
            small_step(k + 1).start()

    def small_hop(d):
        return pltpu.make_async_remote_copy(
            src_ref=small_mine.at[3], dst_ref=small_z.at[d - 1], send_sem=sm_send.at[2 + d],
            recv_sem=sm_recv.at[2 + d], device_id=z_at((z + d) % 4), device_id_type=MESH_ID,
        )

    def load(i, src, dst):
        return pltpu.make_async_copy(src, dst, dist_sem.at[i])

    first_loads = [
        load(0, joint_hbm, joint), load(1, att_hbm, attended), load(2, datt_hbm, dattended),
        load(3, dist_hbm, dist),
    ]
    later_loads = [load(4, normed_hbm, normed), load(5, x_hbm, x_own), load(6, dresid_hbm, dresid)]
    for p in range(3):
        later_loads.append(load(
            7 + p, weight_hbm.at[:, pl.ds(pl.multiple_of(1024 * p + 512 * c, 512), 512)],
            weight.at[:, pl.ds(512 * p, 512)],
        ))
    for q in (4, 5):
        start(loads(q))
    start(first_loads)
    greet(plane_devices(dp, me) + [z_at((z + d) % 4) for d in (1, 2, 3)])
    way_out = Home(result, output, dp, me, out_send, out_recv)
    way_in = Home(dinput, input_gradient, dp, me, in_send, in_recv)
    start(stage1(6))
    meet(4)
    meet(5)

    def go_on(pair):
        @pl.when(pair == 0)
        def _():
            for q in (6, 7):
                start(loads(q))
            start(later_loads)

        @pl.when(pair == 1)
        def _():
            start(stage1(7))

        @pl.when(pair == 2)
        def _():
            start(stage1(3))

    for copy in first_loads:
        copy.wait()

    def pair_step(pair, carry):
        def lanes(block):
            return pl.ds(pl.multiple_of(512 * block + LANES * pair, LANES), LANES)

        here = lanes(0)
        kt_ref[...] = joint[:, lanes(1)].astype(f32).T.astype(bf16)
        product = (attended[:, here].astype(f32) * dattended[:, here].astype(f32)).T
        delta_ref[0:1, :] = jnp.sum(product[:64], 0, keepdims=True)
        delta_ref[1:2, :] = jnp.sum(product[64:], 0, keepdims=True)
        dk_acc[...] = jnp.zeros_like(dk_acc)
        dv_acc[...] = jnp.zeros_like(dv_acc)
        dqt_ref[...] = jnp.zeros_like(dqt_ref)

        def head(h, carry):
            slope = slopes[2 * pair + h]
            for qb in range(4):
                cols = pl.ds(qb * 256, 256)
                queries = head_lanes(joint[cols, here], h)
                grads = head_lanes(dattended[cols, here], h)
                top = lse[pair, pl.ds(h, 1), cols]
                delta = delta_ref[pl.ds(h, 1), cols]
                for kb in range(qb + 1):
                    rows = pl.ds(kb * 256, 256)
                    s = nt(joint[rows, lanes(1)], queries) - slope * dist[rows, cols]
                    p = jnp.exp(s - top)
                    p_ref[rows, :] = p.astype(bf16)
                    dprobs = nt(joint[rows, lanes(2)], grads)
                    ds_ref[rows, :] = (p * (dprobs - delta)).astype(bf16)
                span = pl.ds(0, 256 * (qb + 1))
                dv_acc[span, :] += nn(p_ref[span, :], grads)
                dk_acc[span, :] += nn(ds_ref[span, :], queries)
                dq = nn(kt_ref[:, span], ds_ref[span, :])
                row = lax.broadcasted_iota(jnp.int32, (LANES, 1), 0)
                dqt_ref[:, cols] = jnp.where(row // 64 == h, dq, dqt_ref[:, cols])
            return carry

        lax.fori_loop(0, 2, head, 0)
        djoint[:, lanes(0)] = (dqt_ref[...] * 0.125).T.astype(bf16)
        djoint[:, lanes(1)] = dk_acc[...].astype(bf16)
        djoint[:, lanes(2)] = dv_acc[...].astype(bf16)
        go_on(pair)
        return carry

    lax.fori_loop(0, 4, pair_step, 0)
    for q in (4, 5):
        pieces.join(q)
        pass_on(q, 0)
    for copy in later_loads:
        copy.wait()

    def block_copy(slot, i):
        return pltpu.make_async_copy(
            blocks.at[slot], flat.at[pl.ds(JOINT_AT + 3072 * i, 3072)], block_sem.at[slot]
        )

    for i in range(4):
        if i >= 2:
            block_copy(i % 2, i - 2).wait()
        block = tn(normed[:, 256 * i : 256 * i + 256], djoint[...]).astype(bf16)
        blocks[i % 2] = block.reshape(3072, LANES)
        block_copy(i % 2, i).start()
    for i in (2, 3):
        block_copy(i % 2, i).wait()
    start(stage1(0))
    start(stage1(1))
    for q in (0, 1):
        start(loads(q))

    dn_own, dn_part = dist.at[pl.ds(0, 512)], dist.at[pl.ds(512, 512)]
    dn_part[...] = nt(djoint[other, :], weight[...])
    dn_swap = pltpu.make_async_remote_copy(
        src_ref=dn_part, dst_ref=dn_rx, send_sem=swap_sem.at[0], recv_sem=swap_sem.at[1],
        device_id=core_near, device_id_type=MESH_ID,
    )
    dn_swap.start()
    meet(6)
    start(loads(3))
    meet(7)
    start(loads(2))
    for q in (4, 5):
        pass_on(q, 1)
    dn_own[...] = nt(djoint[own, :], weight[...])
    bias_sums = nn(jnp.ones((8, TOKENS), bf16), djoint[...])
    half = pl.ds(pl.multiple_of(512 * c, 512), 512)
    small_mine[0] = jnp.zeros(small_mine.shape[1:], f32)
    small_mine[0, 2:3, half] = bias_sums[0:1, :512]
    small_mine[0, 3:4, half] = bias_sums[0:1, 1024:]
    small_mine[0, 4:7, :] = mid_sums[0:3, :]
    small_mine[0, 7:11, half] = expand_sums[...]
    small_mine[0, 11:12, :] = mid_sums[3:4, :]
    dn_swap.wait()

    def back_rows(i, carry):
        rows = pl.ds(pl.multiple_of(128 * i, 128), 128)
        values = x_own[rows, :].astype(f32)
        center = values - jnp.mean(values, -1, keepdims=True)
        factor = lax.rsqrt(jnp.mean(center * center, -1, keepdims=True) + norm_epsilon)
        unit = center * factor
        dn = dn_own[rows, :] + dn_rx[rows, :]
        e = dn * gain[0:1, :]
        down = dresid[rows, :] + factor * (
            e - jnp.mean(e, -1, keepdims=True) - unit * jnp.mean(e * unit, -1, keepdims=True)
        )
        dinput[rows, :] = down.astype(bf16)
        small_mine[0, 0:1, :] += jnp.sum(dn * unit, 0, keepdims=True)
        small_mine[0, 1:2, :] += jnp.sum(dn, 0, keepdims=True)
        return carry

    lax.fori_loop(0, 4, back_rows, 0)
    small_step(0).start()
    for q in (6, 7):
        pieces.join(q)
        pass_on(q, 0)
    small_next(0)
    meet(0)
    meet(1)
    start(stage1(2))
    small_next(1)
    meet(3)
    for q in (0, 1):
        pieces.join(q)
        pass_on(q, 0)
    small_next(2)
    for d in (1, 2, 3):
        small_hop(d).start()
    for q in (4, 5):
        finish(q)
    for q in (6, 7):
        pass_on(q, 1)
    way_out.start()
    pieces.join(3)
    pass_on(3, 0)
    meet(2)
    way_in.start()
    for q in (0, 1):
        pass_on(q, 1)
    for q in (6, 7):
        pass_on(q, 2)
    pieces.join(2)
    pass_on(2, 0)
    pass_on(3, 1)
    for q in (0, 1):
        pass_on(q, 2)
    pass_on(2, 1)
    for d in (1, 2, 3):
        small_hop(d).wait()
    small = (small_mine[3] + small_z[1]) + (small_z[0] + small_z[2])
    small_out[...] = small.reshape(small_out.shape)
    for q in (6, 7, 0, 1, 3, 2):
        finish(q)

    last.wait()
    way_out.wait()
    way_in.wait()
    for q in (0, 1, 2, 3, 6, 7):
        for copy in stage1(q):
            copy.wait_send()
    for q in range(8):
        for copy in pieces.second(q):
            copy.wait_send()
        aim = q // 2
        for h in range(3):
            if h < aim:
                @pl.when(z == h)
                def _():
                    hop(q, True).wait_send()
            if h < 3 - aim:
                @pl.when(z == 3 - h)
                def _():
                    hop(q, False).wait_send()


def rear(
    slopes, joint, attended, dattended, dist, lse, normed, weight, x_own, dresid, gain, result,
    mid_sums, expand_sums, mid_a, mid_b, flat,
):
    f32, bf16 = jnp.float32, jnp.bfloat16
    vmem = pl.BlockSpec(memory_space=pltpu.VMEM)
    hbm = pl.BlockSpec(memory_space=pl.ANY)
    home = jax.ShapeDtypeStruct((2, 256, WIDTH), bf16)
    piece = jax.ShapeDtypeStruct((PIECE, LANES), f32)
    return pl.pallas_call(
        rear_kernel,
        out_shape=(
            jax.ShapeDtypeStruct((FLAT_ROWS, LANES), bf16),
            piece,
            piece,
            jax.ShapeDtypeStruct((LANES, LANES), f32),
            home,
            home,
        ),
        in_specs=[pl.BlockSpec(memory_space=pltpu.SMEM)] + [hbm] * 4 + [vmem] + [hbm] * 4 + [vmem]
        + [hbm] + [vmem] * 2 + [hbm] * 3,
        out_specs=[hbm] + [vmem] * 3 + [hbm] * 2,
        scratch_shapes=[
            pltpu.VMEM((TOKENS, 1536), bf16),
            pltpu.VMEM((TOKENS, 512), bf16),
            pltpu.VMEM((TOKENS, 512), bf16),
            pltpu.VMEM((TOKENS, WIDTH), bf16),
            pltpu.VMEM((WIDTH, 1536), bf16),
            pltpu.VMEM((512, WIDTH), bf16),
            pltpu.VMEM((512, WIDTH), f32),
            pltpu.VMEM((TOKENS, TOKENS), f32),
            pltpu.VMEM((TOKENS, 256), bf16),
            pltpu.VMEM((TOKENS, 256), bf16),
            pltpu.VMEM((LANES, TOKENS), bf16),
            pltpu.VMEM((LANES, TOKENS), f32),
            pltpu.VMEM((TOKENS, LANES), f32),
            pltpu.VMEM((TOKENS, LANES), f32),
            pltpu.VMEM((8, TOKENS), f32),
            pltpu.VMEM((TOKENS, 1536), bf16),
            pltpu.VMEM((512, WIDTH), f32),
            pltpu.VMEM((512, WIDTH), bf16),
            pltpu.VMEM((2, 3072, LANES), bf16),
            pltpu.VMEM((4, 2, HALF, LANES), bf16),
            pltpu.VMEM((4, 2, HALF, LANES), bf16),
            pltpu.VMEM((8, 2, HALF, LANES), bf16),
            pltpu.VMEM((8, 2, HALF, LANES), bf16),
            pltpu.VMEM((8, HALF, LANES), bf16),
            pltpu.VMEM((8, HALF, LANES), bf16),
            pltpu.VMEM((8, 2, HALF, LANES), bf16),
            pltpu.VMEM((6, 2, HALF, LANES), bf16),
            pltpu.VMEM((6, 2, HALF, LANES), bf16),
            pltpu.VMEM((PIECE, LANES), f32),
            pltpu.VMEM((4, 16, WIDTH), f32),
            pltpu.VMEM((3, 16, WIDTH), f32),
            pltpu.VMEM((3, 16, WIDTH), f32),
            pltpu.SemaphoreType.DMA((10,)),
            pltpu.SemaphoreType.DMA((2,)),
            pltpu.SemaphoreType.DMA((2,)),
            pltpu.SemaphoreType.DMA((8, 4, 2)),
            pltpu.SemaphoreType.DMA((8, 2, 2)),
            pltpu.SemaphoreType.DMA((8, 2, 2)),
            pltpu.SemaphoreType.DMA((8, 2)),
            pltpu.SemaphoreType.DMA((8, 2)),
            pltpu.SemaphoreType.DMA((8, 2)),
            pltpu.SemaphoreType.DMA((8, 2)),
            pltpu.SemaphoreType.DMA((2,)),
            pltpu.SemaphoreType.DMA((6,)),
            pltpu.SemaphoreType.DMA((6,)),
            pltpu.SemaphoreType.DMA((2,)),
            pltpu.SemaphoreType.DMA((2,)),
            pltpu.SemaphoreType.DMA((2,)),
            pltpu.SemaphoreType.DMA((2,)),
        ],
        input_output_aliases={16: 0},
        compiler_params=pltpu.CompilerParams(
            collective_id=2, has_side_effects=True, vmem_limit_bytes=62 << 20
        ),
        cost_estimate=pl.CostEstimate(flops=30 << 30, bytes_accessed=30 << 20, transcendentals=0),
    )(
        slopes, joint, attended, dattended, dist, lse, normed, weight, x_own, dresid, gain, result,
        mid_sums, expand_sums, mid_a, mid_b, flat,
    )


def middle_kernel(
    attended, x_own, cot, vectors, expand_bias, mixer_hbm, expand_hbm, reduce_hbm,
    result, dresid, dattended, sums, expand_sums, flat, rx_a, rx_b,
    mixer, expand, reduce, att_rx, resid, normal, spread, normed, act, act_rx, dhidden,
    dn_own, dn_part, dn_rx, out_part, out_rx, dbranch, blocks,
    weight_sem, block_sem, send_sem, recv_sem, act_send, act_recv, s1_send, s1_recv,
):
    f32, bf16 = jnp.float32, jnp.bfloat16
    dp = lax.axis_index("dp")
    me = lax.axis_index("group")
    c = dp % 2
    near = (dp + 1 - 2 * c, me)
    own = pl.ds(pl.multiple_of(512 * c, 512), 512)
    other = pl.ds(pl.multiple_of(512 * (1 - c), 512), 512)

    weights = [pltpu.make_async_copy(mixer_hbm, mixer, weight_sem.at[0])]
    for k in range(4):
        part = pl.ds(pl.multiple_of(512 * (2 * k + c), 512), 512)
        weights.append(pltpu.make_async_copy(
            expand_hbm.at[:, part], expand.at[:, pl.ds(512 * k, 512)], weight_sem.at[1 + k]
        ))
    for k in range(4):
        part = pl.ds(pl.multiple_of(512 * (2 * k + c), 512), 512)
        weights.append(pltpu.make_async_copy(
            reduce_hbm.at[part], reduce.at[pl.ds(512 * k, 512)], weight_sem.at[5 + k]
        ))
    for copy in weights:
        copy.start()

    y, x = me // 2, me % 2
    greet([near, (dp, 2 * y + 1 - x), (dp, 2 * (1 - y) + x)])

    def swap(i, src, dst):
        return pltpu.make_async_remote_copy(
            src_ref=src, dst_ref=dst, send_sem=send_sem.at[i], recv_sem=recv_sem.at[i],
            device_id=near, device_id_type=MESH_ID,
        )

    att_swap = swap(0, attended, att_rx)
    normed_swap = swap(1, normed.at[own], normed.at[own])
    dn_swap = swap(2, dn_part, dn_rx)
    out_swap = swap(3, out_part, out_rx)
    branch_swap = swap(4, dbranch.at[own], dbranch.at[own])
    att_swap.start()

    mixer_bias, gain, shift, reduce_bias = (vectors[k : k + 1, :] for k in range(4))

    weights[0].wait()
    resid[...] = nn(attended[own, :], mixer[own, :]) + (x_own[...].astype(f32) + mixer_bias)
    att_swap.wait_recv()
    resid[...] += nn(att_rx[own, :], mixer[other, :])

    def norm_rows(i, carry):
        rows = pl.ds(pl.multiple_of(128 * i, 128), 128)
        here = pl.ds(pl.multiple_of(512 * c + 128 * i, 128), 128)
        values = resid[rows, :]
        center = values - jnp.mean(values, -1, keepdims=True)
        factor = lax.rsqrt(jnp.mean(center * center, -1, keepdims=True) + norm_epsilon)
        unit = center * factor
        normal[rows, :] = unit
        spread[rows, :] = jnp.broadcast_to(factor, (128, LANES))
        normed[here, :] = (unit * gain + shift).astype(bf16)
        return carry

    lax.fori_loop(0, 4, norm_rows, 0)
    normed_swap.start()

    def act_swap(half, k):
        rows = pl.ds(pl.multiple_of(512 * half, 512), 512)
        cols = pl.ds(512 * k, 512)
        return pltpu.make_async_remote_copy(
            src_ref=act.at[rows, cols], dst_ref=act_rx.at[rows, cols],
            send_sem=act_send.at[half, k], recv_sem=act_recv.at[half, k],
            device_id=near, device_id_type=MESH_ID,
        )

    root = math.sqrt(2.0 / math.pi)

    def hidden_block(half, k, first):
        rows = pl.ds(pl.multiple_of(512 * half, 512), 512)
        cols = pl.ds(512 * k, 512)
        u = nn(normed[rows, :], expand[:, cols]) + expand_bias[k : k + 1, :]
        dact = nt(cot[rows, :], reduce[cols, :])
        square = u * u
        t = jnp.tanh(u * (root + (root * 0.044715) * square))
        up = 0.5 + 0.5 * t
        act[rows, cols] = (u * up).astype(bf16)
        slope = up + (0.5 * u) * (1.0 - t * t) * (root + (3.0 * root * 0.044715) * square)
        dh = (dact * slope).astype(bf16)
        dhidden[rows, cols] = dh
        total = jnp.sum(dh.astype(f32), 0, keepdims=True)
        if first:
            expand_sums[k : k + 1, :] = total
        else:
            expand_sums[k : k + 1, :] += total
        act_swap(half, k).start()

    for k in range(4):
        weights[1 + k].wait()
        weights[5 + k].wait()
        hidden_block(c, k, True)
    normed_swap.wait_recv()
    for k in range(4):
        hidden_block(1 - c, k, False)

    def out_copy(slot, part, at):
        return pltpu.make_async_copy(
            blocks.at[slot, pl.ds(2048 * part, 2048)], flat.at[pl.ds(pl.multiple_of(at, 16), 2048)],
            block_sem.at[slot, part],
        )

    right = pl.ds(pl.multiple_of(512 * c, 512), 512)
    sent = []

    def emit(block, places):
        slot = len(sent) % 2
        if len(sent) >= 2:
            for part, at in enumerate(sent[-2]):
                out_copy(slot, part, at).wait()
        blocks[slot, : 2048 * len(places)] = block.astype(bf16).reshape(2048 * len(places), LANES)
        for part, at in enumerate(places):
            out_copy(slot, part, at).start()
        sent.append(places)

    for i in range(4):
        emit(
            tn(normed[:, 256 * i : 256 * i + 256], dhidden[...]),
            [EXPAND_AT + 4096 * i, EXPAND_AT + 4096 * i + 2048],
        )
    for source, parity in ((act, c), (act_rx, 1 - c)):
        if source is act_rx:
            for half in range(2):
                for k in range(4):
                    act_swap(half, k).wait()
        for pair in range(2):
            emit(
                tn(source[:, 1024 * pair : 1024 * pair + 1024], cot[:, right]),
                [REDUCE_AT + 2048 * (2 * k + parity) for k in (2 * pair, 2 * pair + 1)],
            )
    for part, at in list(enumerate(sent[-2])):
        out_copy((len(sent) - 2) % 2, part, at).wait()
    for part, at in list(enumerate(sent[-1])):
        out_copy((len(sent) - 1) % 2, part, at).wait()
    sent.clear()
    stages = []
    for at, q in enumerate(MIDDLE_EARLY):
        stages += first_stage(q, flat, rx_a, rx_b, at, s1_send, s1_recv, dp, me)
    for copy in stages:
        copy.start()

    dn_part[...] = nt(dhidden[other, :], expand[...])
    dn_swap.start()
    out_part[...] = nn(act[other, :], reduce[...]).astype(bf16)
    out_swap.start()

    dn_own[...] = nt(dhidden[own, :], expand[...])
    dn_swap.wait()
    sums[...] = jnp.zeros_like(sums)

    def back_rows(i, carry):
        rows = pl.ds(pl.multiple_of(128 * i, 128), 128)
        here = pl.ds(pl.multiple_of(512 * c + 128 * i, 128), 128)
        dn = dn_own[rows, :] + dn_rx[rows, :]
        unit = normal[rows, :]
        grad = cot[here, :].astype(f32)
        e = dn * gain
        down = grad + spread[rows, 0:1] * (
            e - jnp.mean(e, -1, keepdims=True) - unit * jnp.mean(e * unit, -1, keepdims=True)
        )
        dresid[rows, :] = down
        low = down.astype(bf16)
        dbranch[here, :] = low
        sums[0:1, :] += jnp.sum(low.astype(f32), 0, keepdims=True)
        sums[1:2, :] += jnp.sum(dn * unit, 0, keepdims=True)
        sums[2:3, :] += jnp.sum(dn, 0, keepdims=True)
        sums[3:4, :] += jnp.sum(grad, 0, keepdims=True)
        return carry

    lax.fori_loop(0, 4, back_rows, 0)
    branch_swap.start()
    dattended[own, :] = nt(dbranch[own, :], mixer[own, :]).astype(bf16)
    resid[...] += nn(act[own, :], reduce[...])
    out_swap.wait()
    result[...] = (resid[...] + (out_rx[...].astype(f32) + reduce_bias)).astype(bf16)
    branch_swap.wait()
    dattended[other, :] = nt(dbranch[other, :], mixer[own, :]).astype(bf16)
    emit(tn(attended[...], dbranch[:, right]), [MIXER_AT + 2048 * c])
    emit(tn(att_rx[...], dbranch[:, right]), [MIXER_AT + 2048 * (1 - c)])
    for back in (2, 1):
        for part, at in enumerate(sent[-back]):
            out_copy((len(sent) - back) % 2, part, at).wait()
    att_swap.wait_send()
    normed_swap.wait_send()
    for copy in stages:
        copy.wait()


def middle(attended, x_own, cot, vectors, expand_bias, mixer, expand, reduce):
    f32, bf16 = jnp.float32, jnp.bfloat16
    vmem = pl.BlockSpec(memory_space=pltpu.VMEM)
    hbm = pl.BlockSpec(memory_space=pl.ANY)
    count = len(MIDDLE_EARLY)
    early = jax.ShapeDtypeStruct((count, 2, HALF, LANES), bf16)
    return pl.pallas_call(
        middle_kernel,
        out_shape=(
            jax.ShapeDtypeStruct((512, WIDTH), bf16),
            jax.ShapeDtypeStruct((512, WIDTH), f32),
            jax.ShapeDtypeStruct((TOKENS, 512), bf16),
            jax.ShapeDtypeStruct((8, WIDTH), f32),
            jax.ShapeDtypeStruct((4, 512), f32),
            jax.ShapeDtypeStruct((FLAT_ROWS, LANES), bf16),
            early,
            early,
        ),
        in_specs=[vmem] * 5 + [hbm] * 3,
        out_specs=[vmem] * 5 + [hbm] * 3,
        scratch_shapes=[
            pltpu.VMEM((WIDTH, WIDTH), bf16),
            pltpu.VMEM((WIDTH, 2048), bf16),
            pltpu.VMEM((2048, WIDTH), bf16),
            pltpu.VMEM((TOKENS, 512), bf16),
            pltpu.VMEM((512, WIDTH), f32),
            pltpu.VMEM((512, WIDTH), f32),
            pltpu.VMEM((512, LANES), f32),
            pltpu.VMEM((TOKENS, WIDTH), bf16),
            pltpu.VMEM((TOKENS, 2048), bf16),
            pltpu.VMEM((TOKENS, 2048), bf16),
            pltpu.VMEM((TOKENS, 2048), bf16),
            pltpu.VMEM((512, WIDTH), f32),
            pltpu.VMEM((512, WIDTH), f32),
            pltpu.VMEM((512, WIDTH), f32),
            pltpu.VMEM((512, WIDTH), bf16),
            pltpu.VMEM((512, WIDTH), bf16),
            pltpu.VMEM((TOKENS, WIDTH), bf16),
            pltpu.VMEM((2, 4096, LANES), bf16),
            pltpu.SemaphoreType.DMA((9,)),
            pltpu.SemaphoreType.DMA((2, 2)),
            pltpu.SemaphoreType.DMA((5,)),
            pltpu.SemaphoreType.DMA((5,)),
            pltpu.SemaphoreType.DMA((2, 4)),
            pltpu.SemaphoreType.DMA((2, 4)),
            pltpu.SemaphoreType.DMA((count, 2, 2)),
            pltpu.SemaphoreType.DMA((count, 2, 2)),
        ],
        compiler_params=pltpu.CompilerParams(
            collective_id=1, has_side_effects=True, vmem_limit_bytes=62 << 20
        ),
        cost_estimate=pl.CostEstimate(flops=30 << 30, bytes_accessed=40 << 20, transcendentals=0),
    )(attended, x_own, cot, vectors, expand_bias, mixer, expand, reduce)


def owned_gradient(own, peer, small, c, owner):
    first = jnp.where(c == 0, own, peer).reshape(PIECE // 4, 1, 4, LANES)
    second = jnp.where(c == 0, peer, own).reshape(PIECE // 4, 1, 4, LANES)
    rows = jnp.concatenate([first, second], 1).reshape(2 * PIECE, LANES)
    begin = OWNED_ROWS * owner
    unit = begin // 8
    shift = jnp.where(unit < U_JBIAS, 8, jnp.where(unit < U_MBIAS, 16, 20))
    start = (4 * unit + shift) // 16 * 16

    def window(moved):
        at = begin + 2 * moved - 2 * start
        padded = jnp.pad(rows, ((16, 64), (0, 0)))
        return lax.dynamic_slice_in_dim(padded, jnp.clip(at + 16, 0, 2 * PIECE + 80 - OWNED_ROWS), OWNED_ROWS, 0)

    end_unit = (begin + OWNED_ROWS - 1) // 8
    shift_end = jnp.where(end_unit < U_JBIAS, 8, jnp.where(end_unit < U_MBIAS, 16, 20))
    flat_row = begin + jnp.arange(OWNED_ROWS, dtype=jnp.int32)
    u = flat_row // 8
    moved_row = jnp.where(u < U_JBIAS, 8, jnp.where(u < U_MBIAS, 16, 20))
    big = jnp.where((moved_row == shift)[:, None], window(shift), window(shift_end))
    result_at = jnp.zeros((), jnp.int32)
    inside = jnp.zeros((OWNED_ROWS,), bool)
    for first_unit, end, at in (
        (0, 2, 0), (U_JBIAS, U_MIXER, 16), (U_MBIAS, U_EXPAND, 32), (U_EBIAS, U_REDUCE, 56),
        (U_RBIAS, 12300, 88),
    ):
        inside = inside | ((u >= first_unit) & (u < end))
        holds = (8 * first_unit < begin + OWNED_ROWS) & (8 * end > begin)
        result_at = jnp.where(holds, at + begin - 8 * first_unit, result_at)
    padded = jnp.pad(small[:96], ((OWNED_ROWS, OWNED_ROWS), (0, 0)))
    part = lax.dynamic_slice_in_dim(
        padded, jnp.clip(OWNED_ROWS + result_at, 0, OWNED_ROWS + 96), OWNED_ROWS, 0
    )
    return jnp.where(inside[:, None], part, big)


def on_device_chip(
    dp_size, group_size,
    activations, cotangent, segments, padding, step_count, learn_rate,
    gain_before, shift_before, joint_weight, joint_bias, mixer_weight, mixer_bias,
    gain_middle, shift_middle, expand_weight, expand_bias, reduce_weight, reduce_bias,
    master_weights, first_moment, second_moment,
):
    f32, bf16 = jnp.float32, jnp.bfloat16
    dp = lax.axis_index("dp")
    group = lax.axis_index("group")
    c = dp % 2
    slopes = jnp.exp2(-8.0 * (jnp.arange(8, dtype=f32) + 8.0 * c.astype(f32) + 1.0) / HEADS)
    bias = half_columns(joint_bias[None], c)[0].astype(f32)
    joint_shift = jnp.concatenate([bias[:512], jnp.zeros((512,), f32), bias[512:]])
    joint_scale = jnp.concatenate([jnp.full((512,), 0.125, f32), jnp.ones((1024,), f32)])
    joint_vectors = jnp.stack([joint_shift, joint_scale, *[joint_scale] * 6])
    before = jnp.stack([gain_before, shift_before, *[gain_before] * 6]).astype(f32)
    marks = jnp.concatenate([segments, padding, segments, padding], 0)
    x_own, cot_all, normed_one, joint, dist, attended, lse = front(
        slopes, activations, cotangent, marks, before, joint_vectors, joint_weight
    )
    vectors = jnp.stack(
        [mixer_bias, gain_middle, shift_middle, reduce_bias, *[mixer_bias] * 4]
    ).astype(f32)
    expand_shift = half_columns(expand_bias[None], c).reshape(4, 512).astype(f32)
    result, dresid, dattended, middle_sums, expand_sums, flat, mid_a, mid_b = middle(
        attended, x_own, cot_all, vectors, expand_shift, mixer_weight, expand_weight, reduce_weight
    )
    _, own, peer, small_sum, output, input_gradient = rear(
        slopes, joint, attended, dattended, dist, lse, normed_one, joint_weight, x_own, dresid, before,
        result, middle_sums, expand_sums, mid_a, mid_b, flat,
    )
    owner = dp * group_size + group
    share = owned_gradient(own, peer, small_sum, c, owner).reshape(-1)
    small_share = lax.dynamic_slice_in_dim(small_sum, 3 * owner, 3, 0).reshape(-1)

    moment_step = step_count[0].astype(f32)
    rate = learn_rate[0]
    fix_one = 1.0 - jnp.exp(moment_step * math.log(beta_first))
    fix_two = 1.0 - jnp.exp(moment_step * math.log(beta_second))
    updated_first = beta_first * first_moment + (1.0 - beta_first) * share
    updated_second = beta_second * second_moment + (1.0 - beta_second) * share * share
    updated_master = master_weights - rate * (
        updated_first / fix_one / (jnp.sqrt(updated_second / fix_two) + adam_epsilon)
        + weight_decay * master_weights
    )
    return (output, input_gradient, updated_master, updated_first, updated_second, small_share)


def on_device(dp_size, group_size, activations, *rest):
    if (dp_size, group_size) == (8, 4) and activations.shape == (2, 256, WIDTH):
        return on_device_chip(dp_size, group_size, activations, *rest)
    return on_device_general(activations, *rest)


def solution(mesh):
    in_specs = (
        P("dp", "group", None),
        P("dp", "group", None),
        P("dp", None),
        P("dp", None),
        P(),
        P(),
        P(),
        P(),
        P(),
        P(),
        P(),
        P(),
        P(),
        P(),
        P(),
        P(),
        P(),
        P(),
        P(("dp", "group")),
        P(("dp", "group")),
        P(("dp", "group")),
    )
    out_specs = (
        P("dp", "group", None),
        P("dp", "group", None),
        P(("dp", "group")),
        P(("dp", "group")),
        P(("dp", "group")),
        P(("dp", "group")),
    )
    return jax.shard_map(
        functools.partial(on_device, mesh.shape["dp"], mesh.shape["group"]), mesh=mesh, in_specs=in_specs, out_specs=out_specs, check_vma=False
    )
```

```python
import functools
import math

import jax
import jax.numpy as jnp
from jax import lax
from jax.experimental import pallas as pl
from jax.experimental.pallas import tpu as pltpu
from jax.sharding import PartitionSpec as P

HEADS = 16
DOC_MOST = 800


beta_first = 0.9
beta_second = 0.95
adam_epsilon = 1e-08
weight_decay = 0.1
norm_epsilon = 1e-05
masked_score = -1e30


def shifted(block, axis, distance):
    devices = range(lax.axis_size(axis))
    route = [(i - distance, i) for i in devices if i - distance in devices]
    return lax.ppermute(block, axis, route)


def standardize(values):
    center = values - jnp.mean(values, -1, keepdims=True)
    spread = lax.rsqrt(jnp.mean(center * center, -1, keepdims=True) + norm_epsilon)
    return (center * spread, spread)


def norm_back(dnormed, normed, spread):
    return spread * (
        dnormed
        - jnp.mean(dnormed, -1, keepdims=True)
        - normed * jnp.mean(dnormed * normed, -1, keepdims=True)
    )


def window_mask(segments, padding, member, hop, block_len):
    places = jnp.arange(block_len, dtype=jnp.int32)
    source = member - hop
    query_place = member * block_len + places
    key_place = source * block_len + places
    start = jnp.maximum(source, 0) * block_len
    seg_query = lax.dynamic_slice_in_dim(segments, member * block_len, block_len, 1)
    seg_key = lax.dynamic_slice_in_dim(segments, start, block_len, 1)
    pad_key = lax.dynamic_slice_in_dim(padding, start, block_len, 1)
    earlier = key_place[None, None, :] <= query_place[None, :, None]
    itself = key_place[None, None, :] == query_place[None, :, None]
    allowed = (
        (seg_query[:, :, None] == seg_key[:, None, :])
        & earlier
        & ((pad_key[:, None, :] == 1) | itself)
        & (source >= 0)
    )
    distance = (query_place[:, None] - key_place[None, :]).astype(jnp.float32)
    return (allowed[:, None], distance)


def piece_scores(query4, key4, slopes, distance, score_scale):
    raw = jnp.einsum("sqhd,skhd->shqk", query4, key4, preferred_element_type=jnp.float32)
    return raw * score_scale - slopes[:, None, None] * distance[None]


def on_device_general(
    activations,
    cotangent,
    segments,
    padding,
    step_count,
    learn_rate,
    gain_before,
    shift_before,
    joint_weight,
    joint_bias,
    mixer_weight,
    mixer_bias,
    gain_middle,
    shift_middle,
    expand_weight,
    expand_bias,
    reduce_weight,
    reduce_bias,
    master_weights,
    first_moment,
    second_moment,
):
    seq_count, block_len, width = activations.shape
    head_size = width // HEADS
    row_count = seq_count * block_len
    shape4 = (seq_count, block_len, HEADS, head_size)
    score_scale = 1.0 / math.sqrt(head_size)
    group_size = lax.axis_size("group")
    member = lax.axis_index("group")
    reach = min((DOC_MOST + block_len - 2) // block_len, group_size - 1)
    slopes = jnp.exp2(-8.0 * (jnp.arange(HEADS, dtype=jnp.float32) + 1.0) / HEADS)
    inputs = activations.reshape(row_count, width).astype(jnp.float32)
    gain_one = gain_before.astype(jnp.float32)
    gain_two = gain_middle.astype(jnp.float32)
    normal_one, spread_one = standardize(inputs)
    normed_one = (normal_one * gain_one + shift_before.astype(jnp.float32)).astype(jnp.bfloat16)
    joint = jnp.dot(normed_one, joint_weight, preferred_element_type=jnp.float32)
    bias_joint = joint_bias.astype(jnp.float32)
    query_rows = (joint[:, :width] + bias_joint[:width]).astype(jnp.bfloat16)
    key_rows = joint[:, width : 2 * width].astype(jnp.bfloat16)
    value_rows = (joint[:, 2 * width :] + bias_joint[width:]).astype(jnp.bfloat16)
    own_piece = jnp.stack([key_rows, value_rows]).reshape(2, seq_count, block_len, width)
    query4 = query_rows.reshape(shape4)
    pieces = [own_piece]
    for hop in range(1, reach + 1):
        pieces.append(shifted(own_piece, "group", hop))
    row_top = jnp.full((seq_count, HEADS, block_len), masked_score, jnp.float32)
    row_total = jnp.zeros((seq_count, HEADS, block_len), jnp.float32)
    for hop in range(reach + 1):
        allowed, distance = window_mask(segments, padding, member, hop, block_len)
        scores = piece_scores(query4, pieces[hop][0].reshape(shape4), slopes, distance, score_scale)
        fresh = jnp.maximum(row_top, jnp.max(jnp.where(allowed, scores, masked_score), -1))
        row_total = row_total * jnp.exp(row_top - fresh) + jnp.sum(
            jnp.exp(jnp.where(allowed, scores - fresh[..., None], masked_score)), -1
        )
        row_top = fresh
    log_total = row_top + jnp.log(row_total)
    attended = jnp.zeros(shape4, jnp.float32)
    for hop in range(reach + 1):
        allowed, distance = window_mask(segments, padding, member, hop, block_len)
        scores = piece_scores(query4, pieces[hop][0].reshape(shape4), slopes, distance, score_scale)
        probs = jnp.exp(jnp.where(allowed, scores - log_total[..., None], masked_score)).astype(
            jnp.bfloat16
        )
        attended = attended + jnp.einsum(
            "shqk,skhd->sqhd",
            probs,
            pieces[hop][1].reshape(shape4),
            preferred_element_type=jnp.float32,
        )
    attended_low = attended.reshape(row_count, width).astype(jnp.bfloat16)
    resid = inputs + (
        jnp.dot(attended_low, mixer_weight, preferred_element_type=jnp.float32)
        + mixer_bias.astype(jnp.float32)
    )
    normal_two, spread_two = standardize(resid)
    normed_two = (normal_two * gain_two + shift_middle.astype(jnp.float32)).astype(jnp.bfloat16)
    hidden = jnp.dot(
        normed_two, expand_weight, preferred_element_type=jnp.float32
    ) + expand_bias.astype(jnp.float32)
    act = jax.nn.gelu(hidden, approximate=True).astype(jnp.bfloat16)
    result = resid + (
        jnp.dot(act, reduce_weight, preferred_element_type=jnp.float32)
        + reduce_bias.astype(jnp.float32)
    )
    output = result.astype(jnp.bfloat16).reshape(seq_count, block_len, width)
    cot_low = cotangent.reshape(row_count, width)
    cot_full = cot_low.astype(jnp.float32)
    reduce_grad = jnp.einsum("tf,td->fd", act, cot_low, preferred_element_type=jnp.float32)
    reduce_bias_grad = jnp.sum(cot_full, 0)
    dact = jnp.einsum("td,fd->tf", cot_low, reduce_weight, preferred_element_type=jnp.float32)
    gelu_pull = jax.vjp(lambda inner: jax.nn.gelu(inner, approximate=True), hidden)[1]
    dhidden = gelu_pull(dact)[0].astype(jnp.bfloat16)
    expand_grad = jnp.einsum("td,tf->df", normed_two, dhidden, preferred_element_type=jnp.float32)
    expand_bias_grad = jnp.sum(dhidden.astype(jnp.float32), 0)
    dnormed_two = jnp.einsum(
        "tf,df->td", dhidden, expand_weight, preferred_element_type=jnp.float32
    )
    gain_middle_grad = jnp.sum(dnormed_two * normal_two, 0)
    shift_middle_grad = jnp.sum(dnormed_two, 0)
    dresid = cot_full + norm_back(dnormed_two * gain_two, normal_two, spread_two)
    dbranch = dresid.astype(jnp.bfloat16)
    mixer_grad = jnp.einsum("td,te->de", attended_low, dbranch, preferred_element_type=jnp.float32)
    mixer_bias_grad = jnp.sum(dbranch.astype(jnp.float32), 0)
    dattended = jnp.einsum(
        "te,de->td", dbranch, mixer_weight, preferred_element_type=jnp.float32
    ).astype(jnp.bfloat16)
    dattended4 = dattended.reshape(shape4)
    row_delta = jnp.einsum("sqhd,sqhd->shq", dattended4.astype(jnp.float32), attended)
    dquery = jnp.zeros(shape4, jnp.float32)
    dkv_own = jnp.zeros((2, seq_count, block_len, width), jnp.float32)
    for hop in range(reach + 1):
        piece = pieces[hop]
        key4 = piece[0].reshape(shape4)
        value4 = piece[1].reshape(shape4)
        allowed, distance = window_mask(segments, padding, member, hop, block_len)
        scores = piece_scores(query4, key4, slopes, distance, score_scale)
        probs = jnp.exp(jnp.where(allowed, scores - log_total[..., None], masked_score))
        dvalue = jnp.einsum(
            "shqk,sqhd->skhd",
            probs.astype(jnp.bfloat16),
            dattended4,
            preferred_element_type=jnp.float32,
        )
        dprobs = jnp.einsum(
            "sqhd,skhd->shqk", dattended4, value4, preferred_element_type=jnp.float32
        )
        dscores = (probs * (dprobs - row_delta[..., None])).astype(jnp.bfloat16)
        dquery = dquery + jnp.einsum(
            "shqk,skhd->sqhd", dscores, key4, preferred_element_type=jnp.float32
        )
        dkey = (
            jnp.einsum("shqk,sqhd->skhd", dscores, query4, preferred_element_type=jnp.float32)
            * score_scale
        )
        returned = jnp.stack([dkey, dvalue]).reshape(2, seq_count, block_len, width)
        if hop == 0:
            dkv_own = returned
        else:
            dkv_own = dkv_own + shifted(returned.astype(jnp.bfloat16), "group", -hop).astype(
                returned.dtype
            )
    dquery_low = (dquery * score_scale).reshape(row_count, width).astype(jnp.bfloat16)
    dkey_low = dkv_own[0].reshape(row_count, width).astype(jnp.bfloat16)
    dvalue_low = dkv_own[1].reshape(row_count, width).astype(jnp.bfloat16)
    djoint = jnp.concatenate([dquery_low, dkey_low, dvalue_low], 1)
    joint_grad = jnp.einsum("td,te->de", normed_one, djoint, preferred_element_type=jnp.float32)
    joint_bias_grad = jnp.concatenate(
        [jnp.sum(dquery_low.astype(jnp.float32), 0), jnp.sum(dvalue_low.astype(jnp.float32), 0)]
    )
    dnormed_one = jnp.einsum("te,de->td", djoint, joint_weight, preferred_element_type=jnp.float32)
    gain_before_grad = jnp.sum(dnormed_one * normal_one, 0)
    shift_before_grad = jnp.sum(dnormed_one, 0)
    dinput = dresid + norm_back(dnormed_one * gain_one, normal_one, spread_one)
    input_gradient = dinput.astype(jnp.bfloat16).reshape(seq_count, block_len, width)
    listing = [
        gain_before_grad,
        shift_before_grad,
        joint_grad,
        joint_bias_grad,
        mixer_grad,
        mixer_bias_grad,
        gain_middle_grad,
        shift_middle_grad,
        expand_grad,
        expand_bias_grad,
        reduce_grad,
        reduce_bias_grad,
    ]
    gradient = jnp.concatenate([single.reshape(-1) for single in listing])
    small_list = [
        gain_before_grad,
        shift_before_grad,
        joint_bias_grad,
        mixer_bias_grad,
        gain_middle_grad,
        shift_middle_grad,
        expand_bias_grad,
        reduce_bias_grad,
    ]
    small_local = jnp.concatenate(small_list)
    share, small_share = (
        lax.psum_scatter(gradient, ("dp", "group"), scatter_dimension=0, tiled=True),
        lax.psum_scatter(small_local, ("dp", "group"), scatter_dimension=0, tiled=True),
    )
    moment_step = step_count[0].astype(jnp.float32)
    rate = learn_rate[0]
    fix_one = 1.0 - jnp.exp(moment_step * math.log(beta_first))
    fix_two = 1.0 - jnp.exp(moment_step * math.log(beta_second))
    updated_first = beta_first * first_moment + (1.0 - beta_first) * share
    updated_second = beta_second * second_moment + (1.0 - beta_second) * share * share
    updated_master = master_weights - rate * (
        updated_first / fix_one / (jnp.sqrt(updated_second / fix_two) + adam_epsilon)
        + weight_decay * master_weights
    )
    return (output, input_gradient, updated_master, updated_first, updated_second, small_share)


WIDTH = 1024
HIDDEN = 4096
TOKENS = 1024
LANES = 128
OWNED = 393600
OWNED_ROWS = OWNED // LANES
PIECE = 1568
HALF = PIECE // 2
JOINT_AT, MIXER_AT, EXPAND_AT, REDUCE_AT = 16, 12320, 16432, 32832
FLAT_ROWS = 49248
U_JOINT, U_JBIAS, U_MIXER, U_MBIAS, U_EXPAND, U_EBIAS, U_REDUCE, U_RBIAS = (
    2, 3074, 3076, 4100, 4103, 8199, 8203, 12299,
)


def section_shift(unit):
    return 8 if unit < U_JBIAS else 16 if unit < U_MBIAS else 20


def piece_start(owner):
    unit = OWNED_ROWS * owner // 8
    return (4 * unit + section_shift(unit)) // 16 * 16


def piece_offset(q, y, x):
    at = [piece_start(4 * q + k) // 16 for k in range(4)]
    row = (
        at[0] * (1 - y) * (1 - x) + at[1] * (1 - y) * x + at[2] * y * (1 - x) + at[3] * y * x
    )
    return pl.multiple_of(row * 16, 16)


MESH_ID = pl.DeviceIdType.MESH


def by_rows(step):
    def one(i, carry):
        step(pl.ds(pl.multiple_of(112 * i, 16), 112))
        return carry

    lax.fori_loop(0, HALF // 112, one, 0)


class Pieces:
    def __init__(self, dp, me, flat, own_a, own_b, rx_a1, rx_b1, rx_a2, rx_b2, acc, load_sem, s2_send, s2_recv):
        self.y, self.x = me // 2, me % 2
        self.x_near = (dp, 2 * self.y + (1 - self.x))
        self.y_near = (dp, 2 * (1 - self.y) + self.x)
        self.flat, self.own_a, self.own_b = flat, own_a, own_b
        self.rx_a1, self.rx_b1, self.rx_a2, self.rx_b2, self.acc = rx_a1, rx_b1, rx_a2, rx_b2, acc
        self.load_sem, self.s2_send, self.s2_recv = load_sem, s2_send, s2_recv

    def loads(self, q, own_slot, ready=None):
        slot = q
        out = []
        for k in range(2):
            for way, (row, own) in enumerate((
                (piece_offset(q, k, self.x), self.own_a),
                (piece_offset(q, self.y, k) + HALF, self.own_b),
            )):
                out.append(pltpu.make_async_copy(
                    self.flat.at[pl.ds(row, HALF)], own.at[own_slot, k], self.load_sem.at[slot, way, k]
                ))
            if ready is not None:
                ready_a, ready_b, at = ready
                for way, (src, dst) in enumerate(((ready_a, self.rx_a1), (ready_b, self.rx_b1))):
                    out.append(pltpu.make_async_copy(
                        src.at[at, k], dst.at[slot, k], self.load_sem.at[slot, 2 + way, k]
                    ))
        return out

    def second(self, slot):
        y, x = self.y, self.x
        return [
            pltpu.make_async_remote_copy(
                src_ref=src, dst_ref=dst.at[slot], send_sem=self.s2_send.at[slot, way],
                recv_sem=self.s2_recv.at[slot, way], device_id=near, device_id_type=MESH_ID,
            )
            for way, (src, dst, near) in enumerate((
                (self.rx_a1.at[slot, 1 - y], self.rx_a2, self.y_near),
                (self.rx_b1.at[slot, 1 - x], self.rx_b2, self.x_near),
            ))
        ]

    def meet(self, slot, own_slot):
        y, x = self.y, self.x
        rx_a1, rx_b1, own_a, own_b, acc = self.rx_a1, self.rx_b1, self.own_a, self.own_b, self.acc

        def away(rows):
            rx_a1[slot, 1 - y, rows] = rx_a1[slot, 1 - y, rows] + own_a[own_slot, 1 - y, rows]
            rx_b1[slot, 1 - x, rows] = rx_b1[slot, 1 - x, rows] + own_b[own_slot, 1 - x, rows]

        by_rows(away)
        for copy in self.second(slot):
            copy.start()

        def kept(rows):
            acc[slot, 0, rows] = rx_a1[slot, y, rows] + own_a[own_slot, y, rows]
            acc[slot, 1, rows] = rx_b1[slot, x, rows] + own_b[own_slot, x, rows]

        by_rows(kept)

    def join(self, slot):
        for copy in self.second(slot):
            copy.wait_recv()
        acc, rx_a2, rx_b2 = self.acc, self.rx_a2, self.rx_b2

        def add(rows):
            acc[slot, 0, rows] = acc[slot, 0, rows] + rx_a2[slot, rows]
            acc[slot, 1, rows] = acc[slot, 1, rows] + rx_b2[slot, rows]

        by_rows(add)


MIDDLE_EARLY = (6, 7, 4)


def nn(a, b):
    return lax.dot_general(a, b, (((1,), (0,)), ((), ())), preferred_element_type=jnp.float32)


def nt(a, b):
    return lax.dot_general(a, b, (((1,), (1,)), ((), ())), preferred_element_type=jnp.float32)


def tn(a, b):
    return lax.dot_general(a, b, (((0,), (0,)), ((), ())), preferred_element_type=jnp.float32)


def head_lanes(value, h):
    lane = lax.broadcasted_iota(jnp.int32, (1, LANES), 1)
    return jnp.where(lane // 64 == h, value, jnp.zeros_like(value))


def plane_devices(dp, me):
    z, c = dp // 2, dp % 2
    near = [(2 * z + 1 - c, me)]
    for d in (1, 2, 3):
        near += [(2 * z, (me + d) % 4), (2 * z + 1, (me + d) % 4)]
    return near


def greet(devices):
    barrier = pltpu.get_barrier_semaphore()
    for near in devices:
        pl.semaphore_signal(barrier, inc=1, device_id=near, device_id_type=MESH_ID)
    pl.semaphore_wait(barrier, len(devices))


class Home:
    def __init__(self, rows, out, dp, me, send_sem, recv_sem):
        z, c = dp // 2, dp % 2
        self.here = c == me // 2
        self.turns = []
        for turn in range(2):
            src = rows.at[pl.ds(256 * turn, 256)]
            dst = out.at[me % 2]
            away = pltpu.make_async_remote_copy(
                src_ref=src, dst_ref=dst, send_sem=send_sem.at[turn], recv_sem=recv_sem.at[me % 2],
                device_id=(2 * z + me // 2, 2 * c + turn), device_id_type=MESH_ID,
            )
            near = pltpu.make_async_copy(src, dst, send_sem.at[turn])
            came = pltpu.make_async_remote_copy(
                src_ref=src, dst_ref=out.at[turn], send_sem=send_sem.at[turn],
                recv_sem=recv_sem.at[turn], device_id=(2 * z + me // 2, 2 * c + turn),
                device_id_type=MESH_ID,
            )
            self.turns.append((away, near, came, self.here & (me % 2 == turn)))

    def start(self):
        for away, near, _, stays in self.turns:
            @pl.when(stays)
            def _():
                near.start()

            @pl.when(jnp.logical_not(stays))
            def _():
                away.start()

    def wait(self):
        for away, near, came, stays in self.turns:
            @pl.when(stays)
            def _():
                near.wait()

            @pl.when(jnp.logical_not(stays))
            def _():
                away.wait_send()
                came.wait_recv()


def first_stage(q, flat, rx_a, rx_b, at, send_sem, recv_sem, dp, me):
    y, x = me // 2, me % 2
    x_near = (dp, 2 * y + (1 - x))
    y_near = (dp, 2 * (1 - y) + x)
    out = []
    for k in range(2):
        for way, (row, rx, near) in enumerate((
            (piece_offset(q, k, 1 - x), rx_a, x_near),
            (piece_offset(q, 1 - y, k) + HALF, rx_b, y_near),
        )):
            out.append(pltpu.make_async_remote_copy(
                src_ref=flat.at[pl.ds(row, HALF)], dst_ref=rx.at[at, k],
                send_sem=send_sem.at[at, way, k], recv_sem=recv_sem.at[at, way, k],
                device_id=near, device_id_type=MESH_ID,
            ))
    return out


class Spread:
    def __init__(self, blocks, rows, dp, me, send_sem, recv_sem):
        z, c = dp // 2, dp % 2
        here = c == me // 2
        self.turns = []
        for turn in range(2):
            src = blocks.at[turn]
            dst = rows.at[pl.ds(pl.multiple_of(256 * me, 256), 256)]
            away = pltpu.make_async_remote_copy(
                src_ref=src, dst_ref=dst, send_sem=send_sem.at[turn], recv_sem=recv_sem.at[me % 2],
                device_id=(2 * z + me // 2, 2 * c + turn), device_id_type=MESH_ID,
            )
            near = pltpu.make_async_copy(src, dst, send_sem.at[turn])
            came = pltpu.make_async_remote_copy(
                src_ref=src, dst_ref=rows.at[pl.ds(pl.multiple_of(512 * c + 256 * turn, 256), 256)],
                send_sem=send_sem.at[turn], recv_sem=recv_sem.at[turn],
                device_id=(2 * z + me // 2, 2 * c + turn), device_id_type=MESH_ID,
            )
            self.turns.append((away, near, came, here & (me % 2 == turn)))

    def start(self):
        for away, near, _, stays in self.turns:
            @pl.when(stays)
            def _():
                near.start()

            @pl.when(jnp.logical_not(stays))
            def _():
                away.start()

    def wait_came(self, turn):
        _, near, came, stays = self.turns[turn]

        @pl.when(stays)
        def _():
            near.wait()

        @pl.when(jnp.logical_not(stays))
        def _():
            came.wait_recv()

    def wait_sent(self):
        for away, _, _, stays in self.turns:
            @pl.when(jnp.logical_not(stays))
            def _():
                away.wait_send()


def front_kernel(
    slopes, blocks, cot_blocks, segments, padding, vectors, weight_hbm,
    x_out, cot_out, normed_out, joint_out, dist_out, att_out, lse_out,
    x_all, cot_all, normed, joint, weight, dist, att, lse, seg_rx, pad_rx, columns, s_ref, p_ref, vt_ref, ot_ref,
    weight_sem, out_sem, mark_sem, x_send, x_recv, cot_send, cot_recv, pass_send, pass_recv,
):
    f32, bf16 = jnp.float32, jnp.bfloat16
    dp = lax.axis_index("dp")
    me = lax.axis_index("group")
    c = dp % 2
    core_near = (dp + 1 - 2 * c, me)
    own = pl.ds(pl.multiple_of(512 * c, 512), 512)
    other = pl.ds(pl.multiple_of(512 * (1 - c), 512), 512)

    weights = [
        pltpu.make_async_copy(
            weight_hbm.at[:, pl.ds(pl.multiple_of(1024 * p + 512 * c, 512), 512)],
            weight.at[:, pl.ds(512 * p, 512)], weight_sem.at[p],
        )
        for p in range(3)
    ]
    greet(plane_devices(dp, me))
    x_way = Spread(blocks, x_all, dp, me, x_send, x_recv)
    cot_way = Spread(cot_blocks, cot_all, dp, me, cot_send, cot_recv)
    x_way.start()
    mark_swaps = [
        pltpu.make_async_remote_copy(
            src_ref=src, dst_ref=dst, send_sem=mark_sem.at[0, i], recv_sem=mark_sem.at[1, i],
            device_id=core_near, device_id_type=MESH_ID,
        )
        for i, (src, dst) in enumerate(((segments, seg_rx), (padding, pad_rx)))
    ]
    for copy in mark_swaps:
        copy.start()
    for copy in weights:
        copy.start()

    def hand_over(rows, way, turn):
        at = pl.ds(pl.multiple_of(512 * c + 256 * turn, 256), 256)
        return pltpu.make_async_remote_copy(
            src_ref=rows.at[at], dst_ref=rows.at[at], send_sem=pass_send.at[way, turn],
            recv_sem=pass_recv.at[way, turn], device_id=core_near, device_id_type=MESH_ID,
        )

    for copy in mark_swaps:
        copy.wait()
    odd = me % 2 == 1
    held = c == me // 2

    def row_of(mine, came):
        both = jnp.where(held, mine[...], came[...]).astype(f32)
        return jnp.where(odd, both[1:2], both[0:1])

    seg = row_of(segments, seg_rx)
    pad = row_of(padding, pad_rx)
    kind = lax.broadcasted_iota(jnp.int32, (8, TOKENS), 0)
    columns[...] = jnp.broadcast_to(
        jnp.where(kind == 0, seg, pad).T[:, :8].reshape(TOKENS, 8), (TOKENS, 8)
    )

    def dist_rows(i, carry):
        rows = pl.ds(pl.multiple_of(128 * i, 128), 128)
        key_seg, key_pad = columns[rows, 0:1], columns[rows, 1:2]
        key = (lax.broadcasted_iota(jnp.int32, (128, 1), 0) + 128 * i).astype(f32)
        query = lax.broadcasted_iota(jnp.int32, (128, TOKENS), 1).astype(f32)
        last = jnp.sum(jnp.where(seg <= key_seg, 1.0, 0.0), 1, keepdims=True) - 1.0
        last = jnp.where(key_pad == 1.0, last, key)
        dist[rows, :] = jnp.where((query >= key) & (query <= last), query - key, -masked_score)
        return carry

    lax.fori_loop(0, 8, dist_rows, 0)
    outs = []

    def put(src, dst):
        copy = pltpu.make_async_copy(src, dst, out_sem.at[len(outs)])
        copy.start()
        outs.append(copy)

    put(dist, dist_out)
    gain, shift = vectors[0:1, :], vectors[1:2, :]

    def norm_rows(half):
        def one(i, carry):
            rows = pl.ds(pl.multiple_of(512 * half + 128 * i, 128), 128)
            values = x_all[rows, :].astype(f32)
            center = values - jnp.mean(values, -1, keepdims=True)
            factor = lax.rsqrt(jnp.mean(center * center, -1, keepdims=True) + norm_epsilon)
            normed[rows, :] = (center * factor * gain + shift).astype(bf16)
            return carry

        lax.fori_loop(0, 4, one, 0)
        rows = pl.ds(pl.multiple_of(512 * half, 512), 512)
        lanes = pl.ds(pl.multiple_of(512 * c, 512), 512)
        made = nn(normed[rows, :], weight[...])
        joint[rows, 0:512] = ((made[:, 0:512] + vectors[2:3, lanes]) * 0.125).astype(bf16)
        joint[rows, 512:1024] = made[:, 512:1024].astype(bf16)
        joint[rows, 1024:1536] = (made[:, 1024:1536] + vectors[3:4, lanes]).astype(bf16)

    for turn in range(2):
        x_way.wait_came(turn)
        hand_over(x_all, 0, turn).start()
    x_way.wait_sent()
    cot_way.start()
    put(x_all.at[own], x_out)
    for copy in weights:
        copy.wait()
    norm_rows(c)
    for turn in range(2):
        hand_over(x_all, 0, turn).wait_recv()
    norm_rows(1 - c)
    put(normed, normed_out)
    put(joint, joint_out)

    def pair_step(pair, carry):
        def lanes(block):
            return pl.ds(pl.multiple_of(512 * block + LANES * pair, LANES), LANES)

        vt_ref[...] = joint[:, lanes(2)].astype(f32).T.astype(bf16)
        ot_ref[...] = jnp.zeros_like(ot_ref)

        def head(h, carry):
            slope = slopes[8 * c + 2 * pair + h]
            for qb in range(4):
                cols = pl.ds(qb * 256, 256)
                queries = head_lanes(joint[cols, lanes(0)], h)
                top = None
                for kb in range(qb + 1):
                    rows = pl.ds(kb * 256, 256)
                    s = nt(joint[rows, lanes(1)], queries) - slope * dist[rows, cols]
                    s_ref[rows, :] = s
                    high = jnp.max(s, 0, keepdims=True)
                    top = high if top is None else jnp.maximum(top, high)
                total = None
                for kb in range(qb + 1):
                    rows = pl.ds(kb * 256, 256)
                    p = jnp.exp(s_ref[rows, :] - top)
                    more = jnp.sum(p, 0, keepdims=True)
                    total = more if total is None else total + more
                    p_ref[rows, :] = p.astype(bf16)
                span = pl.ds(0, 256 * (qb + 1))
                out = nn(vt_ref[:, span], p_ref[span, :]) / total
                row = lax.broadcasted_iota(jnp.int32, (LANES, 1), 0)
                ot_ref[:, cols] = jnp.where(row // 64 == h, out, ot_ref[:, cols])
                lse[pair, pl.ds(h, 1), cols] = top + jnp.log(total)
            return carry

        lax.fori_loop(0, 2, head, 0)
        att[:, lanes(0)] = ot_ref[...].T.astype(bf16)

        @pl.when(pair == 2)
        def _():
            for turn in range(2):
                cot_way.wait_came(turn)
                hand_over(cot_all, 1, turn).start()

        return carry

    lax.fori_loop(0, 4, pair_step, 0)
    put(att, att_out)
    put(lse, lse_out)
    for turn in range(2):
        hand_over(cot_all, 1, turn).wait()
        hand_over(x_all, 0, turn).wait_send()
    put(cot_all, cot_out)
    cot_way.wait_sent()
    for copy in outs:
        copy.wait()


def front(slopes, blocks, cot_blocks, segments, padding, vectors, weight):
    f32, bf16 = jnp.float32, jnp.bfloat16
    vmem = pl.BlockSpec(memory_space=pltpu.VMEM)
    hbm = pl.BlockSpec(memory_space=pl.ANY)
    return pl.pallas_call(
        front_kernel,
        out_shape=(
            jax.ShapeDtypeStruct((512, WIDTH), bf16),
            jax.ShapeDtypeStruct((TOKENS, WIDTH), bf16),
            jax.ShapeDtypeStruct((TOKENS, WIDTH), bf16),
            jax.ShapeDtypeStruct((TOKENS, 1536), bf16),
            jax.ShapeDtypeStruct((TOKENS, TOKENS), f32),
            jax.ShapeDtypeStruct((TOKENS, 512), bf16),
            jax.ShapeDtypeStruct((4, 2, TOKENS), f32),
        ),
        in_specs=[pl.BlockSpec(memory_space=pltpu.SMEM)] + [hbm] * 2 + [vmem] * 3 + [hbm],
        out_specs=[hbm] * 7,
        scratch_shapes=[
            pltpu.VMEM((TOKENS, WIDTH), bf16),
            pltpu.VMEM((TOKENS, WIDTH), bf16),
            pltpu.VMEM((TOKENS, WIDTH), bf16),
            pltpu.VMEM((TOKENS, 1536), bf16),
            pltpu.VMEM((WIDTH, 1536), bf16),
            pltpu.VMEM((TOKENS, TOKENS), f32),
            pltpu.VMEM((TOKENS, 512), bf16),
            pltpu.VMEM((4, 2, TOKENS), f32),
            pltpu.VMEM((2, TOKENS), jnp.int32),
            pltpu.VMEM((2, TOKENS), jnp.int32),
            pltpu.VMEM((TOKENS, 8), f32),
            pltpu.VMEM((TOKENS, 256), f32),
            pltpu.VMEM((TOKENS, 256), bf16),
            pltpu.VMEM((LANES, TOKENS), bf16),
            pltpu.VMEM((LANES, TOKENS), f32),
            pltpu.SemaphoreType.DMA((3,)),
            pltpu.SemaphoreType.DMA((7,)),
            pltpu.SemaphoreType.DMA((2, 2)),
            pltpu.SemaphoreType.DMA((2,)),
            pltpu.SemaphoreType.DMA((2,)),
            pltpu.SemaphoreType.DMA((2,)),
            pltpu.SemaphoreType.DMA((2,)),
            pltpu.SemaphoreType.DMA((2, 2)),
            pltpu.SemaphoreType.DMA((2, 2)),
        ],
        compiler_params=pltpu.CompilerParams(
            collective_id=0, has_side_effects=True, vmem_limit_bytes=56 << 20
        ),
        cost_estimate=pl.CostEstimate(flops=10 << 30, bytes_accessed=20 << 20, transcendentals=0),
    )(slopes, blocks, cot_blocks, segments, padding, vectors, weight)


def rear_kernel(
    slopes, joint_hbm, att_hbm, datt_hbm, dist_hbm, lse, normed_hbm, weight_hbm, x_hbm, dresid_hbm, gain,
    result, mid_sums, expand_sums, mid_a, mid_b, flat_in,
    flat, own_out, peer_out, small_out, output, input_gradient,
    joint, attended, dattended, normed, weight, x_own, dresid,
    dist, p_ref, ds_ref, kt_ref, dqt_ref, dk_acc, dv_acc, delta_ref, djoint, dn_rx, dinput, blocks,
    own_a, own_b, rx_a1, rx_b1, rx_a2, rx_b2, acc, rx_up, rx_dn, parting,
    small_mine, small_rx, small_z,
    dist_sem, block_sem, swap_sem, load_sem, s1_send, s1_recv, s2_send, s2_recv, z_send, z_recv,
    last_sem, sm_send, sm_recv, out_send, out_recv, in_send, in_recv,
):
    f32, bf16 = jnp.float32, jnp.bfloat16
    dp = lax.axis_index("dp")
    me = lax.axis_index("group")
    z, c = dp // 2, dp % 2
    y, x = me // 2, me % 2
    x_near = (dp, 2 * y + (1 - x))
    y_near = (dp, 2 * (1 - y) + x)
    core_near = (2 * z + 1 - c, me)
    own = pl.ds(pl.multiple_of(512 * c, 512), 512)
    other = pl.ds(pl.multiple_of(512 * (1 - c), 512), 512)

    def z_at(d):
        return (2 * d + c, me)

    pieces = Pieces(
        dp, me, flat, own_a, own_b, rx_a1, rx_b1, rx_a2, rx_b2, acc, load_sem, s2_send, s2_recv
    )
    own_slot = {6: 0, 7: 1, 4: 2, 5: 3, 0: 0, 1: 1, 3: 2, 2: 3}

    def loads(q):
        ready = (mid_a, mid_b, MIDDLE_EARLY.index(q)) if q in MIDDLE_EARLY else None
        return pieces.loads(q, own_slot[q], ready)

    def start(copies):
        for copy in copies:
            copy.start()

    def stage1(q):
        return first_stage(q, flat, rx_a1, rx_b1, q, s1_send, s1_recv, dp, me)

    def hop(q, up, half):
        way = 0 if up else 1
        return pltpu.make_async_remote_copy(
            src_ref=acc.at[q, half], dst_ref=rx_up.at[q - 2, half] if up else rx_dn.at[q, half],
            send_sem=z_send.at[q, way, half], recv_sem=z_recv.at[q, way, half],
            device_id=z_at((z + 1) % 4 if up else (z + 3) % 4), device_id_type=MESH_ID,
        )

    def meet(q):
        for copy in loads(q):
            copy.wait()
        if q not in MIDDLE_EARLY:
            for copy in stage1(q):
                copy.wait_recv()
        pieces.meet(q, own_slot[q])

    def add_came(q, rx, at, half):
        def add(rows):
            acc[q, half, rows] = acc[q, half, rows] + rx[at, half, rows]

        by_rows(add)

    on_way = {(plane, up): [] for plane in range(4) for up in (False, True)}

    def send_on(plane, q, up, half):
        queue = on_way[plane, up]
        if len(queue) >= 2:
            hop(*queue[-2]).wait_send()
        hop(q, up, half).start()
        queue.append((q, up, half))

    def pass_on(q, h):
        aim = q // 2
        if h < aim:
            @pl.when(z == h)
            def _():
                for half in range(2):
                    if h > 0:
                        hop(q, True, half).wait_recv()
                        add_came(q, rx_up, q - 2, half)
                    send_on(h, q, True, half)
        if h < 3 - aim:
            @pl.when(z == 3 - h)
            def _():
                for half in range(2):
                    if h > 0:
                        hop(q, False, half).wait_recv()
                        add_came(q, rx_dn, q, half)
                    send_on(3 - h, q, False, half)

    last = pltpu.make_async_remote_copy(
        src_ref=parting, dst_ref=peer_out, send_sem=last_sem.at[0], recv_sem=last_sem.at[1],
        device_id=core_near, device_id_type=MESH_ID,
    )

    def finish(q):
        aim = q // 2

        @pl.when(z == aim)
        def _():
            mine = c == q % 2
            for k in range(2):
                if aim > 0:
                    hop(q, True, k).wait_recv()
                if aim < 3:
                    hop(q, False, k).wait_recv()

                def add(i, carry):
                    rows = pl.ds(pl.multiple_of(112 * i, 16), 112)
                    place = pl.ds(pl.multiple_of(HALF * k + 112 * i, 16), 112)
                    total = acc[q, k, rows].astype(f32)
                    if aim > 0:
                        total = total + rx_up[q - 2, k, rows].astype(f32)
                    if aim < 3:
                        total = total + rx_dn[q, k, rows].astype(f32)

                    @pl.when(mine)
                    def _():
                        own_out[place] = total

                    @pl.when(jnp.logical_not(mine))
                    def _():
                        parting[place] = total

                    return carry

                lax.fori_loop(0, HALF // 112, add, 0)

            @pl.when(jnp.logical_not(mine))
            def _():
                last.start()

    def small_step(k):
        near = (core_near, x_near, y_near)[k]
        return pltpu.make_async_remote_copy(
            src_ref=small_mine.at[k], dst_ref=small_rx.at[k], send_sem=sm_send.at[k],
            recv_sem=sm_recv.at[k], device_id=near, device_id_type=MESH_ID,
        )

    def small_next(k):
        small_step(k).wait()
        small_mine[k + 1] = small_mine[k] + small_rx[k]
        if k < 2:
            small_step(k + 1).start()

    def small_hop(d):
        return pltpu.make_async_remote_copy(
            src_ref=small_mine.at[3], dst_ref=small_z.at[d - 1], send_sem=sm_send.at[2 + d],
            recv_sem=sm_recv.at[2 + d], device_id=z_at((z + d) % 4), device_id_type=MESH_ID,
        )

    def load(i, src, dst):
        return pltpu.make_async_copy(src, dst, dist_sem.at[i])

    first_loads = [
        load(0, joint_hbm, joint), load(1, att_hbm, attended), load(2, datt_hbm, dattended),
        load(3, dist_hbm, dist),
    ]
    later_loads = [load(4, normed_hbm, normed), load(5, x_hbm, x_own), load(6, dresid_hbm, dresid)]
    for p in range(3):
        later_loads.append(load(
            7 + p, weight_hbm.at[:, pl.ds(pl.multiple_of(1024 * p + 512 * c, 512), 512)],
            weight.at[:, pl.ds(512 * p, 512)],
        ))
    start(first_loads)
    for q in (7, 6, 4):
        start(loads(q))
    greet(plane_devices(dp, me) + [z_at((z + d) % 4) for d in (1, 2, 3)])
    way_out = Home(result, output, dp, me, out_send, out_recv)
    way_in = Home(dinput, input_gradient, dp, me, in_send, in_recv)
    start(stage1(5))
    start(stage1(3))

    def go_on(pair):
        @pl.when(pair == 0)
        def _():
            start(loads(5))
            start(later_loads)

        @pl.when(pair == 1)
        def _():
            meet(7)

        @pl.when(pair == 2)
        def _():
            for q in (6, 4, 5):
                meet(q)

    for copy in first_loads:
        copy.wait()

    def pair_step(pair, carry):
        def lanes(block):
            return pl.ds(pl.multiple_of(512 * block + LANES * pair, LANES), LANES)

        here = lanes(0)
        kt_ref[...] = joint[:, lanes(1)].astype(f32).T.astype(bf16)
        product = (attended[:, here].astype(f32) * dattended[:, here].astype(f32)).T
        delta_ref[0:1, :] = jnp.sum(product[:64], 0, keepdims=True)
        delta_ref[1:2, :] = jnp.sum(product[64:], 0, keepdims=True)
        dk_acc[...] = jnp.zeros_like(dk_acc)
        dv_acc[...] = jnp.zeros_like(dv_acc)
        dqt_ref[...] = jnp.zeros_like(dqt_ref)

        def head(h, carry):
            slope = slopes[8 * c + 2 * pair + h]
            for qb in range(4):
                cols = pl.ds(qb * 256, 256)
                queries = head_lanes(joint[cols, here], h)
                grads = head_lanes(dattended[cols, here], h)
                top = lse[pair, pl.ds(h, 1), cols]
                delta = delta_ref[pl.ds(h, 1), cols]
                for kb in range(qb + 1):
                    rows = pl.ds(kb * 256, 256)
                    s = nt(joint[rows, lanes(1)], queries) - slope * dist[rows, cols]
                    p = jnp.exp(s - top)
                    p_ref[rows, :] = p.astype(bf16)
                    dprobs = nt(joint[rows, lanes(2)], grads)
                    ds_ref[rows, :] = (p * (dprobs - delta)).astype(bf16)
                span = pl.ds(0, 256 * (qb + 1))
                dv_acc[span, :] += nn(p_ref[span, :], grads)
                dk_acc[span, :] += nn(ds_ref[span, :], queries)
                dq = nn(kt_ref[:, span], ds_ref[span, :])
                row = lax.broadcasted_iota(jnp.int32, (LANES, 1), 0)
                dqt_ref[:, cols] = jnp.where(row // 64 == h, dq, dqt_ref[:, cols])
            return carry

        lax.fori_loop(0, 2, head, 0)
        djoint[:, lanes(0)] = (dqt_ref[...] * 0.125).T.astype(bf16)
        djoint[:, lanes(1)] = dk_acc[...].astype(bf16)
        djoint[:, lanes(2)] = dv_acc[...].astype(bf16)
        go_on(pair)
        return carry

    lax.fori_loop(0, 4, pair_step, 0)
    for copy in later_loads:
        copy.wait()

    def block_copy(slot, i):
        return pltpu.make_async_copy(
            blocks.at[slot], flat.at[pl.ds(JOINT_AT + 3072 * i, 3072)], block_sem.at[slot]
        )

    for i in range(4):
        if i >= 2:
            block_copy(i % 2, i - 2).wait()
        block = tn(normed[:, 256 * i : 256 * i + 256], djoint[...]).astype(bf16)
        blocks[i % 2] = block.reshape(3072, LANES)
        block_copy(i % 2, i).start()
    for i in (2, 3):
        block_copy(i % 2, i).wait()
    start(stage1(0))
    for q in (0, 1, 3, 2):
        start(loads(q))

    dn_own, dn_part = dist.at[pl.ds(0, 512)], dist.at[pl.ds(512, 512)]
    dn_part[...] = nt(djoint[other, :], weight[...])
    dn_swap = pltpu.make_async_remote_copy(
        src_ref=dn_part, dst_ref=dn_rx, send_sem=swap_sem.at[0], recv_sem=swap_sem.at[1],
        device_id=core_near, device_id_type=MESH_ID,
    )
    dn_swap.start()
    pieces.join(6)
    pass_on(6, 0)
    dn_own[...] = nt(djoint[own, :], weight[...])
    bias_sums = nn(jnp.ones((8, TOKENS), bf16), djoint[...])
    half = pl.ds(pl.multiple_of(512 * c, 512), 512)
    small_mine[0] = jnp.zeros(small_mine.shape[1:], f32)
    small_mine[0, 2:3, half] = bias_sums[0:1, :512]
    small_mine[0, 3:4, half] = bias_sums[0:1, 1024:]
    small_mine[0, 4:7, :] = mid_sums[0:3, :]
    small_mine[0, 7:11, half] = expand_sums[...]
    small_mine[0, 11:12, :] = mid_sums[3:4, :]
    pieces.join(5)
    pass_on(6, 1)
    pass_on(5, 0)
    start(stage1(1))
    pieces.join(7)
    pieces.join(4)
    pass_on(5, 1)
    dn_swap.wait()

    def back_rows(i, carry):
        rows = pl.ds(pl.multiple_of(128 * i, 128), 128)
        values = x_own[rows, :].astype(f32)
        center = values - jnp.mean(values, -1, keepdims=True)
        factor = lax.rsqrt(jnp.mean(center * center, -1, keepdims=True) + norm_epsilon)
        unit = center * factor
        dn = dn_own[rows, :] + dn_rx[rows, :]
        e = dn * gain[0:1, :]
        down = dresid[rows, :] + factor * (
            e - jnp.mean(e, -1, keepdims=True) - unit * jnp.mean(e * unit, -1, keepdims=True)
        )
        dinput[rows, :] = down.astype(bf16)
        small_mine[0, 0:1, :] += jnp.sum(dn * unit, 0, keepdims=True)
        small_mine[0, 1:2, :] += jnp.sum(dn, 0, keepdims=True)
        return carry

    lax.fori_loop(0, 4, back_rows, 0)
    small_step(0).start()
    meet(0)
    pass_on(4, 0)
    meet(1)
    pieces.join(0)
    start(stage1(2))
    small_next(0)
    pass_on(7, 0)
    pass_on(0, 0)
    pieces.join(1)
    pass_on(4, 1)
    pass_on(1, 0)
    small_next(1)
    pass_on(6, 2)
    pass_on(0, 1)
    meet(3)
    meet(2)
    small_next(2)
    for d in (1, 2, 3):
        small_hop(d).start()
    pieces.join(3)
    pass_on(3, 0)
    pass_on(7, 1)
    way_in.start()
    pass_on(1, 1)
    finish(5)
    way_out.start()
    pass_on(3, 1)
    finish(6)
    pass_on(0, 2)
    pieces.join(2)
    pass_on(1, 2)
    pass_on(7, 2)
    finish(3)
    pass_on(2, 0)
    finish(7)
    finish(1)
    finish(0)
    pass_on(2, 1)
    finish(4)
    finish(2)
    for d in (1, 2, 3):
        small_hop(d).wait()
    small = (small_mine[3] + small_z[1]) + (small_z[0] + small_z[2])
    small_out[...] = small.reshape(small_out.shape)

    last.wait()
    way_out.wait()
    way_in.wait()
    for q in (0, 1, 2, 3, 5):
        for copy in stage1(q):
            copy.wait_send()
    for q in range(8):
        for copy in pieces.second(q):
            copy.wait_send()
    for (plane, _), queue in on_way.items():
        @pl.when(z == plane)
        def _():
            for sent in queue[-2:]:
                hop(*sent).wait_send()


def rear(
    slopes, joint, attended, dattended, dist, lse, normed, weight, x_own, dresid, gain, result,
    mid_sums, expand_sums, mid_a, mid_b, flat,
):
    f32, bf16 = jnp.float32, jnp.bfloat16
    vmem = pl.BlockSpec(memory_space=pltpu.VMEM)
    hbm = pl.BlockSpec(memory_space=pl.ANY)
    home = jax.ShapeDtypeStruct((2, 256, WIDTH), bf16)
    piece = jax.ShapeDtypeStruct((PIECE, LANES), f32)
    return pl.pallas_call(
        rear_kernel,
        out_shape=(
            jax.ShapeDtypeStruct((FLAT_ROWS, LANES), bf16),
            piece,
            piece,
            jax.ShapeDtypeStruct((LANES, LANES), f32),
            home,
            home,
        ),
        in_specs=[pl.BlockSpec(memory_space=pltpu.SMEM)] + [hbm] * 4 + [vmem] + [hbm] * 4 + [vmem]
        + [hbm] + [vmem] * 2 + [hbm] * 3,
        out_specs=[hbm] + [vmem] * 3 + [hbm] * 2,
        scratch_shapes=[
            pltpu.VMEM((TOKENS, 1536), bf16),
            pltpu.VMEM((TOKENS, 512), bf16),
            pltpu.VMEM((TOKENS, 512), bf16),
            pltpu.VMEM((TOKENS, WIDTH), bf16),
            pltpu.VMEM((WIDTH, 1536), bf16),
            pltpu.VMEM((512, WIDTH), bf16),
            pltpu.VMEM((512, WIDTH), f32),
            pltpu.VMEM((TOKENS, TOKENS), f32),
            pltpu.VMEM((TOKENS, 256), bf16),
            pltpu.VMEM((TOKENS, 256), bf16),
            pltpu.VMEM((LANES, TOKENS), bf16),
            pltpu.VMEM((LANES, TOKENS), f32),
            pltpu.VMEM((TOKENS, LANES), f32),
            pltpu.VMEM((TOKENS, LANES), f32),
            pltpu.VMEM((8, TOKENS), f32),
            pltpu.VMEM((TOKENS, 1536), bf16),
            pltpu.VMEM((512, WIDTH), f32),
            pltpu.VMEM((512, WIDTH), bf16),
            pltpu.VMEM((2, 3072, LANES), bf16),
            pltpu.VMEM((4, 2, HALF, LANES), bf16),
            pltpu.VMEM((4, 2, HALF, LANES), bf16),
            pltpu.VMEM((8, 2, HALF, LANES), bf16),
            pltpu.VMEM((8, 2, HALF, LANES), bf16),
            pltpu.VMEM((8, HALF, LANES), bf16),
            pltpu.VMEM((8, HALF, LANES), bf16),
            pltpu.VMEM((8, 2, HALF, LANES), bf16),
            pltpu.VMEM((6, 2, HALF, LANES), bf16),
            pltpu.VMEM((6, 2, HALF, LANES), bf16),
            pltpu.VMEM((PIECE, LANES), f32),
            pltpu.VMEM((4, 16, WIDTH), f32),
            pltpu.VMEM((3, 16, WIDTH), f32),
            pltpu.VMEM((3, 16, WIDTH), f32),
            pltpu.SemaphoreType.DMA((10,)),
            pltpu.SemaphoreType.DMA((2,)),
            pltpu.SemaphoreType.DMA((2,)),
            pltpu.SemaphoreType.DMA((8, 4, 2)),
            pltpu.SemaphoreType.DMA((8, 2, 2)),
            pltpu.SemaphoreType.DMA((8, 2, 2)),
            pltpu.SemaphoreType.DMA((8, 2)),
            pltpu.SemaphoreType.DMA((8, 2)),
            pltpu.SemaphoreType.DMA((8, 2, 2)),
            pltpu.SemaphoreType.DMA((8, 2, 2)),
            pltpu.SemaphoreType.DMA((2,)),
            pltpu.SemaphoreType.DMA((6,)),
            pltpu.SemaphoreType.DMA((6,)),
            pltpu.SemaphoreType.DMA((2,)),
            pltpu.SemaphoreType.DMA((2,)),
            pltpu.SemaphoreType.DMA((2,)),
            pltpu.SemaphoreType.DMA((2,)),
        ],
        input_output_aliases={16: 0},
        compiler_params=pltpu.CompilerParams(
            collective_id=2, has_side_effects=True, vmem_limit_bytes=62 << 20
        ),
        cost_estimate=pl.CostEstimate(flops=30 << 30, bytes_accessed=30 << 20, transcendentals=0),
    )(
        slopes, joint, attended, dattended, dist, lse, normed, weight, x_own, dresid, gain, result,
        mid_sums, expand_sums, mid_a, mid_b, flat,
    )


def middle_kernel(
    attended, x_own, cot, vectors, mixer_hbm, expand_hbm, reduce_hbm,
    result, dresid, dattended, sums, expand_sums, flat, rx_a, rx_b,
    mixer, expand, reduce, att_rx, resid, normal, spread, normed, act, act_rx, dhidden,
    dn_own, dn_part, dn_rx, out_part, out_rx, dbranch, blocks,
    weight_sem, block_sem, send_sem, recv_sem, act_send, act_recv, s1_send, s1_recv,
):
    f32, bf16 = jnp.float32, jnp.bfloat16
    dp = lax.axis_index("dp")
    me = lax.axis_index("group")
    c = dp % 2
    near = (dp + 1 - 2 * c, me)
    own = pl.ds(pl.multiple_of(512 * c, 512), 512)
    other = pl.ds(pl.multiple_of(512 * (1 - c), 512), 512)

    weights = [pltpu.make_async_copy(mixer_hbm, mixer, weight_sem.at[0])]
    for k in range(4):
        part = pl.ds(pl.multiple_of(512 * (2 * k + c), 512), 512)
        weights.append(pltpu.make_async_copy(
            expand_hbm.at[:, part], expand.at[:, pl.ds(512 * k, 512)], weight_sem.at[1 + k]
        ))
    for k in range(4):
        part = pl.ds(pl.multiple_of(512 * (2 * k + c), 512), 512)
        weights.append(pltpu.make_async_copy(
            reduce_hbm.at[part], reduce.at[pl.ds(512 * k, 512)], weight_sem.at[5 + k]
        ))
    for copy in weights:
        copy.start()

    y, x = me // 2, me % 2
    greet([near, (dp, 2 * y + 1 - x), (dp, 2 * (1 - y) + x)])

    def swap(i, src, dst):
        return pltpu.make_async_remote_copy(
            src_ref=src, dst_ref=dst, send_sem=send_sem.at[i], recv_sem=recv_sem.at[i],
            device_id=near, device_id_type=MESH_ID,
        )

    att_swap = swap(0, attended, att_rx)
    normed_swap = swap(1, normed.at[own], normed.at[own])
    dn_swap = swap(2, dn_part, dn_rx)
    out_swap = swap(3, out_part, out_rx)
    branch_swap = swap(4, dbranch.at[own], dbranch.at[own])
    att_swap.start()

    mixer_bias, gain, shift, reduce_bias = (vectors[k : k + 1, :] for k in range(4, 8))

    weights[0].wait()
    resid[...] = nn(attended[own, :], mixer[own, :]) + (x_own[...].astype(f32) + mixer_bias)
    att_swap.wait_recv()
    resid[...] += nn(att_rx[own, :], mixer[other, :])

    def norm_rows(i, carry):
        rows = pl.ds(pl.multiple_of(128 * i, 128), 128)
        here = pl.ds(pl.multiple_of(512 * c + 128 * i, 128), 128)
        values = resid[rows, :]
        center = values - jnp.mean(values, -1, keepdims=True)
        factor = lax.rsqrt(jnp.mean(center * center, -1, keepdims=True) + norm_epsilon)
        unit = center * factor
        normal[rows, :] = unit
        spread[rows, :] = jnp.broadcast_to(factor, (128, LANES))
        normed[here, :] = (unit * gain + shift).astype(bf16)
        return carry

    lax.fori_loop(0, 4, norm_rows, 0)
    normed_swap.start()

    def act_swap(half, k):
        rows = pl.ds(pl.multiple_of(512 * half, 512), 512)
        cols = pl.ds(pl.multiple_of(512 * k, 512), 512)
        return pltpu.make_async_remote_copy(
            src_ref=act.at[rows, cols], dst_ref=act_rx.at[rows, cols],
            send_sem=act_send.at[half, k], recv_sem=act_recv.at[half, k],
            device_id=near, device_id_type=MESH_ID,
        )

    root = math.sqrt(2.0 / math.pi)
    right = pl.ds(pl.multiple_of(512 * c, 512), 512)

    def hidden_block(half, k, first):
        rows = pl.ds(pl.multiple_of(512 * half, 512), 512)
        cols = pl.ds(pl.multiple_of(512 * k, 512), 512)
        u = nn(normed[rows, :], expand[:, cols]) + vectors[pl.ds(8 + k, 1), right]
        dact = nt(cot[rows, :], reduce[cols, :])
        square = u * u
        t = jnp.tanh(u * (root + (root * 0.044715) * square))
        up = 0.5 + 0.5 * t
        act[rows, cols] = (u * up).astype(bf16)
        slope = up + (0.5 * u) * (1.0 - t * t) * (root + (3.0 * root * 0.044715) * square)
        dh = (dact * slope).astype(bf16)
        dhidden[rows, cols] = dh
        total = jnp.sum(dh.astype(f32), 0, keepdims=True)
        if first:
            expand_sums[pl.ds(k, 1), :] = total
        else:
            expand_sums[pl.ds(k, 1), :] += total
        act_swap(half, k).start()

    def out_copies(slot, places):
        return [
            pltpu.make_async_copy(
                blocks.at[slot, pl.ds(2048 * part, 2048)],
                flat.at[pl.ds(pl.multiple_of(at, 16), 2048)], block_sem.at[slot, part],
            )
            for part, at in enumerate(places)
        ]

    def emit(block, slot, places):
        blocks[slot, : 2048 * len(places)] = block.astype(bf16).reshape(2048 * len(places), LANES)
        for copy in out_copies(slot, places):
            copy.start()

    def drain(slot, places):
        for copy in out_copies(slot, places):
            copy.wait()

    for copy in weights[1:]:
        copy.wait()

    def reduce_places(pair, parity):
        return [REDUCE_AT + 2048 * (2 * (2 * pair + k) + parity) for k in range(2)]

    def hidden_pair(pair, carry):
        def mine(k, carry):
            hidden_block(c, 2 * pair + k, True)
            return carry

        def theirs(k, carry):
            hidden_block(1 - c, 2 * pair + k, False)
            return carry

        lax.fori_loop(0, 2, mine, 0)

        @pl.when(pair == 0)
        def _():
            normed_swap.wait_recv()

        lax.fori_loop(0, 2, theirs, 0)
        left = pl.ds(pl.multiple_of(1024 * pair, 1024), 1024)
        block = tn(act[:, left], cot[:, right])

        @pl.when(pair == 1)
        def _():
            drain(0, reduce_places(0, c))

        emit(block, 0, reduce_places(pair, c))
        for half in range(2):
            for k in range(2):
                act_swap(half, 2 * pair + k).wait()
        block = tn(act_rx[:, left], cot[:, right])

        @pl.when(pair == 1)
        def _():
            drain(1, reduce_places(0, 1 - c))

        emit(block, 1, reduce_places(pair, 1 - c))
        return carry

    lax.fori_loop(0, 2, hidden_pair, 0)
    drain(0, reduce_places(1, c))
    drain(1, reduce_places(1, 1 - c))
    stages = [
        first_stage(q, flat, rx_a, rx_b, at, s1_send, s1_recv, dp, me)
        for at, q in enumerate(MIDDLE_EARLY)
    ]
    for copies in stages[:2]:
        for copy in copies:
            copy.start()

    def expand_places(i):
        return [EXPAND_AT + 4096 * i, EXPAND_AT + 4096 * i + 2048]

    def expand_step(i, carry):
        block = tn(normed[:, pl.ds(pl.multiple_of(256 * i, 256), 256)], dhidden[...])

        @pl.when(i >= 2)
        def _():
            drain(i % 2, expand_places(i - 2))

        emit(block, i % 2, expand_places(i))
        return carry

    lax.fori_loop(0, 4, expand_step, 0)
    drain(0, expand_places(2))
    drain(1, expand_places(3))
    for copies in stages[2:]:
        for copy in copies:
            copy.start()

    dn_part[...] = nt(dhidden[other, :], expand[...])
    dn_swap.start()
    out_part[...] = nn(act[other, :], reduce[...]).astype(bf16)
    out_swap.start()

    dn_own[...] = nt(dhidden[own, :], expand[...])
    dn_swap.wait()
    sums[...] = jnp.zeros_like(sums)

    def back_rows(i, carry):
        rows = pl.ds(pl.multiple_of(128 * i, 128), 128)
        here = pl.ds(pl.multiple_of(512 * c + 128 * i, 128), 128)
        dn = dn_own[rows, :] + dn_rx[rows, :]
        unit = normal[rows, :]
        grad = cot[here, :].astype(f32)
        e = dn * gain
        down = grad + spread[rows, 0:1] * (
            e - jnp.mean(e, -1, keepdims=True) - unit * jnp.mean(e * unit, -1, keepdims=True)
        )
        dresid[rows, :] = down
        low = down.astype(bf16)
        dbranch[here, :] = low
        sums[0:1, :] += jnp.sum(low.astype(f32), 0, keepdims=True)
        sums[1:2, :] += jnp.sum(dn * unit, 0, keepdims=True)
        sums[2:3, :] += jnp.sum(dn, 0, keepdims=True)
        sums[3:4, :] += jnp.sum(grad, 0, keepdims=True)
        return carry

    lax.fori_loop(0, 4, back_rows, 0)
    branch_swap.start()
    dattended[own, :] = nt(dbranch[own, :], mixer[own, :]).astype(bf16)
    resid[...] += nn(act[own, :], reduce[...])
    out_swap.wait()
    result[...] = (resid[...] + (out_rx[...].astype(f32) + reduce_bias)).astype(bf16)
    branch_swap.wait()
    dattended[other, :] = nt(dbranch[other, :], mixer[own, :]).astype(bf16)
    emit(tn(attended[...], dbranch[:, right]), 0, [MIXER_AT + 2048 * c])
    emit(tn(att_rx[...], dbranch[:, right]), 1, [MIXER_AT + 2048 * (1 - c)])
    drain(0, [MIXER_AT + 2048 * c])
    drain(1, [MIXER_AT + 2048 * (1 - c)])
    att_swap.wait_send()
    normed_swap.wait_send()
    for copies in stages:
        for copy in copies:
            copy.wait()


def middle(attended, x_own, cot, vectors, mixer, expand, reduce):
    f32, bf16 = jnp.float32, jnp.bfloat16
    vmem = pl.BlockSpec(memory_space=pltpu.VMEM)
    hbm = pl.BlockSpec(memory_space=pl.ANY)
    count = len(MIDDLE_EARLY)
    early = jax.ShapeDtypeStruct((count, 2, HALF, LANES), bf16)
    return pl.pallas_call(
        middle_kernel,
        out_shape=(
            jax.ShapeDtypeStruct((512, WIDTH), bf16),
            jax.ShapeDtypeStruct((512, WIDTH), f32),
            jax.ShapeDtypeStruct((TOKENS, 512), bf16),
            jax.ShapeDtypeStruct((8, WIDTH), f32),
            jax.ShapeDtypeStruct((4, 512), f32),
            jax.ShapeDtypeStruct((FLAT_ROWS, LANES), bf16),
            early,
            early,
        ),
        in_specs=[vmem] * 4 + [hbm] * 3,
        out_specs=[vmem] * 5 + [hbm] * 3,
        scratch_shapes=[
            pltpu.VMEM((WIDTH, WIDTH), bf16),
            pltpu.VMEM((WIDTH, 2048), bf16),
            pltpu.VMEM((2048, WIDTH), bf16),
            pltpu.VMEM((TOKENS, 512), bf16),
            pltpu.VMEM((512, WIDTH), f32),
            pltpu.VMEM((512, WIDTH), f32),
            pltpu.VMEM((512, LANES), f32),
            pltpu.VMEM((TOKENS, WIDTH), bf16),
            pltpu.VMEM((TOKENS, 2048), bf16),
            pltpu.VMEM((TOKENS, 2048), bf16),
            pltpu.VMEM((TOKENS, 2048), bf16),
            pltpu.VMEM((512, WIDTH), f32),
            pltpu.VMEM((512, WIDTH), f32),
            pltpu.VMEM((512, WIDTH), f32),
            pltpu.VMEM((512, WIDTH), bf16),
            pltpu.VMEM((512, WIDTH), bf16),
            pltpu.VMEM((TOKENS, WIDTH), bf16),
            pltpu.VMEM((2, 4096, LANES), bf16),
            pltpu.SemaphoreType.DMA((9,)),
            pltpu.SemaphoreType.DMA((2, 2)),
            pltpu.SemaphoreType.DMA((5,)),
            pltpu.SemaphoreType.DMA((5,)),
            pltpu.SemaphoreType.DMA((2, 4)),
            pltpu.SemaphoreType.DMA((2, 4)),
            pltpu.SemaphoreType.DMA((count, 2, 2)),
            pltpu.SemaphoreType.DMA((count, 2, 2)),
        ],
        compiler_params=pltpu.CompilerParams(
            collective_id=1, has_side_effects=True, vmem_limit_bytes=62 << 20
        ),
        cost_estimate=pl.CostEstimate(flops=30 << 30, bytes_accessed=40 << 20, transcendentals=0),
    )(attended, x_own, cot, vectors, mixer, expand, reduce)


def owned_gradient(own, peer, small, c, owner):
    first = jnp.where(c == 0, own, peer).reshape(PIECE // 4, 1, 4, LANES)
    second = jnp.where(c == 0, peer, own).reshape(PIECE // 4, 1, 4, LANES)
    rows = jnp.concatenate([first, second], 1).reshape(2 * PIECE, LANES)
    begin = OWNED_ROWS * owner
    unit = begin // 8
    shift = jnp.where(unit < U_JBIAS, 8, jnp.where(unit < U_MBIAS, 16, 20))
    start = (4 * unit + shift) // 16 * 16

    def window(moved):
        at = begin + 2 * moved - 2 * start
        padded = jnp.pad(rows, ((16, 64), (0, 0)))
        return lax.dynamic_slice_in_dim(padded, jnp.clip(at + 16, 0, 2 * PIECE + 80 - OWNED_ROWS), OWNED_ROWS, 0)

    end_unit = (begin + OWNED_ROWS - 1) // 8
    shift_end = jnp.where(end_unit < U_JBIAS, 8, jnp.where(end_unit < U_MBIAS, 16, 20))
    flat_row = begin + jnp.arange(OWNED_ROWS, dtype=jnp.int32)
    u = flat_row // 8
    moved_row = jnp.where(u < U_JBIAS, 8, jnp.where(u < U_MBIAS, 16, 20))
    big = jnp.where((moved_row == shift)[:, None], window(shift), window(shift_end))
    result_at = jnp.zeros((), jnp.int32)
    inside = jnp.zeros((OWNED_ROWS,), bool)
    for first_unit, end, at in (
        (0, 2, 0), (U_JBIAS, U_MIXER, 16), (U_MBIAS, U_EXPAND, 32), (U_EBIAS, U_REDUCE, 56),
        (U_RBIAS, 12300, 88),
    ):
        inside = inside | ((u >= first_unit) & (u < end))
        holds = (8 * first_unit < begin + OWNED_ROWS) & (8 * end > begin)
        result_at = jnp.where(holds, at + begin - 8 * first_unit, result_at)
    padded = jnp.pad(small[:96], ((OWNED_ROWS, OWNED_ROWS), (0, 0)))
    part = lax.dynamic_slice_in_dim(
        padded, jnp.clip(OWNED_ROWS + result_at, 0, OWNED_ROWS + 96), OWNED_ROWS, 0
    )
    return jnp.where(inside[:, None], part, big)


def on_device_chip(
    dp_size, group_size,
    activations, cotangent, segments, padding, step_count, learn_rate,
    gain_before, shift_before, joint_weight, joint_bias, mixer_weight, mixer_bias,
    gain_middle, shift_middle, expand_weight, expand_bias, reduce_weight, reduce_bias,
    master_weights, first_moment, second_moment,
):
    f32, bf16 = jnp.float32, jnp.bfloat16
    dp = lax.axis_index("dp")
    group = lax.axis_index("group")
    c = dp % 2
    slopes = jnp.asarray([2.0 ** (-8.0 * (h + 1) / HEADS) for h in range(HEADS)], f32)
    vectors = jnp.concatenate([
        gain_before, shift_before, joint_bias, mixer_bias, gain_middle, shift_middle, reduce_bias,
        expand_bias,
    ]).astype(f32).reshape(12, WIDTH)
    x_own, cot_all, normed_one, joint, dist, attended, lse = front(
        slopes, activations, cotangent, segments, padding, vectors, joint_weight
    )
    result, dresid, dattended, middle_sums, expand_sums, flat, mid_a, mid_b = middle(
        attended, x_own, cot_all, vectors, mixer_weight, expand_weight, reduce_weight
    )
    _, own, peer, small_sum, output, input_gradient = rear(
        slopes, joint, attended, dattended, dist, lse, normed_one, joint_weight, x_own, dresid, vectors,
        result, middle_sums, expand_sums, mid_a, mid_b, flat,
    )
    owner = dp * group_size + group
    share = owned_gradient(own, peer, small_sum, c, owner).reshape(-1)
    small_share = lax.dynamic_slice_in_dim(small_sum, 3 * owner, 3, 0).reshape(-1)

    moment_step = step_count[0].astype(f32)
    rate = learn_rate[0]
    fix_one = 1.0 - jnp.exp(moment_step * math.log(beta_first))
    fix_two = 1.0 - jnp.exp(moment_step * math.log(beta_second))
    updated_first = beta_first * first_moment + (1.0 - beta_first) * share
    updated_second = beta_second * second_moment + (1.0 - beta_second) * share * share
    updated_master = master_weights - rate * (
        updated_first / fix_one / (jnp.sqrt(updated_second / fix_two) + adam_epsilon)
        + weight_decay * master_weights
    )
    return (output, input_gradient, updated_master, updated_first, updated_second, small_share)


def on_device(dp_size, group_size, activations, *rest):
    if (dp_size, group_size) == (8, 4) and activations.shape == (2, 256, WIDTH):
        return on_device_chip(dp_size, group_size, activations, *rest)
    return on_device_general(activations, *rest)


def solution(mesh):
    in_specs = (
        P("dp", "group", None),
        P("dp", "group", None),
        P("dp", None),
        P("dp", None),
        P(),
        P(),
        P(),
        P(),
        P(),
        P(),
        P(),
        P(),
        P(),
        P(),
        P(),
        P(),
        P(),
        P(),
        P(("dp", "group")),
        P(("dp", "group")),
        P(("dp", "group")),
    )
    out_specs = (
        P("dp", "group", None),
        P("dp", "group", None),
        P(("dp", "group")),
        P(("dp", "group")),
        P(("dp", "group")),
        P(("dp", "group")),
    )
    return jax.shard_map(
        functools.partial(on_device, mesh.shape["dp"], mesh.shape["group"]), mesh=mesh, in_specs=in_specs, out_specs=out_specs, check_vma=False
    )
```

```python
import functools
import math

import jax
import jax.numpy as jnp
from jax import lax
from jax.experimental import pallas as pl
from jax.experimental.pallas import tpu as pltpu
from jax.sharding import PartitionSpec as P

HEADS = 16
DOC_MOST = 800


beta_first = 0.9
beta_second = 0.95
adam_epsilon = 1e-08
weight_decay = 0.1
norm_epsilon = 1e-05
masked_score = -1e30


def shifted(block, axis, distance):
    devices = range(lax.axis_size(axis))
    route = [(i - distance, i) for i in devices if i - distance in devices]
    return lax.ppermute(block, axis, route)


def standardize(values):
    center = values - jnp.mean(values, -1, keepdims=True)
    spread = lax.rsqrt(jnp.mean(center * center, -1, keepdims=True) + norm_epsilon)
    return (center * spread, spread)


def norm_back(dnormed, normed, spread):
    return spread * (
        dnormed
        - jnp.mean(dnormed, -1, keepdims=True)
        - normed * jnp.mean(dnormed * normed, -1, keepdims=True)
    )


def window_mask(segments, padding, member, hop, block_len):
    places = jnp.arange(block_len, dtype=jnp.int32)
    source = member - hop
    query_place = member * block_len + places
    key_place = source * block_len + places
    start = jnp.maximum(source, 0) * block_len
    seg_query = lax.dynamic_slice_in_dim(segments, member * block_len, block_len, 1)
    seg_key = lax.dynamic_slice_in_dim(segments, start, block_len, 1)
    pad_key = lax.dynamic_slice_in_dim(padding, start, block_len, 1)
    earlier = key_place[None, None, :] <= query_place[None, :, None]
    itself = key_place[None, None, :] == query_place[None, :, None]
    allowed = (
        (seg_query[:, :, None] == seg_key[:, None, :])
        & earlier
        & ((pad_key[:, None, :] == 1) | itself)
        & (source >= 0)
    )
    distance = (query_place[:, None] - key_place[None, :]).astype(jnp.float32)
    return (allowed[:, None], distance)


def piece_scores(query4, key4, slopes, distance, score_scale):
    raw = jnp.einsum("sqhd,skhd->shqk", query4, key4, preferred_element_type=jnp.float32)
    return raw * score_scale - slopes[:, None, None] * distance[None]


def on_device_general(
    activations,
    cotangent,
    segments,
    padding,
    step_count,
    learn_rate,
    gain_before,
    shift_before,
    joint_weight,
    joint_bias,
    mixer_weight,
    mixer_bias,
    gain_middle,
    shift_middle,
    expand_weight,
    expand_bias,
    reduce_weight,
    reduce_bias,
    master_weights,
    first_moment,
    second_moment,
):
    seq_count, block_len, width = activations.shape
    head_size = width // HEADS
    row_count = seq_count * block_len
    shape4 = (seq_count, block_len, HEADS, head_size)
    score_scale = 1.0 / math.sqrt(head_size)
    group_size = lax.axis_size("group")
    member = lax.axis_index("group")
    reach = min((DOC_MOST + block_len - 2) // block_len, group_size - 1)
    slopes = jnp.exp2(-8.0 * (jnp.arange(HEADS, dtype=jnp.float32) + 1.0) / HEADS)
    inputs = activations.reshape(row_count, width).astype(jnp.float32)
    gain_one = gain_before.astype(jnp.float32)
    gain_two = gain_middle.astype(jnp.float32)
    normal_one, spread_one = standardize(inputs)
    normed_one = (normal_one * gain_one + shift_before.astype(jnp.float32)).astype(jnp.bfloat16)
    joint = jnp.dot(normed_one, joint_weight, preferred_element_type=jnp.float32)
    bias_joint = joint_bias.astype(jnp.float32)
    query_rows = (joint[:, :width] + bias_joint[:width]).astype(jnp.bfloat16)
    key_rows = joint[:, width : 2 * width].astype(jnp.bfloat16)
    value_rows = (joint[:, 2 * width :] + bias_joint[width:]).astype(jnp.bfloat16)
    own_piece = jnp.stack([key_rows, value_rows]).reshape(2, seq_count, block_len, width)
    query4 = query_rows.reshape(shape4)
    pieces = [own_piece]
    for hop in range(1, reach + 1):
        pieces.append(shifted(own_piece, "group", hop))
    row_top = jnp.full((seq_count, HEADS, block_len), masked_score, jnp.float32)
    row_total = jnp.zeros((seq_count, HEADS, block_len), jnp.float32)
    for hop in range(reach + 1):
        allowed, distance = window_mask(segments, padding, member, hop, block_len)
        scores = piece_scores(query4, pieces[hop][0].reshape(shape4), slopes, distance, score_scale)
        fresh = jnp.maximum(row_top, jnp.max(jnp.where(allowed, scores, masked_score), -1))
        row_total = row_total * jnp.exp(row_top - fresh) + jnp.sum(
            jnp.exp(jnp.where(allowed, scores - fresh[..., None], masked_score)), -1
        )
        row_top = fresh
    log_total = row_top + jnp.log(row_total)
    attended = jnp.zeros(shape4, jnp.float32)
    for hop in range(reach + 1):
        allowed, distance = window_mask(segments, padding, member, hop, block_len)
        scores = piece_scores(query4, pieces[hop][0].reshape(shape4), slopes, distance, score_scale)
        probs = jnp.exp(jnp.where(allowed, scores - log_total[..., None], masked_score)).astype(
            jnp.bfloat16
        )
        attended = attended + jnp.einsum(
            "shqk,skhd->sqhd",
            probs,
            pieces[hop][1].reshape(shape4),
            preferred_element_type=jnp.float32,
        )
    attended_low = attended.reshape(row_count, width).astype(jnp.bfloat16)
    resid = inputs + (
        jnp.dot(attended_low, mixer_weight, preferred_element_type=jnp.float32)
        + mixer_bias.astype(jnp.float32)
    )
    normal_two, spread_two = standardize(resid)
    normed_two = (normal_two * gain_two + shift_middle.astype(jnp.float32)).astype(jnp.bfloat16)
    hidden = jnp.dot(
        normed_two, expand_weight, preferred_element_type=jnp.float32
    ) + expand_bias.astype(jnp.float32)
    act = jax.nn.gelu(hidden, approximate=True).astype(jnp.bfloat16)
    result = resid + (
        jnp.dot(act, reduce_weight, preferred_element_type=jnp.float32)
        + reduce_bias.astype(jnp.float32)
    )
    output = result.astype(jnp.bfloat16).reshape(seq_count, block_len, width)
    cot_low = cotangent.reshape(row_count, width)
    cot_full = cot_low.astype(jnp.float32)
    reduce_grad = jnp.einsum("tf,td->fd", act, cot_low, preferred_element_type=jnp.float32)
    reduce_bias_grad = jnp.sum(cot_full, 0)
    dact = jnp.einsum("td,fd->tf", cot_low, reduce_weight, preferred_element_type=jnp.float32)
    gelu_pull = jax.vjp(lambda inner: jax.nn.gelu(inner, approximate=True), hidden)[1]
    dhidden = gelu_pull(dact)[0].astype(jnp.bfloat16)
    expand_grad = jnp.einsum("td,tf->df", normed_two, dhidden, preferred_element_type=jnp.float32)
    expand_bias_grad = jnp.sum(dhidden.astype(jnp.float32), 0)
    dnormed_two = jnp.einsum(
        "tf,df->td", dhidden, expand_weight, preferred_element_type=jnp.float32
    )
    gain_middle_grad = jnp.sum(dnormed_two * normal_two, 0)
    shift_middle_grad = jnp.sum(dnormed_two, 0)
    dresid = cot_full + norm_back(dnormed_two * gain_two, normal_two, spread_two)
    dbranch = dresid.astype(jnp.bfloat16)
    mixer_grad = jnp.einsum("td,te->de", attended_low, dbranch, preferred_element_type=jnp.float32)
    mixer_bias_grad = jnp.sum(dbranch.astype(jnp.float32), 0)
    dattended = jnp.einsum(
        "te,de->td", dbranch, mixer_weight, preferred_element_type=jnp.float32
    ).astype(jnp.bfloat16)
    dattended4 = dattended.reshape(shape4)
    row_delta = jnp.einsum("sqhd,sqhd->shq", dattended4.astype(jnp.float32), attended)
    dquery = jnp.zeros(shape4, jnp.float32)
    dkv_own = jnp.zeros((2, seq_count, block_len, width), jnp.float32)
    for hop in range(reach + 1):
        piece = pieces[hop]
        key4 = piece[0].reshape(shape4)
        value4 = piece[1].reshape(shape4)
        allowed, distance = window_mask(segments, padding, member, hop, block_len)
        scores = piece_scores(query4, key4, slopes, distance, score_scale)
        probs = jnp.exp(jnp.where(allowed, scores - log_total[..., None], masked_score))
        dvalue = jnp.einsum(
            "shqk,sqhd->skhd",
            probs.astype(jnp.bfloat16),
            dattended4,
            preferred_element_type=jnp.float32,
        )
        dprobs = jnp.einsum(
            "sqhd,skhd->shqk", dattended4, value4, preferred_element_type=jnp.float32
        )
        dscores = (probs * (dprobs - row_delta[..., None])).astype(jnp.bfloat16)
        dquery = dquery + jnp.einsum(
            "shqk,skhd->sqhd", dscores, key4, preferred_element_type=jnp.float32
        )
        dkey = (
            jnp.einsum("shqk,sqhd->skhd", dscores, query4, preferred_element_type=jnp.float32)
            * score_scale
        )
        returned = jnp.stack([dkey, dvalue]).reshape(2, seq_count, block_len, width)
        if hop == 0:
            dkv_own = returned
        else:
            dkv_own = dkv_own + shifted(returned.astype(jnp.bfloat16), "group", -hop).astype(
                returned.dtype
            )
    dquery_low = (dquery * score_scale).reshape(row_count, width).astype(jnp.bfloat16)
    dkey_low = dkv_own[0].reshape(row_count, width).astype(jnp.bfloat16)
    dvalue_low = dkv_own[1].reshape(row_count, width).astype(jnp.bfloat16)
    djoint = jnp.concatenate([dquery_low, dkey_low, dvalue_low], 1)
    joint_grad = jnp.einsum("td,te->de", normed_one, djoint, preferred_element_type=jnp.float32)
    joint_bias_grad = jnp.concatenate(
        [jnp.sum(dquery_low.astype(jnp.float32), 0), jnp.sum(dvalue_low.astype(jnp.float32), 0)]
    )
    dnormed_one = jnp.einsum("te,de->td", djoint, joint_weight, preferred_element_type=jnp.float32)
    gain_before_grad = jnp.sum(dnormed_one * normal_one, 0)
    shift_before_grad = jnp.sum(dnormed_one, 0)
    dinput = dresid + norm_back(dnormed_one * gain_one, normal_one, spread_one)
    input_gradient = dinput.astype(jnp.bfloat16).reshape(seq_count, block_len, width)
    listing = [
        gain_before_grad,
        shift_before_grad,
        joint_grad,
        joint_bias_grad,
        mixer_grad,
        mixer_bias_grad,
        gain_middle_grad,
        shift_middle_grad,
        expand_grad,
        expand_bias_grad,
        reduce_grad,
        reduce_bias_grad,
    ]
    gradient = jnp.concatenate([single.reshape(-1) for single in listing])
    small_list = [
        gain_before_grad,
        shift_before_grad,
        joint_bias_grad,
        mixer_bias_grad,
        gain_middle_grad,
        shift_middle_grad,
        expand_bias_grad,
        reduce_bias_grad,
    ]
    small_local = jnp.concatenate(small_list)
    share, small_share = (
        lax.psum_scatter(gradient, ("dp", "group"), scatter_dimension=0, tiled=True),
        lax.psum_scatter(small_local, ("dp", "group"), scatter_dimension=0, tiled=True),
    )
    moment_step = step_count[0].astype(jnp.float32)
    rate = learn_rate[0]
    fix_one = 1.0 - jnp.exp(moment_step * math.log(beta_first))
    fix_two = 1.0 - jnp.exp(moment_step * math.log(beta_second))
    updated_first = beta_first * first_moment + (1.0 - beta_first) * share
    updated_second = beta_second * second_moment + (1.0 - beta_second) * share * share
    updated_master = master_weights - rate * (
        updated_first / fix_one / (jnp.sqrt(updated_second / fix_two) + adam_epsilon)
        + weight_decay * master_weights
    )
    return (output, input_gradient, updated_master, updated_first, updated_second, small_share)


WIDTH = 1024
HIDDEN = 4096
TOKENS = 1024
LANES = 128
OWNED = 393600
OWNED_ROWS = OWNED // LANES
PIECE = 1568
HALF = PIECE // 2
JOINT_AT, MIXER_AT, EXPAND_AT, REDUCE_AT = 16, 12320, 16432, 32832
FLAT_ROWS = 49248
U_JOINT, U_JBIAS, U_MIXER, U_MBIAS, U_EXPAND, U_EBIAS, U_REDUCE, U_RBIAS = (
    2, 3074, 3076, 4100, 4103, 8199, 8203, 12299,
)


def section_shift(unit):
    return 8 if unit < U_JBIAS else 16 if unit < U_MBIAS else 20


def piece_start(owner):
    unit = OWNED_ROWS * owner // 8
    return (4 * unit + section_shift(unit)) // 16 * 16


def piece_offset(q, y, x):
    at = [piece_start(4 * q + k) // 16 for k in range(4)]
    row = (
        at[0] * (1 - y) * (1 - x) + at[1] * (1 - y) * x + at[2] * y * (1 - x) + at[3] * y * x
    )
    return pl.multiple_of(row * 16, 16)


MESH_ID = pl.DeviceIdType.MESH


def by_rows(step):
    def one(i, carry):
        step(pl.ds(pl.multiple_of(112 * i, 16), 112))
        return carry

    lax.fori_loop(0, HALF // 112, one, 0)


class Pieces:
    def __init__(self, dp, me, flat, own_a, own_b, rx_a1, rx_b1, rx_a2, rx_b2, acc, load_sem, s2_send, s2_recv):
        self.y, self.x = me // 2, me % 2
        self.x_near = (dp, 2 * self.y + (1 - self.x))
        self.y_near = (dp, 2 * (1 - self.y) + self.x)
        self.flat, self.own_a, self.own_b = flat, own_a, own_b
        self.rx_a1, self.rx_b1, self.rx_a2, self.rx_b2, self.acc = rx_a1, rx_b1, rx_a2, rx_b2, acc
        self.load_sem, self.s2_send, self.s2_recv = load_sem, s2_send, s2_recv

    def loads(self, q, own_slot, ready=None):
        slot = q
        out = []
        for k in range(2):
            for way, (row, own) in enumerate((
                (piece_offset(q, k, self.x), self.own_a),
                (piece_offset(q, self.y, k) + HALF, self.own_b),
            )):
                out.append(pltpu.make_async_copy(
                    self.flat.at[pl.ds(row, HALF)], own.at[own_slot, k], self.load_sem.at[slot, way, k]
                ))
            if ready is not None:
                ready_a, ready_b, at = ready
                for way, (src, dst) in enumerate(((ready_a, self.rx_a1), (ready_b, self.rx_b1))):
                    out.append(pltpu.make_async_copy(
                        src.at[at, k], dst.at[slot, k], self.load_sem.at[slot, 2 + way, k]
                    ))
        return out

    def second(self, slot):
        y, x = self.y, self.x
        return [
            pltpu.make_async_remote_copy(
                src_ref=src, dst_ref=dst.at[slot], send_sem=self.s2_send.at[slot, way],
                recv_sem=self.s2_recv.at[slot, way], device_id=near, device_id_type=MESH_ID,
            )
            for way, (src, dst, near) in enumerate((
                (self.rx_a1.at[slot, 1 - y], self.rx_a2, self.y_near),
                (self.rx_b1.at[slot, 1 - x], self.rx_b2, self.x_near),
            ))
        ]

    def meet(self, slot, own_slot):
        y, x = self.y, self.x
        rx_a1, rx_b1, own_a, own_b, acc = self.rx_a1, self.rx_b1, self.own_a, self.own_b, self.acc

        def away(rows):
            rx_a1[slot, 1 - y, rows] = rx_a1[slot, 1 - y, rows] + own_a[own_slot, 1 - y, rows]
            rx_b1[slot, 1 - x, rows] = rx_b1[slot, 1 - x, rows] + own_b[own_slot, 1 - x, rows]

        by_rows(away)
        for copy in self.second(slot):
            copy.start()

        def kept(rows):
            acc[slot, 0, rows] = rx_a1[slot, y, rows] + own_a[own_slot, y, rows]
            acc[slot, 1, rows] = rx_b1[slot, x, rows] + own_b[own_slot, x, rows]

        by_rows(kept)

    def join(self, slot):
        for copy in self.second(slot):
            copy.wait_recv()
        acc, rx_a2, rx_b2 = self.acc, self.rx_a2, self.rx_b2

        def add(rows):
            acc[slot, 0, rows] = acc[slot, 0, rows] + rx_a2[slot, rows]
            acc[slot, 1, rows] = acc[slot, 1, rows] + rx_b2[slot, rows]

        by_rows(add)


MIDDLE_EARLY = (6, 7, 4)


def nn(a, b):
    return lax.dot_general(a, b, (((1,), (0,)), ((), ())), preferred_element_type=jnp.float32)


def nt(a, b):
    return lax.dot_general(a, b, (((1,), (1,)), ((), ())), preferred_element_type=jnp.float32)


def tn(a, b):
    return lax.dot_general(a, b, (((0,), (0,)), ((), ())), preferred_element_type=jnp.float32)


def head_lanes(value, h):
    lane = lax.broadcasted_iota(jnp.int32, (1, LANES), 1)
    return jnp.where(lane // 64 == h, value, jnp.zeros_like(value))


def plane_devices(dp, me):
    z, c = dp // 2, dp % 2
    near = [(2 * z + 1 - c, me)]
    for d in (1, 2, 3):
        near += [(2 * z, (me + d) % 4), (2 * z + 1, (me + d) % 4)]
    return near


def greet(devices):
    barrier = pltpu.get_barrier_semaphore()
    for near in devices:
        pl.semaphore_signal(barrier, inc=1, device_id=near, device_id_type=MESH_ID)
    pl.semaphore_wait(barrier, len(devices))


class Home:
    def __init__(self, rows, out, dp, me, send_sem, recv_sem):
        z, c = dp // 2, dp % 2
        self.here = c == me // 2
        self.turns = []
        for turn in range(2):
            src = rows.at[pl.ds(256 * turn, 256)]
            dst = out.at[me % 2]
            away = pltpu.make_async_remote_copy(
                src_ref=src, dst_ref=dst, send_sem=send_sem.at[turn], recv_sem=recv_sem.at[me % 2],
                device_id=(2 * z + me // 2, 2 * c + turn), device_id_type=MESH_ID,
            )
            near = pltpu.make_async_copy(src, dst, send_sem.at[turn])
            came = pltpu.make_async_remote_copy(
                src_ref=src, dst_ref=out.at[turn], send_sem=send_sem.at[turn],
                recv_sem=recv_sem.at[turn], device_id=(2 * z + me // 2, 2 * c + turn),
                device_id_type=MESH_ID,
            )
            self.turns.append((away, near, came, self.here & (me % 2 == turn)))

    def start(self):
        for away, near, _, stays in self.turns:
            @pl.when(stays)
            def _():
                near.start()

            @pl.when(jnp.logical_not(stays))
            def _():
                away.start()

    def wait(self):
        for away, near, came, stays in self.turns:
            @pl.when(stays)
            def _():
                near.wait()

            @pl.when(jnp.logical_not(stays))
            def _():
                away.wait_send()
                came.wait_recv()


def first_stage(q, flat, rx_a, rx_b, at, send_sem, recv_sem, dp, me):
    y, x = me // 2, me % 2
    x_near = (dp, 2 * y + (1 - x))
    y_near = (dp, 2 * (1 - y) + x)
    out = []
    for k in range(2):
        for way, (row, rx, near) in enumerate((
            (piece_offset(q, k, 1 - x), rx_a, x_near),
            (piece_offset(q, 1 - y, k) + HALF, rx_b, y_near),
        )):
            out.append(pltpu.make_async_remote_copy(
                src_ref=flat.at[pl.ds(row, HALF)], dst_ref=rx.at[at, k],
                send_sem=send_sem.at[at, way, k], recv_sem=recv_sem.at[at, way, k],
                device_id=near, device_id_type=MESH_ID,
            ))
    return out


class Spread:
    def __init__(self, blocks, rows, dp, me, send_sem, recv_sem):
        z, c = dp // 2, dp % 2
        here = c == me // 2
        self.turns = []
        for turn in range(2):
            src = blocks.at[turn]
            dst = rows.at[pl.ds(pl.multiple_of(256 * me, 256), 256)]
            away = pltpu.make_async_remote_copy(
                src_ref=src, dst_ref=dst, send_sem=send_sem.at[turn], recv_sem=recv_sem.at[me % 2],
                device_id=(2 * z + me // 2, 2 * c + turn), device_id_type=MESH_ID,
            )
            near = pltpu.make_async_copy(src, dst, send_sem.at[turn])
            came = pltpu.make_async_remote_copy(
                src_ref=src, dst_ref=rows.at[pl.ds(pl.multiple_of(512 * c + 256 * turn, 256), 256)],
                send_sem=send_sem.at[turn], recv_sem=recv_sem.at[turn],
                device_id=(2 * z + me // 2, 2 * c + turn), device_id_type=MESH_ID,
            )
            self.turns.append((away, near, came, here & (me % 2 == turn)))

    def start(self):
        for away, near, _, stays in self.turns:
            @pl.when(stays)
            def _():
                near.start()

            @pl.when(jnp.logical_not(stays))
            def _():
                away.start()

    def wait_came(self, turn):
        _, near, came, stays = self.turns[turn]

        @pl.when(stays)
        def _():
            near.wait()

        @pl.when(jnp.logical_not(stays))
        def _():
            came.wait_recv()

    def wait_sent(self):
        for away, _, _, stays in self.turns:
            @pl.when(jnp.logical_not(stays))
            def _():
                away.wait_send()


def front_kernel(
    slopes, blocks, cot_blocks, segments, padding, gain_in, shift_in, bias_in, weight_hbm,
    x_out, cot_out, normed_out, joint_out, dist_out, att_out, lse_out,
    x_all, cot_all, normed, joint, weight, dist, att, lse, seg_rx, pad_rx, vectors, columns, s_ref, p_ref, vt_ref, ot_ref,
    weight_sem, out_sem, mark_sem, x_send, x_recv, cot_send, cot_recv, pass_send, pass_recv,
):
    f32, bf16 = jnp.float32, jnp.bfloat16
    dp = lax.axis_index("dp")
    me = lax.axis_index("group")
    c = dp % 2
    core_near = (dp + 1 - 2 * c, me)
    own = pl.ds(pl.multiple_of(512 * c, 512), 512)
    other = pl.ds(pl.multiple_of(512 * (1 - c), 512), 512)

    weights = [
        pltpu.make_async_copy(
            weight_hbm.at[:, pl.ds(pl.multiple_of(1024 * p + 512 * c, 512), 512)],
            weight.at[:, pl.ds(512 * p, 512)], weight_sem.at[p],
        )
        for p in range(3)
    ]
    greet(plane_devices(dp, me))
    x_way = Spread(blocks, x_all, dp, me, x_send, x_recv)
    cot_way = Spread(cot_blocks, cot_all, dp, me, cot_send, cot_recv)
    x_way.start()
    vectors[0:1, :] = gain_in[...].astype(f32).reshape(1, WIDTH)
    vectors[1:2, :] = shift_in[...].astype(f32).reshape(1, WIDTH)
    vectors[2:4, :] = bias_in[...].astype(f32).reshape(2, WIDTH)
    mark_swaps = [
        pltpu.make_async_remote_copy(
            src_ref=src, dst_ref=dst, send_sem=mark_sem.at[0, i], recv_sem=mark_sem.at[1, i],
            device_id=core_near, device_id_type=MESH_ID,
        )
        for i, (src, dst) in enumerate(((segments, seg_rx), (padding, pad_rx)))
    ]
    for copy in mark_swaps:
        copy.start()
    for copy in weights:
        copy.start()

    def hand_over(rows, way, turn):
        at = pl.ds(pl.multiple_of(512 * c + 256 * turn, 256), 256)
        return pltpu.make_async_remote_copy(
            src_ref=rows.at[at], dst_ref=rows.at[at], send_sem=pass_send.at[way, turn],
            recv_sem=pass_recv.at[way, turn], device_id=core_near, device_id_type=MESH_ID,
        )

    for copy in mark_swaps:
        copy.wait()
    odd = me % 2 == 1
    held = c == me // 2

    def row_of(mine, came):
        both = jnp.where(held, mine[...], came[...]).astype(f32)
        return jnp.where(odd, both[1:2], both[0:1])

    seg = row_of(segments, seg_rx)
    pad = row_of(padding, pad_rx)
    kind = lax.broadcasted_iota(jnp.int32, (8, TOKENS), 0)
    columns[...] = jnp.broadcast_to(
        jnp.where(kind == 0, seg, pad).T[:, :8].reshape(TOKENS, 8), (TOKENS, 8)
    )

    def dist_rows(i, carry):
        rows = pl.ds(pl.multiple_of(128 * i, 128), 128)
        key_seg, key_pad = columns[rows, 0:1], columns[rows, 1:2]
        key = (lax.broadcasted_iota(jnp.int32, (128, 1), 0) + 128 * i).astype(f32)
        query = lax.broadcasted_iota(jnp.int32, (128, TOKENS), 1).astype(f32)
        last = jnp.sum(jnp.where(seg <= key_seg, 1.0, 0.0), 1, keepdims=True) - 1.0
        last = jnp.where(key_pad == 1.0, last, key)
        dist[rows, :] = jnp.where((query >= key) & (query <= last), query - key, -masked_score)
        return carry

    lax.fori_loop(0, 8, dist_rows, 0)
    outs = []

    def put(src, dst):
        copy = pltpu.make_async_copy(src, dst, out_sem.at[len(outs)])
        copy.start()
        outs.append(copy)

    put(dist, dist_out)
    gain, shift = vectors[0:1, :], vectors[1:2, :]

    def norm_rows(half):
        def one(i, carry):
            rows = pl.ds(pl.multiple_of(512 * half + 128 * i, 128), 128)
            values = x_all[rows, :].astype(f32)
            center = values - jnp.mean(values, -1, keepdims=True)
            factor = lax.rsqrt(jnp.mean(center * center, -1, keepdims=True) + norm_epsilon)
            normed[rows, :] = (center * factor * gain + shift).astype(bf16)
            return carry

        lax.fori_loop(0, 4, one, 0)
        rows = pl.ds(pl.multiple_of(512 * half, 512), 512)
        lanes = pl.ds(pl.multiple_of(512 * c, 512), 512)
        made = nn(normed[rows, :], weight[...])
        joint[rows, 0:512] = ((made[:, 0:512] + vectors[2:3, lanes]) * 0.125).astype(bf16)
        joint[rows, 512:1024] = made[:, 512:1024].astype(bf16)
        joint[rows, 1024:1536] = (made[:, 1024:1536] + vectors[3:4, lanes]).astype(bf16)

    for turn in range(2):
        x_way.wait_came(turn)
        hand_over(x_all, 0, turn).start()
    x_way.wait_sent()
    cot_way.start()
    put(x_all.at[own], x_out)
    for copy in weights:
        copy.wait()
    norm_rows(c)
    for turn in range(2):
        hand_over(x_all, 0, turn).wait_recv()
    norm_rows(1 - c)
    put(normed, normed_out)
    put(joint, joint_out)

    def pair_step(pair, carry):
        def lanes(block):
            return pl.ds(pl.multiple_of(512 * block + LANES * pair, LANES), LANES)

        vt_ref[...] = joint[:, lanes(2)].astype(f32).T.astype(bf16)
        ot_ref[...] = jnp.zeros_like(ot_ref)

        def head(h, carry):
            slope = slopes[8 * c + 2 * pair + h]
            for qb in range(4):
                cols = pl.ds(qb * 256, 256)
                queries = head_lanes(joint[cols, lanes(0)], h)
                top = None
                for kb in range(qb + 1):
                    rows = pl.ds(kb * 256, 256)
                    s = nt(joint[rows, lanes(1)], queries) - slope * dist[rows, cols]
                    s_ref[rows, :] = s
                    high = jnp.max(s, 0, keepdims=True)
                    top = high if top is None else jnp.maximum(top, high)
                total = None
                for kb in range(qb + 1):
                    rows = pl.ds(kb * 256, 256)
                    p = jnp.exp(s_ref[rows, :] - top)
                    more = jnp.sum(p, 0, keepdims=True)
                    total = more if total is None else total + more
                    p_ref[rows, :] = p.astype(bf16)
                span = pl.ds(0, 256 * (qb + 1))
                out = nn(vt_ref[:, span], p_ref[span, :]) / total
                row = lax.broadcasted_iota(jnp.int32, (LANES, 1), 0)
                ot_ref[:, cols] = jnp.where(row // 64 == h, out, ot_ref[:, cols])
                lse[pair, pl.ds(h, 1), cols] = top + jnp.log(total)
            return carry

        lax.fori_loop(0, 2, head, 0)
        att[:, lanes(0)] = ot_ref[...].T.astype(bf16)

        @pl.when(pair == 2)
        def _():
            for turn in range(2):
                cot_way.wait_came(turn)
                hand_over(cot_all, 1, turn).start()

        return carry

    lax.fori_loop(0, 4, pair_step, 0)
    put(att, att_out)
    put(lse, lse_out)
    for turn in range(2):
        hand_over(cot_all, 1, turn).wait()
        hand_over(x_all, 0, turn).wait_send()
    put(cot_all, cot_out)
    cot_way.wait_sent()
    for copy in outs:
        copy.wait()


def front(slopes, blocks, cot_blocks, segments, padding, gain, shift, bias, weight):
    f32, bf16 = jnp.float32, jnp.bfloat16
    vmem = pl.BlockSpec(memory_space=pltpu.VMEM)
    hbm = pl.BlockSpec(memory_space=pl.ANY)
    return pl.pallas_call(
        front_kernel,
        out_shape=(
            jax.ShapeDtypeStruct((512, WIDTH), bf16),
            jax.ShapeDtypeStruct((TOKENS, WIDTH), bf16),
            jax.ShapeDtypeStruct((TOKENS, WIDTH), bf16),
            jax.ShapeDtypeStruct((TOKENS, 1536), bf16),
            jax.ShapeDtypeStruct((TOKENS, TOKENS), f32),
            jax.ShapeDtypeStruct((TOKENS, 512), bf16),
            jax.ShapeDtypeStruct((4, 2, TOKENS), f32),
        ),
        in_specs=[pl.BlockSpec(memory_space=pltpu.SMEM)] + [hbm] * 2 + [vmem] * 5 + [hbm],
        out_specs=[hbm] * 7,
        scratch_shapes=[
            pltpu.VMEM((TOKENS, WIDTH), bf16),
            pltpu.VMEM((TOKENS, WIDTH), bf16),
            pltpu.VMEM((TOKENS, WIDTH), bf16),
            pltpu.VMEM((TOKENS, 1536), bf16),
            pltpu.VMEM((WIDTH, 1536), bf16),
            pltpu.VMEM((TOKENS, TOKENS), f32),
            pltpu.VMEM((TOKENS, 512), bf16),
            pltpu.VMEM((4, 2, TOKENS), f32),
            pltpu.VMEM((2, TOKENS), jnp.int32),
            pltpu.VMEM((2, TOKENS), jnp.int32),
            pltpu.VMEM((8, WIDTH), f32),
            pltpu.VMEM((TOKENS, 8), f32),
            pltpu.VMEM((TOKENS, 256), f32),
            pltpu.VMEM((TOKENS, 256), bf16),
            pltpu.VMEM((LANES, TOKENS), bf16),
            pltpu.VMEM((LANES, TOKENS), f32),
            pltpu.SemaphoreType.DMA((3,)),
            pltpu.SemaphoreType.DMA((7,)),
            pltpu.SemaphoreType.DMA((2, 2)),
            pltpu.SemaphoreType.DMA((2,)),
            pltpu.SemaphoreType.DMA((2,)),
            pltpu.SemaphoreType.DMA((2,)),
            pltpu.SemaphoreType.DMA((2,)),
            pltpu.SemaphoreType.DMA((2, 2)),
            pltpu.SemaphoreType.DMA((2, 2)),
        ],
        compiler_params=pltpu.CompilerParams(
            collective_id=0, has_side_effects=True, vmem_limit_bytes=62 << 20
        ),
        cost_estimate=pl.CostEstimate(flops=10 << 30, bytes_accessed=20 << 20, transcendentals=0),
    )(slopes, blocks, cot_blocks, segments, padding, gain, shift, bias, weight)


def rear_kernel(
    slopes, joint_hbm, att_hbm, datt_hbm, dist_hbm, lse, normed_hbm, weight_hbm, x_hbm, dresid_hbm,
    result, mid_sums, expand_sums, mid_a, mid_b, flat_in,
    flat, own_out, peer_out, small_out, output, input_gradient,
    joint, attended, dattended, normed, weight, x_own, dresid,
    dist, p_ref, ds_ref, kt_ref, dqt_ref, dk_acc, dv_acc, delta_ref, djoint, dn_rx, dinput, blocks,
    own_a, own_b, rx_a1, rx_b1, rx_a2, rx_b2, acc, rx_up, rx_dn, parting,
    small_mine, small_rx, small_z,
    dist_sem, block_sem, swap_sem, load_sem, s1_send, s1_recv, s2_send, s2_recv, z_send, z_recv,
    last_sem, sm_send, sm_recv, out_send, out_recv, in_send, in_recv,
):
    f32, bf16 = jnp.float32, jnp.bfloat16
    dp = lax.axis_index("dp")
    me = lax.axis_index("group")
    z, c = dp // 2, dp % 2
    y, x = me // 2, me % 2
    x_near = (dp, 2 * y + (1 - x))
    y_near = (dp, 2 * (1 - y) + x)
    core_near = (2 * z + 1 - c, me)
    own = pl.ds(pl.multiple_of(512 * c, 512), 512)
    other = pl.ds(pl.multiple_of(512 * (1 - c), 512), 512)

    def z_at(d):
        return (2 * d + c, me)

    pieces = Pieces(
        dp, me, flat, own_a, own_b, rx_a1, rx_b1, rx_a2, rx_b2, acc, load_sem, s2_send, s2_recv
    )
    own_slot = {6: 0, 7: 1, 4: 2, 5: 3, 0: 0, 1: 1, 3: 2, 2: 3}

    def loads(q):
        ready = (mid_a, mid_b, MIDDLE_EARLY.index(q)) if q in MIDDLE_EARLY else None
        return pieces.loads(q, own_slot[q], ready)

    def start(copies):
        for copy in copies:
            copy.start()

    def stage1(q):
        return first_stage(q, flat, rx_a1, rx_b1, q, s1_send, s1_recv, dp, me)

    def hop(q, up, half):
        way = 0 if up else 1
        return pltpu.make_async_remote_copy(
            src_ref=acc.at[q, half], dst_ref=rx_up.at[q - 2, half] if up else rx_dn.at[q, half],
            send_sem=z_send.at[q, way, half], recv_sem=z_recv.at[q, way, half],
            device_id=z_at((z + 1) % 4 if up else (z + 3) % 4), device_id_type=MESH_ID,
        )

    def meet(q):
        for copy in loads(q):
            copy.wait()
        if q not in MIDDLE_EARLY:
            for copy in stage1(q):
                copy.wait_recv()
        pieces.meet(q, own_slot[q])

    def add_came(q, rx, at, half):
        def add(rows):
            acc[q, half, rows] = acc[q, half, rows] + rx[at, half, rows]

        by_rows(add)

    on_way = {(plane, up): [] for plane in range(4) for up in (False, True)}

    def send_on(plane, q, up, half):
        queue = on_way[plane, up]
        if len(queue) >= 2:
            hop(*queue[-2]).wait_send()
        hop(q, up, half).start()
        queue.append((q, up, half))

    def pass_on(q, h):
        aim = q // 2
        if h < aim:
            @pl.when(z == h)
            def _():
                for half in range(2):
                    if h > 0:
                        hop(q, True, half).wait_recv()
                        add_came(q, rx_up, q - 2, half)
                    send_on(h, q, True, half)
        if h < 3 - aim:
            @pl.when(z == 3 - h)
            def _():
                for half in range(2):
                    if h > 0:
                        hop(q, False, half).wait_recv()
                        add_came(q, rx_dn, q, half)
                    send_on(3 - h, q, False, half)

    last = pltpu.make_async_remote_copy(
        src_ref=parting, dst_ref=peer_out, send_sem=last_sem.at[0], recv_sem=last_sem.at[1],
        device_id=core_near, device_id_type=MESH_ID,
    )

    def finish(q):
        aim = q // 2

        @pl.when(z == aim)
        def _():
            mine = c == q % 2
            for k in range(2):
                if aim > 0:
                    hop(q, True, k).wait_recv()
                if aim < 3:
                    hop(q, False, k).wait_recv()

                def add(i, carry):
                    rows = pl.ds(pl.multiple_of(112 * i, 16), 112)
                    place = pl.ds(pl.multiple_of(HALF * k + 112 * i, 16), 112)
                    total = acc[q, k, rows].astype(f32)
                    if aim > 0:
                        total = total + rx_up[q - 2, k, rows].astype(f32)
                    if aim < 3:
                        total = total + rx_dn[q, k, rows].astype(f32)

                    @pl.when(mine)
                    def _():
                        own_out[place] = total

                    @pl.when(jnp.logical_not(mine))
                    def _():
                        parting[place] = total

                    return carry

                lax.fori_loop(0, HALF // 112, add, 0)

            @pl.when(jnp.logical_not(mine))
            def _():
                last.start()

    def small_step(k):
        near = (core_near, x_near, y_near)[k]
        return pltpu.make_async_remote_copy(
            src_ref=small_mine.at[k], dst_ref=small_rx.at[k], send_sem=sm_send.at[k],
            recv_sem=sm_recv.at[k], device_id=near, device_id_type=MESH_ID,
        )

    def small_next(k):
        small_step(k).wait()
        small_mine[k + 1] = small_mine[k] + small_rx[k]
        if k < 2:
            small_step(k + 1).start()

    def small_hop(d):
        return pltpu.make_async_remote_copy(
            src_ref=small_mine.at[3], dst_ref=small_z.at[d - 1], send_sem=sm_send.at[2 + d],
            recv_sem=sm_recv.at[2 + d], device_id=z_at((z + d) % 4), device_id_type=MESH_ID,
        )

    def load(i, src, dst):
        return pltpu.make_async_copy(src, dst, dist_sem.at[i])

    first_loads = [
        load(0, joint_hbm, joint), load(1, att_hbm, attended), load(2, datt_hbm, dattended),
        load(3, dist_hbm, dist),
    ]
    later_loads = [load(4, normed_hbm, normed), load(5, x_hbm, x_own), load(6, dresid_hbm, dresid)]
    for p in range(3):
        later_loads.append(load(
            7 + p, weight_hbm.at[:, pl.ds(pl.multiple_of(1024 * p + 512 * c, 512), 512)],
            weight.at[:, pl.ds(512 * p, 512)],
        ))
    start(first_loads)
    for q in (7, 6, 4):
        start(loads(q))
    greet(plane_devices(dp, me) + [z_at((z + d) % 4) for d in (1, 2, 3)])
    way_out = Home(result, output, dp, me, out_send, out_recv)
    way_in = Home(dinput, input_gradient, dp, me, in_send, in_recv)
    start(stage1(5))
    start(stage1(3))

    def go_on(pair):
        @pl.when(pair == 0)
        def _():
            start(loads(5))
            start(later_loads)

        @pl.when(pair == 1)
        def _():
            meet(7)

        @pl.when(pair == 2)
        def _():
            for q in (6, 4, 5):
                meet(q)

    for copy in first_loads:
        copy.wait()

    def pair_step(pair, carry):
        def lanes(block):
            return pl.ds(pl.multiple_of(512 * block + LANES * pair, LANES), LANES)

        here = lanes(0)
        kt_ref[...] = joint[:, lanes(1)].astype(f32).T.astype(bf16)
        product = (attended[:, here].astype(f32) * dattended[:, here].astype(f32)).T
        delta_ref[0:1, :] = jnp.sum(product[:64], 0, keepdims=True)
        delta_ref[1:2, :] = jnp.sum(product[64:], 0, keepdims=True)
        dk_acc[...] = jnp.zeros_like(dk_acc)
        dv_acc[...] = jnp.zeros_like(dv_acc)
        dqt_ref[...] = jnp.zeros_like(dqt_ref)

        def head(h, carry):
            slope = slopes[8 * c + 2 * pair + h]
            for qb in range(4):
                cols = pl.ds(qb * 256, 256)
                queries = head_lanes(joint[cols, here], h)
                grads = head_lanes(dattended[cols, here], h)
                top = lse[pair, pl.ds(h, 1), cols]
                delta = delta_ref[pl.ds(h, 1), cols]
                for kb in range(qb + 1):
                    rows = pl.ds(kb * 256, 256)
                    s = nt(joint[rows, lanes(1)], queries) - slope * dist[rows, cols]
                    p = jnp.exp(s - top)
                    p_ref[rows, :] = p.astype(bf16)
                    dprobs = nt(joint[rows, lanes(2)], grads)
                    ds_ref[rows, :] = (p * (dprobs - delta)).astype(bf16)
                span = pl.ds(0, 256 * (qb + 1))
                dv_acc[span, :] += nn(p_ref[span, :], grads)
                dk_acc[span, :] += nn(ds_ref[span, :], queries)
                dq = nn(kt_ref[:, span], ds_ref[span, :])
                row = lax.broadcasted_iota(jnp.int32, (LANES, 1), 0)
                dqt_ref[:, cols] = jnp.where(row // 64 == h, dq, dqt_ref[:, cols])
            return carry

        lax.fori_loop(0, 2, head, 0)
        djoint[:, lanes(0)] = (dqt_ref[...] * 0.125).T.astype(bf16)
        djoint[:, lanes(1)] = dk_acc[...].astype(bf16)
        djoint[:, lanes(2)] = dv_acc[...].astype(bf16)
        go_on(pair)
        return carry

    lax.fori_loop(0, 4, pair_step, 0)
    for copy in later_loads:
        copy.wait()

    def block_copy(slot, i):
        return pltpu.make_async_copy(
            blocks.at[slot], flat.at[pl.ds(JOINT_AT + 3072 * i, 3072)], block_sem.at[slot]
        )

    for i in range(4):
        if i >= 2:
            block_copy(i % 2, i - 2).wait()
        block = tn(normed[:, 256 * i : 256 * i + 256], djoint[...]).astype(bf16)
        blocks[i % 2] = block.reshape(3072, LANES)
        block_copy(i % 2, i).start()
    for i in (2, 3):
        block_copy(i % 2, i).wait()
    start(stage1(0))
    for q in (0, 1, 3, 2):
        start(loads(q))

    dn_own, dn_part = dist.at[pl.ds(0, 512)], dist.at[pl.ds(512, 512)]
    dn_part[...] = nt(djoint[other, :], weight[...])
    dn_swap = pltpu.make_async_remote_copy(
        src_ref=dn_part, dst_ref=dn_rx, send_sem=swap_sem.at[0], recv_sem=swap_sem.at[1],
        device_id=core_near, device_id_type=MESH_ID,
    )
    dn_swap.start()
    pieces.join(6)
    pass_on(6, 0)
    dn_own[...] = nt(djoint[own, :], weight[...])
    bias_sums = nn(jnp.ones((8, TOKENS), bf16), djoint[...])
    half = pl.ds(pl.multiple_of(512 * c, 512), 512)
    small_mine[0] = jnp.zeros(small_mine.shape[1:], f32)
    small_mine[0, 2:3, half] = bias_sums[0:1, :512]
    small_mine[0, 3:4, half] = bias_sums[0:1, 1024:]
    small_mine[0, 4:7, :] = mid_sums[0:3, :]
    small_mine[0, 7:11, half] = expand_sums[...]
    small_mine[0, 11:12, :] = mid_sums[3:4, :]
    pieces.join(5)
    pass_on(6, 1)
    pass_on(5, 0)
    start(stage1(1))
    pieces.join(7)
    pieces.join(4)
    pass_on(5, 1)
    dn_swap.wait()

    def back_rows(i, carry):
        rows = pl.ds(pl.multiple_of(128 * i, 128), 128)
        values = x_own[rows, :].astype(f32)
        center = values - jnp.mean(values, -1, keepdims=True)
        factor = lax.rsqrt(jnp.mean(center * center, -1, keepdims=True) + norm_epsilon)
        unit = center * factor
        dn = dn_own[rows, :] + dn_rx[rows, :]
        e = dn * mid_sums[4:5, :]
        down = dresid[rows, :] + factor * (
            e - jnp.mean(e, -1, keepdims=True) - unit * jnp.mean(e * unit, -1, keepdims=True)
        )
        dinput[rows, :] = down.astype(bf16)
        small_mine[0, 0:1, :] += jnp.sum(dn * unit, 0, keepdims=True)
        small_mine[0, 1:2, :] += jnp.sum(dn, 0, keepdims=True)
        return carry

    lax.fori_loop(0, 4, back_rows, 0)
    small_step(0).start()
    meet(0)
    pass_on(4, 0)
    meet(1)
    pieces.join(0)
    start(stage1(2))
    small_next(0)
    pass_on(7, 0)
    pass_on(0, 0)
    pieces.join(1)
    pass_on(4, 1)
    pass_on(1, 0)
    small_next(1)
    pass_on(6, 2)
    pass_on(0, 1)
    meet(3)
    meet(2)
    small_next(2)
    for d in (1, 2, 3):
        small_hop(d).start()
    pieces.join(3)
    pass_on(3, 0)
    pass_on(7, 1)
    way_in.start()
    pass_on(1, 1)
    finish(5)
    way_out.start()
    pass_on(3, 1)
    finish(6)
    pass_on(0, 2)
    pieces.join(2)
    pass_on(1, 2)
    pass_on(7, 2)
    finish(3)
    pass_on(2, 0)
    finish(7)
    finish(1)
    finish(0)
    pass_on(2, 1)
    finish(4)
    finish(2)
    for d in (1, 2, 3):
        small_hop(d).wait()
    small = (small_mine[3] + small_z[1]) + (small_z[0] + small_z[2])
    small_out[...] = small.reshape(small_out.shape)

    last.wait()
    way_out.wait()
    way_in.wait()
    for q in (0, 1, 2, 3, 5):
        for copy in stage1(q):
            copy.wait_send()
    for q in range(8):
        for copy in pieces.second(q):
            copy.wait_send()
    for (plane, _), queue in on_way.items():
        @pl.when(z == plane)
        def _():
            for sent in queue[-2:]:
                hop(*sent).wait_send()


def rear(
    slopes, joint, attended, dattended, dist, lse, normed, weight, x_own, dresid, result,
    mid_sums, expand_sums, mid_a, mid_b, flat,
):
    f32, bf16 = jnp.float32, jnp.bfloat16
    vmem = pl.BlockSpec(memory_space=pltpu.VMEM)
    hbm = pl.BlockSpec(memory_space=pl.ANY)
    home = jax.ShapeDtypeStruct((2, 256, WIDTH), bf16)
    piece = jax.ShapeDtypeStruct((PIECE, LANES), f32)
    return pl.pallas_call(
        rear_kernel,
        out_shape=(
            jax.ShapeDtypeStruct((FLAT_ROWS, LANES), bf16),
            piece,
            piece,
            jax.ShapeDtypeStruct((LANES, LANES), f32),
            home,
            home,
        ),
        in_specs=[pl.BlockSpec(memory_space=pltpu.SMEM)] + [hbm] * 4 + [vmem] + [hbm] * 5
        + [vmem] * 2 + [hbm] * 3,
        out_specs=[hbm] + [vmem] * 3 + [hbm] * 2,
        scratch_shapes=[
            pltpu.VMEM((TOKENS, 1536), bf16),
            pltpu.VMEM((TOKENS, 512), bf16),
            pltpu.VMEM((TOKENS, 512), bf16),
            pltpu.VMEM((TOKENS, WIDTH), bf16),
            pltpu.VMEM((WIDTH, 1536), bf16),
            pltpu.VMEM((512, WIDTH), bf16),
            pltpu.VMEM((512, WIDTH), f32),
            pltpu.VMEM((TOKENS, TOKENS), f32),
            pltpu.VMEM((TOKENS, 256), bf16),
            pltpu.VMEM((TOKENS, 256), bf16),
            pltpu.VMEM((LANES, TOKENS), bf16),
            pltpu.VMEM((LANES, TOKENS), f32),
            pltpu.VMEM((TOKENS, LANES), f32),
            pltpu.VMEM((TOKENS, LANES), f32),
            pltpu.VMEM((8, TOKENS), f32),
            pltpu.VMEM((TOKENS, 1536), bf16),
            pltpu.VMEM((512, WIDTH), f32),
            pltpu.VMEM((512, WIDTH), bf16),
            pltpu.VMEM((2, 3072, LANES), bf16),
            pltpu.VMEM((4, 2, HALF, LANES), bf16),
            pltpu.VMEM((4, 2, HALF, LANES), bf16),
            pltpu.VMEM((8, 2, HALF, LANES), bf16),
            pltpu.VMEM((8, 2, HALF, LANES), bf16),
            pltpu.VMEM((8, HALF, LANES), bf16),
            pltpu.VMEM((8, HALF, LANES), bf16),
            pltpu.VMEM((8, 2, HALF, LANES), bf16),
            pltpu.VMEM((6, 2, HALF, LANES), bf16),
            pltpu.VMEM((6, 2, HALF, LANES), bf16),
            pltpu.VMEM((PIECE, LANES), f32),
            pltpu.VMEM((4, 16, WIDTH), f32),
            pltpu.VMEM((3, 16, WIDTH), f32),
            pltpu.VMEM((3, 16, WIDTH), f32),
            pltpu.SemaphoreType.DMA((10,)),
            pltpu.SemaphoreType.DMA((2,)),
            pltpu.SemaphoreType.DMA((2,)),
            pltpu.SemaphoreType.DMA((8, 4, 2)),
            pltpu.SemaphoreType.DMA((8, 2, 2)),
            pltpu.SemaphoreType.DMA((8, 2, 2)),
            pltpu.SemaphoreType.DMA((8, 2)),
            pltpu.SemaphoreType.DMA((8, 2)),
            pltpu.SemaphoreType.DMA((8, 2, 2)),
            pltpu.SemaphoreType.DMA((8, 2, 2)),
            pltpu.SemaphoreType.DMA((2,)),
            pltpu.SemaphoreType.DMA((6,)),
            pltpu.SemaphoreType.DMA((6,)),
            pltpu.SemaphoreType.DMA((2,)),
            pltpu.SemaphoreType.DMA((2,)),
            pltpu.SemaphoreType.DMA((2,)),
            pltpu.SemaphoreType.DMA((2,)),
        ],
        input_output_aliases={15: 0},
        compiler_params=pltpu.CompilerParams(
            collective_id=2, has_side_effects=True, vmem_limit_bytes=62 << 20
        ),
        cost_estimate=pl.CostEstimate(flops=30 << 30, bytes_accessed=30 << 20, transcendentals=0),
    )(
        slopes, joint, attended, dattended, dist, lse, normed, weight, x_own, dresid, result,
        mid_sums, expand_sums, mid_a, mid_b, flat,
    )


def middle_kernel(
    attended, x_own, cot, mixer_bias_in, gain_in, shift_in, reduce_bias_in, expand_bias_in, gain_before_in,
    mixer_hbm, expand_hbm, reduce_hbm,
    result, dresid, dattended, sums, expand_sums, flat, rx_a, rx_b,
    vectors, mixer, expand, reduce, att_rx, resid, normal, spread, normed, act, act_rx, dhidden,
    dn_own, dn_part, dn_rx, out_part, out_rx, dbranch, blocks,
    weight_sem, block_sem, send_sem, recv_sem, act_send, act_recv, s1_send, s1_recv,
):
    f32, bf16 = jnp.float32, jnp.bfloat16
    dp = lax.axis_index("dp")
    me = lax.axis_index("group")
    c = dp % 2
    near = (dp + 1 - 2 * c, me)
    own = pl.ds(pl.multiple_of(512 * c, 512), 512)
    other = pl.ds(pl.multiple_of(512 * (1 - c), 512), 512)

    weights = [pltpu.make_async_copy(mixer_hbm, mixer, weight_sem.at[0])]
    for k in range(4):
        part = pl.ds(pl.multiple_of(512 * (2 * k + c), 512), 512)
        weights.append(pltpu.make_async_copy(
            expand_hbm.at[:, part], expand.at[:, pl.ds(512 * k, 512)], weight_sem.at[1 + k]
        ))
    for k in range(4):
        part = pl.ds(pl.multiple_of(512 * (2 * k + c), 512), 512)
        weights.append(pltpu.make_async_copy(
            reduce_hbm.at[part], reduce.at[pl.ds(512 * k, 512)], weight_sem.at[5 + k]
        ))
    for copy in weights:
        copy.start()

    y, x = me // 2, me % 2
    greet([near, (dp, 2 * y + 1 - x), (dp, 2 * (1 - y) + x)])

    def swap(i, src, dst):
        return pltpu.make_async_remote_copy(
            src_ref=src, dst_ref=dst, send_sem=send_sem.at[i], recv_sem=recv_sem.at[i],
            device_id=near, device_id_type=MESH_ID,
        )

    att_swap = swap(0, attended, att_rx)
    normed_swap = swap(1, normed.at[own], normed.at[own])
    dn_swap = swap(2, dn_part, dn_rx)
    out_swap = swap(3, out_part, out_rx)
    branch_swap = swap(4, dbranch.at[own], dbranch.at[own])
    att_swap.start()

    for k, given in enumerate((mixer_bias_in, gain_in, shift_in, reduce_bias_in)):
        vectors[k : k + 1, :] = given[...].astype(f32).reshape(1, WIDTH)
    vectors[4:8, :] = expand_bias_in[...].astype(f32).reshape(4, WIDTH)
    mixer_bias, gain, shift, reduce_bias = (vectors[k : k + 1, :] for k in range(4))

    weights[0].wait()
    resid[...] = nn(attended[own, :], mixer[own, :]) + (x_own[...].astype(f32) + mixer_bias)
    att_swap.wait_recv()
    resid[...] += nn(att_rx[own, :], mixer[other, :])

    def norm_rows(i, carry):
        rows = pl.ds(pl.multiple_of(128 * i, 128), 128)
        here = pl.ds(pl.multiple_of(512 * c + 128 * i, 128), 128)
        values = resid[rows, :]
        center = values - jnp.mean(values, -1, keepdims=True)
        factor = lax.rsqrt(jnp.mean(center * center, -1, keepdims=True) + norm_epsilon)
        unit = center * factor
        normal[rows, :] = unit
        spread[rows, :] = jnp.broadcast_to(factor, (128, LANES))
        normed[here, :] = (unit * gain + shift).astype(bf16)
        return carry

    lax.fori_loop(0, 4, norm_rows, 0)
    normed_swap.start()

    def act_swap(half, k):
        rows = pl.ds(pl.multiple_of(512 * half, 512), 512)
        cols = pl.ds(pl.multiple_of(512 * k, 512), 512)
        return pltpu.make_async_remote_copy(
            src_ref=act.at[rows, cols], dst_ref=act_rx.at[rows, cols],
            send_sem=act_send.at[half, k], recv_sem=act_recv.at[half, k],
            device_id=near, device_id_type=MESH_ID,
        )

    root = math.sqrt(2.0 / math.pi)
    right = pl.ds(pl.multiple_of(512 * c, 512), 512)

    def hidden_block(half, k, first):
        rows = pl.ds(pl.multiple_of(512 * half, 512), 512)
        cols = pl.ds(pl.multiple_of(512 * k, 512), 512)
        u = nn(normed[rows, :], expand[:, cols]) + vectors[pl.ds(4 + k, 1), right]
        dact = nt(cot[rows, :], reduce[cols, :])
        square = u * u
        t = jnp.tanh(u * (root + (root * 0.044715) * square))
        up = 0.5 + 0.5 * t
        act[rows, cols] = (u * up).astype(bf16)
        slope = up + (0.5 * u) * (1.0 - t * t) * (root + (3.0 * root * 0.044715) * square)
        dh = (dact * slope).astype(bf16)
        dhidden[rows, cols] = dh
        total = jnp.sum(dh.astype(f32), 0, keepdims=True)
        if first:
            expand_sums[pl.ds(k, 1), :] = total
        else:
            expand_sums[pl.ds(k, 1), :] += total
        act_swap(half, k).start()

    def out_copies(slot, places):
        return [
            pltpu.make_async_copy(
                blocks.at[slot, pl.ds(2048 * part, 2048)],
                flat.at[pl.ds(pl.multiple_of(at, 16), 2048)], block_sem.at[slot, part],
            )
            for part, at in enumerate(places)
        ]

    def emit(block, slot, places):
        blocks[slot, : 2048 * len(places)] = block.astype(bf16).reshape(2048 * len(places), LANES)
        for copy in out_copies(slot, places):
            copy.start()

    def drain(slot, places):
        for copy in out_copies(slot, places):
            copy.wait()

    for copy in weights[1:]:
        copy.wait()

    def reduce_places(pair, parity):
        return [REDUCE_AT + 2048 * (2 * (2 * pair + k) + parity) for k in range(2)]

    def hidden_pair(pair, carry):
        def mine(k, carry):
            hidden_block(c, 2 * pair + k, True)
            return carry

        def theirs(k, carry):
            hidden_block(1 - c, 2 * pair + k, False)
            return carry

        lax.fori_loop(0, 2, mine, 0)

        @pl.when(pair == 0)
        def _():
            normed_swap.wait_recv()

        lax.fori_loop(0, 2, theirs, 0)
        left = pl.ds(pl.multiple_of(1024 * pair, 1024), 1024)
        block = tn(act[:, left], cot[:, right])

        @pl.when(pair == 1)
        def _():
            drain(0, reduce_places(0, c))

        emit(block, 0, reduce_places(pair, c))
        for half in range(2):
            for k in range(2):
                act_swap(half, 2 * pair + k).wait()
        block = tn(act_rx[:, left], cot[:, right])

        @pl.when(pair == 1)
        def _():
            drain(1, reduce_places(0, 1 - c))

        emit(block, 1, reduce_places(pair, 1 - c))
        return carry

    lax.fori_loop(0, 2, hidden_pair, 0)
    drain(0, reduce_places(1, c))
    drain(1, reduce_places(1, 1 - c))
    stages = [
        first_stage(q, flat, rx_a, rx_b, at, s1_send, s1_recv, dp, me)
        for at, q in enumerate(MIDDLE_EARLY)
    ]
    for copies in stages[:2]:
        for copy in copies:
            copy.start()

    def expand_places(i):
        return [EXPAND_AT + 4096 * i, EXPAND_AT + 4096 * i + 2048]

    def expand_step(i, carry):
        block = tn(normed[:, pl.ds(pl.multiple_of(256 * i, 256), 256)], dhidden[...])

        @pl.when(i >= 2)
        def _():
            drain(i % 2, expand_places(i - 2))

        emit(block, i % 2, expand_places(i))
        return carry

    lax.fori_loop(0, 4, expand_step, 0)
    drain(0, expand_places(2))
    drain(1, expand_places(3))
    for copies in stages[2:]:
        for copy in copies:
            copy.start()

    dn_part[...] = nt(dhidden[other, :], expand[...])
    dn_swap.start()
    out_part[...] = nn(act[other, :], reduce[...]).astype(bf16)
    out_swap.start()

    dn_own[...] = nt(dhidden[own, :], expand[...])
    dn_swap.wait()
    sums[...] = jnp.zeros_like(sums)
    sums[4:5, :] = gain_before_in[...].astype(f32).reshape(1, WIDTH)

    def back_rows(i, carry):
        rows = pl.ds(pl.multiple_of(128 * i, 128), 128)
        here = pl.ds(pl.multiple_of(512 * c + 128 * i, 128), 128)
        dn = dn_own[rows, :] + dn_rx[rows, :]
        unit = normal[rows, :]
        grad = cot[here, :].astype(f32)
        e = dn * gain
        down = grad + spread[rows, 0:1] * (
            e - jnp.mean(e, -1, keepdims=True) - unit * jnp.mean(e * unit, -1, keepdims=True)
        )
        dresid[rows, :] = down
        low = down.astype(bf16)
        dbranch[here, :] = low
        sums[0:1, :] += jnp.sum(low.astype(f32), 0, keepdims=True)
        sums[1:2, :] += jnp.sum(dn * unit, 0, keepdims=True)
        sums[2:3, :] += jnp.sum(dn, 0, keepdims=True)
        sums[3:4, :] += jnp.sum(grad, 0, keepdims=True)
        return carry

    lax.fori_loop(0, 4, back_rows, 0)
    branch_swap.start()
    dattended[own, :] = nt(dbranch[own, :], mixer[own, :]).astype(bf16)
    resid[...] += nn(act[own, :], reduce[...])
    out_swap.wait()
    result[...] = (resid[...] + (out_rx[...].astype(f32) + reduce_bias)).astype(bf16)
    branch_swap.wait()
    dattended[other, :] = nt(dbranch[other, :], mixer[own, :]).astype(bf16)
    emit(tn(attended[...], dbranch[:, right]), 0, [MIXER_AT + 2048 * c])
    emit(tn(att_rx[...], dbranch[:, right]), 1, [MIXER_AT + 2048 * (1 - c)])
    drain(0, [MIXER_AT + 2048 * c])
    drain(1, [MIXER_AT + 2048 * (1 - c)])
    att_swap.wait_send()
    normed_swap.wait_send()
    for copies in stages:
        for copy in copies:
            copy.wait()


def middle(attended, x_own, cot, small, mixer, expand, reduce):
    f32, bf16 = jnp.float32, jnp.bfloat16
    vmem = pl.BlockSpec(memory_space=pltpu.VMEM)
    hbm = pl.BlockSpec(memory_space=pl.ANY)
    count = len(MIDDLE_EARLY)
    early = jax.ShapeDtypeStruct((count, 2, HALF, LANES), bf16)
    return pl.pallas_call(
        middle_kernel,
        out_shape=(
            jax.ShapeDtypeStruct((512, WIDTH), bf16),
            jax.ShapeDtypeStruct((512, WIDTH), f32),
            jax.ShapeDtypeStruct((TOKENS, 512), bf16),
            jax.ShapeDtypeStruct((8, WIDTH), f32),
            jax.ShapeDtypeStruct((4, 512), f32),
            jax.ShapeDtypeStruct((FLAT_ROWS, LANES), bf16),
            early,
            early,
        ),
        in_specs=[vmem] * 9 + [hbm] * 3,
        out_specs=[vmem] * 5 + [hbm] * 3,
        scratch_shapes=[
            pltpu.VMEM((8, WIDTH), f32),
            pltpu.VMEM((WIDTH, WIDTH), bf16),
            pltpu.VMEM((WIDTH, 2048), bf16),
            pltpu.VMEM((2048, WIDTH), bf16),
            pltpu.VMEM((TOKENS, 512), bf16),
            pltpu.VMEM((512, WIDTH), f32),
            pltpu.VMEM((512, WIDTH), f32),
            pltpu.VMEM((512, LANES), f32),
            pltpu.VMEM((TOKENS, WIDTH), bf16),
            pltpu.VMEM((TOKENS, 2048), bf16),
            pltpu.VMEM((TOKENS, 2048), bf16),
            pltpu.VMEM((TOKENS, 2048), bf16),
            pltpu.VMEM((512, WIDTH), f32),
            pltpu.VMEM((512, WIDTH), f32),
            pltpu.VMEM((512, WIDTH), f32),
            pltpu.VMEM((512, WIDTH), bf16),
            pltpu.VMEM((512, WIDTH), bf16),
            pltpu.VMEM((TOKENS, WIDTH), bf16),
            pltpu.VMEM((2, 4096, LANES), bf16),
            pltpu.SemaphoreType.DMA((9,)),
            pltpu.SemaphoreType.DMA((2, 2)),
            pltpu.SemaphoreType.DMA((5,)),
            pltpu.SemaphoreType.DMA((5,)),
            pltpu.SemaphoreType.DMA((2, 4)),
            pltpu.SemaphoreType.DMA((2, 4)),
            pltpu.SemaphoreType.DMA((count, 2, 2)),
            pltpu.SemaphoreType.DMA((count, 2, 2)),
        ],
        compiler_params=pltpu.CompilerParams(
            collective_id=1, has_side_effects=True, vmem_limit_bytes=62 << 20
        ),
        cost_estimate=pl.CostEstimate(flops=30 << 30, bytes_accessed=40 << 20, transcendentals=0),
    )(attended, x_own, cot, *small, mixer, expand, reduce)


UPDATE_ROWS = 616


def owner_table(owners):
    smalls = ((0, 2, 0), (U_JBIAS, U_MIXER, 16), (U_MBIAS, U_EXPAND, 32), (U_EBIAS, U_REDUCE, 56),
              (U_RBIAS, 12300, 88))
    table = []
    for owner in range(owners):
        begin = OWNED_ROWS * owner
        end = begin + OWNED_ROWS
        start = piece_start(owner)
        shift, later = section_shift(begin // 8), section_shift((end - 1) // 8)
        turn = next((8 * u - begin for u in (U_JBIAS, U_MBIAS) if begin < 8 * u < end), OWNED_ROWS)
        row = [begin + 2 * shift - 2 * start, begin + 2 * later - 2 * start, turn, 0, 0, 0, 3 * owner, 0]
        for first, past, at in smalls:
            if 8 * first < end and 8 * past > begin:
                row[3] = at + begin - 8 * first
                row[4] = max(8 * first - begin, 0)
                row[5] = min(8 * past - begin, OWNED_ROWS)
        assert 0 <= row[0] <= row[1] <= 2 * PIECE - 5 * UPDATE_ROWS
        table.append(row)
    return table


def update_kernel(
    table, step_count, learn_rate, master, first, second, own, peer, small, out_hbm, in_hbm,
    new_master, new_first, new_second, small_share, out_copy, in_copy,
    rows, small_rows, held, sem,
):
    f32 = jnp.float32
    i = pl.program_id(0)
    c = lax.axis_index("dp") % 2
    owner = lax.axis_index("dp") * lax.axis_size("group") + lax.axis_index("group")
    place = [table[owner, k] for k in range(7)]
    pairs = ((out_hbm, out_copy), (in_hbm, in_copy))
    fetch = [pltpu.make_async_copy(src, held.at[k], sem.at[k]) for k, (src, _) in enumerate(pairs)]
    give = [pltpu.make_async_copy(held.at[k], dst, sem.at[2 + k]) for k, (_, dst) in enumerate(pairs)]

    @pl.when(i == 0)
    def _():
        for copy in fetch:
            copy.start()
        small_rows[...] = jnp.zeros_like(small_rows)
        small_rows[UPDATE_ROWS : UPDATE_ROWS + LANES, :] = small[...]
        small_share[...] = small_rows[pl.ds(UPDATE_ROWS + place[6], 3), :]

        def weave(k, carry):
            part = pl.ds(pl.multiple_of(112 * k, 16), 112)
            mine, other = own[part, :], peer[part, :]
            even = jnp.where(c == 0, mine, other).reshape(28, 4, LANES)
            odd = jnp.where(c == 0, other, mine).reshape(28, 4, LANES)
            rows[pl.ds(pl.multiple_of(224 * k, 32), 224), :] = jnp.concatenate([even, odd], 1).reshape(
                224, LANES
            )
            return carry

        lax.fori_loop(0, PIECE // 112, weave, 0)

    @pl.when(i == 2)
    def _():
        for copy in fetch:
            copy.wait()
        for copy in give:
            copy.start()

    base = UPDATE_ROWS * i
    k = lax.broadcasted_iota(jnp.int32, (UPDATE_ROWS, LANES), 0) + base
    grad = jnp.where(
        k < place[2],
        rows[pl.ds(place[0] + base, UPDATE_ROWS), :],
        rows[pl.ds(place[1] + base, UPDATE_ROWS), :],
    )
    at = jnp.clip(place[3] + base, -UPDATE_ROWS, LANES) + UPDATE_ROWS
    grad = jnp.where(
        (k >= place[4]) & (k < place[5]), small_rows[pl.ds(at, UPDATE_ROWS), :], grad
    )
    rate = learn_rate[0]
    moment_step = jnp.full((1, LANES), step_count[0].astype(f32))
    fix_one = 1.0 - jnp.exp(moment_step * math.log(beta_first))
    fix_two = 1.0 - jnp.exp(moment_step * math.log(beta_second))
    one = beta_first * first[...] + (1.0 - beta_first) * grad
    two = beta_second * second[...] + (1.0 - beta_second) * grad * grad
    weights = master[...]
    new_first[...] = one
    new_second[...] = two
    new_master[...] = weights - rate * (
        one / fix_one / (jnp.sqrt(two / fix_two) + adam_epsilon) + weight_decay * weights
    )

    @pl.when(i == pl.num_programs(0) - 1)
    def _():
        for copy in give:
            copy.wait()


def update(table, step_count, learn_rate, master, first, second, own, peer, small, output, input_gradient):
    f32 = jnp.float32
    smem = pl.BlockSpec(memory_space=pltpu.SMEM)
    hbm = pl.BlockSpec(memory_space=pl.ANY)
    block = pl.BlockSpec((UPDATE_ROWS, LANES), lambda i: (i, 0))

    def whole(shape):
        return pl.BlockSpec(shape, lambda i: (0, 0))

    flat = jax.ShapeDtypeStruct((OWNED_ROWS, LANES), f32)
    home = jax.ShapeDtypeStruct(output.shape, output.dtype)
    new = pl.pallas_call(
        update_kernel,
        grid=(5,),
        out_shape=(flat, flat, flat, jax.ShapeDtypeStruct((3, LANES), f32), home, home),
        in_specs=[smem, smem, smem] + [block] * 3
        + [whole((PIECE, LANES)), whole((PIECE, LANES)), whole((LANES, LANES))] + [hbm] * 2,
        out_specs=[block] * 3 + [whole((3, LANES))] + [hbm] * 2,
        scratch_shapes=[
            pltpu.VMEM((2 * PIECE, LANES), f32),
            pltpu.VMEM((2 * UPDATE_ROWS + LANES, LANES), f32),
            pltpu.VMEM((2,) + output.shape, output.dtype),
            pltpu.SemaphoreType.DMA((4,)),
        ],
        compiler_params=pltpu.CompilerParams(vmem_limit_bytes=62 << 20),
    )(
        table, step_count, learn_rate, *[whole_array.reshape(OWNED_ROWS, LANES) for whole_array in (master, first, second)],
        own, peer, small, output, input_gradient,
    )
    return [part.reshape(-1) for part in new[:4]] + list(new[4:])


def on_device_chip(
    dp_size, group_size,
    activations, cotangent, segments, padding, step_count, learn_rate,
    gain_before, shift_before, joint_weight, joint_bias, mixer_weight, mixer_bias,
    gain_middle, shift_middle, expand_weight, expand_bias, reduce_weight, reduce_bias,
    master_weights, first_moment, second_moment,
):
    f32, bf16 = jnp.float32, jnp.bfloat16
    dp = lax.axis_index("dp")
    group = lax.axis_index("group")
    c = dp % 2
    slopes = jnp.asarray([2.0 ** (-8.0 * (h + 1) / HEADS) for h in range(HEADS)], f32)
    x_own, cot_all, normed_one, joint, dist, attended, lse = front(
        slopes, activations, cotangent, segments, padding, gain_before, shift_before, joint_bias,
        joint_weight,
    )
    result, dresid, dattended, middle_sums, expand_sums, flat, mid_a, mid_b = middle(
        attended, x_own, cot_all, (mixer_bias, gain_middle, shift_middle, reduce_bias, expand_bias, gain_before),
        mixer_weight, expand_weight, reduce_weight,
    )
    _, own, peer, small_sum, output, input_gradient = rear(
        slopes, joint, attended, dattended, dist, lse, normed_one, joint_weight, x_own, dresid,
        result, middle_sums, expand_sums, mid_a, mid_b, flat,
    )
    table = jnp.asarray(owner_table(dp_size * group_size), jnp.int32)
    new_master, new_first, new_second, small_share, output, input_gradient = update(
        table, step_count, learn_rate, master_weights, first_moment, second_moment, own, peer, small_sum, output,
        input_gradient,
    )
    return (output, input_gradient, new_master, new_first, new_second, small_share)


def on_device(dp_size, group_size, activations, *rest):
    if (dp_size, group_size) == (8, 4) and activations.shape == (2, 256, WIDTH):
        return on_device_chip(dp_size, group_size, activations, *rest)
    return on_device_general(activations, *rest)


def solution(mesh):
    in_specs = (
        P("dp", "group", None),
        P("dp", "group", None),
        P("dp", None),
        P("dp", None),
        P(),
        P(),
        P(),
        P(),
        P(),
        P(),
        P(),
        P(),
        P(),
        P(),
        P(),
        P(),
        P(),
        P(),
        P(("dp", "group")),
        P(("dp", "group")),
        P(("dp", "group")),
    )
    out_specs = (
        P("dp", "group", None),
        P("dp", "group", None),
        P(("dp", "group")),
        P(("dp", "group")),
        P(("dp", "group")),
        P(("dp", "group")),
    )
    return jax.shard_map(
        functools.partial(on_device, mesh.shape["dp"], mesh.shape["group"]), mesh=mesh, in_specs=in_specs, out_specs=out_specs, check_vma=False
    )
```

```python
import functools
import math

import jax
import jax.numpy as jnp
from jax import lax
from jax.experimental import pallas as pl
from jax.experimental.pallas import tpu as pltpu
from jax.sharding import PartitionSpec as P

HEADS = 16
DOC_MOST = 800


beta_first = 0.9
beta_second = 0.95
adam_epsilon = 1e-08
weight_decay = 0.1
norm_epsilon = 1e-05
masked_score = -1e30


def shifted(block, axis, distance):
    devices = range(lax.axis_size(axis))
    route = [(i - distance, i) for i in devices if i - distance in devices]
    return lax.ppermute(block, axis, route)


def standardize(values):
    center = values - jnp.mean(values, -1, keepdims=True)
    spread = lax.rsqrt(jnp.mean(center * center, -1, keepdims=True) + norm_epsilon)
    return (center * spread, spread)


def norm_back(dnormed, normed, spread):
    return spread * (
        dnormed
        - jnp.mean(dnormed, -1, keepdims=True)
        - normed * jnp.mean(dnormed * normed, -1, keepdims=True)
    )


def window_mask(segments, padding, member, hop, block_len):
    places = jnp.arange(block_len, dtype=jnp.int32)
    source = member - hop
    query_place = member * block_len + places
    key_place = source * block_len + places
    start = jnp.maximum(source, 0) * block_len
    seg_query = lax.dynamic_slice_in_dim(segments, member * block_len, block_len, 1)
    seg_key = lax.dynamic_slice_in_dim(segments, start, block_len, 1)
    pad_key = lax.dynamic_slice_in_dim(padding, start, block_len, 1)
    earlier = key_place[None, None, :] <= query_place[None, :, None]
    itself = key_place[None, None, :] == query_place[None, :, None]
    allowed = (
        (seg_query[:, :, None] == seg_key[:, None, :])
        & earlier
        & ((pad_key[:, None, :] == 1) | itself)
        & (source >= 0)
    )
    distance = (query_place[:, None] - key_place[None, :]).astype(jnp.float32)
    return (allowed[:, None], distance)


def piece_scores(query4, key4, slopes, distance, score_scale):
    raw = jnp.einsum("sqhd,skhd->shqk", query4, key4, preferred_element_type=jnp.float32)
    return raw * score_scale - slopes[:, None, None] * distance[None]


def on_device_general(
    activations,
    cotangent,
    segments,
    padding,
    step_count,
    learn_rate,
    gain_before,
    shift_before,
    joint_weight,
    joint_bias,
    mixer_weight,
    mixer_bias,
    gain_middle,
    shift_middle,
    expand_weight,
    expand_bias,
    reduce_weight,
    reduce_bias,
    master_weights,
    first_moment,
    second_moment,
):
    seq_count, block_len, width = activations.shape
    head_size = width // HEADS
    row_count = seq_count * block_len
    shape4 = (seq_count, block_len, HEADS, head_size)
    score_scale = 1.0 / math.sqrt(head_size)
    group_size = lax.axis_size("group")
    member = lax.axis_index("group")
    reach = min((DOC_MOST + block_len - 2) // block_len, group_size - 1)
    slopes = jnp.exp2(-8.0 * (jnp.arange(HEADS, dtype=jnp.float32) + 1.0) / HEADS)
    inputs = activations.reshape(row_count, width).astype(jnp.float32)
    gain_one = gain_before.astype(jnp.float32)
    gain_two = gain_middle.astype(jnp.float32)
    normal_one, spread_one = standardize(inputs)
    normed_one = (normal_one * gain_one + shift_before.astype(jnp.float32)).astype(jnp.bfloat16)
    joint = jnp.dot(normed_one, joint_weight, preferred_element_type=jnp.float32)
    bias_joint = joint_bias.astype(jnp.float32)
    query_rows = (joint[:, :width] + bias_joint[:width]).astype(jnp.bfloat16)
    key_rows = joint[:, width : 2 * width].astype(jnp.bfloat16)
    value_rows = (joint[:, 2 * width :] + bias_joint[width:]).astype(jnp.bfloat16)
    own_piece = jnp.stack([key_rows, value_rows]).reshape(2, seq_count, block_len, width)
    query4 = query_rows.reshape(shape4)
    pieces = [own_piece]
    for hop in range(1, reach + 1):
        pieces.append(shifted(own_piece, "group", hop))
    row_top = jnp.full((seq_count, HEADS, block_len), masked_score, jnp.float32)
    row_total = jnp.zeros((seq_count, HEADS, block_len), jnp.float32)
    for hop in range(reach + 1):
        allowed, distance = window_mask(segments, padding, member, hop, block_len)
        scores = piece_scores(query4, pieces[hop][0].reshape(shape4), slopes, distance, score_scale)
        fresh = jnp.maximum(row_top, jnp.max(jnp.where(allowed, scores, masked_score), -1))
        row_total = row_total * jnp.exp(row_top - fresh) + jnp.sum(
            jnp.exp(jnp.where(allowed, scores - fresh[..., None], masked_score)), -1
        )
        row_top = fresh
    log_total = row_top + jnp.log(row_total)
    attended = jnp.zeros(shape4, jnp.float32)
    for hop in range(reach + 1):
        allowed, distance = window_mask(segments, padding, member, hop, block_len)
        scores = piece_scores(query4, pieces[hop][0].reshape(shape4), slopes, distance, score_scale)
        probs = jnp.exp(jnp.where(allowed, scores - log_total[..., None], masked_score)).astype(
            jnp.bfloat16
        )
        attended = attended + jnp.einsum(
            "shqk,skhd->sqhd",
            probs,
            pieces[hop][1].reshape(shape4),
            preferred_element_type=jnp.float32,
        )
    attended_low = attended.reshape(row_count, width).astype(jnp.bfloat16)
    resid = inputs + (
        jnp.dot(attended_low, mixer_weight, preferred_element_type=jnp.float32)
        + mixer_bias.astype(jnp.float32)
    )
    normal_two, spread_two = standardize(resid)
    normed_two = (normal_two * gain_two + shift_middle.astype(jnp.float32)).astype(jnp.bfloat16)
    hidden = jnp.dot(
        normed_two, expand_weight, preferred_element_type=jnp.float32
    ) + expand_bias.astype(jnp.float32)
    act = jax.nn.gelu(hidden, approximate=True).astype(jnp.bfloat16)
    result = resid + (
        jnp.dot(act, reduce_weight, preferred_element_type=jnp.float32)
        + reduce_bias.astype(jnp.float32)
    )
    output = result.astype(jnp.bfloat16).reshape(seq_count, block_len, width)
    cot_low = cotangent.reshape(row_count, width)
    cot_full = cot_low.astype(jnp.float32)
    reduce_grad = jnp.einsum("tf,td->fd", act, cot_low, preferred_element_type=jnp.float32)
    reduce_bias_grad = jnp.sum(cot_full, 0)
    dact = jnp.einsum("td,fd->tf", cot_low, reduce_weight, preferred_element_type=jnp.float32)
    gelu_pull = jax.vjp(lambda inner: jax.nn.gelu(inner, approximate=True), hidden)[1]
    dhidden = gelu_pull(dact)[0].astype(jnp.bfloat16)
    expand_grad = jnp.einsum("td,tf->df", normed_two, dhidden, preferred_element_type=jnp.float32)
    expand_bias_grad = jnp.sum(dhidden.astype(jnp.float32), 0)
    dnormed_two = jnp.einsum(
        "tf,df->td", dhidden, expand_weight, preferred_element_type=jnp.float32
    )
    gain_middle_grad = jnp.sum(dnormed_two * normal_two, 0)
    shift_middle_grad = jnp.sum(dnormed_two, 0)
    dresid = cot_full + norm_back(dnormed_two * gain_two, normal_two, spread_two)
    dbranch = dresid.astype(jnp.bfloat16)
    mixer_grad = jnp.einsum("td,te->de", attended_low, dbranch, preferred_element_type=jnp.float32)
    mixer_bias_grad = jnp.sum(dbranch.astype(jnp.float32), 0)
    dattended = jnp.einsum(
        "te,de->td", dbranch, mixer_weight, preferred_element_type=jnp.float32
    ).astype(jnp.bfloat16)
    dattended4 = dattended.reshape(shape4)
    row_delta = jnp.einsum("sqhd,sqhd->shq", dattended4.astype(jnp.float32), attended)
    dquery = jnp.zeros(shape4, jnp.float32)
    dkv_own = jnp.zeros((2, seq_count, block_len, width), jnp.float32)
    for hop in range(reach + 1):
        piece = pieces[hop]
        key4 = piece[0].reshape(shape4)
        value4 = piece[1].reshape(shape4)
        allowed, distance = window_mask(segments, padding, member, hop, block_len)
        scores = piece_scores(query4, key4, slopes, distance, score_scale)
        probs = jnp.exp(jnp.where(allowed, scores - log_total[..., None], masked_score))
        dvalue = jnp.einsum(
            "shqk,sqhd->skhd",
            probs.astype(jnp.bfloat16),
            dattended4,
            preferred_element_type=jnp.float32,
        )
        dprobs = jnp.einsum(
            "sqhd,skhd->shqk", dattended4, value4, preferred_element_type=jnp.float32
        )
        dscores = (probs * (dprobs - row_delta[..., None])).astype(jnp.bfloat16)
        dquery = dquery + jnp.einsum(
            "shqk,skhd->sqhd", dscores, key4, preferred_element_type=jnp.float32
        )
        dkey = (
            jnp.einsum("shqk,sqhd->skhd", dscores, query4, preferred_element_type=jnp.float32)
            * score_scale
        )
        returned = jnp.stack([dkey, dvalue]).reshape(2, seq_count, block_len, width)
        if hop == 0:
            dkv_own = returned
        else:
            dkv_own = dkv_own + shifted(returned.astype(jnp.bfloat16), "group", -hop).astype(
                returned.dtype
            )
    dquery_low = (dquery * score_scale).reshape(row_count, width).astype(jnp.bfloat16)
    dkey_low = dkv_own[0].reshape(row_count, width).astype(jnp.bfloat16)
    dvalue_low = dkv_own[1].reshape(row_count, width).astype(jnp.bfloat16)
    djoint = jnp.concatenate([dquery_low, dkey_low, dvalue_low], 1)
    joint_grad = jnp.einsum("td,te->de", normed_one, djoint, preferred_element_type=jnp.float32)
    joint_bias_grad = jnp.concatenate(
        [jnp.sum(dquery_low.astype(jnp.float32), 0), jnp.sum(dvalue_low.astype(jnp.float32), 0)]
    )
    dnormed_one = jnp.einsum("te,de->td", djoint, joint_weight, preferred_element_type=jnp.float32)
    gain_before_grad = jnp.sum(dnormed_one * normal_one, 0)
    shift_before_grad = jnp.sum(dnormed_one, 0)
    dinput = dresid + norm_back(dnormed_one * gain_one, normal_one, spread_one)
    input_gradient = dinput.astype(jnp.bfloat16).reshape(seq_count, block_len, width)
    listing = [
        gain_before_grad,
        shift_before_grad,
        joint_grad,
        joint_bias_grad,
        mixer_grad,
        mixer_bias_grad,
        gain_middle_grad,
        shift_middle_grad,
        expand_grad,
        expand_bias_grad,
        reduce_grad,
        reduce_bias_grad,
    ]
    gradient = jnp.concatenate([single.reshape(-1) for single in listing])
    small_list = [
        gain_before_grad,
        shift_before_grad,
        joint_bias_grad,
        mixer_bias_grad,
        gain_middle_grad,
        shift_middle_grad,
        expand_bias_grad,
        reduce_bias_grad,
    ]
    small_local = jnp.concatenate(small_list)
    share, small_share = (
        lax.psum_scatter(gradient, ("dp", "group"), scatter_dimension=0, tiled=True),
        lax.psum_scatter(small_local, ("dp", "group"), scatter_dimension=0, tiled=True),
    )
    moment_step = step_count[0].astype(jnp.float32)
    rate = learn_rate[0]
    fix_one = 1.0 - jnp.exp(moment_step * math.log(beta_first))
    fix_two = 1.0 - jnp.exp(moment_step * math.log(beta_second))
    updated_first = beta_first * first_moment + (1.0 - beta_first) * share
    updated_second = beta_second * second_moment + (1.0 - beta_second) * share * share
    updated_master = master_weights - rate * (
        updated_first / fix_one / (jnp.sqrt(updated_second / fix_two) + adam_epsilon)
        + weight_decay * master_weights
    )
    return (output, input_gradient, updated_master, updated_first, updated_second, small_share)


WIDTH = 1024
HIDDEN = 4096
TOKENS = 1024
LANES = 128
OWNED = 393600
OWNED_ROWS = OWNED // LANES
PIECE = 1568
HALF = PIECE // 2
JOINT_AT, MIXER_AT, EXPAND_AT, REDUCE_AT = 16, 12320, 16432, 32832
FLAT_ROWS = 49248
U_JOINT, U_JBIAS, U_MIXER, U_MBIAS, U_EXPAND, U_EBIAS, U_REDUCE, U_RBIAS = (
    2, 3074, 3076, 4100, 4103, 8199, 8203, 12299,
)


def section_shift(unit):
    return 8 if unit < U_JBIAS else 16 if unit < U_MBIAS else 20


def piece_start(owner):
    unit = OWNED_ROWS * owner // 8
    return (4 * unit + section_shift(unit)) // 16 * 16


def piece_offset(q, y, x):
    at = [piece_start(4 * q + k) // 16 for k in range(4)]
    row = (
        at[0] * (1 - y) * (1 - x) + at[1] * (1 - y) * x + at[2] * y * (1 - x) + at[3] * y * x
    )
    return pl.multiple_of(row * 16, 16)


MESH_ID = pl.DeviceIdType.MESH


def by_rows(step):
    def one(i, carry):
        step(pl.ds(pl.multiple_of(112 * i, 16), 112))
        return carry

    lax.fori_loop(0, HALF // 112, one, 0)


class Pieces:
    def __init__(self, dp, me, flat, own_a, own_b, rx_a1, rx_b1, rx_a2, rx_b2, acc, load_sem, s2_send, s2_recv):
        self.y, self.x = me // 2, me % 2
        self.x_near = (dp, 2 * self.y + (1 - self.x))
        self.y_near = (dp, 2 * (1 - self.y) + self.x)
        self.flat, self.own_a, self.own_b = flat, own_a, own_b
        self.rx_a1, self.rx_b1, self.rx_a2, self.rx_b2, self.acc = rx_a1, rx_b1, rx_a2, rx_b2, acc
        self.load_sem, self.s2_send, self.s2_recv = load_sem, s2_send, s2_recv

    def loads(self, q, own_slot, ready=None):
        slot = q
        out = []
        for k in range(2):
            for way, (row, own) in enumerate((
                (piece_offset(q, k, self.x), self.own_a),
                (piece_offset(q, self.y, k) + HALF, self.own_b),
            )):
                out.append(pltpu.make_async_copy(
                    self.flat.at[pl.ds(row, HALF)], own.at[own_slot, k], self.load_sem.at[slot, way, k]
                ))
            if ready is not None:
                ready_a, ready_b, at = ready
                for way, (src, dst) in enumerate(((ready_a, self.rx_a1), (ready_b, self.rx_b1))):
                    out.append(pltpu.make_async_copy(
                        src.at[at, k], dst.at[slot, k], self.load_sem.at[slot, 2 + way, k]
                    ))
        return out

    def second(self, slot):
        y, x = self.y, self.x
        return [
            pltpu.make_async_remote_copy(
                src_ref=src, dst_ref=dst.at[slot], send_sem=self.s2_send.at[slot, way],
                recv_sem=self.s2_recv.at[slot, way], device_id=near, device_id_type=MESH_ID,
            )
            for way, (src, dst, near) in enumerate((
                (self.rx_a1.at[slot, 1 - y], self.rx_a2, self.y_near),
                (self.rx_b1.at[slot, 1 - x], self.rx_b2, self.x_near),
            ))
        ]

    def meet(self, slot, own_slot):
        y, x = self.y, self.x
        rx_a1, rx_b1, own_a, own_b, acc = self.rx_a1, self.rx_b1, self.own_a, self.own_b, self.acc

        def away(rows):
            rx_a1[slot, 1 - y, rows] = rx_a1[slot, 1 - y, rows] + own_a[own_slot, 1 - y, rows]
            rx_b1[slot, 1 - x, rows] = rx_b1[slot, 1 - x, rows] + own_b[own_slot, 1 - x, rows]

        by_rows(away)
        for copy in self.second(slot):
            copy.start()

        def kept(rows):
            acc[slot, 0, rows] = rx_a1[slot, y, rows] + own_a[own_slot, y, rows]
            acc[slot, 1, rows] = rx_b1[slot, x, rows] + own_b[own_slot, x, rows]

        by_rows(kept)

    def join(self, slot):
        for copy in self.second(slot):
            copy.wait_recv()
        acc, rx_a2, rx_b2 = self.acc, self.rx_a2, self.rx_b2

        def add(rows):
            acc[slot, 0, rows] = acc[slot, 0, rows] + rx_a2[slot, rows]
            acc[slot, 1, rows] = acc[slot, 1, rows] + rx_b2[slot, rows]

        by_rows(add)


MIDDLE_EARLY = (6, 7, 4)


def nn(a, b):
    return lax.dot_general(a, b, (((1,), (0,)), ((), ())), preferred_element_type=jnp.float32)


def nt(a, b):
    return lax.dot_general(a, b, (((1,), (1,)), ((), ())), preferred_element_type=jnp.float32)


def tn(a, b):
    return lax.dot_general(a, b, (((0,), (0,)), ((), ())), preferred_element_type=jnp.float32)


def head_lanes(value, h):
    lane = lax.broadcasted_iota(jnp.int32, (1, LANES), 1)
    return jnp.where(lane // 64 == h, value, jnp.zeros_like(value))


def plane_devices(dp, me):
    z, c = dp // 2, dp % 2
    near = [(2 * z + 1 - c, me)]
    for d in (1, 2, 3):
        near += [(2 * z, (me + d) % 4), (2 * z + 1, (me + d) % 4)]
    return near


def greet(devices):
    barrier = pltpu.get_barrier_semaphore()
    for near in devices:
        pl.semaphore_signal(barrier, inc=1, device_id=near, device_id_type=MESH_ID)
    pl.semaphore_wait(barrier, len(devices))


class Home:
    def __init__(self, rows, out, dp, me, send_sem, recv_sem):
        z, c = dp // 2, dp % 2
        self.here = c == me // 2
        self.turns = []
        for turn in range(2):
            src = rows.at[pl.ds(256 * turn, 256)]
            dst = out.at[me % 2]
            away = pltpu.make_async_remote_copy(
                src_ref=src, dst_ref=dst, send_sem=send_sem.at[turn], recv_sem=recv_sem.at[me % 2],
                device_id=(2 * z + me // 2, 2 * c + turn), device_id_type=MESH_ID,
            )
            near = pltpu.make_async_copy(src, dst, send_sem.at[turn])
            came = pltpu.make_async_remote_copy(
                src_ref=src, dst_ref=out.at[turn], send_sem=send_sem.at[turn],
                recv_sem=recv_sem.at[turn], device_id=(2 * z + me // 2, 2 * c + turn),
                device_id_type=MESH_ID,
            )
            self.turns.append((away, near, came, self.here & (me % 2 == turn)))

    def start(self):
        for away, near, _, stays in self.turns:
            @pl.when(stays)
            def _():
                near.start()

            @pl.when(jnp.logical_not(stays))
            def _():
                away.start()

    def wait(self):
        for away, near, came, stays in self.turns:
            @pl.when(stays)
            def _():
                near.wait()

            @pl.when(jnp.logical_not(stays))
            def _():
                away.wait_send()
                came.wait_recv()


def first_stage(q, flat, rx_a, rx_b, at, send_sem, recv_sem, dp, me):
    y, x = me // 2, me % 2
    x_near = (dp, 2 * y + (1 - x))
    y_near = (dp, 2 * (1 - y) + x)
    out = []
    for k in range(2):
        for way, (row, rx, near) in enumerate((
            (piece_offset(q, k, 1 - x), rx_a, x_near),
            (piece_offset(q, 1 - y, k) + HALF, rx_b, y_near),
        )):
            out.append(pltpu.make_async_remote_copy(
                src_ref=flat.at[pl.ds(row, HALF)], dst_ref=rx.at[at, k],
                send_sem=send_sem.at[at, way, k], recv_sem=recv_sem.at[at, way, k],
                device_id=near, device_id_type=MESH_ID,
            ))
    return out


def both_heads(value):
    return jnp.concatenate([head_lanes(value, 0), head_lanes(value, 1)], 0)


class Spread:
    def __init__(self, blocks, rows, dp, me, send_sem, recv_sem):
        z, c = dp // 2, dp % 2
        here = c == me // 2
        self.turns = []
        for turn in range(2):
            src = blocks.at[turn]
            dst = rows.at[pl.ds(pl.multiple_of(256 * me, 256), 256)]
            away = pltpu.make_async_remote_copy(
                src_ref=src, dst_ref=dst, send_sem=send_sem.at[turn], recv_sem=recv_sem.at[me % 2],
                device_id=(2 * z + me // 2, 2 * c + turn), device_id_type=MESH_ID,
            )
            near = pltpu.make_async_copy(src, dst, send_sem.at[turn])
            came = pltpu.make_async_remote_copy(
                src_ref=src, dst_ref=rows.at[pl.ds(pl.multiple_of(512 * c + 256 * turn, 256), 256)],
                send_sem=send_sem.at[turn], recv_sem=recv_sem.at[turn],
                device_id=(2 * z + me // 2, 2 * c + turn), device_id_type=MESH_ID,
            )
            self.turns.append((away, near, came, here & (me % 2 == turn)))

    def start(self):
        for away, near, _, stays in self.turns:
            @pl.when(stays)
            def _():
                near.start()

            @pl.when(jnp.logical_not(stays))
            def _():
                away.start()

    def wait_came(self, turn):
        _, near, came, stays = self.turns[turn]

        @pl.when(stays)
        def _():
            near.wait()

        @pl.when(jnp.logical_not(stays))
        def _():
            came.wait_recv()

    def wait_sent(self):
        for away, _, _, stays in self.turns:
            @pl.when(jnp.logical_not(stays))
            def _():
                away.wait_send()


def front_kernel(
    slopes, blocks, cot_blocks, segments, padding, gain_in, shift_in, bias_in, weight_hbm,
    x_out, cot_out, normed_out, joint_out, dist_out, att_out, lse_out,
    x_all, cot_all, normed, joint, weight, dist, att, lse, seg_rx, pad_rx, vectors, columns, s_ref, p_ref, vt_ref, ot_ref,
    weight_sem, out_sem, mark_sem, x_send, x_recv, cot_send, cot_recv, pass_send, pass_recv,
):
    f32, bf16 = jnp.float32, jnp.bfloat16
    dp = lax.axis_index("dp")
    me = lax.axis_index("group")
    c = dp % 2
    core_near = (dp + 1 - 2 * c, me)
    own = pl.ds(pl.multiple_of(512 * c, 512), 512)
    other = pl.ds(pl.multiple_of(512 * (1 - c), 512), 512)

    weights = [
        pltpu.make_async_copy(
            weight_hbm.at[:, pl.ds(pl.multiple_of(1024 * p + 512 * c, 512), 512)],
            weight.at[:, pl.ds(512 * p, 512)], weight_sem.at[p],
        )
        for p in range(3)
    ]
    greet(plane_devices(dp, me))
    x_way = Spread(blocks, x_all, dp, me, x_send, x_recv)
    cot_way = Spread(cot_blocks, cot_all, dp, me, cot_send, cot_recv)
    x_way.start()
    vectors[0:1, :] = gain_in[...].astype(f32).reshape(1, WIDTH)
    vectors[1:2, :] = shift_in[...].astype(f32).reshape(1, WIDTH)
    vectors[2:4, :] = bias_in[...].astype(f32).reshape(2, WIDTH)
    mark_swaps = [
        pltpu.make_async_remote_copy(
            src_ref=src, dst_ref=dst, send_sem=mark_sem.at[0, i], recv_sem=mark_sem.at[1, i],
            device_id=core_near, device_id_type=MESH_ID,
        )
        for i, (src, dst) in enumerate(((segments, seg_rx), (padding, pad_rx)))
    ]
    for copy in mark_swaps:
        copy.start()
    for copy in weights:
        copy.start()

    def hand_over(rows, way, turn):
        at = pl.ds(pl.multiple_of(512 * c + 256 * turn, 256), 256)
        return pltpu.make_async_remote_copy(
            src_ref=rows.at[at], dst_ref=rows.at[at], send_sem=pass_send.at[way, turn],
            recv_sem=pass_recv.at[way, turn], device_id=core_near, device_id_type=MESH_ID,
        )

    for copy in mark_swaps:
        copy.wait()
    odd = me % 2 == 1
    held = c == me // 2

    def row_of(mine, came):
        both = jnp.where(held, mine[...], came[...]).astype(f32)
        return jnp.where(odd, both[1:2], both[0:1])

    seg = row_of(segments, seg_rx)
    pad = row_of(padding, pad_rx)
    kind = lax.broadcasted_iota(jnp.int32, (8, TOKENS), 0)
    columns[...] = jnp.broadcast_to(
        jnp.where(kind == 0, seg, pad).T[:, :8].reshape(TOKENS, 8), (TOKENS, 8)
    )

    def dist_rows(i, carry):
        rows = pl.ds(pl.multiple_of(128 * i, 128), 128)
        key_seg, key_pad = columns[rows, 0:1], columns[rows, 1:2]
        key = (lax.broadcasted_iota(jnp.int32, (128, 1), 0) + 128 * i).astype(f32)
        query = lax.broadcasted_iota(jnp.int32, (128, TOKENS), 1).astype(f32)
        last = jnp.sum(jnp.where(seg <= key_seg, 1.0, 0.0), 1, keepdims=True) - 1.0
        last = jnp.where(key_pad == 1.0, last, key)
        dist[rows, :] = jnp.where((query >= key) & (query <= last), query - key, -masked_score)
        return carry

    lax.fori_loop(0, 8, dist_rows, 0)
    outs = []

    def put(src, dst):
        copy = pltpu.make_async_copy(src, dst, out_sem.at[len(outs)])
        copy.start()
        outs.append(copy)

    put(dist, dist_out)
    gain, shift = vectors[0:1, :], vectors[1:2, :]

    def norm_rows(half):
        def one(i, carry):
            rows = pl.ds(pl.multiple_of(512 * half + 128 * i, 128), 128)
            values = x_all[rows, :].astype(f32)
            center = values - jnp.mean(values, -1, keepdims=True)
            factor = lax.rsqrt(jnp.mean(center * center, -1, keepdims=True) + norm_epsilon)
            normed[rows, :] = (center * factor * gain + shift).astype(bf16)
            return carry

        lax.fori_loop(0, 4, one, 0)
        rows = pl.ds(pl.multiple_of(512 * half, 512), 512)
        lanes = pl.ds(pl.multiple_of(512 * c, 512), 512)
        made = nn(normed[rows, :], weight[...])
        joint[rows, 0:512] = ((made[:, 0:512] + vectors[2:3, lanes]) * 0.125).astype(bf16)
        joint[rows, 512:1024] = made[:, 512:1024].astype(bf16)
        joint[rows, 1024:1536] = (made[:, 1024:1536] + vectors[3:4, lanes]).astype(bf16)

    for turn in range(2):
        x_way.wait_came(turn)
        hand_over(x_all, 0, turn).start()
    x_way.wait_sent()
    cot_way.start()
    put(x_all.at[own], x_out)
    for copy in weights:
        copy.wait()
    norm_rows(c)
    for turn in range(2):
        hand_over(x_all, 0, turn).wait_recv()
    norm_rows(1 - c)
    put(normed, normed_out)
    put(joint, joint_out)

    def pair_step(pair, carry):
        def lanes(block):
            return pl.ds(pl.multiple_of(512 * block + LANES * pair, LANES), LANES)

        vt_ref[...] = joint[:, lanes(2)].astype(f32).T.astype(bf16)
        slope = [slopes[8 * c + 2 * pair + h] for h in range(2)]

        def scores(qb):
            cols = pl.ds(qb * 256, 256)
            queries = both_heads(joint[cols, lanes(0)])
            top = None
            for kb in range(qb + 1):
                rows = pl.ds(kb * 256, 256)
                raw = nt(joint[rows, lanes(1)], queries)
                far = dist[rows, cols]
                parts = [raw[:, 256 * h : 256 * h + 256] - slope[h] * far for h in range(2)]
                for h in range(2):
                    s_ref[qb % 2, rows, 256 * h : 256 * h + 256] = parts[h]
                high = jnp.concatenate([jnp.max(part, 0, keepdims=True) for part in parts], 1)
                top = high if top is None else jnp.maximum(top, high)
            return top

        def weigh(qb, top):
            cols = pl.ds(qb * 256, 256)
            span = pl.ds(0, 256 * (qb + 1))
            total = None
            for kb in range(qb + 1):
                rows = pl.ds(kb * 256, 256)
                p = jnp.exp(s_ref[qb % 2, rows, :] - top)
                more = jnp.sum(p, 0, keepdims=True)
                total = more if total is None else total + more
                p_ref[qb % 2, rows, :] = p.astype(bf16)
            out = nn(vt_ref[:, span], p_ref[qb % 2, span, :]) / total
            ot_ref[0:64, cols] = out[0:64, 0:256]
            ot_ref[64:128, cols] = out[64:128, 256:512]
            row = top + jnp.log(total)
            for h in range(2):
                lse[pair, h : h + 1, cols] = row[:, 256 * h : 256 * h + 256]

        top = scores(0)
        for qb in range(4):
            after = scores(qb + 1) if qb < 3 else None
            weigh(qb, top)
            top = after
        att[:, lanes(0)] = ot_ref[...].T.astype(bf16)

        @pl.when(pair == 2)
        def _():
            for turn in range(2):
                cot_way.wait_came(turn)
                hand_over(cot_all, 1, turn).start()

        return carry

    lax.fori_loop(0, 4, pair_step, 0)
    put(att, att_out)
    put(lse, lse_out)
    for turn in range(2):
        hand_over(cot_all, 1, turn).wait()
        hand_over(x_all, 0, turn).wait_send()
    put(cot_all, cot_out)
    cot_way.wait_sent()
    for copy in outs:
        copy.wait()


def front(slopes, blocks, cot_blocks, segments, padding, gain, shift, bias, weight):
    f32, bf16 = jnp.float32, jnp.bfloat16
    vmem = pl.BlockSpec(memory_space=pltpu.VMEM)
    hbm = pl.BlockSpec(memory_space=pl.ANY)
    return pl.pallas_call(
        front_kernel,
        out_shape=(
            jax.ShapeDtypeStruct((512, WIDTH), bf16),
            jax.ShapeDtypeStruct((TOKENS, WIDTH), bf16),
            jax.ShapeDtypeStruct((TOKENS, WIDTH), bf16),
            jax.ShapeDtypeStruct((TOKENS, 1536), bf16),
            jax.ShapeDtypeStruct((TOKENS, TOKENS), f32),
            jax.ShapeDtypeStruct((TOKENS, 512), bf16),
            jax.ShapeDtypeStruct((4, 2, TOKENS), f32),
        ),
        in_specs=[pl.BlockSpec(memory_space=pltpu.SMEM)] + [hbm] * 2 + [vmem] * 5 + [hbm],
        out_specs=[hbm] * 7,
        scratch_shapes=[
            pltpu.VMEM((TOKENS, WIDTH), bf16),
            pltpu.VMEM((TOKENS, WIDTH), bf16),
            pltpu.VMEM((TOKENS, WIDTH), bf16),
            pltpu.VMEM((TOKENS, 1536), bf16),
            pltpu.VMEM((WIDTH, 1536), bf16),
            pltpu.VMEM((TOKENS, TOKENS), f32),
            pltpu.VMEM((TOKENS, 512), bf16),
            pltpu.VMEM((4, 2, TOKENS), f32),
            pltpu.VMEM((2, TOKENS), jnp.int32),
            pltpu.VMEM((2, TOKENS), jnp.int32),
            pltpu.VMEM((8, WIDTH), f32),
            pltpu.VMEM((TOKENS, 8), f32),
            pltpu.VMEM((2, TOKENS, 512), f32),
            pltpu.VMEM((2, TOKENS, 512), bf16),
            pltpu.VMEM((LANES, TOKENS), bf16),
            pltpu.VMEM((LANES, TOKENS), f32),
            pltpu.SemaphoreType.DMA((3,)),
            pltpu.SemaphoreType.DMA((7,)),
            pltpu.SemaphoreType.DMA((2, 2)),
            pltpu.SemaphoreType.DMA((2,)),
            pltpu.SemaphoreType.DMA((2,)),
            pltpu.SemaphoreType.DMA((2,)),
            pltpu.SemaphoreType.DMA((2,)),
            pltpu.SemaphoreType.DMA((2, 2)),
            pltpu.SemaphoreType.DMA((2, 2)),
        ],
        compiler_params=pltpu.CompilerParams(
            collective_id=0, has_side_effects=True, vmem_limit_bytes=62 << 20
        ),
        cost_estimate=pl.CostEstimate(flops=10 << 30, bytes_accessed=20 << 20, transcendentals=0),
    )(slopes, blocks, cot_blocks, segments, padding, gain, shift, bias, weight)


def rear_kernel(
    slopes, joint_hbm, att_hbm, datt_hbm, dist_hbm, lse, normed_hbm, weight_hbm, x_hbm, dresid_hbm,
    result, mid_sums, expand_sums, mid_a, mid_b, flat_in,
    flat, own_out, peer_out, small_out, output, input_gradient,
    joint, attended, dattended, normed, weight, x_own, dresid,
    dist, p_ref, ds_ref, kt_ref, dqt_ref, dk_acc, dv_acc, delta_ref, djoint, dn_rx, dinput, blocks,
    own_a, own_b, rx_a1, rx_b1, rx_a2, rx_b2, acc, rx_up, rx_dn, parting,
    small_mine, small_rx, small_z,
    dist_sem, block_sem, swap_sem, load_sem, s1_send, s1_recv, s2_send, s2_recv, z_send, z_recv,
    last_sem, sm_send, sm_recv, out_send, out_recv, in_send, in_recv,
):
    f32, bf16 = jnp.float32, jnp.bfloat16
    dp = lax.axis_index("dp")
    me = lax.axis_index("group")
    z, c = dp // 2, dp % 2
    y, x = me // 2, me % 2
    x_near = (dp, 2 * y + (1 - x))
    y_near = (dp, 2 * (1 - y) + x)
    core_near = (2 * z + 1 - c, me)
    own = pl.ds(pl.multiple_of(512 * c, 512), 512)
    other = pl.ds(pl.multiple_of(512 * (1 - c), 512), 512)

    def z_at(d):
        return (2 * d + c, me)

    pieces = Pieces(
        dp, me, flat, own_a, own_b, rx_a1, rx_b1, rx_a2, rx_b2, acc, load_sem, s2_send, s2_recv
    )
    own_slot = {6: 0, 7: 1, 4: 2, 5: 3, 0: 0, 1: 1, 3: 2, 2: 3}

    def loads(q):
        ready = (mid_a, mid_b, MIDDLE_EARLY.index(q)) if q in MIDDLE_EARLY else None
        return pieces.loads(q, own_slot[q], ready)

    def start(copies):
        for copy in copies:
            copy.start()

    def stage1(q):
        return first_stage(q, flat, rx_a1, rx_b1, q, s1_send, s1_recv, dp, me)

    def hop(q, up, half):
        way = 0 if up else 1
        return pltpu.make_async_remote_copy(
            src_ref=acc.at[q, half], dst_ref=rx_up.at[q - 2, half] if up else rx_dn.at[q, half],
            send_sem=z_send.at[q, way, half], recv_sem=z_recv.at[q, way, half],
            device_id=z_at((z + 1) % 4 if up else (z + 3) % 4), device_id_type=MESH_ID,
        )

    def meet(q):
        for copy in loads(q):
            copy.wait()
        if q not in MIDDLE_EARLY:
            for copy in stage1(q):
                copy.wait_recv()
        pieces.meet(q, own_slot[q])

    def add_came(q, rx, at, half):
        def add(rows):
            acc[q, half, rows] = acc[q, half, rows] + rx[at, half, rows]

        by_rows(add)

    on_way = {(plane, up): [] for plane in range(4) for up in (False, True)}

    def send_on(plane, q, up, half):
        queue = on_way[plane, up]
        if len(queue) >= 2:
            hop(*queue[-2]).wait_send()
        hop(q, up, half).start()
        queue.append((q, up, half))

    def pass_on(q, h):
        aim = q // 2
        if h < aim:
            @pl.when(z == h)
            def _():
                for half in range(2):
                    if h > 0:
                        hop(q, True, half).wait_recv()
                        add_came(q, rx_up, q - 2, half)
                    send_on(h, q, True, half)
        if h < 3 - aim:
            @pl.when(z == 3 - h)
            def _():
                for half in range(2):
                    if h > 0:
                        hop(q, False, half).wait_recv()
                        add_came(q, rx_dn, q, half)
                    send_on(3 - h, q, False, half)

    last = pltpu.make_async_remote_copy(
        src_ref=parting, dst_ref=peer_out, send_sem=last_sem.at[0], recv_sem=last_sem.at[1],
        device_id=core_near, device_id_type=MESH_ID,
    )

    def finish(q):
        aim = q // 2

        @pl.when(z == aim)
        def _():
            mine = c == q % 2
            for k in range(2):
                if aim > 0:
                    hop(q, True, k).wait_recv()
                if aim < 3:
                    hop(q, False, k).wait_recv()

                def add(i, carry):
                    rows = pl.ds(pl.multiple_of(112 * i, 16), 112)
                    place = pl.ds(pl.multiple_of(HALF * k + 112 * i, 16), 112)
                    total = acc[q, k, rows].astype(f32)
                    if aim > 0:
                        total = total + rx_up[q - 2, k, rows].astype(f32)
                    if aim < 3:
                        total = total + rx_dn[q, k, rows].astype(f32)

                    @pl.when(mine)
                    def _():
                        own_out[place] = total

                    @pl.when(jnp.logical_not(mine))
                    def _():
                        parting[place] = total

                    return carry

                lax.fori_loop(0, HALF // 112, add, 0)

            @pl.when(jnp.logical_not(mine))
            def _():
                last.start()

    def small_step(k):
        near = (core_near, x_near, y_near)[k]
        return pltpu.make_async_remote_copy(
            src_ref=small_mine.at[k], dst_ref=small_rx.at[k], send_sem=sm_send.at[k],
            recv_sem=sm_recv.at[k], device_id=near, device_id_type=MESH_ID,
        )

    def small_next(k):
        small_step(k).wait()
        small_mine[k + 1] = small_mine[k] + small_rx[k]
        if k < 2:
            small_step(k + 1).start()

    def small_hop(d):
        return pltpu.make_async_remote_copy(
            src_ref=small_mine.at[3], dst_ref=small_z.at[d - 1], send_sem=sm_send.at[2 + d],
            recv_sem=sm_recv.at[2 + d], device_id=z_at((z + d) % 4), device_id_type=MESH_ID,
        )

    def load(i, src, dst):
        return pltpu.make_async_copy(src, dst, dist_sem.at[i])

    first_loads = [
        load(0, joint_hbm, joint), load(1, att_hbm, attended), load(2, datt_hbm, dattended),
        load(3, dist_hbm, dist),
    ]
    later_loads = [load(4, normed_hbm, normed), load(5, x_hbm, x_own), load(6, dresid_hbm, dresid)]
    for p in range(3):
        later_loads.append(load(
            7 + p, weight_hbm.at[:, pl.ds(pl.multiple_of(1024 * p + 512 * c, 512), 512)],
            weight.at[:, pl.ds(512 * p, 512)],
        ))
    start(first_loads)
    for q in (7, 6, 4):
        start(loads(q))
    greet(plane_devices(dp, me) + [z_at((z + d) % 4) for d in (1, 2, 3)])
    way_out = Home(result, output, dp, me, out_send, out_recv)
    way_in = Home(dinput, input_gradient, dp, me, in_send, in_recv)
    start(stage1(5))
    start(stage1(3))

    def go_on(pair):
        @pl.when(pair == 0)
        def _():
            start(loads(5))
            start(later_loads)

        @pl.when(pair == 1)
        def _():
            meet(7)

        @pl.when(pair == 2)
        def _():
            for q in (6, 4, 5):
                meet(q)

    for copy in first_loads:
        copy.wait()

    def pair_step(pair, carry):
        def lanes(block):
            return pl.ds(pl.multiple_of(512 * block + LANES * pair, LANES), LANES)

        here = lanes(0)
        kt_ref[...] = joint[:, lanes(1)].astype(f32).T.astype(bf16)
        product = (attended[:, here].astype(f32) * dattended[:, here].astype(f32)).T
        delta_ref[0:1, :] = jnp.sum(product[:64], 0, keepdims=True)
        delta_ref[1:2, :] = jnp.sum(product[64:], 0, keepdims=True)
        dk_acc[...] = jnp.zeros_like(dk_acc)
        dv_acc[...] = jnp.zeros_like(dv_acc)
        slope = [slopes[8 * c + 2 * pair + h] for h in range(2)]

        def pairs_of(qb):
            cols = pl.ds(qb * 256, 256)
            queries = both_heads(joint[cols, here])
            grads = both_heads(dattended[cols, here])
            for kb in range(qb + 1):
                rows = pl.ds(kb * 256, 256)
                raw = nt(joint[rows, lanes(1)], queries)
                dprobs = nt(joint[rows, lanes(2)], grads)
                far = dist[rows, cols]
                for h in range(2):
                    side = slice(256 * h, 256 * h + 256)
                    p = jnp.exp(raw[:, side] - slope[h] * far - lse[pair, h : h + 1, cols])
                    p_ref[qb % 2, rows, side] = p.astype(bf16)
                    ds_ref[qb % 2, rows, side] = (
                        p * (dprobs[:, side] - delta_ref[h : h + 1, cols])
                    ).astype(bf16)

        def sums_of(qb):
            cols = pl.ds(qb * 256, 256)
            span = pl.ds(0, 256 * (qb + 1))
            dv_acc[span, :] += nn(p_ref[qb % 2, span, :], both_heads(dattended[cols, here]))
            dk_acc[span, :] += nn(ds_ref[qb % 2, span, :], both_heads(joint[cols, here]))
            dq = nn(kt_ref[:, span], ds_ref[qb % 2, span, :])
            dqt_ref[0:64, cols] = dq[0:64, 0:256]
            dqt_ref[64:128, cols] = dq[64:128, 256:512]

        pairs_of(0)
        for qb in range(4):
            if qb < 3:
                pairs_of(qb + 1)
            sums_of(qb)
        djoint[:, lanes(0)] = (dqt_ref[...] * 0.125).T.astype(bf16)
        djoint[:, lanes(1)] = dk_acc[...].astype(bf16)
        djoint[:, lanes(2)] = dv_acc[...].astype(bf16)
        go_on(pair)
        return carry

    lax.fori_loop(0, 4, pair_step, 0)
    for copy in later_loads:
        copy.wait()

    def block_copy(slot, i):
        return pltpu.make_async_copy(
            blocks.at[slot], flat.at[pl.ds(JOINT_AT + 3072 * i, 3072)], block_sem.at[slot]
        )

    for i in range(4):
        if i >= 2:
            block_copy(i % 2, i - 2).wait()
        block = tn(normed[:, 256 * i : 256 * i + 256], djoint[...]).astype(bf16)
        blocks[i % 2] = block.reshape(3072, LANES)
        block_copy(i % 2, i).start()
    for i in (2, 3):
        block_copy(i % 2, i).wait()
    start(stage1(0))
    for q in (0, 1, 3, 2):
        start(loads(q))

    dn_own, dn_part = dist.at[pl.ds(0, 512)], dist.at[pl.ds(512, 512)]
    dn_part[...] = nt(djoint[other, :], weight[...])
    dn_swap = pltpu.make_async_remote_copy(
        src_ref=dn_part, dst_ref=dn_rx, send_sem=swap_sem.at[0], recv_sem=swap_sem.at[1],
        device_id=core_near, device_id_type=MESH_ID,
    )
    dn_swap.start()
    pieces.join(6)
    pass_on(6, 0)
    dn_own[...] = nt(djoint[own, :], weight[...])
    bias_sums = nn(jnp.ones((8, TOKENS), bf16), djoint[...])
    half = pl.ds(pl.multiple_of(512 * c, 512), 512)
    small_mine[0] = jnp.zeros(small_mine.shape[1:], f32)
    small_mine[0, 2:3, half] = bias_sums[0:1, :512]
    small_mine[0, 3:4, half] = bias_sums[0:1, 1024:]
    small_mine[0, 4:7, :] = mid_sums[0:3, :]
    small_mine[0, 7:11, half] = expand_sums[...]
    small_mine[0, 11:12, :] = mid_sums[3:4, :]
    pieces.join(5)
    pass_on(6, 1)
    pass_on(5, 0)
    start(stage1(1))
    pieces.join(7)
    pieces.join(4)
    pass_on(5, 1)
    dn_swap.wait()

    def back_rows(i, carry):
        rows = pl.ds(pl.multiple_of(128 * i, 128), 128)
        values = x_own[rows, :].astype(f32)
        center = values - jnp.mean(values, -1, keepdims=True)
        factor = lax.rsqrt(jnp.mean(center * center, -1, keepdims=True) + norm_epsilon)
        unit = center * factor
        dn = dn_own[rows, :] + dn_rx[rows, :]
        e = dn * mid_sums[4:5, :]
        down = dresid[rows, :] + factor * (
            e - jnp.mean(e, -1, keepdims=True) - unit * jnp.mean(e * unit, -1, keepdims=True)
        )
        dinput[rows, :] = down.astype(bf16)
        small_mine[0, 0:1, :] += jnp.sum(dn * unit, 0, keepdims=True)
        small_mine[0, 1:2, :] += jnp.sum(dn, 0, keepdims=True)
        return carry

    lax.fori_loop(0, 4, back_rows, 0)
    small_step(0).start()
    meet(0)
    pass_on(4, 0)
    meet(1)
    pieces.join(0)
    start(stage1(2))
    small_next(0)
    pass_on(7, 0)
    pass_on(0, 0)
    pieces.join(1)
    pass_on(4, 1)
    pass_on(1, 0)
    small_next(1)
    pass_on(6, 2)
    pass_on(0, 1)
    meet(3)
    meet(2)
    small_next(2)
    for d in (1, 2, 3):
        small_hop(d).start()
    pieces.join(3)
    pass_on(3, 0)
    pass_on(7, 1)
    way_in.start()
    pass_on(1, 1)
    finish(5)
    way_out.start()
    pass_on(3, 1)
    finish(6)
    pass_on(0, 2)
    pieces.join(2)
    pass_on(1, 2)
    pass_on(7, 2)
    finish(3)
    pass_on(2, 0)
    finish(7)
    finish(1)
    finish(0)
    pass_on(2, 1)
    finish(4)
    finish(2)
    for d in (1, 2, 3):
        small_hop(d).wait()
    small = (small_mine[3] + small_z[1]) + (small_z[0] + small_z[2])
    small_out[...] = small.reshape(small_out.shape)

    last.wait()
    way_out.wait()
    way_in.wait()
    for q in (0, 1, 2, 3, 5):
        for copy in stage1(q):
            copy.wait_send()
    for q in range(8):
        for copy in pieces.second(q):
            copy.wait_send()
    for (plane, _), queue in on_way.items():
        @pl.when(z == plane)
        def _():
            for sent in queue[-2:]:
                hop(*sent).wait_send()


def rear(
    slopes, joint, attended, dattended, dist, lse, normed, weight, x_own, dresid, result,
    mid_sums, expand_sums, mid_a, mid_b, flat,
):
    f32, bf16 = jnp.float32, jnp.bfloat16
    vmem = pl.BlockSpec(memory_space=pltpu.VMEM)
    hbm = pl.BlockSpec(memory_space=pl.ANY)
    home = jax.ShapeDtypeStruct((2, 256, WIDTH), bf16)
    piece = jax.ShapeDtypeStruct((PIECE, LANES), f32)
    return pl.pallas_call(
        rear_kernel,
        out_shape=(
            jax.ShapeDtypeStruct((FLAT_ROWS, LANES), bf16),
            piece,
            piece,
            jax.ShapeDtypeStruct((LANES, LANES), f32),
            home,
            home,
        ),
        in_specs=[pl.BlockSpec(memory_space=pltpu.SMEM)] + [hbm] * 4 + [vmem] + [hbm] * 5
        + [vmem] * 2 + [hbm] * 3,
        out_specs=[hbm] + [vmem] * 3 + [hbm] * 2,
        scratch_shapes=[
            pltpu.VMEM((TOKENS, 1536), bf16),
            pltpu.VMEM((TOKENS, 512), bf16),
            pltpu.VMEM((TOKENS, 512), bf16),
            pltpu.VMEM((TOKENS, WIDTH), bf16),
            pltpu.VMEM((WIDTH, 1536), bf16),
            pltpu.VMEM((512, WIDTH), bf16),
            pltpu.VMEM((512, WIDTH), f32),
            pltpu.VMEM((TOKENS, TOKENS), f32),
            pltpu.VMEM((2, TOKENS, 512), bf16),
            pltpu.VMEM((2, TOKENS, 512), bf16),
            pltpu.VMEM((LANES, TOKENS), bf16),
            pltpu.VMEM((LANES, TOKENS), f32),
            pltpu.VMEM((TOKENS, LANES), f32),
            pltpu.VMEM((TOKENS, LANES), f32),
            pltpu.VMEM((8, TOKENS), f32),
            pltpu.VMEM((TOKENS, 1536), bf16),
            pltpu.VMEM((512, WIDTH), f32),
            pltpu.VMEM((512, WIDTH), bf16),
            pltpu.VMEM((2, 3072, LANES), bf16),
            pltpu.VMEM((4, 2, HALF, LANES), bf16),
            pltpu.VMEM((4, 2, HALF, LANES), bf16),
            pltpu.VMEM((8, 2, HALF, LANES), bf16),
            pltpu.VMEM((8, 2, HALF, LANES), bf16),
            pltpu.VMEM((8, HALF, LANES), bf16),
            pltpu.VMEM((8, HALF, LANES), bf16),
            pltpu.VMEM((8, 2, HALF, LANES), bf16),
            pltpu.VMEM((6, 2, HALF, LANES), bf16),
            pltpu.VMEM((6, 2, HALF, LANES), bf16),
            pltpu.VMEM((PIECE, LANES), f32),
            pltpu.VMEM((4, 16, WIDTH), f32),
            pltpu.VMEM((3, 16, WIDTH), f32),
            pltpu.VMEM((3, 16, WIDTH), f32),
            pltpu.SemaphoreType.DMA((10,)),
            pltpu.SemaphoreType.DMA((2,)),
            pltpu.SemaphoreType.DMA((2,)),
            pltpu.SemaphoreType.DMA((8, 4, 2)),
            pltpu.SemaphoreType.DMA((8, 2, 2)),
            pltpu.SemaphoreType.DMA((8, 2, 2)),
            pltpu.SemaphoreType.DMA((8, 2)),
            pltpu.SemaphoreType.DMA((8, 2)),
            pltpu.SemaphoreType.DMA((8, 2, 2)),
            pltpu.SemaphoreType.DMA((8, 2, 2)),
            pltpu.SemaphoreType.DMA((2,)),
            pltpu.SemaphoreType.DMA((6,)),
            pltpu.SemaphoreType.DMA((6,)),
            pltpu.SemaphoreType.DMA((2,)),
            pltpu.SemaphoreType.DMA((2,)),
            pltpu.SemaphoreType.DMA((2,)),
            pltpu.SemaphoreType.DMA((2,)),
        ],
        input_output_aliases={15: 0},
        compiler_params=pltpu.CompilerParams(
            collective_id=2, has_side_effects=True, vmem_limit_bytes=62 << 20
        ),
        cost_estimate=pl.CostEstimate(flops=30 << 30, bytes_accessed=30 << 20, transcendentals=0),
    )(
        slopes, joint, attended, dattended, dist, lse, normed, weight, x_own, dresid, result,
        mid_sums, expand_sums, mid_a, mid_b, flat,
    )


def middle_kernel(
    attended, x_own, cot, mixer_bias_in, gain_in, shift_in, reduce_bias_in, expand_bias_in, gain_before_in,
    mixer_hbm, expand_hbm, reduce_hbm,
    result, dresid, dattended, sums, expand_sums, flat, rx_a, rx_b,
    vectors, mixer, expand, reduce, att_rx, resid, normal, spread, normed, act, act_rx, dhidden,
    dn_own, dn_part, dn_rx, out_part, out_rx, dbranch, blocks,
    weight_sem, block_sem, send_sem, recv_sem, act_send, act_recv, s1_send, s1_recv,
):
    f32, bf16 = jnp.float32, jnp.bfloat16
    dp = lax.axis_index("dp")
    me = lax.axis_index("group")
    c = dp % 2
    near = (dp + 1 - 2 * c, me)
    own = pl.ds(pl.multiple_of(512 * c, 512), 512)
    other = pl.ds(pl.multiple_of(512 * (1 - c), 512), 512)

    weights = [pltpu.make_async_copy(mixer_hbm, mixer, weight_sem.at[0])]
    for k in range(4):
        part = pl.ds(pl.multiple_of(512 * (2 * k + c), 512), 512)
        weights.append(pltpu.make_async_copy(
            expand_hbm.at[:, part], expand.at[:, pl.ds(512 * k, 512)], weight_sem.at[1 + k]
        ))
    for k in range(4):
        part = pl.ds(pl.multiple_of(512 * (2 * k + c), 512), 512)
        weights.append(pltpu.make_async_copy(
            reduce_hbm.at[part], reduce.at[pl.ds(512 * k, 512)], weight_sem.at[5 + k]
        ))
    for copy in weights:
        copy.start()

    y, x = me // 2, me % 2
    greet([near, (dp, 2 * y + 1 - x), (dp, 2 * (1 - y) + x)])

    def swap(i, src, dst):
        return pltpu.make_async_remote_copy(
            src_ref=src, dst_ref=dst, send_sem=send_sem.at[i], recv_sem=recv_sem.at[i],
            device_id=near, device_id_type=MESH_ID,
        )

    att_swap = swap(0, attended, att_rx)
    normed_swap = swap(1, normed.at[own], normed.at[own])
    dn_swap = swap(2, dn_part, dn_rx)
    out_swap = swap(3, out_part, out_rx)
    branch_swap = swap(4, dbranch.at[own], dbranch.at[own])
    att_swap.start()

    for k, given in enumerate((mixer_bias_in, gain_in, shift_in, reduce_bias_in)):
        vectors[k : k + 1, :] = given[...].astype(f32).reshape(1, WIDTH)
    vectors[4:8, :] = expand_bias_in[...].astype(f32).reshape(4, WIDTH)
    mixer_bias, gain, shift, reduce_bias = (vectors[k : k + 1, :] for k in range(4))

    weights[0].wait()
    resid[...] = nn(attended[own, :], mixer[own, :]) + (x_own[...].astype(f32) + mixer_bias)
    att_swap.wait_recv()
    resid[...] += nn(att_rx[own, :], mixer[other, :])

    def norm_rows(i, carry):
        rows = pl.ds(pl.multiple_of(128 * i, 128), 128)
        here = pl.ds(pl.multiple_of(512 * c + 128 * i, 128), 128)
        values = resid[rows, :]
        center = values - jnp.mean(values, -1, keepdims=True)
        factor = lax.rsqrt(jnp.mean(center * center, -1, keepdims=True) + norm_epsilon)
        unit = center * factor
        normal[rows, :] = unit
        spread[rows, :] = jnp.broadcast_to(factor, (128, LANES))
        normed[here, :] = (unit * gain + shift).astype(bf16)
        return carry

    lax.fori_loop(0, 4, norm_rows, 0)
    normed_swap.start()

    def act_swap(half, k):
        rows = pl.ds(pl.multiple_of(512 * half, 512), 512)
        cols = pl.ds(pl.multiple_of(512 * k, 512), 512)
        return pltpu.make_async_remote_copy(
            src_ref=act.at[rows, cols], dst_ref=act_rx.at[rows, cols],
            send_sem=act_send.at[half, k], recv_sem=act_recv.at[half, k],
            device_id=near, device_id_type=MESH_ID,
        )

    root = math.sqrt(2.0 / math.pi)
    right = pl.ds(pl.multiple_of(512 * c, 512), 512)

    def hidden_block(half, k, first):
        rows = pl.ds(pl.multiple_of(512 * half, 512), 512)
        cols = pl.ds(pl.multiple_of(512 * k, 512), 512)
        u = nn(normed[rows, :], expand[:, cols]) + vectors[pl.ds(4 + k, 1), right]
        dact = nt(cot[rows, :], reduce[cols, :])
        square = u * u
        t = jnp.tanh(u * (root + (root * 0.044715) * square))
        up = 0.5 + 0.5 * t
        act[rows, cols] = (u * up).astype(bf16)
        slope = up + (0.5 * u) * (1.0 - t * t) * (root + (3.0 * root * 0.044715) * square)
        dh = (dact * slope).astype(bf16)
        dhidden[rows, cols] = dh
        total = jnp.sum(dh.astype(f32), 0, keepdims=True)
        if first:
            expand_sums[pl.ds(k, 1), :] = total
        else:
            expand_sums[pl.ds(k, 1), :] += total
        act_swap(half, k).start()

    def out_copies(slot, places):
        return [
            pltpu.make_async_copy(
                blocks.at[slot, pl.ds(2048 * part, 2048)],
                flat.at[pl.ds(pl.multiple_of(at, 16), 2048)], block_sem.at[slot, part],
            )
            for part, at in enumerate(places)
        ]

    def emit(block, slot, places):
        blocks[slot, : 2048 * len(places)] = block.astype(bf16).reshape(2048 * len(places), LANES)
        for copy in out_copies(slot, places):
            copy.start()

    def drain(slot, places):
        for copy in out_copies(slot, places):
            copy.wait()

    for copy in weights[1:]:
        copy.wait()

    def reduce_places(pair, parity):
        return [REDUCE_AT + 2048 * (2 * (2 * pair + k) + parity) for k in range(2)]

    def hidden_pair(pair, carry):
        def mine(k, carry):
            hidden_block(c, 2 * pair + k, True)
            return carry

        def theirs(k, carry):
            hidden_block(1 - c, 2 * pair + k, False)
            return carry

        lax.fori_loop(0, 2, mine, 0)

        @pl.when(pair == 0)
        def _():
            normed_swap.wait_recv()

        lax.fori_loop(0, 2, theirs, 0)
        left = pl.ds(pl.multiple_of(1024 * pair, 1024), 1024)
        block = tn(act[:, left], cot[:, right])

        @pl.when(pair == 1)
        def _():
            drain(0, reduce_places(0, c))

        emit(block, 0, reduce_places(pair, c))
        for half in range(2):
            for k in range(2):
                act_swap(half, 2 * pair + k).wait()
        block = tn(act_rx[:, left], cot[:, right])

        @pl.when(pair == 1)
        def _():
            drain(1, reduce_places(0, 1 - c))

        emit(block, 1, reduce_places(pair, 1 - c))
        return carry

    lax.fori_loop(0, 2, hidden_pair, 0)
    drain(0, reduce_places(1, c))
    drain(1, reduce_places(1, 1 - c))
    stages = [
        first_stage(q, flat, rx_a, rx_b, at, s1_send, s1_recv, dp, me)
        for at, q in enumerate(MIDDLE_EARLY)
    ]
    for copies in stages[:2]:
        for copy in copies:
            copy.start()

    def expand_places(i):
        return [EXPAND_AT + 4096 * i, EXPAND_AT + 4096 * i + 2048]

    def expand_step(i, carry):
        block = tn(normed[:, pl.ds(pl.multiple_of(256 * i, 256), 256)], dhidden[...])

        @pl.when(i >= 2)
        def _():
            drain(i % 2, expand_places(i - 2))

        emit(block, i % 2, expand_places(i))
        return carry

    lax.fori_loop(0, 4, expand_step, 0)
    drain(0, expand_places(2))
    drain(1, expand_places(3))
    for copies in stages[2:]:
        for copy in copies:
            copy.start()

    dn_part[...] = nt(dhidden[other, :], expand[...])
    dn_swap.start()
    out_part[...] = nn(act[other, :], reduce[...]).astype(bf16)
    out_swap.start()

    dn_own[...] = nt(dhidden[own, :], expand[...])
    dn_swap.wait()
    sums[...] = jnp.zeros_like(sums)
    sums[4:5, :] = gain_before_in[...].astype(f32).reshape(1, WIDTH)

    def back_rows(i, carry):
        rows = pl.ds(pl.multiple_of(128 * i, 128), 128)
        here = pl.ds(pl.multiple_of(512 * c + 128 * i, 128), 128)
        dn = dn_own[rows, :] + dn_rx[rows, :]
        unit = normal[rows, :]
        grad = cot[here, :].astype(f32)
        e = dn * gain
        down = grad + spread[rows, 0:1] * (
            e - jnp.mean(e, -1, keepdims=True) - unit * jnp.mean(e * unit, -1, keepdims=True)
        )
        dresid[rows, :] = down
        low = down.astype(bf16)
        dbranch[here, :] = low
        sums[0:1, :] += jnp.sum(low.astype(f32), 0, keepdims=True)
        sums[1:2, :] += jnp.sum(dn * unit, 0, keepdims=True)
        sums[2:3, :] += jnp.sum(dn, 0, keepdims=True)
        sums[3:4, :] += jnp.sum(grad, 0, keepdims=True)
        return carry

    lax.fori_loop(0, 4, back_rows, 0)
    branch_swap.start()
    dattended[own, :] = nt(dbranch[own, :], mixer[own, :]).astype(bf16)
    resid[...] += nn(act[own, :], reduce[...])
    out_swap.wait()
    result[...] = (resid[...] + (out_rx[...].astype(f32) + reduce_bias)).astype(bf16)
    branch_swap.wait()
    dattended[other, :] = nt(dbranch[other, :], mixer[own, :]).astype(bf16)
    emit(tn(attended[...], dbranch[:, right]), 0, [MIXER_AT + 2048 * c])
    emit(tn(att_rx[...], dbranch[:, right]), 1, [MIXER_AT + 2048 * (1 - c)])
    drain(0, [MIXER_AT + 2048 * c])
    drain(1, [MIXER_AT + 2048 * (1 - c)])
    att_swap.wait_send()
    normed_swap.wait_send()
    for copies in stages:
        for copy in copies:
            copy.wait()


def middle(attended, x_own, cot, small, mixer, expand, reduce):
    f32, bf16 = jnp.float32, jnp.bfloat16
    vmem = pl.BlockSpec(memory_space=pltpu.VMEM)
    hbm = pl.BlockSpec(memory_space=pl.ANY)
    count = len(MIDDLE_EARLY)
    early = jax.ShapeDtypeStruct((count, 2, HALF, LANES), bf16)
    return pl.pallas_call(
        middle_kernel,
        out_shape=(
            jax.ShapeDtypeStruct((512, WIDTH), bf16),
            jax.ShapeDtypeStruct((512, WIDTH), f32),
            jax.ShapeDtypeStruct((TOKENS, 512), bf16),
            jax.ShapeDtypeStruct((8, WIDTH), f32),
            jax.ShapeDtypeStruct((4, 512), f32),
            jax.ShapeDtypeStruct((FLAT_ROWS, LANES), bf16),
            early,
            early,
        ),
        in_specs=[vmem] * 9 + [hbm] * 3,
        out_specs=[vmem] * 5 + [hbm] * 3,
        scratch_shapes=[
            pltpu.VMEM((8, WIDTH), f32),
            pltpu.VMEM((WIDTH, WIDTH), bf16),
            pltpu.VMEM((WIDTH, 2048), bf16),
            pltpu.VMEM((2048, WIDTH), bf16),
            pltpu.VMEM((TOKENS, 512), bf16),
            pltpu.VMEM((512, WIDTH), f32),
            pltpu.VMEM((512, WIDTH), f32),
            pltpu.VMEM((512, LANES), f32),
            pltpu.VMEM((TOKENS, WIDTH), bf16),
            pltpu.VMEM((TOKENS, 2048), bf16),
            pltpu.VMEM((TOKENS, 2048), bf16),
            pltpu.VMEM((TOKENS, 2048), bf16),
            pltpu.VMEM((512, WIDTH), f32),
            pltpu.VMEM((512, WIDTH), f32),
            pltpu.VMEM((512, WIDTH), f32),
            pltpu.VMEM((512, WIDTH), bf16),
            pltpu.VMEM((512, WIDTH), bf16),
            pltpu.VMEM((TOKENS, WIDTH), bf16),
            pltpu.VMEM((2, 4096, LANES), bf16),
            pltpu.SemaphoreType.DMA((9,)),
            pltpu.SemaphoreType.DMA((2, 2)),
            pltpu.SemaphoreType.DMA((5,)),
            pltpu.SemaphoreType.DMA((5,)),
            pltpu.SemaphoreType.DMA((2, 4)),
            pltpu.SemaphoreType.DMA((2, 4)),
            pltpu.SemaphoreType.DMA((count, 2, 2)),
            pltpu.SemaphoreType.DMA((count, 2, 2)),
        ],
        compiler_params=pltpu.CompilerParams(
            collective_id=1, has_side_effects=True, vmem_limit_bytes=62 << 20
        ),
        cost_estimate=pl.CostEstimate(flops=30 << 30, bytes_accessed=40 << 20, transcendentals=0),
    )(attended, x_own, cot, *small, mixer, expand, reduce)


UPDATE_ROWS = 616


def owner_table(owners):
    smalls = ((0, 2, 0), (U_JBIAS, U_MIXER, 16), (U_MBIAS, U_EXPAND, 32), (U_EBIAS, U_REDUCE, 56),
              (U_RBIAS, 12300, 88))
    table = []
    for owner in range(owners):
        begin = OWNED_ROWS * owner
        end = begin + OWNED_ROWS
        start = piece_start(owner)
        shift, later = section_shift(begin // 8), section_shift((end - 1) // 8)
        turn = next((8 * u - begin for u in (U_JBIAS, U_MBIAS) if begin < 8 * u < end), OWNED_ROWS)
        row = [begin + 2 * shift - 2 * start, begin + 2 * later - 2 * start, turn, 0, 0, 0, 3 * owner, 0]
        for first, past, at in smalls:
            if 8 * first < end and 8 * past > begin:
                row[3] = at + begin - 8 * first
                row[4] = max(8 * first - begin, 0)
                row[5] = min(8 * past - begin, OWNED_ROWS)
        assert 0 <= row[0] <= row[1] <= 2 * PIECE - 5 * UPDATE_ROWS
        table.append(row)
    return table


def update_kernel(
    table, step_count, learn_rate, master, first, second, own, peer, small, out_hbm, in_hbm,
    new_master, new_first, new_second, small_share, out_copy, in_copy,
    rows, small_rows, held, sem,
):
    f32 = jnp.float32
    i = pl.program_id(0)
    c = lax.axis_index("dp") % 2
    owner = lax.axis_index("dp") * lax.axis_size("group") + lax.axis_index("group")
    place = [table[owner, k] for k in range(7)]
    pairs = ((out_hbm, out_copy), (in_hbm, in_copy))
    fetch = [pltpu.make_async_copy(src, held.at[k], sem.at[k]) for k, (src, _) in enumerate(pairs)]
    give = [pltpu.make_async_copy(held.at[k], dst, sem.at[2 + k]) for k, (_, dst) in enumerate(pairs)]

    @pl.when(i == 0)
    def _():
        for copy in fetch:
            copy.start()
        small_rows[...] = jnp.zeros_like(small_rows)
        small_rows[UPDATE_ROWS : UPDATE_ROWS + LANES, :] = small[...]
        small_share[...] = small_rows[pl.ds(UPDATE_ROWS + place[6], 3), :]

        def weave(k, carry):
            part = pl.ds(pl.multiple_of(112 * k, 16), 112)
            mine, other = own[part, :], peer[part, :]
            even = jnp.where(c == 0, mine, other).reshape(28, 4, LANES)
            odd = jnp.where(c == 0, other, mine).reshape(28, 4, LANES)
            rows[pl.ds(pl.multiple_of(224 * k, 32), 224), :] = jnp.concatenate([even, odd], 1).reshape(
                224, LANES
            )
            return carry

        lax.fori_loop(0, PIECE // 112, weave, 0)

    @pl.when(i == 2)
    def _():
        for copy in fetch:
            copy.wait()
        for copy in give:
            copy.start()

    base = UPDATE_ROWS * i
    k = lax.broadcasted_iota(jnp.int32, (UPDATE_ROWS, LANES), 0) + base
    grad = jnp.where(
        k < place[2],
        rows[pl.ds(place[0] + base, UPDATE_ROWS), :],
        rows[pl.ds(place[1] + base, UPDATE_ROWS), :],
    )
    at = jnp.clip(place[3] + base, -UPDATE_ROWS, LANES) + UPDATE_ROWS
    grad = jnp.where(
        (k >= place[4]) & (k < place[5]), small_rows[pl.ds(at, UPDATE_ROWS), :], grad
    )
    rate = learn_rate[0]
    moment_step = jnp.full((1, LANES), step_count[0].astype(f32))
    fix_one = 1.0 - jnp.exp(moment_step * math.log(beta_first))
    fix_two = 1.0 - jnp.exp(moment_step * math.log(beta_second))
    one = beta_first * first[...] + (1.0 - beta_first) * grad
    two = beta_second * second[...] + (1.0 - beta_second) * grad * grad
    weights = master[...]
    new_first[...] = one
    new_second[...] = two
    new_master[...] = weights - rate * (
        one / fix_one / (jnp.sqrt(two / fix_two) + adam_epsilon) + weight_decay * weights
    )

    @pl.when(i == pl.num_programs(0) - 1)
    def _():
        for copy in give:
            copy.wait()


def update(table, step_count, learn_rate, master, first, second, own, peer, small, output, input_gradient):
    f32 = jnp.float32
    smem = pl.BlockSpec(memory_space=pltpu.SMEM)
    hbm = pl.BlockSpec(memory_space=pl.ANY)
    block = pl.BlockSpec((UPDATE_ROWS, LANES), lambda i: (i, 0))

    def whole(shape):
        return pl.BlockSpec(shape, lambda i: (0, 0))

    flat = jax.ShapeDtypeStruct((OWNED_ROWS, LANES), f32)
    home = jax.ShapeDtypeStruct(output.shape, output.dtype)
    new = pl.pallas_call(
        update_kernel,
        grid=(5,),
        out_shape=(flat, flat, flat, jax.ShapeDtypeStruct((3, LANES), f32), home, home),
        in_specs=[smem, smem, smem] + [block] * 3
        + [whole((PIECE, LANES)), whole((PIECE, LANES)), whole((LANES, LANES))] + [hbm] * 2,
        out_specs=[block] * 3 + [whole((3, LANES))] + [hbm] * 2,
        scratch_shapes=[
            pltpu.VMEM((2 * PIECE, LANES), f32),
            pltpu.VMEM((2 * UPDATE_ROWS + LANES, LANES), f32),
            pltpu.VMEM((2,) + output.shape, output.dtype),
            pltpu.SemaphoreType.DMA((4,)),
        ],
        compiler_params=pltpu.CompilerParams(vmem_limit_bytes=62 << 20),
    )(
        table, step_count, learn_rate, *[whole_array.reshape(OWNED_ROWS, LANES) for whole_array in (master, first, second)],
        own, peer, small, output, input_gradient,
    )
    return [part.reshape(-1) for part in new[:4]] + list(new[4:])


def on_device_chip(
    dp_size, group_size,
    activations, cotangent, segments, padding, step_count, learn_rate,
    gain_before, shift_before, joint_weight, joint_bias, mixer_weight, mixer_bias,
    gain_middle, shift_middle, expand_weight, expand_bias, reduce_weight, reduce_bias,
    master_weights, first_moment, second_moment,
):
    f32, bf16 = jnp.float32, jnp.bfloat16
    dp = lax.axis_index("dp")
    group = lax.axis_index("group")
    c = dp % 2
    slopes = jnp.asarray([2.0 ** (-8.0 * (h + 1) / HEADS) for h in range(HEADS)], f32)
    x_own, cot_all, normed_one, joint, dist, attended, lse = front(
        slopes, activations, cotangent, segments, padding, gain_before, shift_before, joint_bias,
        joint_weight,
    )
    result, dresid, dattended, middle_sums, expand_sums, flat, mid_a, mid_b = middle(
        attended, x_own, cot_all, (mixer_bias, gain_middle, shift_middle, reduce_bias, expand_bias, gain_before),
        mixer_weight, expand_weight, reduce_weight,
    )
    _, own, peer, small_sum, output, input_gradient = rear(
        slopes, joint, attended, dattended, dist, lse, normed_one, joint_weight, x_own, dresid,
        result, middle_sums, expand_sums, mid_a, mid_b, flat,
    )
    table = jnp.asarray(owner_table(dp_size * group_size), jnp.int32)
    new_master, new_first, new_second, small_share, output, input_gradient = update(
        table, step_count, learn_rate, master_weights, first_moment, second_moment, own, peer, small_sum, output,
        input_gradient,
    )
    return (output, input_gradient, new_master, new_first, new_second, small_share)


def on_device(dp_size, group_size, activations, *rest):
    if (dp_size, group_size) == (8, 4) and activations.shape == (2, 256, WIDTH):
        return on_device_chip(dp_size, group_size, activations, *rest)
    return on_device_general(activations, *rest)


def solution(mesh):
    in_specs = (
        P("dp", "group", None),
        P("dp", "group", None),
        P("dp", None),
        P("dp", None),
        P(),
        P(),
        P(),
        P(),
        P(),
        P(),
        P(),
        P(),
        P(),
        P(),
        P(),
        P(),
        P(),
        P(),
        P(("dp", "group")),
        P(("dp", "group")),
        P(("dp", "group")),
    )
    out_specs = (
        P("dp", "group", None),
        P("dp", "group", None),
        P(("dp", "group")),
        P(("dp", "group")),
        P(("dp", "group")),
        P(("dp", "group")),
    )
    return jax.shard_map(
        functools.partial(on_device, mesh.shape["dp"], mesh.shape["group"]), mesh=mesh, in_specs=in_specs, out_specs=out_specs, check_vma=False
    )
```

```python
import functools
import math

import jax
import jax.numpy as jnp
from jax import lax
from jax.experimental import pallas as pl
from jax.experimental.pallas import tpu as pltpu
from jax.sharding import PartitionSpec as P

HEADS = 16
DOC_MOST = 800


beta_first = 0.9
beta_second = 0.95
adam_epsilon = 1e-08
weight_decay = 0.1
norm_epsilon = 1e-05
masked_score = -1e30


def shifted(block, axis, distance):
    devices = range(lax.axis_size(axis))
    route = [(i - distance, i) for i in devices if i - distance in devices]
    return lax.ppermute(block, axis, route)


def standardize(values):
    center = values - jnp.mean(values, -1, keepdims=True)
    spread = lax.rsqrt(jnp.mean(center * center, -1, keepdims=True) + norm_epsilon)
    return (center * spread, spread)


def norm_back(dnormed, normed, spread):
    return spread * (
        dnormed
        - jnp.mean(dnormed, -1, keepdims=True)
        - normed * jnp.mean(dnormed * normed, -1, keepdims=True)
    )


def window_mask(segments, padding, member, hop, block_len):
    places = jnp.arange(block_len, dtype=jnp.int32)
    source = member - hop
    query_place = member * block_len + places
    key_place = source * block_len + places
    start = jnp.maximum(source, 0) * block_len
    seg_query = lax.dynamic_slice_in_dim(segments, member * block_len, block_len, 1)
    seg_key = lax.dynamic_slice_in_dim(segments, start, block_len, 1)
    pad_key = lax.dynamic_slice_in_dim(padding, start, block_len, 1)
    earlier = key_place[None, None, :] <= query_place[None, :, None]
    itself = key_place[None, None, :] == query_place[None, :, None]
    allowed = (
        (seg_query[:, :, None] == seg_key[:, None, :])
        & earlier
        & ((pad_key[:, None, :] == 1) | itself)
        & (source >= 0)
    )
    distance = (query_place[:, None] - key_place[None, :]).astype(jnp.float32)
    return (allowed[:, None], distance)


def piece_scores(query4, key4, slopes, distance, score_scale):
    raw = jnp.einsum("sqhd,skhd->shqk", query4, key4, preferred_element_type=jnp.float32)
    return raw * score_scale - slopes[:, None, None] * distance[None]


def on_device_general(
    activations,
    cotangent,
    segments,
    padding,
    step_count,
    learn_rate,
    gain_before,
    shift_before,
    joint_weight,
    joint_bias,
    mixer_weight,
    mixer_bias,
    gain_middle,
    shift_middle,
    expand_weight,
    expand_bias,
    reduce_weight,
    reduce_bias,
    master_weights,
    first_moment,
    second_moment,
):
    seq_count, block_len, width = activations.shape
    head_size = width // HEADS
    row_count = seq_count * block_len
    shape4 = (seq_count, block_len, HEADS, head_size)
    score_scale = 1.0 / math.sqrt(head_size)
    group_size = lax.axis_size("group")
    member = lax.axis_index("group")
    reach = min((DOC_MOST + block_len - 2) // block_len, group_size - 1)
    slopes = jnp.exp2(-8.0 * (jnp.arange(HEADS, dtype=jnp.float32) + 1.0) / HEADS)
    inputs = activations.reshape(row_count, width).astype(jnp.float32)
    gain_one = gain_before.astype(jnp.float32)
    gain_two = gain_middle.astype(jnp.float32)
    normal_one, spread_one = standardize(inputs)
    normed_one = (normal_one * gain_one + shift_before.astype(jnp.float32)).astype(jnp.bfloat16)
    joint = jnp.dot(normed_one, joint_weight, preferred_element_type=jnp.float32)
    bias_joint = joint_bias.astype(jnp.float32)
    query_rows = (joint[:, :width] + bias_joint[:width]).astype(jnp.bfloat16)
    key_rows = joint[:, width : 2 * width].astype(jnp.bfloat16)
    value_rows = (joint[:, 2 * width :] + bias_joint[width:]).astype(jnp.bfloat16)
    own_piece = jnp.stack([key_rows, value_rows]).reshape(2, seq_count, block_len, width)
    query4 = query_rows.reshape(shape4)
    pieces = [own_piece]
    for hop in range(1, reach + 1):
        pieces.append(shifted(own_piece, "group", hop))
    row_top = jnp.full((seq_count, HEADS, block_len), masked_score, jnp.float32)
    row_total = jnp.zeros((seq_count, HEADS, block_len), jnp.float32)
    for hop in range(reach + 1):
        allowed, distance = window_mask(segments, padding, member, hop, block_len)
        scores = piece_scores(query4, pieces[hop][0].reshape(shape4), slopes, distance, score_scale)
        fresh = jnp.maximum(row_top, jnp.max(jnp.where(allowed, scores, masked_score), -1))
        row_total = row_total * jnp.exp(row_top - fresh) + jnp.sum(
            jnp.exp(jnp.where(allowed, scores - fresh[..., None], masked_score)), -1
        )
        row_top = fresh
    log_total = row_top + jnp.log(row_total)
    attended = jnp.zeros(shape4, jnp.float32)
    for hop in range(reach + 1):
        allowed, distance = window_mask(segments, padding, member, hop, block_len)
        scores = piece_scores(query4, pieces[hop][0].reshape(shape4), slopes, distance, score_scale)
        probs = jnp.exp(jnp.where(allowed, scores - log_total[..., None], masked_score)).astype(
            jnp.bfloat16
        )
        attended = attended + jnp.einsum(
            "shqk,skhd->sqhd",
            probs,
            pieces[hop][1].reshape(shape4),
            preferred_element_type=jnp.float32,
        )
    attended_low = attended.reshape(row_count, width).astype(jnp.bfloat16)
    resid = inputs + (
        jnp.dot(attended_low, mixer_weight, preferred_element_type=jnp.float32)
        + mixer_bias.astype(jnp.float32)
    )
    normal_two, spread_two = standardize(resid)
    normed_two = (normal_two * gain_two + shift_middle.astype(jnp.float32)).astype(jnp.bfloat16)
    hidden = jnp.dot(
        normed_two, expand_weight, preferred_element_type=jnp.float32
    ) + expand_bias.astype(jnp.float32)
    act = jax.nn.gelu(hidden, approximate=True).astype(jnp.bfloat16)
    result = resid + (
        jnp.dot(act, reduce_weight, preferred_element_type=jnp.float32)
        + reduce_bias.astype(jnp.float32)
    )
    output = result.astype(jnp.bfloat16).reshape(seq_count, block_len, width)
    cot_low = cotangent.reshape(row_count, width)
    cot_full = cot_low.astype(jnp.float32)
    reduce_grad = jnp.einsum("tf,td->fd", act, cot_low, preferred_element_type=jnp.float32)
    reduce_bias_grad = jnp.sum(cot_full, 0)
    dact = jnp.einsum("td,fd->tf", cot_low, reduce_weight, preferred_element_type=jnp.float32)
    gelu_pull = jax.vjp(lambda inner: jax.nn.gelu(inner, approximate=True), hidden)[1]
    dhidden = gelu_pull(dact)[0].astype(jnp.bfloat16)
    expand_grad = jnp.einsum("td,tf->df", normed_two, dhidden, preferred_element_type=jnp.float32)
    expand_bias_grad = jnp.sum(dhidden.astype(jnp.float32), 0)
    dnormed_two = jnp.einsum(
        "tf,df->td", dhidden, expand_weight, preferred_element_type=jnp.float32
    )
    gain_middle_grad = jnp.sum(dnormed_two * normal_two, 0)
    shift_middle_grad = jnp.sum(dnormed_two, 0)
    dresid = cot_full + norm_back(dnormed_two * gain_two, normal_two, spread_two)
    dbranch = dresid.astype(jnp.bfloat16)
    mixer_grad = jnp.einsum("td,te->de", attended_low, dbranch, preferred_element_type=jnp.float32)
    mixer_bias_grad = jnp.sum(dbranch.astype(jnp.float32), 0)
    dattended = jnp.einsum(
        "te,de->td", dbranch, mixer_weight, preferred_element_type=jnp.float32
    ).astype(jnp.bfloat16)
    dattended4 = dattended.reshape(shape4)
    row_delta = jnp.einsum("sqhd,sqhd->shq", dattended4.astype(jnp.float32), attended)
    dquery = jnp.zeros(shape4, jnp.float32)
    dkv_own = jnp.zeros((2, seq_count, block_len, width), jnp.float32)
    for hop in range(reach + 1):
        piece = pieces[hop]
        key4 = piece[0].reshape(shape4)
        value4 = piece[1].reshape(shape4)
        allowed, distance = window_mask(segments, padding, member, hop, block_len)
        scores = piece_scores(query4, key4, slopes, distance, score_scale)
        probs = jnp.exp(jnp.where(allowed, scores - log_total[..., None], masked_score))
        dvalue = jnp.einsum(
            "shqk,sqhd->skhd",
            probs.astype(jnp.bfloat16),
            dattended4,
            preferred_element_type=jnp.float32,
        )
        dprobs = jnp.einsum(
            "sqhd,skhd->shqk", dattended4, value4, preferred_element_type=jnp.float32
        )
        dscores = (probs * (dprobs - row_delta[..., None])).astype(jnp.bfloat16)
        dquery = dquery + jnp.einsum(
            "shqk,skhd->sqhd", dscores, key4, preferred_element_type=jnp.float32
        )
        dkey = (
            jnp.einsum("shqk,sqhd->skhd", dscores, query4, preferred_element_type=jnp.float32)
            * score_scale
        )
        returned = jnp.stack([dkey, dvalue]).reshape(2, seq_count, block_len, width)
        if hop == 0:
            dkv_own = returned
        else:
            dkv_own = dkv_own + shifted(returned.astype(jnp.bfloat16), "group", -hop).astype(
                returned.dtype
            )
    dquery_low = (dquery * score_scale).reshape(row_count, width).astype(jnp.bfloat16)
    dkey_low = dkv_own[0].reshape(row_count, width).astype(jnp.bfloat16)
    dvalue_low = dkv_own[1].reshape(row_count, width).astype(jnp.bfloat16)
    djoint = jnp.concatenate([dquery_low, dkey_low, dvalue_low], 1)
    joint_grad = jnp.einsum("td,te->de", normed_one, djoint, preferred_element_type=jnp.float32)
    joint_bias_grad = jnp.concatenate(
        [jnp.sum(dquery_low.astype(jnp.float32), 0), jnp.sum(dvalue_low.astype(jnp.float32), 0)]
    )
    dnormed_one = jnp.einsum("te,de->td", djoint, joint_weight, preferred_element_type=jnp.float32)
    gain_before_grad = jnp.sum(dnormed_one * normal_one, 0)
    shift_before_grad = jnp.sum(dnormed_one, 0)
    dinput = dresid + norm_back(dnormed_one * gain_one, normal_one, spread_one)
    input_gradient = dinput.astype(jnp.bfloat16).reshape(seq_count, block_len, width)
    listing = [
        gain_before_grad,
        shift_before_grad,
        joint_grad,
        joint_bias_grad,
        mixer_grad,
        mixer_bias_grad,
        gain_middle_grad,
        shift_middle_grad,
        expand_grad,
        expand_bias_grad,
        reduce_grad,
        reduce_bias_grad,
    ]
    gradient = jnp.concatenate([single.reshape(-1) for single in listing])
    small_list = [
        gain_before_grad,
        shift_before_grad,
        joint_bias_grad,
        mixer_bias_grad,
        gain_middle_grad,
        shift_middle_grad,
        expand_bias_grad,
        reduce_bias_grad,
    ]
    small_local = jnp.concatenate(small_list)
    share, small_share = (
        lax.psum_scatter(gradient, ("dp", "group"), scatter_dimension=0, tiled=True),
        lax.psum_scatter(small_local, ("dp", "group"), scatter_dimension=0, tiled=True),
    )
    moment_step = step_count[0].astype(jnp.float32)
    rate = learn_rate[0]
    fix_one = 1.0 - jnp.exp(moment_step * math.log(beta_first))
    fix_two = 1.0 - jnp.exp(moment_step * math.log(beta_second))
    updated_first = beta_first * first_moment + (1.0 - beta_first) * share
    updated_second = beta_second * second_moment + (1.0 - beta_second) * share * share
    updated_master = master_weights - rate * (
        updated_first / fix_one / (jnp.sqrt(updated_second / fix_two) + adam_epsilon)
        + weight_decay * master_weights
    )
    return (output, input_gradient, updated_master, updated_first, updated_second, small_share)


WIDTH = 1024
HIDDEN = 4096
TOKENS = 1024
LANES = 128
OWNED = 393600
OWNED_ROWS = OWNED // LANES
PIECE = 1568
HALF = PIECE // 2
JOINT_AT, MIXER_AT, EXPAND_AT, REDUCE_AT = 16, 12320, 16432, 32832
FLAT_ROWS = 49248
U_JOINT, U_JBIAS, U_MIXER, U_MBIAS, U_EXPAND, U_EBIAS, U_REDUCE, U_RBIAS = (
    2, 3074, 3076, 4100, 4103, 8199, 8203, 12299,
)


def section_shift(unit):
    return 8 if unit < U_JBIAS else 16 if unit < U_MBIAS else 20


def piece_start(owner):
    unit = OWNED_ROWS * owner // 8
    return (4 * unit + section_shift(unit)) // 16 * 16


def piece_offset(q, y, x):
    at = [piece_start(4 * q + k) // 16 for k in range(4)]
    row = (
        at[0] * (1 - y) * (1 - x) + at[1] * (1 - y) * x + at[2] * y * (1 - x) + at[3] * y * x
    )
    return pl.multiple_of(row * 16, 16)


MESH_ID = pl.DeviceIdType.MESH


def by_rows(step):
    def one(i, carry):
        step(pl.ds(pl.multiple_of(112 * i, 16), 112))
        return carry

    lax.fori_loop(0, HALF // 112, one, 0)


class Pieces:
    def __init__(self, dp, me, flat, own_a, own_b, rx_a1, rx_b1, rx_a2, rx_b2, acc, load_sem, s2_send, s2_recv):
        self.y, self.x = me // 2, me % 2
        self.x_near = (dp, 2 * self.y + (1 - self.x))
        self.y_near = (dp, 2 * (1 - self.y) + self.x)
        self.flat, self.own_a, self.own_b = flat, own_a, own_b
        self.rx_a1, self.rx_b1, self.rx_a2, self.rx_b2, self.acc = rx_a1, rx_b1, rx_a2, rx_b2, acc
        self.load_sem, self.s2_send, self.s2_recv = load_sem, s2_send, s2_recv

    def loads(self, q, own_slot, ready=None):
        slot = q
        out = []
        for k in range(2):
            for way, (row, own) in enumerate((
                (piece_offset(q, k, self.x), self.own_a),
                (piece_offset(q, self.y, k) + HALF, self.own_b),
            )):
                out.append(pltpu.make_async_copy(
                    self.flat.at[pl.ds(row, HALF)], own.at[own_slot, k], self.load_sem.at[slot, way, k]
                ))
            if ready is not None:
                ready_a, ready_b, at = ready
                for way, (src, dst) in enumerate(((ready_a, self.rx_a1), (ready_b, self.rx_b1))):
                    out.append(pltpu.make_async_copy(
                        src.at[at, k], dst.at[slot, k], self.load_sem.at[slot, 2 + way, k]
                    ))
        return out

    def second(self, slot):
        y, x = self.y, self.x
        return [
            pltpu.make_async_remote_copy(
                src_ref=src, dst_ref=dst.at[slot], send_sem=self.s2_send.at[slot, way],
                recv_sem=self.s2_recv.at[slot, way], device_id=near, device_id_type=MESH_ID,
            )
            for way, (src, dst, near) in enumerate((
                (self.rx_a1.at[slot, 1 - y], self.rx_a2, self.y_near),
                (self.rx_b1.at[slot, 1 - x], self.rx_b2, self.x_near),
            ))
        ]

    def meet(self, slot, own_slot):
        y, x = self.y, self.x
        rx_a1, rx_b1, own_a, own_b, acc = self.rx_a1, self.rx_b1, self.own_a, self.own_b, self.acc

        def away(rows):
            rx_a1[slot, 1 - y, rows] = rx_a1[slot, 1 - y, rows] + own_a[own_slot, 1 - y, rows]
            rx_b1[slot, 1 - x, rows] = rx_b1[slot, 1 - x, rows] + own_b[own_slot, 1 - x, rows]

        by_rows(away)
        for copy in self.second(slot):
            copy.start()

        def kept(rows):
            acc[slot, 0, rows] = rx_a1[slot, y, rows] + own_a[own_slot, y, rows]
            acc[slot, 1, rows] = rx_b1[slot, x, rows] + own_b[own_slot, x, rows]

        by_rows(kept)

    def join(self, slot):
        for copy in self.second(slot):
            copy.wait_recv()
        acc, rx_a2, rx_b2 = self.acc, self.rx_a2, self.rx_b2

        def add(rows):
            acc[slot, 0, rows] = acc[slot, 0, rows] + rx_a2[slot, rows]
            acc[slot, 1, rows] = acc[slot, 1, rows] + rx_b2[slot, rows]

        by_rows(add)


MIDDLE_EARLY = (7, 6, 4, 5)


def nn(a, b):
    return lax.dot_general(a, b, (((1,), (0,)), ((), ())), preferred_element_type=jnp.float32)


def nt(a, b):
    return lax.dot_general(a, b, (((1,), (1,)), ((), ())), preferred_element_type=jnp.float32)


def tn(a, b):
    return lax.dot_general(a, b, (((0,), (0,)), ((), ())), preferred_element_type=jnp.float32)


def head_lanes(value, h):
    lane = lax.broadcasted_iota(jnp.int32, (1, LANES), 1)
    return jnp.where(lane // 64 == h, value, jnp.zeros_like(value))


def plane_devices(dp, me):
    z, c = dp // 2, dp % 2
    near = [(2 * z + 1 - c, me)]
    for d in (1, 2, 3):
        near += [(2 * z, (me + d) % 4), (2 * z + 1, (me + d) % 4)]
    return near


def greet(devices):
    barrier = pltpu.get_barrier_semaphore()
    for near in devices:
        pl.semaphore_signal(barrier, inc=1, device_id=near, device_id_type=MESH_ID)
    pl.semaphore_wait(barrier, len(devices))


class Home:
    def __init__(self, rows, out, dp, me, send_sem, recv_sem):
        z, c = dp // 2, dp % 2
        self.here = c == me // 2
        self.turns = []
        for turn in range(2):
            src = rows.at[pl.ds(256 * turn, 256)]
            dst = out.at[me % 2]
            away = pltpu.make_async_remote_copy(
                src_ref=src, dst_ref=dst, send_sem=send_sem.at[turn], recv_sem=recv_sem.at[me % 2],
                device_id=(2 * z + me // 2, 2 * c + turn), device_id_type=MESH_ID,
            )
            near = pltpu.make_async_copy(src, dst, send_sem.at[turn])
            came = pltpu.make_async_remote_copy(
                src_ref=src, dst_ref=out.at[turn], send_sem=send_sem.at[turn],
                recv_sem=recv_sem.at[turn], device_id=(2 * z + me // 2, 2 * c + turn),
                device_id_type=MESH_ID,
            )
            self.turns.append((away, near, came, self.here & (me % 2 == turn)))

    def start(self):
        for away, near, _, stays in self.turns:
            @pl.when(stays)
            def _():
                near.start()

            @pl.when(jnp.logical_not(stays))
            def _():
                away.start()

    def wait(self):
        for away, near, came, stays in self.turns:
            @pl.when(stays)
            def _():
                near.wait()

            @pl.when(jnp.logical_not(stays))
            def _():
                away.wait_send()
                came.wait_recv()


def first_stage(q, flat, rx_a, rx_b, at, send_sem, recv_sem, dp, me):
    y, x = me // 2, me % 2
    x_near = (dp, 2 * y + (1 - x))
    y_near = (dp, 2 * (1 - y) + x)
    out = []
    for k in range(2):
        for way, (row, rx, near) in enumerate((
            (piece_offset(q, k, 1 - x), rx_a, x_near),
            (piece_offset(q, 1 - y, k) + HALF, rx_b, y_near),
        )):
            out.append(pltpu.make_async_remote_copy(
                src_ref=flat.at[pl.ds(row, HALF)], dst_ref=rx.at[at, k],
                send_sem=send_sem.at[at, way, k], recv_sem=recv_sem.at[at, way, k],
                device_id=near, device_id_type=MESH_ID,
            ))
    return out


def both_heads(value):
    return jnp.concatenate([head_lanes(value, 0), head_lanes(value, 1)], 0)


class Spread:
    def __init__(self, blocks, rows, dp, me, send_sem, recv_sem):
        z, c = dp // 2, dp % 2
        here = c == me // 2
        self.turns = []
        for turn in range(2):
            src = blocks.at[turn]
            dst = rows.at[pl.ds(pl.multiple_of(256 * me, 256), 256)]
            away = pltpu.make_async_remote_copy(
                src_ref=src, dst_ref=dst, send_sem=send_sem.at[turn], recv_sem=recv_sem.at[me % 2],
                device_id=(2 * z + me // 2, 2 * c + turn), device_id_type=MESH_ID,
            )
            near = pltpu.make_async_copy(src, dst, send_sem.at[turn])
            came = pltpu.make_async_remote_copy(
                src_ref=src, dst_ref=rows.at[pl.ds(pl.multiple_of(512 * c + 256 * turn, 256), 256)],
                send_sem=send_sem.at[turn], recv_sem=recv_sem.at[turn],
                device_id=(2 * z + me // 2, 2 * c + turn), device_id_type=MESH_ID,
            )
            self.turns.append((away, near, came, here & (me % 2 == turn)))

    def start(self):
        for away, near, _, stays in self.turns:
            @pl.when(stays)
            def _():
                near.start()

            @pl.when(jnp.logical_not(stays))
            def _():
                away.start()

    def wait_came(self, turn):
        _, near, came, stays = self.turns[turn]

        @pl.when(stays)
        def _():
            near.wait()

        @pl.when(jnp.logical_not(stays))
        def _():
            came.wait_recv()

    def wait_sent(self):
        for away, _, _, stays in self.turns:
            @pl.when(jnp.logical_not(stays))
            def _():
                away.wait_send()


def front_kernel(
    slopes, blocks, cot_blocks, segments, padding, gain_in, shift_in, bias_in, weight_hbm,
    x_out, cot_out, normed_out, joint_out, dist_out, att_out, lse_out,
    x_all, cot_all, normed, joint, weight, dist, att, lse, seg_rx, pad_rx, vectors, columns, s_ref, p_ref, vt_ref, ot_ref,
    weight_sem, out_sem, mark_sem, x_send, x_recv, cot_send, cot_recv, pass_send, pass_recv,
):
    f32, bf16 = jnp.float32, jnp.bfloat16
    dp = lax.axis_index("dp")
    me = lax.axis_index("group")
    c = dp % 2
    core_near = (dp + 1 - 2 * c, me)
    own = pl.ds(pl.multiple_of(512 * c, 512), 512)
    other = pl.ds(pl.multiple_of(512 * (1 - c), 512), 512)

    weights = [
        pltpu.make_async_copy(
            weight_hbm.at[:, pl.ds(pl.multiple_of(1024 * p + 512 * c, 512), 512)],
            weight.at[:, pl.ds(512 * p, 512)], weight_sem.at[p],
        )
        for p in range(3)
    ]
    greet(plane_devices(dp, me))
    x_way = Spread(blocks, x_all, dp, me, x_send, x_recv)
    cot_way = Spread(cot_blocks, cot_all, dp, me, cot_send, cot_recv)
    x_way.start()
    vectors[0:1, :] = gain_in[...].astype(f32).reshape(1, WIDTH)
    vectors[1:2, :] = shift_in[...].astype(f32).reshape(1, WIDTH)
    vectors[2:4, :] = bias_in[...].astype(f32).reshape(2, WIDTH)
    mark_swaps = [
        pltpu.make_async_remote_copy(
            src_ref=src, dst_ref=dst, send_sem=mark_sem.at[0, i], recv_sem=mark_sem.at[1, i],
            device_id=core_near, device_id_type=MESH_ID,
        )
        for i, (src, dst) in enumerate(((segments, seg_rx), (padding, pad_rx)))
    ]
    for copy in mark_swaps:
        copy.start()
    for copy in weights:
        copy.start()

    def hand_over(rows, way, turn):
        at = pl.ds(pl.multiple_of(512 * c + 256 * turn, 256), 256)
        return pltpu.make_async_remote_copy(
            src_ref=rows.at[at], dst_ref=rows.at[at], send_sem=pass_send.at[way, turn],
            recv_sem=pass_recv.at[way, turn], device_id=core_near, device_id_type=MESH_ID,
        )

    for copy in mark_swaps:
        copy.wait()
    odd = me % 2 == 1
    held = c == me // 2

    def row_of(mine, came):
        both = jnp.where(held, mine[...], came[...]).astype(f32)
        return jnp.where(odd, both[1:2], both[0:1])

    seg = row_of(segments, seg_rx)
    pad = row_of(padding, pad_rx)
    kind = lax.broadcasted_iota(jnp.int32, (8, TOKENS), 0)
    columns[...] = jnp.broadcast_to(
        jnp.where(kind == 0, seg, pad).T[:, :8].reshape(TOKENS, 8), (TOKENS, 8)
    )

    def dist_rows(i, carry):
        rows = pl.ds(pl.multiple_of(128 * i, 128), 128)
        key_seg, key_pad = columns[rows, 0:1], columns[rows, 1:2]
        key = (lax.broadcasted_iota(jnp.int32, (128, 1), 0) + 128 * i).astype(f32)
        query = lax.broadcasted_iota(jnp.int32, (128, TOKENS), 1).astype(f32)
        last = jnp.sum(jnp.where(seg <= key_seg, 1.0, 0.0), 1, keepdims=True) - 1.0
        last = jnp.where(key_pad == 1.0, last, key)
        dist[rows, :] = jnp.where((query >= key) & (query <= last), query - key, -masked_score)
        return carry

    lax.fori_loop(0, 8, dist_rows, 0)
    outs = []

    def put(src, dst):
        copy = pltpu.make_async_copy(src, dst, out_sem.at[len(outs)])
        copy.start()
        outs.append(copy)

    put(dist, dist_out)
    gain, shift = vectors[0:1, :], vectors[1:2, :]

    def norm_rows(half):
        def one(i, carry):
            rows = pl.ds(pl.multiple_of(512 * half + 128 * i, 128), 128)
            values = x_all[rows, :].astype(f32)
            center = values - jnp.mean(values, -1, keepdims=True)
            factor = lax.rsqrt(jnp.mean(center * center, -1, keepdims=True) + norm_epsilon)
            normed[rows, :] = (center * factor * gain + shift).astype(bf16)
            return carry

        lax.fori_loop(0, 4, one, 0)
        rows = pl.ds(pl.multiple_of(512 * half, 512), 512)
        lanes = pl.ds(pl.multiple_of(512 * c, 512), 512)
        made = nn(normed[rows, :], weight[...])
        joint[rows, 0:512] = ((made[:, 0:512] + vectors[2:3, lanes]) * 0.125).astype(bf16)
        joint[rows, 512:1024] = made[:, 512:1024].astype(bf16)
        joint[rows, 1024:1536] = (made[:, 1024:1536] + vectors[3:4, lanes]).astype(bf16)

    for turn in range(2):
        x_way.wait_came(turn)
        hand_over(x_all, 0, turn).start()
    x_way.wait_sent()
    cot_way.start()
    put(x_all.at[own], x_out)
    for copy in weights:
        copy.wait()
    norm_rows(c)
    for turn in range(2):
        hand_over(x_all, 0, turn).wait_recv()
    norm_rows(1 - c)
    put(normed, normed_out)
    put(joint, joint_out)

    def pair_step(pair, carry):
        def lanes(block):
            return pl.ds(pl.multiple_of(512 * block + LANES * pair, LANES), LANES)

        vt_ref[...] = joint[:, lanes(2)].astype(f32).T.astype(bf16)
        slope = [slopes[8 * c + 2 * pair + h] for h in range(2)]

        def scores(qb):
            cols = pl.ds(qb * 256, 256)
            queries = both_heads(joint[cols, lanes(0)])
            top = None
            for kb in range(qb + 1):
                rows = pl.ds(kb * 256, 256)
                raw = nt(joint[rows, lanes(1)], queries)
                far = dist[rows, cols]
                parts = [raw[:, 256 * h : 256 * h + 256] - slope[h] * far for h in range(2)]
                for h in range(2):
                    s_ref[qb % 2, rows, 256 * h : 256 * h + 256] = parts[h]
                high = jnp.concatenate([jnp.max(part, 0, keepdims=True) for part in parts], 1)
                top = high if top is None else jnp.maximum(top, high)
            return top

        def weigh(qb, top):
            cols = pl.ds(qb * 256, 256)
            span = pl.ds(0, 256 * (qb + 1))
            total = None
            for kb in range(qb + 1):
                rows = pl.ds(kb * 256, 256)
                p = jnp.exp(s_ref[qb % 2, rows, :] - top)
                more = jnp.sum(p, 0, keepdims=True)
                total = more if total is None else total + more
                p_ref[qb % 2, rows, :] = p.astype(bf16)
            out = nn(vt_ref[:, span], p_ref[qb % 2, span, :]) / total
            ot_ref[0:64, cols] = out[0:64, 0:256]
            ot_ref[64:128, cols] = out[64:128, 256:512]
            row = top + jnp.log(total)
            for h in range(2):
                lse[pair, h : h + 1, cols] = row[:, 256 * h : 256 * h + 256]

        top = scores(0)
        for qb in range(4):
            after = scores(qb + 1) if qb < 3 else None
            weigh(qb, top)
            top = after
        att[:, lanes(0)] = ot_ref[...].T.astype(bf16)

        @pl.when(pair == 2)
        def _():
            for turn in range(2):
                cot_way.wait_came(turn)
                hand_over(cot_all, 1, turn).start()

        return carry

    lax.fori_loop(0, 4, pair_step, 0)
    put(att, att_out)
    put(lse, lse_out)
    for turn in range(2):
        hand_over(cot_all, 1, turn).wait()
        hand_over(x_all, 0, turn).wait_send()
    put(cot_all, cot_out)
    cot_way.wait_sent()
    for copy in outs:
        copy.wait()


def front(slopes, blocks, cot_blocks, segments, padding, gain, shift, bias, weight):
    f32, bf16 = jnp.float32, jnp.bfloat16
    vmem = pl.BlockSpec(memory_space=pltpu.VMEM)
    hbm = pl.BlockSpec(memory_space=pl.ANY)
    return pl.pallas_call(
        front_kernel,
        out_shape=(
            jax.ShapeDtypeStruct((512, WIDTH), bf16),
            jax.ShapeDtypeStruct((TOKENS, WIDTH), bf16),
            jax.ShapeDtypeStruct((TOKENS, WIDTH), bf16),
            jax.ShapeDtypeStruct((TOKENS, 1536), bf16),
            jax.ShapeDtypeStruct((TOKENS, TOKENS), f32),
            jax.ShapeDtypeStruct((TOKENS, 512), bf16),
            jax.ShapeDtypeStruct((4, 2, TOKENS), f32),
        ),
        in_specs=[pl.BlockSpec(memory_space=pltpu.SMEM)] + [hbm] * 2 + [vmem] * 5 + [hbm],
        out_specs=[hbm] * 7,
        scratch_shapes=[
            pltpu.VMEM((TOKENS, WIDTH), bf16),
            pltpu.VMEM((TOKENS, WIDTH), bf16),
            pltpu.VMEM((TOKENS, WIDTH), bf16),
            pltpu.VMEM((TOKENS, 1536), bf16),
            pltpu.VMEM((WIDTH, 1536), bf16),
            pltpu.VMEM((TOKENS, TOKENS), f32),
            pltpu.VMEM((TOKENS, 512), bf16),
            pltpu.VMEM((4, 2, TOKENS), f32),
            pltpu.VMEM((2, TOKENS), jnp.int32),
            pltpu.VMEM((2, TOKENS), jnp.int32),
            pltpu.VMEM((8, WIDTH), f32),
            pltpu.VMEM((TOKENS, 8), f32),
            pltpu.VMEM((2, TOKENS, 512), f32),
            pltpu.VMEM((2, TOKENS, 512), bf16),
            pltpu.VMEM((LANES, TOKENS), bf16),
            pltpu.VMEM((LANES, TOKENS), f32),
            pltpu.SemaphoreType.DMA((3,)),
            pltpu.SemaphoreType.DMA((7,)),
            pltpu.SemaphoreType.DMA((2, 2)),
            pltpu.SemaphoreType.DMA((2,)),
            pltpu.SemaphoreType.DMA((2,)),
            pltpu.SemaphoreType.DMA((2,)),
            pltpu.SemaphoreType.DMA((2,)),
            pltpu.SemaphoreType.DMA((2, 2)),
            pltpu.SemaphoreType.DMA((2, 2)),
        ],
        compiler_params=pltpu.CompilerParams(
            collective_id=0, has_side_effects=True, vmem_limit_bytes=62 << 20
        ),
        cost_estimate=pl.CostEstimate(flops=10 << 30, bytes_accessed=20 << 20, transcendentals=0),
    )(slopes, blocks, cot_blocks, segments, padding, gain, shift, bias, weight)


PLAN = (
    ("greet",), ("i1", 3), ("load",), ("meet", 5), ("a0",), ("a1",), ("meet", 3), ("meet", 6), ("a2",),
    ("meet", 4), ("a3",), ("join", 5), ("meet", 7), ("hop", 5, 0), ("J",), ("i1", 0), ("join", 7),
    ("join", 4), ("dnp",), ("hop", 7, 0), ("hop", 5, 1), ("join", 6), ("join", 3), ("dno",), ("i1", 1),
    ("hop", 4, 0), ("meet", 0), ("hop", 3, 0), ("hop", 7, 1), ("meet", 1), ("join", 0), ("hop", 0, 0),
    ("i1", 2), ("hop", 3, 1), ("hop", 6, 0), ("join", 1), ("hop", 1, 0), ("hop", 0, 1), ("hop", 4, 1),
    ("meet", 2), ("ln",), ("home", "i"), ("hop", 7, 2), ("hop", 6, 1), ("hop", 1, 1), ("join", 2),
    ("hop", 2, 0), ("hop", 0, 2), ("fin", 3), ("fin", 5), ("fin", 7), ("home", "o"), ("hop", 6, 2),
    ("fin", 4), ("hop", 2, 1), ("hop", 1, 2), ("fin", 6), ("fin", 2), ("fin", 0), ("fin", 1), ("end",),
)


def rear_kernel(
    slopes, joint_hbm, att_hbm, datt_hbm, dist_hbm, lse, normed_hbm, weight_hbm, x_hbm, dresid_hbm,
    result, mid_sums, expand_sums, mid_a, mid_b, flat_in,
    flat, own_out, peer_out, small_out, output, input_gradient,
    joint, attended, dattended, normed, weight, x_own, dresid,
    dist, p_ref, ds_ref, kt_ref, dqt_ref, dk_acc, dv_acc, delta_ref, djoint, dn_rx, dinput, blocks,
    own_a, own_b, rx_a1, rx_b1, rx_a2, rx_b2, acc, rx_up, rx_dn, parting,
    small_mine, small_rx, small_z,
    dist_sem, block_sem, swap_sem, load_sem, s1_send, s1_recv, s2_send, s2_recv, z_send, z_recv,
    last_sem, sm_send, sm_recv, out_send, out_recv, in_send, in_recv,
):
    f32, bf16 = jnp.float32, jnp.bfloat16
    dp = lax.axis_index("dp")
    me = lax.axis_index("group")
    z, c = dp // 2, dp % 2
    y, x = me // 2, me % 2
    x_near = (dp, 2 * y + (1 - x))
    y_near = (dp, 2 * (1 - y) + x)
    core_near = (2 * z + 1 - c, me)
    own = pl.ds(pl.multiple_of(512 * c, 512), 512)
    other = pl.ds(pl.multiple_of(512 * (1 - c), 512), 512)

    def z_at(d):
        return (2 * d + c, me)

    pieces = Pieces(
        dp, me, flat, own_a, own_b, rx_a1, rx_b1, rx_a2, rx_b2, acc, load_sem, s2_send, s2_recv
    )
    meets = [step[1] for step in PLAN if step[0] == "meet"]
    own_slot = {q: at % 4 for at, q in enumerate(meets)}
    loaded, met = [], []

    def load_ahead(joint_done):
        for q in meets[: len(met) + 4]:
            if q not in loaded and (joint_done or q > 1):
                loaded.append(q)
                start(loads(q))

    def loads(q):
        ready = (mid_a, mid_b, MIDDLE_EARLY.index(q)) if q in MIDDLE_EARLY else None
        return pieces.loads(q, own_slot[q], ready)

    def start(copies):
        for copy in copies:
            copy.start()

    def stage1(q):
        return first_stage(q, flat, rx_a1, rx_b1, q, s1_send, s1_recv, dp, me)

    def hop(q, up, half):
        way = 0 if up else 1
        return pltpu.make_async_remote_copy(
            src_ref=acc.at[q, half], dst_ref=rx_up.at[q - 2, half] if up else rx_dn.at[q, half],
            send_sem=z_send.at[q, way, half], recv_sem=z_recv.at[q, way, half],
            device_id=z_at((z + 1) % 4 if up else (z + 3) % 4), device_id_type=MESH_ID,
        )

    def meet(q):
        for copy in loads(q):
            copy.wait()
        if q not in MIDDLE_EARLY:
            for copy in stage1(q):
                copy.wait_recv()
        pieces.meet(q, own_slot[q])

    def add_came(q, rx, at, half):
        def add(rows):
            acc[q, half, rows] = acc[q, half, rows] + rx[at, half, rows]

        by_rows(add)

    on_way = {(plane, up): [] for plane in range(4) for up in (False, True)}

    def send_on(plane, q, up, half):
        queue = on_way[plane, up]
        if len(queue) >= 2:
            hop(*queue[-2]).wait_send()
        hop(q, up, half).start()
        queue.append((q, up, half))

    def pass_on(q, h):
        aim = q // 2
        if h < aim:
            @pl.when(z == h)
            def _():
                for half in range(2):
                    if h > 0:
                        hop(q, True, half).wait_recv()
                        add_came(q, rx_up, q - 2, half)
                    send_on(h, q, True, half)
        if h < 3 - aim:
            @pl.when(z == 3 - h)
            def _():
                for half in range(2):
                    if h > 0:
                        hop(q, False, half).wait_recv()
                        add_came(q, rx_dn, q, half)
                    send_on(3 - h, q, False, half)

    last = pltpu.make_async_remote_copy(
        src_ref=parting, dst_ref=peer_out, send_sem=last_sem.at[0], recv_sem=last_sem.at[1],
        device_id=core_near, device_id_type=MESH_ID,
    )

    def finish(q):
        aim = q // 2

        @pl.when(z == aim)
        def _():
            mine = c == q % 2
            for k in range(2):
                if aim > 0:
                    hop(q, True, k).wait_recv()
                if aim < 3:
                    hop(q, False, k).wait_recv()

                def add(i, carry):
                    rows = pl.ds(pl.multiple_of(112 * i, 16), 112)
                    place = pl.ds(pl.multiple_of(HALF * k + 112 * i, 16), 112)
                    total = acc[q, k, rows].astype(f32)
                    if aim > 0:
                        total = total + rx_up[q - 2, k, rows].astype(f32)
                    if aim < 3:
                        total = total + rx_dn[q, k, rows].astype(f32)

                    @pl.when(mine)
                    def _():
                        own_out[place] = total

                    @pl.when(jnp.logical_not(mine))
                    def _():
                        parting[place] = total

                    return carry

                lax.fori_loop(0, HALF // 112, add, 0)

            @pl.when(jnp.logical_not(mine))
            def _():
                last.start()

    def small_step(k):
        near = (core_near, x_near, y_near)[k]
        return pltpu.make_async_remote_copy(
            src_ref=small_mine.at[k], dst_ref=small_rx.at[k], send_sem=sm_send.at[k],
            recv_sem=sm_recv.at[k], device_id=near, device_id_type=MESH_ID,
        )

    def small_next(k):
        small_step(k).wait()
        small_mine[k + 1] = small_mine[k] + small_rx[k]
        if k < 2:
            small_step(k + 1).start()

    def small_hop(d):
        return pltpu.make_async_remote_copy(
            src_ref=small_mine.at[3], dst_ref=small_z.at[d - 1], send_sem=sm_send.at[2 + d],
            recv_sem=sm_recv.at[2 + d], device_id=z_at((z + d) % 4), device_id_type=MESH_ID,
        )

    def load(i, src, dst):
        return pltpu.make_async_copy(src, dst, dist_sem.at[i])

    first_loads = [
        load(0, joint_hbm, joint), load(1, att_hbm, attended), load(2, datt_hbm, dattended),
        load(3, dist_hbm, dist),
    ]
    later_loads = [load(4, normed_hbm, normed), load(5, x_hbm, x_own), load(6, dresid_hbm, dresid)]
    for p in range(3):
        later_loads.append(load(
            7 + p, weight_hbm.at[:, pl.ds(pl.multiple_of(1024 * p + 512 * c, 512), 512)],
            weight.at[:, pl.ds(512 * p, 512)],
        ))
    way_out = Home(result, output, dp, me, out_send, out_recv)
    way_in = Home(dinput, input_gradient, dp, me, in_send, in_recv)
    joint_done = []
    small_left = []

    def small_end():
        for d in (1, 2, 3):
            small_hop(d).start()

    def move(step):
        kind, *at = step
        if kind == "i1":
            start(stage1(at[0]))
        elif kind == "meet":
            meet(at[0])
            met.append(at[0])
            load_ahead(bool(joint_done))
        elif kind == "join":
            pieces.join(at[0])
        elif kind == "hop":
            pass_on(*at)
        elif kind == "fin":
            finish(at[0])
        elif kind == "home":
            (way_out if at[0] == "o" else way_in).start()
        else:
            compute[kind]()
        if small_left:
            wait = small_left.pop(0)
            if wait is not None:
                wait()

    names = [step[0] for step in PLAN]
    attention = [names.index(name) for name in ("a0", "a1", "a2", "a3")]

    def go_on(pair):
        for turn in range(3):
            @pl.when(pair == turn)
            def _():
                if turn == 0:
                    start(later_loads)
                for step in PLAN[attention[turn] + 1 : attention[turn + 1]]:
                    move(step)

    def greet_all():
        start(first_loads)
        load_ahead(False)
        greet(plane_devices(dp, me) + [z_at((z + d) % 4) for d in (1, 2, 3)])

    def wait_loads():
        for copy in first_loads:
            copy.wait()

    compute = {"greet": greet_all, "load": wait_loads}
    for step in PLAN[: attention[0]]:
        move(step)


    def pair_step(pair, carry):
        def lanes(block):
            return pl.ds(pl.multiple_of(512 * block + LANES * pair, LANES), LANES)

        here = lanes(0)
        kt_ref[...] = joint[:, lanes(1)].astype(f32).T.astype(bf16)
        product = (attended[:, here].astype(f32) * dattended[:, here].astype(f32)).T
        delta_ref[0:1, :] = jnp.sum(product[:64], 0, keepdims=True)
        delta_ref[1:2, :] = jnp.sum(product[64:], 0, keepdims=True)
        dk_acc[...] = jnp.zeros_like(dk_acc)
        dv_acc[...] = jnp.zeros_like(dv_acc)
        slope = [slopes[8 * c + 2 * pair + h] for h in range(2)]

        def pairs_of(qb):
            cols = pl.ds(qb * 256, 256)
            queries = both_heads(joint[cols, here])
            grads = both_heads(dattended[cols, here])
            for kb in range(qb + 1):
                rows = pl.ds(kb * 256, 256)
                raw = nt(joint[rows, lanes(1)], queries)
                dprobs = nt(joint[rows, lanes(2)], grads)
                far = dist[rows, cols]
                for h in range(2):
                    side = slice(256 * h, 256 * h + 256)
                    p = jnp.exp(raw[:, side] - slope[h] * far - lse[pair, h : h + 1, cols])
                    p_ref[qb % 2, rows, side] = p.astype(bf16)
                    ds_ref[qb % 2, rows, side] = (
                        p * (dprobs[:, side] - delta_ref[h : h + 1, cols])
                    ).astype(bf16)

        def sums_of(qb):
            cols = pl.ds(qb * 256, 256)
            span = pl.ds(0, 256 * (qb + 1))
            dv_acc[span, :] += nn(p_ref[qb % 2, span, :], both_heads(dattended[cols, here]))
            dk_acc[span, :] += nn(ds_ref[qb % 2, span, :], both_heads(joint[cols, here]))
            dq = nn(kt_ref[:, span], ds_ref[qb % 2, span, :])
            dqt_ref[0:64, cols] = dq[0:64, 0:256]
            dqt_ref[64:128, cols] = dq[64:128, 256:512]

        pairs_of(0)
        for qb in range(4):
            if qb < 3:
                pairs_of(qb + 1)
            sums_of(qb)
        djoint[:, lanes(0)] = (dqt_ref[...] * 0.125).T.astype(bf16)
        djoint[:, lanes(1)] = dk_acc[...].astype(bf16)
        djoint[:, lanes(2)] = dv_acc[...].astype(bf16)
        go_on(pair)
        return carry

    lax.fori_loop(0, 4, pair_step, 0)

    def block_copy(slot, i):
        return pltpu.make_async_copy(
            blocks.at[slot], flat.at[pl.ds(JOINT_AT + 3072 * i, 3072)], block_sem.at[slot]
        )

    def joint_gradient():
        for copy in later_loads:
            copy.wait()
        for i in range(4):
            if i >= 2:
                block_copy(i % 2, i - 2).wait()
            block = tn(normed[:, 256 * i : 256 * i + 256], djoint[...]).astype(bf16)
            blocks[i % 2] = block.reshape(3072, LANES)
            block_copy(i % 2, i).start()
        for i in (2, 3):
            block_copy(i % 2, i).wait()
        joint_done.append(True)
        load_ahead(True)

    dn_own, dn_part = dist.at[pl.ds(0, 512)], dist.at[pl.ds(512, 512)]
    dn_swap = pltpu.make_async_remote_copy(
        src_ref=dn_part, dst_ref=dn_rx, send_sem=swap_sem.at[0], recv_sem=swap_sem.at[1],
        device_id=core_near, device_id_type=MESH_ID,
    )

    def norm_part():
        dn_part[...] = nt(djoint[other, :], weight[...])
        dn_swap.start()

    def norm_own():
        dn_own[...] = nt(djoint[own, :], weight[...])
        bias_sums = nn(jnp.ones((8, TOKENS), bf16), djoint[...])
        half = pl.ds(pl.multiple_of(512 * c, 512), 512)
        small_mine[0] = jnp.zeros(small_mine.shape[1:], f32)
        small_mine[0, 2:3, half] = bias_sums[0:1, :512]
        small_mine[0, 3:4, half] = bias_sums[0:1, 1024:]
        small_mine[0, 4:7, :] = mid_sums[0:3, :]
        small_mine[0, 7:11, half] = expand_sums[...]
        small_mine[0, 11:12, :] = mid_sums[3:4, :]

    def norm_back_rows():
        dn_swap.wait()

        def back_rows(i, carry):
            rows = pl.ds(pl.multiple_of(128 * i, 128), 128)
            values = x_own[rows, :].astype(f32)
            center = values - jnp.mean(values, -1, keepdims=True)
            factor = lax.rsqrt(jnp.mean(center * center, -1, keepdims=True) + norm_epsilon)
            unit = center * factor
            dn = dn_own[rows, :] + dn_rx[rows, :]
            e = dn * mid_sums[4:5, :]
            down = dresid[rows, :] + factor * (
                e - jnp.mean(e, -1, keepdims=True) - unit * jnp.mean(e * unit, -1, keepdims=True)
            )
            dinput[rows, :] = down.astype(bf16)
            small_mine[0, 0:1, :] += jnp.sum(dn * unit, 0, keepdims=True)
            small_mine[0, 1:2, :] += jnp.sum(dn, 0, keepdims=True)
            return carry

        lax.fori_loop(0, 4, back_rows, 0)
        small_step(0).start()
        for k in range(3):
            small_left.extend([None, None, functools.partial(small_next, k)])
        small_left.append(small_end)

    def rest_of_small():
        while small_left:
            wait = small_left.pop(0)
            if wait is not None:
                wait()
        for d in (1, 2, 3):
            small_hop(d).wait()

    compute.update(
        J=joint_gradient, dnp=norm_part, dno=norm_own, ln=norm_back_rows, end=rest_of_small
    )
    for step in PLAN[attention[3] + 1 :]:
        move(step)
    small = (small_mine[3] + small_z[1]) + (small_z[0] + small_z[2])
    small_out[...] = small.reshape(small_out.shape)

    last.wait()
    way_out.wait()
    way_in.wait()
    for q in sorted(set(range(8)) - set(MIDDLE_EARLY)):
        for copy in stage1(q):
            copy.wait_send()
    for q in range(8):
        for copy in pieces.second(q):
            copy.wait_send()
    for (plane, _), queue in on_way.items():
        @pl.when(z == plane)
        def _():
            for sent in queue[-2:]:
                hop(*sent).wait_send()


def rear(
    slopes, joint, attended, dattended, dist, lse, normed, weight, x_own, dresid, result,
    mid_sums, expand_sums, mid_a, mid_b, flat,
):
    f32, bf16 = jnp.float32, jnp.bfloat16
    vmem = pl.BlockSpec(memory_space=pltpu.VMEM)
    hbm = pl.BlockSpec(memory_space=pl.ANY)
    home = jax.ShapeDtypeStruct((2, 256, WIDTH), bf16)
    piece = jax.ShapeDtypeStruct((PIECE, LANES), f32)
    return pl.pallas_call(
        rear_kernel,
        out_shape=(
            jax.ShapeDtypeStruct((FLAT_ROWS, LANES), bf16),
            piece,
            piece,
            jax.ShapeDtypeStruct((LANES, LANES), f32),
            home,
            home,
        ),
        in_specs=[pl.BlockSpec(memory_space=pltpu.SMEM)] + [hbm] * 4 + [vmem] + [hbm] * 5
        + [vmem] * 2 + [hbm] * 3,
        out_specs=[hbm] + [vmem] * 3 + [hbm] * 2,
        scratch_shapes=[
            pltpu.VMEM((TOKENS, 1536), bf16),
            pltpu.VMEM((TOKENS, 512), bf16),
            pltpu.VMEM((TOKENS, 512), bf16),
            pltpu.VMEM((TOKENS, WIDTH), bf16),
            pltpu.VMEM((WIDTH, 1536), bf16),
            pltpu.VMEM((512, WIDTH), bf16),
            pltpu.VMEM((512, WIDTH), f32),
            pltpu.VMEM((TOKENS, TOKENS), f32),
            pltpu.VMEM((2, TOKENS, 512), bf16),
            pltpu.VMEM((2, TOKENS, 512), bf16),
            pltpu.VMEM((LANES, TOKENS), bf16),
            pltpu.VMEM((LANES, TOKENS), f32),
            pltpu.VMEM((TOKENS, LANES), f32),
            pltpu.VMEM((TOKENS, LANES), f32),
            pltpu.VMEM((8, TOKENS), f32),
            pltpu.VMEM((TOKENS, 1536), bf16),
            pltpu.VMEM((512, WIDTH), f32),
            pltpu.VMEM((512, WIDTH), bf16),
            pltpu.VMEM((2, 3072, LANES), bf16),
            pltpu.VMEM((4, 2, HALF, LANES), bf16),
            pltpu.VMEM((4, 2, HALF, LANES), bf16),
            pltpu.VMEM((8, 2, HALF, LANES), bf16),
            pltpu.VMEM((8, 2, HALF, LANES), bf16),
            pltpu.VMEM((8, HALF, LANES), bf16),
            pltpu.VMEM((8, HALF, LANES), bf16),
            pltpu.VMEM((8, 2, HALF, LANES), bf16),
            pltpu.VMEM((6, 2, HALF, LANES), bf16),
            pltpu.VMEM((6, 2, HALF, LANES), bf16),
            pltpu.VMEM((PIECE, LANES), f32),
            pltpu.VMEM((4, 16, WIDTH), f32),
            pltpu.VMEM((3, 16, WIDTH), f32),
            pltpu.VMEM((3, 16, WIDTH), f32),
            pltpu.SemaphoreType.DMA((10,)),
            pltpu.SemaphoreType.DMA((2,)),
            pltpu.SemaphoreType.DMA((2,)),
            pltpu.SemaphoreType.DMA((8, 4, 2)),
            pltpu.SemaphoreType.DMA((8, 2, 2)),
            pltpu.SemaphoreType.DMA((8, 2, 2)),
            pltpu.SemaphoreType.DMA((8, 2)),
            pltpu.SemaphoreType.DMA((8, 2)),
            pltpu.SemaphoreType.DMA((8, 2, 2)),
            pltpu.SemaphoreType.DMA((8, 2, 2)),
            pltpu.SemaphoreType.DMA((2,)),
            pltpu.SemaphoreType.DMA((6,)),
            pltpu.SemaphoreType.DMA((6,)),
            pltpu.SemaphoreType.DMA((2,)),
            pltpu.SemaphoreType.DMA((2,)),
            pltpu.SemaphoreType.DMA((2,)),
            pltpu.SemaphoreType.DMA((2,)),
        ],
        input_output_aliases={15: 0},
        compiler_params=pltpu.CompilerParams(
            collective_id=2, has_side_effects=True, vmem_limit_bytes=62 << 20
        ),
        cost_estimate=pl.CostEstimate(flops=30 << 30, bytes_accessed=30 << 20, transcendentals=0),
    )(
        slopes, joint, attended, dattended, dist, lse, normed, weight, x_own, dresid, result,
        mid_sums, expand_sums, mid_a, mid_b, flat,
    )


def middle_kernel(
    attended, x_own, cot, mixer_bias_in, gain_in, shift_in, reduce_bias_in, expand_bias_in, gain_before_in,
    mixer_hbm, expand_hbm, reduce_hbm,
    result, dresid, dattended, sums, expand_sums, flat, rx_a, rx_b,
    vectors, mixer, expand, reduce, att_rx, resid, normal, spread, normed, act, act_rx, dhidden,
    dn_own, dn_part, dn_rx, out_part, out_rx, dbranch, blocks,
    weight_sem, block_sem, send_sem, recv_sem, act_send, act_recv, s1_send, s1_recv,
):
    f32, bf16 = jnp.float32, jnp.bfloat16
    dp = lax.axis_index("dp")
    me = lax.axis_index("group")
    c = dp % 2
    near = (dp + 1 - 2 * c, me)
    own = pl.ds(pl.multiple_of(512 * c, 512), 512)
    other = pl.ds(pl.multiple_of(512 * (1 - c), 512), 512)

    weights = [pltpu.make_async_copy(mixer_hbm, mixer, weight_sem.at[0])]
    for k in range(4):
        part = pl.ds(pl.multiple_of(512 * (2 * k + c), 512), 512)
        weights.append(pltpu.make_async_copy(
            expand_hbm.at[:, part], expand.at[:, pl.ds(512 * k, 512)], weight_sem.at[1 + k]
        ))
    for k in range(4):
        part = pl.ds(pl.multiple_of(512 * (2 * k + c), 512), 512)
        weights.append(pltpu.make_async_copy(
            reduce_hbm.at[part], reduce.at[pl.ds(512 * k, 512)], weight_sem.at[5 + k]
        ))
    for copy in weights:
        copy.start()

    y, x = me // 2, me % 2
    greet([near, (dp, 2 * y + 1 - x), (dp, 2 * (1 - y) + x)])

    def swap(i, src, dst):
        return pltpu.make_async_remote_copy(
            src_ref=src, dst_ref=dst, send_sem=send_sem.at[i], recv_sem=recv_sem.at[i],
            device_id=near, device_id_type=MESH_ID,
        )

    att_swap = swap(0, attended, att_rx)
    normed_swap = swap(1, normed.at[own], normed.at[own])
    dn_swap = swap(2, dn_part, dn_rx)
    out_swap = swap(3, out_part, out_rx)
    branch_swap = swap(4, dbranch.at[own], dbranch.at[own])
    att_swap.start()

    for k, given in enumerate((mixer_bias_in, gain_in, shift_in, reduce_bias_in)):
        vectors[k : k + 1, :] = given[...].astype(f32).reshape(1, WIDTH)
    vectors[4:8, :] = expand_bias_in[...].astype(f32).reshape(4, WIDTH)
    mixer_bias, gain, shift, reduce_bias = (vectors[k : k + 1, :] for k in range(4))

    weights[0].wait()
    resid[...] = nn(attended[own, :], mixer[own, :]) + (x_own[...].astype(f32) + mixer_bias)
    att_swap.wait_recv()
    resid[...] += nn(att_rx[own, :], mixer[other, :])

    def norm_rows(i, carry):
        rows = pl.ds(pl.multiple_of(128 * i, 128), 128)
        here = pl.ds(pl.multiple_of(512 * c + 128 * i, 128), 128)
        values = resid[rows, :]
        center = values - jnp.mean(values, -1, keepdims=True)
        factor = lax.rsqrt(jnp.mean(center * center, -1, keepdims=True) + norm_epsilon)
        unit = center * factor
        normal[rows, :] = unit
        spread[rows, :] = jnp.broadcast_to(factor, (128, LANES))
        normed[here, :] = (unit * gain + shift).astype(bf16)
        return carry

    lax.fori_loop(0, 4, norm_rows, 0)
    normed_swap.start()

    def act_swap(half, k):
        rows = pl.ds(pl.multiple_of(512 * half, 512), 512)
        cols = pl.ds(pl.multiple_of(512 * k, 512), 512)
        return pltpu.make_async_remote_copy(
            src_ref=act.at[rows, cols], dst_ref=act_rx.at[rows, cols],
            send_sem=act_send.at[half, k], recv_sem=act_recv.at[half, k],
            device_id=near, device_id_type=MESH_ID,
        )

    root = math.sqrt(2.0 / math.pi)
    right = pl.ds(pl.multiple_of(512 * c, 512), 512)

    def products(half, k):
        rows = pl.ds(pl.multiple_of(512 * half, 512), 512)
        cols = pl.ds(pl.multiple_of(512 * k, 512), 512)
        u = nn(normed[rows, :], expand[:, cols]) + vectors[pl.ds(4 + k, 1), right]
        return u, nt(cot[rows, :], reduce[cols, :])

    def gelu_block(half, k, first, u, dact):
        rows = pl.ds(pl.multiple_of(512 * half, 512), 512)
        cols = pl.ds(pl.multiple_of(512 * k, 512), 512)
        square = u * u
        t = jnp.tanh(u * (root + (root * 0.044715) * square))
        up = 0.5 + 0.5 * t
        act[rows, cols] = (u * up).astype(bf16)
        slope = up + (0.5 * u) * (1.0 - t * t) * (root + (3.0 * root * 0.044715) * square)
        dh = (dact * slope).astype(bf16)
        dhidden[rows, cols] = dh
        total = jnp.sum(dh.astype(f32), 0, keepdims=True)
        if first:
            expand_sums[pl.ds(k, 1), :] = total
        else:
            expand_sums[pl.ds(k, 1), :] += total
        act_swap(half, k).start()

    def out_copies(slot, places):
        return [
            pltpu.make_async_copy(
                blocks.at[slot, pl.ds(2048 * part, 2048)],
                flat.at[pl.ds(pl.multiple_of(at, 16), 2048)], block_sem.at[slot, part],
            )
            for part, at in enumerate(places)
        ]

    def emit(block, slot, places):
        blocks[slot, : 2048 * len(places)] = block.astype(bf16).reshape(2048 * len(places), LANES)
        for copy in out_copies(slot, places):
            copy.start()

    def drain(slot, places):
        for copy in out_copies(slot, places):
            copy.wait()

    for copy in weights[1:]:
        copy.wait()

    def reduce_places(pair, parity):
        return [REDUCE_AT + 2048 * (2 * (2 * pair + k) + parity) for k in range(2)]

    stages = [
        first_stage(q, flat, rx_a, rx_b, at, s1_send, s1_recv, dp, me)
        for at, q in enumerate(MIDDLE_EARLY)
    ]

    def hidden_pair(turn, carry):
        pair = 1 - turn
        k = [2 * pair, 2 * pair + 1]
        a = products(c, k[0])
        b = products(c, k[1])
        gelu_block(c, k[0], True, *a)

        @pl.when(turn == 0)
        def _():
            normed_swap.wait_recv()

        @pl.when(turn == 1)
        def _():
            drain(0, reduce_places(1, c))
            drain(1, reduce_places(1, 1 - c))
            for copy in stages[0]:
                copy.start()

        a = products(1 - c, k[0])
        gelu_block(c, k[1], True, *b)
        b = products(1 - c, k[1])
        gelu_block(1 - c, k[0], False, *a)
        gelu_block(1 - c, k[1], False, *b)
        left = pl.ds(pl.multiple_of(1024 * pair, 1024), 1024)
        emit(tn(act[:, left], cot[:, right]), 0, reduce_places(pair, c))
        for half in range(2):
            for one in k:
                act_swap(half, one).wait()
        emit(tn(act_rx[:, left], cot[:, right]), 1, reduce_places(pair, 1 - c))
        return carry

    lax.fori_loop(0, 2, hidden_pair, 0)
    drain(0, reduce_places(0, c))
    drain(1, reduce_places(0, 1 - c))
    for copy in stages[1]:
        copy.start()

    def expand_places(i):
        return [EXPAND_AT + 4096 * i, EXPAND_AT + 4096 * i + 2048]

    def expand_step(i, carry):
        block = tn(normed[:, pl.ds(pl.multiple_of(256 * i, 256), 256)], dhidden[...])

        @pl.when(i >= 2)
        def _():
            drain(i % 2, expand_places(i - 2))

        emit(block, i % 2, expand_places(i))
        return carry

    lax.fori_loop(0, 4, expand_step, 0)
    drain(0, expand_places(2))
    drain(1, expand_places(3))
    for copies in stages[2:]:
        for copy in copies:
            copy.start()

    dn_part[...] = nt(dhidden[other, :], expand[...])
    dn_swap.start()
    out_part[...] = nn(act[other, :], reduce[...]).astype(bf16)
    out_swap.start()

    dn_own[...] = nt(dhidden[own, :], expand[...])
    dn_swap.wait()
    sums[...] = jnp.zeros_like(sums)
    sums[4:5, :] = gain_before_in[...].astype(f32).reshape(1, WIDTH)

    def back_rows(i, carry):
        rows = pl.ds(pl.multiple_of(128 * i, 128), 128)
        here = pl.ds(pl.multiple_of(512 * c + 128 * i, 128), 128)
        dn = dn_own[rows, :] + dn_rx[rows, :]
        unit = normal[rows, :]
        grad = cot[here, :].astype(f32)
        e = dn * gain
        down = grad + spread[rows, 0:1] * (
            e - jnp.mean(e, -1, keepdims=True) - unit * jnp.mean(e * unit, -1, keepdims=True)
        )
        dresid[rows, :] = down
        low = down.astype(bf16)
        dbranch[here, :] = low
        sums[0:1, :] += jnp.sum(low.astype(f32), 0, keepdims=True)
        sums[1:2, :] += jnp.sum(dn * unit, 0, keepdims=True)
        sums[2:3, :] += jnp.sum(dn, 0, keepdims=True)
        sums[3:4, :] += jnp.sum(grad, 0, keepdims=True)
        return carry

    lax.fori_loop(0, 4, back_rows, 0)
    branch_swap.start()
    dattended[own, :] = nt(dbranch[own, :], mixer[own, :]).astype(bf16)
    resid[...] += nn(act[own, :], reduce[...])
    out_swap.wait()
    result[...] = (resid[...] + (out_rx[...].astype(f32) + reduce_bias)).astype(bf16)
    branch_swap.wait()
    dattended[other, :] = nt(dbranch[other, :], mixer[own, :]).astype(bf16)
    emit(tn(attended[...], dbranch[:, right]), 0, [MIXER_AT + 2048 * c])
    emit(tn(att_rx[...], dbranch[:, right]), 1, [MIXER_AT + 2048 * (1 - c)])
    drain(0, [MIXER_AT + 2048 * c])
    drain(1, [MIXER_AT + 2048 * (1 - c)])
    att_swap.wait_send()
    normed_swap.wait_send()
    for copies in stages:
        for copy in copies:
            copy.wait()


def middle(attended, x_own, cot, small, mixer, expand, reduce):
    f32, bf16 = jnp.float32, jnp.bfloat16
    vmem = pl.BlockSpec(memory_space=pltpu.VMEM)
    hbm = pl.BlockSpec(memory_space=pl.ANY)
    count = len(MIDDLE_EARLY)
    early = jax.ShapeDtypeStruct((count, 2, HALF, LANES), bf16)
    return pl.pallas_call(
        middle_kernel,
        out_shape=(
            jax.ShapeDtypeStruct((512, WIDTH), bf16),
            jax.ShapeDtypeStruct((512, WIDTH), f32),
            jax.ShapeDtypeStruct((TOKENS, 512), bf16),
            jax.ShapeDtypeStruct((8, WIDTH), f32),
            jax.ShapeDtypeStruct((4, 512), f32),
            jax.ShapeDtypeStruct((FLAT_ROWS, LANES), bf16),
            early,
            early,
        ),
        in_specs=[vmem] * 9 + [hbm] * 3,
        out_specs=[vmem] * 5 + [hbm] * 3,
        scratch_shapes=[
            pltpu.VMEM((8, WIDTH), f32),
            pltpu.VMEM((WIDTH, WIDTH), bf16),
            pltpu.VMEM((WIDTH, 2048), bf16),
            pltpu.VMEM((2048, WIDTH), bf16),
            pltpu.VMEM((TOKENS, 512), bf16),
            pltpu.VMEM((512, WIDTH), f32),
            pltpu.VMEM((512, WIDTH), f32),
            pltpu.VMEM((512, LANES), f32),
            pltpu.VMEM((TOKENS, WIDTH), bf16),
            pltpu.VMEM((TOKENS, 2048), bf16),
            pltpu.VMEM((TOKENS, 2048), bf16),
            pltpu.VMEM((TOKENS, 2048), bf16),
            pltpu.VMEM((512, WIDTH), f32),
            pltpu.VMEM((512, WIDTH), f32),
            pltpu.VMEM((512, WIDTH), f32),
            pltpu.VMEM((512, WIDTH), bf16),
            pltpu.VMEM((512, WIDTH), bf16),
            pltpu.VMEM((TOKENS, WIDTH), bf16),
            pltpu.VMEM((2, 4096, LANES), bf16),
            pltpu.SemaphoreType.DMA((9,)),
            pltpu.SemaphoreType.DMA((2, 2)),
            pltpu.SemaphoreType.DMA((5,)),
            pltpu.SemaphoreType.DMA((5,)),
            pltpu.SemaphoreType.DMA((2, 4)),
            pltpu.SemaphoreType.DMA((2, 4)),
            pltpu.SemaphoreType.DMA((count, 2, 2)),
            pltpu.SemaphoreType.DMA((count, 2, 2)),
        ],
        compiler_params=pltpu.CompilerParams(
            collective_id=1, has_side_effects=True, vmem_limit_bytes=62 << 20
        ),
        cost_estimate=pl.CostEstimate(flops=30 << 30, bytes_accessed=40 << 20, transcendentals=0),
    )(attended, x_own, cot, *small, mixer, expand, reduce)


UPDATE_ROWS = 616


def owner_table(owners):
    smalls = ((0, 2, 0), (U_JBIAS, U_MIXER, 16), (U_MBIAS, U_EXPAND, 32), (U_EBIAS, U_REDUCE, 56),
              (U_RBIAS, 12300, 88))
    table = []
    for owner in range(owners):
        begin = OWNED_ROWS * owner
        end = begin + OWNED_ROWS
        start = piece_start(owner)
        shift, later = section_shift(begin // 8), section_shift((end - 1) // 8)
        turn = next((8 * u - begin for u in (U_JBIAS, U_MBIAS) if begin < 8 * u < end), OWNED_ROWS)
        row = [begin + 2 * shift - 2 * start, begin + 2 * later - 2 * start, turn, 0, 0, 0, 3 * owner, 0]
        for first, past, at in smalls:
            if 8 * first < end and 8 * past > begin:
                row[3] = at + begin - 8 * first
                row[4] = max(8 * first - begin, 0)
                row[5] = min(8 * past - begin, OWNED_ROWS)
        assert 0 <= row[0] <= row[1] <= 2 * PIECE - 5 * UPDATE_ROWS
        table.append(row)
    return table


def update_kernel(
    table, step_count, learn_rate, master, first, second, own, peer, small, out_hbm, in_hbm,
    new_master, new_first, new_second, small_share, out_copy, in_copy,
    rows, small_rows, held, sem,
):
    f32 = jnp.float32
    i = pl.program_id(0)
    c = lax.axis_index("dp") % 2
    owner = lax.axis_index("dp") * lax.axis_size("group") + lax.axis_index("group")
    place = [table[owner, k] for k in range(7)]
    pairs = ((out_hbm, out_copy), (in_hbm, in_copy))
    fetch = [pltpu.make_async_copy(src, held.at[k], sem.at[k]) for k, (src, _) in enumerate(pairs)]
    give = [pltpu.make_async_copy(held.at[k], dst, sem.at[2 + k]) for k, (_, dst) in enumerate(pairs)]

    @pl.when(i == 0)
    def _():
        for copy in fetch:
            copy.start()
        small_rows[...] = jnp.zeros_like(small_rows)
        small_rows[UPDATE_ROWS : UPDATE_ROWS + LANES, :] = small[...]
        small_share[...] = small_rows[pl.ds(UPDATE_ROWS + place[6], 3), :]

        def weave(k, carry):
            part = pl.ds(pl.multiple_of(112 * k, 16), 112)
            mine, other = own[part, :], peer[part, :]
            even = jnp.where(c == 0, mine, other).reshape(28, 4, LANES)
            odd = jnp.where(c == 0, other, mine).reshape(28, 4, LANES)
            rows[pl.ds(pl.multiple_of(224 * k, 32), 224), :] = jnp.concatenate([even, odd], 1).reshape(
                224, LANES
            )
            return carry

        lax.fori_loop(0, PIECE // 112, weave, 0)

    @pl.when(i == 2)
    def _():
        for copy in fetch:
            copy.wait()
        for copy in give:
            copy.start()

    base = UPDATE_ROWS * i
    k = lax.broadcasted_iota(jnp.int32, (UPDATE_ROWS, LANES), 0) + base
    grad = jnp.where(
        k < place[2],
        rows[pl.ds(place[0] + base, UPDATE_ROWS), :],
        rows[pl.ds(place[1] + base, UPDATE_ROWS), :],
    )
    at = jnp.clip(place[3] + base, -UPDATE_ROWS, LANES) + UPDATE_ROWS
    grad = jnp.where(
        (k >= place[4]) & (k < place[5]), small_rows[pl.ds(at, UPDATE_ROWS), :], grad
    )
    rate = learn_rate[0]
    moment_step = jnp.full((1, LANES), step_count[0].astype(f32))
    fix_one = 1.0 - jnp.exp(moment_step * math.log(beta_first))
    fix_two = 1.0 - jnp.exp(moment_step * math.log(beta_second))
    one = beta_first * first[...] + (1.0 - beta_first) * grad
    two = beta_second * second[...] + (1.0 - beta_second) * grad * grad
    weights = master[...]
    new_first[...] = one
    new_second[...] = two
    new_master[...] = weights - rate * (
        one / fix_one / (jnp.sqrt(two / fix_two) + adam_epsilon) + weight_decay * weights
    )

    @pl.when(i == pl.num_programs(0) - 1)
    def _():
        for copy in give:
            copy.wait()


def update(table, step_count, learn_rate, master, first, second, own, peer, small, output, input_gradient):
    f32 = jnp.float32
    smem = pl.BlockSpec(memory_space=pltpu.SMEM)
    hbm = pl.BlockSpec(memory_space=pl.ANY)
    block = pl.BlockSpec((UPDATE_ROWS, LANES), lambda i: (i, 0))

    def whole(shape):
        return pl.BlockSpec(shape, lambda i: (0, 0))

    flat = jax.ShapeDtypeStruct((OWNED_ROWS, LANES), f32)
    home = jax.ShapeDtypeStruct(output.shape, output.dtype)
    new = pl.pallas_call(
        update_kernel,
        grid=(5,),
        out_shape=(flat, flat, flat, jax.ShapeDtypeStruct((3, LANES), f32), home, home),
        in_specs=[smem, smem, smem] + [block] * 3
        + [whole((PIECE, LANES)), whole((PIECE, LANES)), whole((LANES, LANES))] + [hbm] * 2,
        out_specs=[block] * 3 + [whole((3, LANES))] + [hbm] * 2,
        scratch_shapes=[
            pltpu.VMEM((2 * PIECE, LANES), f32),
            pltpu.VMEM((2 * UPDATE_ROWS + LANES, LANES), f32),
            pltpu.VMEM((2,) + output.shape, output.dtype),
            pltpu.SemaphoreType.DMA((4,)),
        ],
        compiler_params=pltpu.CompilerParams(vmem_limit_bytes=62 << 20),
    )(
        table, step_count, learn_rate, *[whole_array.reshape(OWNED_ROWS, LANES) for whole_array in (master, first, second)],
        own, peer, small, output, input_gradient,
    )
    return [part.reshape(-1) for part in new[:4]] + list(new[4:])


def on_device_chip(
    dp_size, group_size,
    activations, cotangent, segments, padding, step_count, learn_rate,
    gain_before, shift_before, joint_weight, joint_bias, mixer_weight, mixer_bias,
    gain_middle, shift_middle, expand_weight, expand_bias, reduce_weight, reduce_bias,
    master_weights, first_moment, second_moment,
):
    f32, bf16 = jnp.float32, jnp.bfloat16
    dp = lax.axis_index("dp")
    group = lax.axis_index("group")
    c = dp % 2
    slopes = jnp.asarray([2.0 ** (-8.0 * (h + 1) / HEADS) for h in range(HEADS)], f32)
    x_own, cot_all, normed_one, joint, dist, attended, lse = front(
        slopes, activations, cotangent, segments, padding, gain_before, shift_before, joint_bias,
        joint_weight,
    )
    result, dresid, dattended, middle_sums, expand_sums, flat, mid_a, mid_b = middle(
        attended, x_own, cot_all, (mixer_bias, gain_middle, shift_middle, reduce_bias, expand_bias, gain_before),
        mixer_weight, expand_weight, reduce_weight,
    )
    _, own, peer, small_sum, output, input_gradient = rear(
        slopes, joint, attended, dattended, dist, lse, normed_one, joint_weight, x_own, dresid,
        result, middle_sums, expand_sums, mid_a, mid_b, flat,
    )
    table = jnp.asarray(owner_table(dp_size * group_size), jnp.int32)
    new_master, new_first, new_second, small_share, output, input_gradient = update(
        table, step_count, learn_rate, master_weights, first_moment, second_moment, own, peer, small_sum, output,
        input_gradient,
    )
    return (output, input_gradient, new_master, new_first, new_second, small_share)


def on_device(dp_size, group_size, activations, *rest):
    if (dp_size, group_size) == (8, 4) and activations.shape == (2, 256, WIDTH):
        return on_device_chip(dp_size, group_size, activations, *rest)
    return on_device_general(activations, *rest)


def solution(mesh):
    in_specs = (
        P("dp", "group", None),
        P("dp", "group", None),
        P("dp", None),
        P("dp", None),
        P(),
        P(),
        P(),
        P(),
        P(),
        P(),
        P(),
        P(),
        P(),
        P(),
        P(),
        P(),
        P(),
        P(),
        P(("dp", "group")),
        P(("dp", "group")),
        P(("dp", "group")),
    )
    out_specs = (
        P("dp", "group", None),
        P("dp", "group", None),
        P(("dp", "group")),
        P(("dp", "group")),
        P(("dp", "group")),
        P(("dp", "group")),
    )
    return jax.shard_map(
        functools.partial(on_device, mesh.shape["dp"], mesh.shape["group"]), mesh=mesh, in_specs=in_specs, out_specs=out_specs, check_vma=False
    )
```

```python
import functools
import math

import jax
import jax.numpy as jnp
from jax import lax
from jax.experimental import pallas as pl
from jax.experimental.pallas import tpu as pltpu
from jax.sharding import PartitionSpec as P

HEADS = 16
DOC_MOST = 800


beta_first = 0.9
beta_second = 0.95
adam_epsilon = 1e-08
weight_decay = 0.1
norm_epsilon = 1e-05
masked_score = -1e30


def shifted(block, axis, distance):
    devices = range(lax.axis_size(axis))
    route = [(i - distance, i) for i in devices if i - distance in devices]
    return lax.ppermute(block, axis, route)


def standardize(values):
    center = values - jnp.mean(values, -1, keepdims=True)
    spread = lax.rsqrt(jnp.mean(center * center, -1, keepdims=True) + norm_epsilon)
    return (center * spread, spread)


def norm_back(dnormed, normed, spread):
    return spread * (
        dnormed
        - jnp.mean(dnormed, -1, keepdims=True)
        - normed * jnp.mean(dnormed * normed, -1, keepdims=True)
    )


def window_mask(segments, padding, member, hop, block_len):
    places = jnp.arange(block_len, dtype=jnp.int32)
    source = member - hop
    query_place = member * block_len + places
    key_place = source * block_len + places
    start = jnp.maximum(source, 0) * block_len
    seg_query = lax.dynamic_slice_in_dim(segments, member * block_len, block_len, 1)
    seg_key = lax.dynamic_slice_in_dim(segments, start, block_len, 1)
    pad_key = lax.dynamic_slice_in_dim(padding, start, block_len, 1)
    earlier = key_place[None, None, :] <= query_place[None, :, None]
    itself = key_place[None, None, :] == query_place[None, :, None]
    allowed = (
        (seg_query[:, :, None] == seg_key[:, None, :])
        & earlier
        & ((pad_key[:, None, :] == 1) | itself)
        & (source >= 0)
    )
    distance = (query_place[:, None] - key_place[None, :]).astype(jnp.float32)
    return (allowed[:, None], distance)


def piece_scores(query4, key4, slopes, distance, score_scale):
    raw = jnp.einsum("sqhd,skhd->shqk", query4, key4, preferred_element_type=jnp.float32)
    return raw * score_scale - slopes[:, None, None] * distance[None]


def on_device_general(
    activations,
    cotangent,
    segments,
    padding,
    step_count,
    learn_rate,
    gain_before,
    shift_before,
    joint_weight,
    joint_bias,
    mixer_weight,
    mixer_bias,
    gain_middle,
    shift_middle,
    expand_weight,
    expand_bias,
    reduce_weight,
    reduce_bias,
    master_weights,
    first_moment,
    second_moment,
):
    seq_count, block_len, width = activations.shape
    head_size = width // HEADS
    row_count = seq_count * block_len
    shape4 = (seq_count, block_len, HEADS, head_size)
    score_scale = 1.0 / math.sqrt(head_size)
    group_size = lax.axis_size("group")
    member = lax.axis_index("group")
    reach = min((DOC_MOST + block_len - 2) // block_len, group_size - 1)
    slopes = jnp.exp2(-8.0 * (jnp.arange(HEADS, dtype=jnp.float32) + 1.0) / HEADS)
    inputs = activations.reshape(row_count, width).astype(jnp.float32)
    gain_one = gain_before.astype(jnp.float32)
    gain_two = gain_middle.astype(jnp.float32)
    normal_one, spread_one = standardize(inputs)
    normed_one = (normal_one * gain_one + shift_before.astype(jnp.float32)).astype(jnp.bfloat16)
    joint = jnp.dot(normed_one, joint_weight, preferred_element_type=jnp.float32)
    bias_joint = joint_bias.astype(jnp.float32)
    query_rows = (joint[:, :width] + bias_joint[:width]).astype(jnp.bfloat16)
    key_rows = joint[:, width : 2 * width].astype(jnp.bfloat16)
    value_rows = (joint[:, 2 * width :] + bias_joint[width:]).astype(jnp.bfloat16)
    own_piece = jnp.stack([key_rows, value_rows]).reshape(2, seq_count, block_len, width)
    query4 = query_rows.reshape(shape4)
    pieces = [own_piece]
    for hop in range(1, reach + 1):
        pieces.append(shifted(own_piece, "group", hop))
    row_top = jnp.full((seq_count, HEADS, block_len), masked_score, jnp.float32)
    row_total = jnp.zeros((seq_count, HEADS, block_len), jnp.float32)
    for hop in range(reach + 1):
        allowed, distance = window_mask(segments, padding, member, hop, block_len)
        scores = piece_scores(query4, pieces[hop][0].reshape(shape4), slopes, distance, score_scale)
        fresh = jnp.maximum(row_top, jnp.max(jnp.where(allowed, scores, masked_score), -1))
        row_total = row_total * jnp.exp(row_top - fresh) + jnp.sum(
            jnp.exp(jnp.where(allowed, scores - fresh[..., None], masked_score)), -1
        )
        row_top = fresh
    log_total = row_top + jnp.log(row_total)
    attended = jnp.zeros(shape4, jnp.float32)
    for hop in range(reach + 1):
        allowed, distance = window_mask(segments, padding, member, hop, block_len)
        scores = piece_scores(query4, pieces[hop][0].reshape(shape4), slopes, distance, score_scale)
        probs = jnp.exp(jnp.where(allowed, scores - log_total[..., None], masked_score)).astype(
            jnp.bfloat16
        )
        attended = attended + jnp.einsum(
            "shqk,skhd->sqhd",
            probs,
            pieces[hop][1].reshape(shape4),
            preferred_element_type=jnp.float32,
        )
    attended_low = attended.reshape(row_count, width).astype(jnp.bfloat16)
    resid = inputs + (
        jnp.dot(attended_low, mixer_weight, preferred_element_type=jnp.float32)
        + mixer_bias.astype(jnp.float32)
    )
    normal_two, spread_two = standardize(resid)
    normed_two = (normal_two * gain_two + shift_middle.astype(jnp.float32)).astype(jnp.bfloat16)
    hidden = jnp.dot(
        normed_two, expand_weight, preferred_element_type=jnp.float32
    ) + expand_bias.astype(jnp.float32)
    act = jax.nn.gelu(hidden, approximate=True).astype(jnp.bfloat16)
    result = resid + (
        jnp.dot(act, reduce_weight, preferred_element_type=jnp.float32)
        + reduce_bias.astype(jnp.float32)
    )
    output = result.astype(jnp.bfloat16).reshape(seq_count, block_len, width)
    cot_low = cotangent.reshape(row_count, width)
    cot_full = cot_low.astype(jnp.float32)
    reduce_grad = jnp.einsum("tf,td->fd", act, cot_low, preferred_element_type=jnp.float32)
    reduce_bias_grad = jnp.sum(cot_full, 0)
    dact = jnp.einsum("td,fd->tf", cot_low, reduce_weight, preferred_element_type=jnp.float32)
    gelu_pull = jax.vjp(lambda inner: jax.nn.gelu(inner, approximate=True), hidden)[1]
    dhidden = gelu_pull(dact)[0].astype(jnp.bfloat16)
    expand_grad = jnp.einsum("td,tf->df", normed_two, dhidden, preferred_element_type=jnp.float32)
    expand_bias_grad = jnp.sum(dhidden.astype(jnp.float32), 0)
    dnormed_two = jnp.einsum(
        "tf,df->td", dhidden, expand_weight, preferred_element_type=jnp.float32
    )
    gain_middle_grad = jnp.sum(dnormed_two * normal_two, 0)
    shift_middle_grad = jnp.sum(dnormed_two, 0)
    dresid = cot_full + norm_back(dnormed_two * gain_two, normal_two, spread_two)
    dbranch = dresid.astype(jnp.bfloat16)
    mixer_grad = jnp.einsum("td,te->de", attended_low, dbranch, preferred_element_type=jnp.float32)
    mixer_bias_grad = jnp.sum(dbranch.astype(jnp.float32), 0)
    dattended = jnp.einsum(
        "te,de->td", dbranch, mixer_weight, preferred_element_type=jnp.float32
    ).astype(jnp.bfloat16)
    dattended4 = dattended.reshape(shape4)
    row_delta = jnp.einsum("sqhd,sqhd->shq", dattended4.astype(jnp.float32), attended)
    dquery = jnp.zeros(shape4, jnp.float32)
    dkv_own = jnp.zeros((2, seq_count, block_len, width), jnp.float32)
    for hop in range(reach + 1):
        piece = pieces[hop]
        key4 = piece[0].reshape(shape4)
        value4 = piece[1].reshape(shape4)
        allowed, distance = window_mask(segments, padding, member, hop, block_len)
        scores = piece_scores(query4, key4, slopes, distance, score_scale)
        probs = jnp.exp(jnp.where(allowed, scores - log_total[..., None], masked_score))
        dvalue = jnp.einsum(
            "shqk,sqhd->skhd",
            probs.astype(jnp.bfloat16),
            dattended4,
            preferred_element_type=jnp.float32,
        )
        dprobs = jnp.einsum(
            "sqhd,skhd->shqk", dattended4, value4, preferred_element_type=jnp.float32
        )
        dscores = (probs * (dprobs - row_delta[..., None])).astype(jnp.bfloat16)
        dquery = dquery + jnp.einsum(
            "shqk,skhd->sqhd", dscores, key4, preferred_element_type=jnp.float32
        )
        dkey = (
            jnp.einsum("shqk,sqhd->skhd", dscores, query4, preferred_element_type=jnp.float32)
            * score_scale
        )
        returned = jnp.stack([dkey, dvalue]).reshape(2, seq_count, block_len, width)
        if hop == 0:
            dkv_own = returned
        else:
            dkv_own = dkv_own + shifted(returned.astype(jnp.bfloat16), "group", -hop).astype(
                returned.dtype
            )
    dquery_low = (dquery * score_scale).reshape(row_count, width).astype(jnp.bfloat16)
    dkey_low = dkv_own[0].reshape(row_count, width).astype(jnp.bfloat16)
    dvalue_low = dkv_own[1].reshape(row_count, width).astype(jnp.bfloat16)
    djoint = jnp.concatenate([dquery_low, dkey_low, dvalue_low], 1)
    joint_grad = jnp.einsum("td,te->de", normed_one, djoint, preferred_element_type=jnp.float32)
    joint_bias_grad = jnp.concatenate(
        [jnp.sum(dquery_low.astype(jnp.float32), 0), jnp.sum(dvalue_low.astype(jnp.float32), 0)]
    )
    dnormed_one = jnp.einsum("te,de->td", djoint, joint_weight, preferred_element_type=jnp.float32)
    gain_before_grad = jnp.sum(dnormed_one * normal_one, 0)
    shift_before_grad = jnp.sum(dnormed_one, 0)
    dinput = dresid + norm_back(dnormed_one * gain_one, normal_one, spread_one)
    input_gradient = dinput.astype(jnp.bfloat16).reshape(seq_count, block_len, width)
    listing = [
        gain_before_grad,
        shift_before_grad,
        joint_grad,
        joint_bias_grad,
        mixer_grad,
        mixer_bias_grad,
        gain_middle_grad,
        shift_middle_grad,
        expand_grad,
        expand_bias_grad,
        reduce_grad,
        reduce_bias_grad,
    ]
    gradient = jnp.concatenate([single.reshape(-1) for single in listing])
    small_list = [
        gain_before_grad,
        shift_before_grad,
        joint_bias_grad,
        mixer_bias_grad,
        gain_middle_grad,
        shift_middle_grad,
        expand_bias_grad,
        reduce_bias_grad,
    ]
    small_local = jnp.concatenate(small_list)
    share, small_share = (
        lax.psum_scatter(gradient, ("dp", "group"), scatter_dimension=0, tiled=True),
        lax.psum_scatter(small_local, ("dp", "group"), scatter_dimension=0, tiled=True),
    )
    moment_step = step_count[0].astype(jnp.float32)
    rate = learn_rate[0]
    fix_one = 1.0 - jnp.exp(moment_step * math.log(beta_first))
    fix_two = 1.0 - jnp.exp(moment_step * math.log(beta_second))
    updated_first = beta_first * first_moment + (1.0 - beta_first) * share
    updated_second = beta_second * second_moment + (1.0 - beta_second) * share * share
    updated_master = master_weights - rate * (
        updated_first / fix_one / (jnp.sqrt(updated_second / fix_two) + adam_epsilon)
        + weight_decay * master_weights
    )
    return (output, input_gradient, updated_master, updated_first, updated_second, small_share)


WIDTH = 1024
HIDDEN = 4096
TOKENS = 1024
LANES = 128
OWNED = 393600
OWNED_ROWS = OWNED // LANES
PIECE = 1568
HALF = PIECE // 2
JOINT_AT, MIXER_AT, EXPAND_AT, REDUCE_AT = 16, 12320, 16432, 32832
FLAT_ROWS = 49248
U_JOINT, U_JBIAS, U_MIXER, U_MBIAS, U_EXPAND, U_EBIAS, U_REDUCE, U_RBIAS = (
    2, 3074, 3076, 4100, 4103, 8199, 8203, 12299,
)


def section_shift(unit):
    return 8 if unit < U_JBIAS else 16 if unit < U_MBIAS else 20


def piece_start(owner):
    unit = OWNED_ROWS * owner // 8
    return (4 * unit + section_shift(unit)) // 16 * 16


def piece_offset(q, y, x):
    at = [piece_start(4 * q + k) // 16 for k in range(4)]
    row = (
        at[0] * (1 - y) * (1 - x) + at[1] * (1 - y) * x + at[2] * y * (1 - x) + at[3] * y * x
    )
    return pl.multiple_of(row * 16, 16)


MESH_ID = pl.DeviceIdType.MESH


def by_rows(step):
    def one(i, carry):
        step(pl.ds(pl.multiple_of(112 * i, 16), 112))
        return carry

    lax.fori_loop(0, HALF // 112, one, 0)


class Pieces:
    def __init__(self, dp, me, flat, own_a, own_b, rx_a1, rx_b1, rx_a2, rx_b2, acc, load_sem, s2_send, s2_recv):
        self.y, self.x = me // 2, me % 2
        self.x_near = (dp, 2 * self.y + (1 - self.x))
        self.y_near = (dp, 2 * (1 - self.y) + self.x)
        self.flat, self.own_a, self.own_b = flat, own_a, own_b
        self.rx_a1, self.rx_b1, self.rx_a2, self.rx_b2, self.acc = rx_a1, rx_b1, rx_a2, rx_b2, acc
        self.load_sem, self.s2_send, self.s2_recv = load_sem, s2_send, s2_recv

    def loads(self, q, own_slot, ready=None):
        slot = q
        out = []
        for k in range(2):
            for way, (row, own) in enumerate((
                (piece_offset(q, k, self.x), self.own_a),
                (piece_offset(q, self.y, k) + HALF, self.own_b),
            )):
                out.append(pltpu.make_async_copy(
                    self.flat.at[pl.ds(row, HALF)], own.at[own_slot, k], self.load_sem.at[slot, way, k]
                ))
            if ready is not None:
                ready_a, ready_b, at = ready
                for way, (src, dst) in enumerate(((ready_a, self.rx_a1), (ready_b, self.rx_b1))):
                    out.append(pltpu.make_async_copy(
                        src.at[at, k], dst.at[slot, k], self.load_sem.at[slot, 2 + way, k]
                    ))
        return out

    def second(self, slot):
        y, x = self.y, self.x
        return [
            pltpu.make_async_remote_copy(
                src_ref=src, dst_ref=dst.at[slot], send_sem=self.s2_send.at[slot, way],
                recv_sem=self.s2_recv.at[slot, way], device_id=near, device_id_type=MESH_ID,
            )
            for way, (src, dst, near) in enumerate((
                (self.rx_a1.at[slot, 1 - y], self.rx_a2, self.y_near),
                (self.rx_b1.at[slot, 1 - x], self.rx_b2, self.x_near),
            ))
        ]

    def meet(self, slot, own_slot):
        y, x = self.y, self.x
        rx_a1, rx_b1, own_a, own_b, acc = self.rx_a1, self.rx_b1, self.own_a, self.own_b, self.acc

        def away(rows):
            rx_a1[slot, 1 - y, rows] = rx_a1[slot, 1 - y, rows] + own_a[own_slot, 1 - y, rows]
            rx_b1[slot, 1 - x, rows] = rx_b1[slot, 1 - x, rows] + own_b[own_slot, 1 - x, rows]

        by_rows(away)
        for copy in self.second(slot):
            copy.start()

        def kept(rows):
            acc[slot, 0, rows] = rx_a1[slot, y, rows] + own_a[own_slot, y, rows]
            acc[slot, 1, rows] = rx_b1[slot, x, rows] + own_b[own_slot, x, rows]

        by_rows(kept)

    def join(self, slot):
        for copy in self.second(slot):
            copy.wait_recv()
        acc, rx_a2, rx_b2 = self.acc, self.rx_a2, self.rx_b2

        def add(rows):
            acc[slot, 0, rows] = acc[slot, 0, rows] + rx_a2[slot, rows]
            acc[slot, 1, rows] = acc[slot, 1, rows] + rx_b2[slot, rows]

        by_rows(add)


MIDDLE_EARLY = (7, 6, 4)


def nn(a, b):
    return lax.dot_general(a, b, (((1,), (0,)), ((), ())), preferred_element_type=jnp.float32)


def nt(a, b):
    return lax.dot_general(a, b, (((1,), (1,)), ((), ())), preferred_element_type=jnp.float32)


def tn(a, b):
    return lax.dot_general(a, b, (((0,), (0,)), ((), ())), preferred_element_type=jnp.float32)


def head_lanes(value, h):
    lane = lax.broadcasted_iota(jnp.int32, (1, LANES), 1)
    return jnp.where(lane // 64 == h, value, jnp.zeros_like(value))


def plane_devices(dp, me):
    z, c = dp // 2, dp % 2
    near = [(2 * z + 1 - c, me)]
    for d in (1, 2, 3):
        near += [(2 * z, (me + d) % 4), (2 * z + 1, (me + d) % 4)]
    return near


def greet(devices):
    barrier = pltpu.get_barrier_semaphore()
    for near in devices:
        pl.semaphore_signal(barrier, inc=1, device_id=near, device_id_type=MESH_ID)
    pl.semaphore_wait(barrier, len(devices))


class Home:
    def __init__(self, rows, out, dp, me, send_sem, recv_sem):
        z, c = dp // 2, dp % 2
        self.here = c == me // 2
        self.turns = []
        for turn in range(2):
            src = rows.at[pl.ds(256 * turn, 256)]
            dst = out.at[me % 2]
            away = pltpu.make_async_remote_copy(
                src_ref=src, dst_ref=dst, send_sem=send_sem.at[turn], recv_sem=recv_sem.at[me % 2],
                device_id=(2 * z + me // 2, 2 * c + turn), device_id_type=MESH_ID,
            )
            near = pltpu.make_async_copy(src, dst, send_sem.at[turn])
            came = pltpu.make_async_remote_copy(
                src_ref=src, dst_ref=out.at[turn], send_sem=send_sem.at[turn],
                recv_sem=recv_sem.at[turn], device_id=(2 * z + me // 2, 2 * c + turn),
                device_id_type=MESH_ID,
            )
            self.turns.append((away, near, came, self.here & (me % 2 == turn)))

    def start(self):
        for away, near, _, stays in self.turns:
            @pl.when(stays)
            def _():
                near.start()

            @pl.when(jnp.logical_not(stays))
            def _():
                away.start()

    def wait(self):
        for away, near, came, stays in self.turns:
            @pl.when(stays)
            def _():
                near.wait()

            @pl.when(jnp.logical_not(stays))
            def _():
                away.wait_send()
                came.wait_recv()


def first_stage(q, flat, rx_a, rx_b, at, send_sem, recv_sem, dp, me):
    y, x = me // 2, me % 2
    x_near = (dp, 2 * y + (1 - x))
    y_near = (dp, 2 * (1 - y) + x)
    out = []
    for k in range(2):
        for way, (row, rx, near) in enumerate((
            (piece_offset(q, k, 1 - x), rx_a, x_near),
            (piece_offset(q, 1 - y, k) + HALF, rx_b, y_near),
        )):
            out.append(pltpu.make_async_remote_copy(
                src_ref=flat.at[pl.ds(row, HALF)], dst_ref=rx.at[at, k],
                send_sem=send_sem.at[at, way, k], recv_sem=recv_sem.at[at, way, k],
                device_id=near, device_id_type=MESH_ID,
            ))
    return out


def both_heads(value):
    return jnp.concatenate([head_lanes(value, 0), head_lanes(value, 1)], 0)


class Spread:
    def __init__(self, blocks, rows, dp, me, send_sem, recv_sem):
        z, c = dp // 2, dp % 2
        here = c == me // 2
        self.turns = []
        for turn in range(2):
            src = blocks.at[turn]
            dst = rows.at[pl.ds(pl.multiple_of(256 * me, 256), 256)]
            away = pltpu.make_async_remote_copy(
                src_ref=src, dst_ref=dst, send_sem=send_sem.at[turn], recv_sem=recv_sem.at[me % 2],
                device_id=(2 * z + me // 2, 2 * c + turn), device_id_type=MESH_ID,
            )
            near = pltpu.make_async_copy(src, dst, send_sem.at[turn])
            came = pltpu.make_async_remote_copy(
                src_ref=src, dst_ref=rows.at[pl.ds(pl.multiple_of(512 * c + 256 * turn, 256), 256)],
                send_sem=send_sem.at[turn], recv_sem=recv_sem.at[turn],
                device_id=(2 * z + me // 2, 2 * c + turn), device_id_type=MESH_ID,
            )
            self.turns.append((away, near, came, here & (me % 2 == turn)))

    def start(self):
        for away, near, _, stays in self.turns:
            @pl.when(stays)
            def _():
                near.start()

            @pl.when(jnp.logical_not(stays))
            def _():
                away.start()

    def wait_came(self, turn):
        _, near, came, stays = self.turns[turn]

        @pl.when(stays)
        def _():
            near.wait()

        @pl.when(jnp.logical_not(stays))
        def _():
            came.wait_recv()

    def wait_sent(self):
        for away, _, _, stays in self.turns:
            @pl.when(jnp.logical_not(stays))
            def _():
                away.wait_send()


def front_kernel(
    slopes, blocks, cot_blocks, segments, padding, gain_in, shift_in, bias_in, weight_hbm,
    x_out, cot_out, normed_out, joint_out, dist_out, att_out, lse_out,
    x_all, cot_all, normed, joint, weight, dist, att, lse, seg_rx, pad_rx, vectors, columns, s_ref, p_ref, vt_ref, ot_ref,
    weight_sem, out_sem, mark_sem, x_send, x_recv, cot_send, cot_recv, pass_send, pass_recv,
):
    f32, bf16 = jnp.float32, jnp.bfloat16
    dp = lax.axis_index("dp")
    me = lax.axis_index("group")
    c = dp % 2
    core_near = (dp + 1 - 2 * c, me)
    own = pl.ds(pl.multiple_of(512 * c, 512), 512)
    other = pl.ds(pl.multiple_of(512 * (1 - c), 512), 512)

    weights = [
        pltpu.make_async_copy(
            weight_hbm.at[:, pl.ds(pl.multiple_of(1024 * p + 512 * c, 512), 512)],
            weight.at[:, pl.ds(512 * p, 512)], weight_sem.at[p],
        )
        for p in range(3)
    ]
    greet(plane_devices(dp, me))
    x_way = Spread(blocks, x_all, dp, me, x_send, x_recv)
    cot_way = Spread(cot_blocks, cot_all, dp, me, cot_send, cot_recv)
    x_way.start()
    vectors[0:1, :] = gain_in[...].astype(f32).reshape(1, WIDTH)
    vectors[1:2, :] = shift_in[...].astype(f32).reshape(1, WIDTH)
    vectors[2:4, :] = bias_in[...].astype(f32).reshape(2, WIDTH)
    mark_swaps = [
        pltpu.make_async_remote_copy(
            src_ref=src, dst_ref=dst, send_sem=mark_sem.at[0, i], recv_sem=mark_sem.at[1, i],
            device_id=core_near, device_id_type=MESH_ID,
        )
        for i, (src, dst) in enumerate(((segments, seg_rx), (padding, pad_rx)))
    ]
    for copy in mark_swaps:
        copy.start()
    for copy in weights:
        copy.start()

    def hand_over(rows, way, turn):
        at = pl.ds(pl.multiple_of(512 * c + 256 * turn, 256), 256)
        return pltpu.make_async_remote_copy(
            src_ref=rows.at[at], dst_ref=rows.at[at], send_sem=pass_send.at[way, turn],
            recv_sem=pass_recv.at[way, turn], device_id=core_near, device_id_type=MESH_ID,
        )

    for copy in mark_swaps:
        copy.wait()
    odd = me % 2 == 1
    held = c == me // 2

    def row_of(mine, came):
        both = jnp.where(held, mine[...], came[...]).astype(f32)
        return jnp.where(odd, both[1:2], both[0:1])

    seg = row_of(segments, seg_rx)
    pad = row_of(padding, pad_rx)
    kind = lax.broadcasted_iota(jnp.int32, (8, TOKENS), 0)
    columns[...] = jnp.broadcast_to(
        jnp.where(kind == 0, seg, pad).T[:, :8].reshape(TOKENS, 8), (TOKENS, 8)
    )

    def dist_rows(i, carry):
        rows = pl.ds(pl.multiple_of(128 * i, 128), 128)
        key_seg, key_pad = columns[rows, 0:1], columns[rows, 1:2]
        key = (lax.broadcasted_iota(jnp.int32, (128, 1), 0) + 128 * i).astype(f32)
        query = lax.broadcasted_iota(jnp.int32, (128, TOKENS), 1).astype(f32)
        last = jnp.sum(jnp.where(seg <= key_seg, 1.0, 0.0), 1, keepdims=True) - 1.0
        last = jnp.where(key_pad == 1.0, last, key)
        dist[rows, :] = jnp.where((query >= key) & (query <= last), query - key, -masked_score)
        return carry

    lax.fori_loop(0, 8, dist_rows, 0)
    outs = []

    def put(src, dst):
        copy = pltpu.make_async_copy(src, dst, out_sem.at[len(outs)])
        copy.start()
        outs.append(copy)

    put(dist, dist_out)
    gain, shift = vectors[0:1, :], vectors[1:2, :]

    def norm_rows(half):
        def one(i, carry):
            rows = pl.ds(pl.multiple_of(512 * half + 128 * i, 128), 128)
            values = x_all[rows, :].astype(f32)
            center = values - jnp.mean(values, -1, keepdims=True)
            factor = lax.rsqrt(jnp.mean(center * center, -1, keepdims=True) + norm_epsilon)
            normed[rows, :] = (center * factor * gain + shift).astype(bf16)
            return carry

        lax.fori_loop(0, 4, one, 0)
        rows = pl.ds(pl.multiple_of(512 * half, 512), 512)
        lanes = pl.ds(pl.multiple_of(512 * c, 512), 512)
        made = nn(normed[rows, :], weight[...])
        joint[rows, 0:512] = ((made[:, 0:512] + vectors[2:3, lanes]) * 0.125).astype(bf16)
        joint[rows, 512:1024] = made[:, 512:1024].astype(bf16)
        joint[rows, 1024:1536] = (made[:, 1024:1536] + vectors[3:4, lanes]).astype(bf16)

    for turn in range(2):
        x_way.wait_came(turn)
        hand_over(x_all, 0, turn).start()
    x_way.wait_sent()
    cot_way.start()
    put(x_all.at[own], x_out)
    for copy in weights:
        copy.wait()
    norm_rows(c)
    for turn in range(2):
        hand_over(x_all, 0, turn).wait_recv()
    norm_rows(1 - c)
    put(normed, normed_out)
    put(joint, joint_out)

    def pair_step(pair, carry):
        def lanes(block):
            return pl.ds(pl.multiple_of(512 * block + LANES * pair, LANES), LANES)

        vt_ref[...] = joint[:, lanes(2)].astype(f32).T.astype(bf16)
        slope = [slopes[8 * c + 2 * pair + h] for h in range(2)]

        def scores(qb):
            cols = pl.ds(qb * 256, 256)
            queries = both_heads(joint[cols, lanes(0)])
            top = None
            for kb in range(qb + 1):
                rows = pl.ds(kb * 256, 256)
                raw = nt(joint[rows, lanes(1)], queries)
                far = dist[rows, cols]
                parts = [raw[:, 256 * h : 256 * h + 256] - slope[h] * far for h in range(2)]
                for h in range(2):
                    s_ref[qb % 2, rows, 256 * h : 256 * h + 256] = parts[h]
                high = jnp.concatenate([jnp.max(part, 0, keepdims=True) for part in parts], 1)
                top = high if top is None else jnp.maximum(top, high)
            return top

        def weigh(qb, top):
            cols = pl.ds(qb * 256, 256)
            span = pl.ds(0, 256 * (qb + 1))
            total = None
            for kb in range(qb + 1):
                rows = pl.ds(kb * 256, 256)
                p = jnp.exp(s_ref[qb % 2, rows, :] - top)
                more = jnp.sum(p, 0, keepdims=True)
                total = more if total is None else total + more
                p_ref[qb % 2, rows, :] = p.astype(bf16)
            out = nn(vt_ref[:, span], p_ref[qb % 2, span, :]) / total
            ot_ref[0:64, cols] = out[0:64, 0:256]
            ot_ref[64:128, cols] = out[64:128, 256:512]
            row = top + jnp.log(total)
            for h in range(2):
                lse[pair, h : h + 1, cols] = row[:, 256 * h : 256 * h + 256]

        top = scores(0)
        for qb in range(4):
            after = scores(qb + 1) if qb < 3 else None
            weigh(qb, top)
            top = after
        att[:, lanes(0)] = ot_ref[...].T.astype(bf16)

        @pl.when(pair == 2)
        def _():
            for turn in range(2):
                cot_way.wait_came(turn)
                hand_over(cot_all, 1, turn).start()

        return carry

    lax.fori_loop(0, 4, pair_step, 0)
    put(att, att_out)
    put(lse, lse_out)
    for turn in range(2):
        hand_over(cot_all, 1, turn).wait()
        hand_over(x_all, 0, turn).wait_send()
    put(cot_all, cot_out)
    cot_way.wait_sent()
    for copy in outs:
        copy.wait()


def front(slopes, blocks, cot_blocks, segments, padding, gain, shift, bias, weight):
    f32, bf16 = jnp.float32, jnp.bfloat16
    vmem = pl.BlockSpec(memory_space=pltpu.VMEM)
    hbm = pl.BlockSpec(memory_space=pl.ANY)
    return pl.pallas_call(
        front_kernel,
        out_shape=(
            jax.ShapeDtypeStruct((512, WIDTH), bf16),
            jax.ShapeDtypeStruct((TOKENS, WIDTH), bf16),
            jax.ShapeDtypeStruct((TOKENS, WIDTH), bf16),
            jax.ShapeDtypeStruct((TOKENS, 1536), bf16),
            jax.ShapeDtypeStruct((TOKENS, TOKENS), f32),
            jax.ShapeDtypeStruct((TOKENS, 512), bf16),
            jax.ShapeDtypeStruct((4, 2, TOKENS), f32),
        ),
        in_specs=[pl.BlockSpec(memory_space=pltpu.SMEM)] + [hbm] * 2 + [vmem] * 5 + [hbm],
        out_specs=[hbm] * 7,
        scratch_shapes=[
            pltpu.VMEM((TOKENS, WIDTH), bf16),
            pltpu.VMEM((TOKENS, WIDTH), bf16),
            pltpu.VMEM((TOKENS, WIDTH), bf16),
            pltpu.VMEM((TOKENS, 1536), bf16),
            pltpu.VMEM((WIDTH, 1536), bf16),
            pltpu.VMEM((TOKENS, TOKENS), f32),
            pltpu.VMEM((TOKENS, 512), bf16),
            pltpu.VMEM((4, 2, TOKENS), f32),
            pltpu.VMEM((2, TOKENS), jnp.int32),
            pltpu.VMEM((2, TOKENS), jnp.int32),
            pltpu.VMEM((8, WIDTH), f32),
            pltpu.VMEM((TOKENS, 8), f32),
            pltpu.VMEM((2, TOKENS, 512), f32),
            pltpu.VMEM((2, TOKENS, 512), bf16),
            pltpu.VMEM((LANES, TOKENS), bf16),
            pltpu.VMEM((LANES, TOKENS), f32),
            pltpu.SemaphoreType.DMA((3,)),
            pltpu.SemaphoreType.DMA((7,)),
            pltpu.SemaphoreType.DMA((2, 2)),
            pltpu.SemaphoreType.DMA((2,)),
            pltpu.SemaphoreType.DMA((2,)),
            pltpu.SemaphoreType.DMA((2,)),
            pltpu.SemaphoreType.DMA((2,)),
            pltpu.SemaphoreType.DMA((2, 2)),
            pltpu.SemaphoreType.DMA((2, 2)),
        ],
        compiler_params=pltpu.CompilerParams(
            collective_id=0, has_side_effects=True, vmem_limit_bytes=62 << 20
        ),
        cost_estimate=pl.CostEstimate(flops=10 << 30, bytes_accessed=20 << 20, transcendentals=0),
    )(slopes, blocks, cot_blocks, segments, padding, gain, shift, bias, weight)


PLAN = (
    ("greet",), ("i1", 5), ("load",), ("a0",), ("i1", 3), ("meet", 6), ("a1",), ("meet", 5), ("a2",),
    ("meet", 4), ("a3",), ("J",), ("i1", 0), ("join", 4), ("join", 5), ("dnp",), ("hop", 4, 0), ("join", 6),
    ("i1", 1), ("meet", 7), ("meet", 0), ("hop", 4, 1), ("hop", 5, 0), ("hop", 5, 1), ("join", 7),
    ("meet", 1), ("hop", 6, 0), ("join", 0), ("hop", 0, 0), ("meet", 3), ("join", 1), ("i1", 2),
    ("hop", 1, 0), ("hop", 7, 0), ("hop", 6, 1), ("join", 3), ("hop", 0, 1), ("hop", 7, 1), ("fin", 5),
    ("hop", 3, 0), ("meet", 2), ("hop", 1, 1), ("hop", 6, 2), ("dno",), ("home", "o"), ("hop", 0, 2),
    ("hop", 3, 1), ("hop", 1, 2), ("hop", 7, 2), ("join", 2), ("hop", 2, 0), ("ln",), ("fin", 0),
    ("fin", 6), ("home", "i"), ("fin", 3), ("hop", 2, 1), ("fin", 1), ("fin", 7), ("fin", 4), ("fin", 2),
    ("end",),
)


def rear_kernel(
    slopes, joint_hbm, att_hbm, datt_hbm, dist_hbm, lse, normed_hbm, weight_hbm, x_hbm, dresid_hbm,
    result, mid_sums, expand_sums, mid_a, mid_b, flat_in,
    flat, own_out, peer_out, small_out, output, input_gradient,
    joint, attended, dattended, normed, weight, x_own, dresid,
    dist, p_ref, ds_ref, kt_ref, dqt_ref, dk_acc, dv_acc, delta_ref, djoint, dn_rx, dinput, blocks,
    own_a, own_b, rx_a1, rx_b1, rx_a2, rx_b2, acc, rx_up, rx_dn, parting,
    small_mine, small_rx, small_z,
    dist_sem, block_sem, swap_sem, load_sem, s1_send, s1_recv, s2_send, s2_recv, z_send, z_recv,
    last_sem, sm_send, sm_recv, out_send, out_recv, in_send, in_recv,
):
    f32, bf16 = jnp.float32, jnp.bfloat16
    dp = lax.axis_index("dp")
    me = lax.axis_index("group")
    z, c = dp // 2, dp % 2
    y, x = me // 2, me % 2
    x_near = (dp, 2 * y + (1 - x))
    y_near = (dp, 2 * (1 - y) + x)
    core_near = (2 * z + 1 - c, me)
    own = pl.ds(pl.multiple_of(512 * c, 512), 512)
    other = pl.ds(pl.multiple_of(512 * (1 - c), 512), 512)

    def z_at(d):
        return (2 * d + c, me)

    pieces = Pieces(
        dp, me, flat, own_a, own_b, rx_a1, rx_b1, rx_a2, rx_b2, acc, load_sem, s2_send, s2_recv
    )
    meets = [step[1] for step in PLAN if step[0] == "meet"]
    own_slot = {q: at % 4 for at, q in enumerate(meets)}
    loaded, met = [], []

    def load_ahead(joint_done):
        for q in meets[: len(met) + 4]:
            if q not in loaded and (joint_done or q > 1):
                loaded.append(q)
                start(loads(q))

    def loads(q):
        ready = (mid_a, mid_b, MIDDLE_EARLY.index(q)) if q in MIDDLE_EARLY else None
        return pieces.loads(q, own_slot[q], ready)

    def start(copies):
        for copy in copies:
            copy.start()

    def stage1(q):
        return first_stage(q, flat, rx_a1, rx_b1, q, s1_send, s1_recv, dp, me)

    def hop(q, up, half):
        way = 0 if up else 1
        return pltpu.make_async_remote_copy(
            src_ref=acc.at[q, half], dst_ref=rx_up.at[q - 2, half] if up else rx_dn.at[q, half],
            send_sem=z_send.at[q, way, half], recv_sem=z_recv.at[q, way, half],
            device_id=z_at((z + 1) % 4 if up else (z + 3) % 4), device_id_type=MESH_ID,
        )

    def meet(q):
        for copy in loads(q):
            copy.wait()
        if q not in MIDDLE_EARLY:
            for copy in stage1(q):
                copy.wait_recv()
        pieces.meet(q, own_slot[q])

    def add_came(q, rx, at, half):
        def add(rows):
            acc[q, half, rows] = acc[q, half, rows] + rx[at, half, rows]

        by_rows(add)

    on_way = {(plane, up): [] for plane in range(4) for up in (False, True)}

    def send_on(plane, q, up, half):
        queue = on_way[plane, up]
        if len(queue) >= 2:
            hop(*queue[-2]).wait_send()
        hop(q, up, half).start()
        queue.append((q, up, half))

    def pass_on(q, h):
        aim = q // 2
        if h < aim:
            @pl.when(z == h)
            def _():
                for half in range(2):
                    if h > 0:
                        hop(q, True, half).wait_recv()
                        add_came(q, rx_up, q - 2, half)
                    send_on(h, q, True, half)
        if h < 3 - aim:
            @pl.when(z == 3 - h)
            def _():
                for half in range(2):
                    if h > 0:
                        hop(q, False, half).wait_recv()
                        add_came(q, rx_dn, q, half)
                    send_on(3 - h, q, False, half)

    last = pltpu.make_async_remote_copy(
        src_ref=parting, dst_ref=peer_out, send_sem=last_sem.at[0], recv_sem=last_sem.at[1],
        device_id=core_near, device_id_type=MESH_ID,
    )

    def finish(q):
        aim = q // 2

        @pl.when(z == aim)
        def _():
            mine = c == q % 2
            for k in range(2):
                if aim > 0:
                    hop(q, True, k).wait_recv()
                if aim < 3:
                    hop(q, False, k).wait_recv()

                def add(i, carry):
                    rows = pl.ds(pl.multiple_of(112 * i, 16), 112)
                    place = pl.ds(pl.multiple_of(HALF * k + 112 * i, 16), 112)
                    total = acc[q, k, rows].astype(f32)
                    if aim > 0:
                        total = total + rx_up[q - 2, k, rows].astype(f32)
                    if aim < 3:
                        total = total + rx_dn[q, k, rows].astype(f32)

                    @pl.when(mine)
                    def _():
                        own_out[place] = total

                    @pl.when(jnp.logical_not(mine))
                    def _():
                        parting[place] = total

                    return carry

                lax.fori_loop(0, HALF // 112, add, 0)

            @pl.when(jnp.logical_not(mine))
            def _():
                last.start()

    def small_step(k):
        near = (core_near, x_near, y_near)[k]
        return pltpu.make_async_remote_copy(
            src_ref=small_mine.at[k], dst_ref=small_rx.at[k], send_sem=sm_send.at[k],
            recv_sem=sm_recv.at[k], device_id=near, device_id_type=MESH_ID,
        )

    def small_next(k):
        small_step(k).wait()
        small_mine[k + 1] = small_mine[k] + small_rx[k]
        if k < 2:
            small_step(k + 1).start()

    def small_hop(d):
        return pltpu.make_async_remote_copy(
            src_ref=small_mine.at[3], dst_ref=small_z.at[d - 1], send_sem=sm_send.at[2 + d],
            recv_sem=sm_recv.at[2 + d], device_id=z_at((z + d) % 4), device_id_type=MESH_ID,
        )

    def load(i, src, dst):
        return pltpu.make_async_copy(src, dst, dist_sem.at[i])

    first_loads = [
        load(0, joint_hbm, joint), load(1, att_hbm, attended), load(2, datt_hbm, dattended),
        load(3, dist_hbm, dist),
    ]
    later_loads = [load(4, normed_hbm, normed), load(5, x_hbm, x_own), load(6, dresid_hbm, dresid)]
    for p in range(3):
        later_loads.append(load(
            7 + p, weight_hbm.at[:, pl.ds(pl.multiple_of(1024 * p + 512 * c, 512), 512)],
            weight.at[:, pl.ds(512 * p, 512)],
        ))
    way_out = Home(result, output, dp, me, out_send, out_recv)
    way_in = Home(dinput, input_gradient, dp, me, in_send, in_recv)
    joint_done = []
    small_left = []

    def small_end():
        for d in (1, 2, 3):
            small_hop(d).start()

    def move(step):
        kind, *at = step
        if kind == "i1":
            start(stage1(at[0]))
        elif kind == "meet":
            meet(at[0])
            met.append(at[0])
            load_ahead(bool(joint_done))
        elif kind == "join":
            pieces.join(at[0])
        elif kind == "hop":
            pass_on(*at)
        elif kind == "fin":
            finish(at[0])
        elif kind == "home":
            (way_out if at[0] == "o" else way_in).start()
        else:
            compute[kind]()
        if small_left:
            wait = small_left.pop(0)
            if wait is not None:
                wait()

    names = [step[0] for step in PLAN]
    attention = [names.index(name) for name in ("a0", "a1", "a2", "a3")]

    def go_on(pair):
        for turn in range(3):
            @pl.when(pair == turn)
            def _():
                if turn == 0:
                    start(later_loads)
                for step in PLAN[attention[turn] + 1 : attention[turn + 1]]:
                    move(step)

    def greet_all():
        start(first_loads)
        load_ahead(False)
        greet(plane_devices(dp, me) + [z_at((z + d) % 4) for d in (1, 2, 3)])

    def wait_loads():
        for copy in first_loads:
            copy.wait()

    compute = {"greet": greet_all, "load": wait_loads}
    for step in PLAN[: attention[0]]:
        move(step)


    def pair_step(pair, carry):
        def lanes(block):
            return pl.ds(pl.multiple_of(512 * block + LANES * pair, LANES), LANES)

        here = lanes(0)
        kt_ref[...] = joint[:, lanes(1)].astype(f32).T.astype(bf16)
        product = (attended[:, here].astype(f32) * dattended[:, here].astype(f32)).T
        delta_ref[0:1, :] = jnp.sum(product[:64], 0, keepdims=True)
        delta_ref[1:2, :] = jnp.sum(product[64:], 0, keepdims=True)
        dk_acc[...] = jnp.zeros_like(dk_acc)
        dv_acc[...] = jnp.zeros_like(dv_acc)
        slope = [slopes[8 * c + 2 * pair + h] for h in range(2)]

        def pairs_of(qb):
            cols = pl.ds(qb * 256, 256)
            queries = both_heads(joint[cols, here])
            grads = both_heads(dattended[cols, here])
            for kb in range(qb + 1):
                rows = pl.ds(kb * 256, 256)
                raw = nt(joint[rows, lanes(1)], queries)
                dprobs = nt(joint[rows, lanes(2)], grads)
                far = dist[rows, cols]
                for h in range(2):
                    side = slice(256 * h, 256 * h + 256)
                    p = jnp.exp(raw[:, side] - slope[h] * far - lse[pair, h : h + 1, cols])
                    p_ref[qb % 2, rows, side] = p.astype(bf16)
                    ds_ref[qb % 2, rows, side] = (
                        p * (dprobs[:, side] - delta_ref[h : h + 1, cols])
                    ).astype(bf16)

        def sums_of(qb):
            cols = pl.ds(qb * 256, 256)
            span = pl.ds(0, 256 * (qb + 1))
            dv_acc[span, :] += nn(p_ref[qb % 2, span, :], both_heads(dattended[cols, here]))
            dk_acc[span, :] += nn(ds_ref[qb % 2, span, :], both_heads(joint[cols, here]))
            dq = nn(kt_ref[:, span], ds_ref[qb % 2, span, :])
            dqt_ref[0:64, cols] = dq[0:64, 0:256]
            dqt_ref[64:128, cols] = dq[64:128, 256:512]

        pairs_of(0)
        for qb in range(4):
            if qb < 3:
                pairs_of(qb + 1)
            sums_of(qb)
        djoint[:, lanes(0)] = (dqt_ref[...] * 0.125).T.astype(bf16)
        djoint[:, lanes(1)] = dk_acc[...].astype(bf16)
        djoint[:, lanes(2)] = dv_acc[...].astype(bf16)
        go_on(pair)
        return carry

    lax.fori_loop(0, 4, pair_step, 0)

    def block_copy(slot, i):
        return pltpu.make_async_copy(
            blocks.at[slot], flat.at[pl.ds(JOINT_AT + 3072 * i, 3072)], block_sem.at[slot]
        )

    def joint_gradient():
        for copy in later_loads:
            copy.wait()
        for i in range(4):
            if i >= 2:
                block_copy(i % 2, i - 2).wait()
            block = tn(normed[:, 256 * i : 256 * i + 256], djoint[...]).astype(bf16)
            blocks[i % 2] = block.reshape(3072, LANES)
            block_copy(i % 2, i).start()
        for i in (2, 3):
            block_copy(i % 2, i).wait()
        joint_done.append(True)
        load_ahead(True)

    dn_own, dn_part = dist.at[pl.ds(0, 512)], dist.at[pl.ds(512, 512)]
    dn_swap = pltpu.make_async_remote_copy(
        src_ref=dn_part, dst_ref=dn_rx, send_sem=swap_sem.at[0], recv_sem=swap_sem.at[1],
        device_id=core_near, device_id_type=MESH_ID,
    )

    def norm_part():
        dn_part[...] = nt(djoint[other, :], weight[...])
        dn_swap.start()

    def norm_own():
        dn_own[...] = nt(djoint[own, :], weight[...])
        bias_sums = nn(jnp.ones((8, TOKENS), bf16), djoint[...])
        half = pl.ds(pl.multiple_of(512 * c, 512), 512)
        small_mine[0] = jnp.zeros(small_mine.shape[1:], f32)
        small_mine[0, 2:3, half] = bias_sums[0:1, :512]
        small_mine[0, 3:4, half] = bias_sums[0:1, 1024:]
        small_mine[0, 4:7, :] = mid_sums[0:3, :]
        small_mine[0, 7:11, half] = expand_sums[...]
        small_mine[0, 11:12, :] = mid_sums[3:4, :]

    def norm_back_rows():
        dn_swap.wait()

        def back_rows(i, carry):
            rows = pl.ds(pl.multiple_of(128 * i, 128), 128)
            values = x_own[rows, :].astype(f32)
            center = values - jnp.mean(values, -1, keepdims=True)
            factor = lax.rsqrt(jnp.mean(center * center, -1, keepdims=True) + norm_epsilon)
            unit = center * factor
            dn = dn_own[rows, :] + dn_rx[rows, :]
            e = dn * mid_sums[4:5, :]
            down = dresid[rows, :] + factor * (
                e - jnp.mean(e, -1, keepdims=True) - unit * jnp.mean(e * unit, -1, keepdims=True)
            )
            dinput[rows, :] = down.astype(bf16)
            small_mine[0, 0:1, :] += jnp.sum(dn * unit, 0, keepdims=True)
            small_mine[0, 1:2, :] += jnp.sum(dn, 0, keepdims=True)
            return carry

        lax.fori_loop(0, 4, back_rows, 0)
        small_step(0).start()
        for k in range(3):
            small_left.extend([None, None, functools.partial(small_next, k)])
        small_left.append(small_end)

    def rest_of_small():
        while small_left:
            wait = small_left.pop(0)
            if wait is not None:
                wait()
        for d in (1, 2, 3):
            small_hop(d).wait()

    compute.update(
        J=joint_gradient, dnp=norm_part, dno=norm_own, ln=norm_back_rows, end=rest_of_small
    )
    for step in PLAN[attention[3] + 1 :]:
        move(step)
    small = (small_mine[3] + small_z[1]) + (small_z[0] + small_z[2])
    small_out[...] = small.reshape(small_out.shape)

    last.wait()
    way_out.wait()
    way_in.wait()
    for q in sorted(set(range(8)) - set(MIDDLE_EARLY)):
        for copy in stage1(q):
            copy.wait_send()
    for q in range(8):
        for copy in pieces.second(q):
            copy.wait_send()
    for (plane, _), queue in on_way.items():
        @pl.when(z == plane)
        def _():
            for sent in queue[-2:]:
                hop(*sent).wait_send()


def rear(
    slopes, joint, attended, dattended, dist, lse, normed, weight, x_own, dresid, result,
    mid_sums, expand_sums, mid_a, mid_b, flat,
):
    f32, bf16 = jnp.float32, jnp.bfloat16
    vmem = pl.BlockSpec(memory_space=pltpu.VMEM)
    hbm = pl.BlockSpec(memory_space=pl.ANY)
    home = jax.ShapeDtypeStruct((2, 256, WIDTH), bf16)
    piece = jax.ShapeDtypeStruct((PIECE, LANES), f32)
    return pl.pallas_call(
        rear_kernel,
        out_shape=(
            jax.ShapeDtypeStruct((FLAT_ROWS, LANES), bf16),
            piece,
            piece,
            jax.ShapeDtypeStruct((LANES, LANES), f32),
            home,
            home,
        ),
        in_specs=[pl.BlockSpec(memory_space=pltpu.SMEM)] + [hbm] * 4 + [vmem] + [hbm] * 5
        + [vmem] * 2 + [hbm] * 3,
        out_specs=[hbm] + [vmem] * 3 + [hbm] * 2,
        scratch_shapes=[
            pltpu.VMEM((TOKENS, 1536), bf16),
            pltpu.VMEM((TOKENS, 512), bf16),
            pltpu.VMEM((TOKENS, 512), bf16),
            pltpu.VMEM((TOKENS, WIDTH), bf16),
            pltpu.VMEM((WIDTH, 1536), bf16),
            pltpu.VMEM((512, WIDTH), bf16),
            pltpu.VMEM((512, WIDTH), f32),
            pltpu.VMEM((TOKENS, TOKENS), f32),
            pltpu.VMEM((2, TOKENS, 512), bf16),
            pltpu.VMEM((2, TOKENS, 512), bf16),
            pltpu.VMEM((LANES, TOKENS), bf16),
            pltpu.VMEM((LANES, TOKENS), f32),
            pltpu.VMEM((TOKENS, LANES), f32),
            pltpu.VMEM((TOKENS, LANES), f32),
            pltpu.VMEM((8, TOKENS), f32),
            pltpu.VMEM((TOKENS, 1536), bf16),
            pltpu.VMEM((512, WIDTH), f32),
            pltpu.VMEM((512, WIDTH), bf16),
            pltpu.VMEM((2, 3072, LANES), bf16),
            pltpu.VMEM((4, 2, HALF, LANES), bf16),
            pltpu.VMEM((4, 2, HALF, LANES), bf16),
            pltpu.VMEM((8, 2, HALF, LANES), bf16),
            pltpu.VMEM((8, 2, HALF, LANES), bf16),
            pltpu.VMEM((8, HALF, LANES), bf16),
            pltpu.VMEM((8, HALF, LANES), bf16),
            pltpu.VMEM((8, 2, HALF, LANES), bf16),
            pltpu.VMEM((6, 2, HALF, LANES), bf16),
            pltpu.VMEM((6, 2, HALF, LANES), bf16),
            pltpu.VMEM((PIECE, LANES), f32),
            pltpu.VMEM((4, 16, WIDTH), f32),
            pltpu.VMEM((3, 16, WIDTH), f32),
            pltpu.VMEM((3, 16, WIDTH), f32),
            pltpu.SemaphoreType.DMA((10,)),
            pltpu.SemaphoreType.DMA((2,)),
            pltpu.SemaphoreType.DMA((2,)),
            pltpu.SemaphoreType.DMA((8, 4, 2)),
            pltpu.SemaphoreType.DMA((8, 2, 2)),
            pltpu.SemaphoreType.DMA((8, 2, 2)),
            pltpu.SemaphoreType.DMA((8, 2)),
            pltpu.SemaphoreType.DMA((8, 2)),
            pltpu.SemaphoreType.DMA((8, 2, 2)),
            pltpu.SemaphoreType.DMA((8, 2, 2)),
            pltpu.SemaphoreType.DMA((2,)),
            pltpu.SemaphoreType.DMA((6,)),
            pltpu.SemaphoreType.DMA((6,)),
            pltpu.SemaphoreType.DMA((2,)),
            pltpu.SemaphoreType.DMA((2,)),
            pltpu.SemaphoreType.DMA((2,)),
            pltpu.SemaphoreType.DMA((2,)),
        ],
        input_output_aliases={15: 0},
        compiler_params=pltpu.CompilerParams(
            collective_id=2, has_side_effects=True, vmem_limit_bytes=62 << 20
        ),
        cost_estimate=pl.CostEstimate(flops=30 << 30, bytes_accessed=30 << 20, transcendentals=0),
    )(
        slopes, joint, attended, dattended, dist, lse, normed, weight, x_own, dresid, result,
        mid_sums, expand_sums, mid_a, mid_b, flat,
    )


def middle_kernel(
    attended, x_own, cot, mixer_bias_in, gain_in, shift_in, reduce_bias_in, expand_bias_in, gain_before_in,
    mixer_hbm, expand_hbm, reduce_hbm,
    result, dresid, dattended, sums, expand_sums, flat, rx_a, rx_b,
    vectors, mixer, expand, reduce, att_rx, resid, normal, spread, normed, act, act_rx, dhidden,
    dn_own, dn_part, dn_rx, out_part, out_rx, dbranch, blocks,
    weight_sem, block_sem, send_sem, recv_sem, act_send, act_recv, s1_send, s1_recv,
):
    f32, bf16 = jnp.float32, jnp.bfloat16
    dp = lax.axis_index("dp")
    me = lax.axis_index("group")
    c = dp % 2
    near = (dp + 1 - 2 * c, me)
    own = pl.ds(pl.multiple_of(512 * c, 512), 512)
    other = pl.ds(pl.multiple_of(512 * (1 - c), 512), 512)

    weights = [pltpu.make_async_copy(mixer_hbm, mixer, weight_sem.at[0])]
    for k in range(4):
        part = pl.ds(pl.multiple_of(512 * (2 * k + c), 512), 512)
        weights.append(pltpu.make_async_copy(
            expand_hbm.at[:, part], expand.at[:, pl.ds(512 * k, 512)], weight_sem.at[1 + k]
        ))
    for k in range(4):
        part = pl.ds(pl.multiple_of(512 * (2 * k + c), 512), 512)
        weights.append(pltpu.make_async_copy(
            reduce_hbm.at[part], reduce.at[pl.ds(512 * k, 512)], weight_sem.at[5 + k]
        ))
    for copy in weights:
        copy.start()

    y, x = me // 2, me % 2
    greet([near, (dp, 2 * y + 1 - x), (dp, 2 * (1 - y) + x)])

    def swap(i, src, dst):
        return pltpu.make_async_remote_copy(
            src_ref=src, dst_ref=dst, send_sem=send_sem.at[i], recv_sem=recv_sem.at[i],
            device_id=near, device_id_type=MESH_ID,
        )

    att_swap = swap(0, attended, att_rx)
    normed_swap = swap(1, normed.at[own], normed.at[own])
    dn_swap = swap(2, dn_part, dn_rx)
    out_swap = swap(3, out_part, out_rx)
    branch_swap = swap(4, dbranch.at[own], dbranch.at[own])
    att_swap.start()

    for k, given in enumerate((mixer_bias_in, gain_in, shift_in, reduce_bias_in)):
        vectors[k : k + 1, :] = given[...].astype(f32).reshape(1, WIDTH)
    vectors[4:8, :] = expand_bias_in[...].astype(f32).reshape(4, WIDTH)
    mixer_bias, gain, shift, reduce_bias = (vectors[k : k + 1, :] for k in range(4))

    weights[0].wait()
    resid[...] = nn(attended[own, :], mixer[own, :]) + (x_own[...].astype(f32) + mixer_bias)
    att_swap.wait_recv()
    resid[...] += nn(att_rx[own, :], mixer[other, :])

    def norm_rows(i, carry):
        rows = pl.ds(pl.multiple_of(128 * i, 128), 128)
        here = pl.ds(pl.multiple_of(512 * c + 128 * i, 128), 128)
        values = resid[rows, :]
        center = values - jnp.mean(values, -1, keepdims=True)
        factor = lax.rsqrt(jnp.mean(center * center, -1, keepdims=True) + norm_epsilon)
        unit = center * factor
        normal[rows, :] = unit
        spread[rows, :] = jnp.broadcast_to(factor, (128, LANES))
        normed[here, :] = (unit * gain + shift).astype(bf16)
        return carry

    lax.fori_loop(0, 4, norm_rows, 0)
    normed_swap.start()

    def act_swap(half, k):
        rows = pl.ds(pl.multiple_of(512 * half, 512), 512)
        cols = pl.ds(pl.multiple_of(512 * k, 512), 512)
        return pltpu.make_async_remote_copy(
            src_ref=act.at[rows, cols], dst_ref=act_rx.at[rows, cols],
            send_sem=act_send.at[half, k], recv_sem=act_recv.at[half, k],
            device_id=near, device_id_type=MESH_ID,
        )

    root = math.sqrt(2.0 / math.pi)
    right = pl.ds(pl.multiple_of(512 * c, 512), 512)

    def products(half, k):
        rows = pl.ds(pl.multiple_of(512 * half, 512), 512)
        cols = pl.ds(pl.multiple_of(512 * k, 512), 512)
        u = nn(normed[rows, :], expand[:, cols]) + vectors[pl.ds(4 + k, 1), right]
        return u, nt(cot[rows, :], reduce[cols, :])

    def gelu_block(half, k, first, u, dact):
        rows = pl.ds(pl.multiple_of(512 * half, 512), 512)
        cols = pl.ds(pl.multiple_of(512 * k, 512), 512)
        square = u * u
        t = jnp.tanh(u * (root + (root * 0.044715) * square))
        up = 0.5 + 0.5 * t
        act[rows, cols] = (u * up).astype(bf16)
        slope = up + (0.5 * u) * (1.0 - t * t) * (root + (3.0 * root * 0.044715) * square)
        dh = (dact * slope).astype(bf16)
        dhidden[rows, cols] = dh
        total = jnp.sum(dh.astype(f32), 0, keepdims=True)
        if first:
            expand_sums[pl.ds(k, 1), :] = total
        else:
            expand_sums[pl.ds(k, 1), :] += total
        act_swap(half, k).start()

    def out_copies(slot, places):
        return [
            pltpu.make_async_copy(
                blocks.at[slot, pl.ds(2048 * part, 2048)],
                flat.at[pl.ds(pl.multiple_of(at, 16), 2048)], block_sem.at[slot, part],
            )
            for part, at in enumerate(places)
        ]

    def emit(block, slot, places):
        blocks[slot, : 2048 * len(places)] = block.astype(bf16).reshape(2048 * len(places), LANES)
        for copy in out_copies(slot, places):
            copy.start()

    def drain(slot, places):
        for copy in out_copies(slot, places):
            copy.wait()

    for copy in weights[1:]:
        copy.wait()

    def reduce_places(pair, parity):
        return [REDUCE_AT + 2048 * (2 * (2 * pair + k) + parity) for k in range(2)]

    stages = [
        first_stage(q, flat, rx_a, rx_b, at, s1_send, s1_recv, dp, me)
        for at, q in enumerate(MIDDLE_EARLY)
    ]

    def hidden_pair(turn, carry):
        pair = 1 - turn
        k = [2 * pair, 2 * pair + 1]
        a = products(c, k[0])
        b = products(c, k[1])
        gelu_block(c, k[0], True, *a)

        @pl.when(turn == 0)
        def _():
            normed_swap.wait_recv()

        @pl.when(turn == 1)
        def _():
            drain(0, reduce_places(1, c))
            drain(1, reduce_places(1, 1 - c))
            for copy in stages[0]:
                copy.start()

        a = products(1 - c, k[0])
        gelu_block(c, k[1], True, *b)
        b = products(1 - c, k[1])
        gelu_block(1 - c, k[0], False, *a)
        gelu_block(1 - c, k[1], False, *b)
        left = pl.ds(pl.multiple_of(1024 * pair, 1024), 1024)
        emit(tn(act[:, left], cot[:, right]), 0, reduce_places(pair, c))
        for half in range(2):
            for one in k:
                act_swap(half, one).wait()
        emit(tn(act_rx[:, left], cot[:, right]), 1, reduce_places(pair, 1 - c))
        return carry

    lax.fori_loop(0, 2, hidden_pair, 0)
    drain(0, reduce_places(0, c))
    drain(1, reduce_places(0, 1 - c))
    for copy in stages[1]:
        copy.start()

    def expand_places(i):
        return [EXPAND_AT + 4096 * i, EXPAND_AT + 4096 * i + 2048]

    def expand_step(i, carry):
        block = tn(normed[:, pl.ds(pl.multiple_of(256 * i, 256), 256)], dhidden[...])

        @pl.when(i >= 2)
        def _():
            drain(i % 2, expand_places(i - 2))

        emit(block, i % 2, expand_places(i))
        return carry

    lax.fori_loop(0, 4, expand_step, 0)
    drain(0, expand_places(2))
    drain(1, expand_places(3))
    for copies in stages[2:]:
        for copy in copies:
            copy.start()

    dn_part[...] = nt(dhidden[other, :], expand[...])
    dn_swap.start()
    out_part[...] = nn(act[other, :], reduce[...]).astype(bf16)
    out_swap.start()

    dn_own[...] = nt(dhidden[own, :], expand[...])
    dn_swap.wait()
    sums[...] = jnp.zeros_like(sums)
    sums[4:5, :] = gain_before_in[...].astype(f32).reshape(1, WIDTH)

    def back_rows(i, carry):
        rows = pl.ds(pl.multiple_of(128 * i, 128), 128)
        here = pl.ds(pl.multiple_of(512 * c + 128 * i, 128), 128)
        dn = dn_own[rows, :] + dn_rx[rows, :]
        unit = normal[rows, :]
        grad = cot[here, :].astype(f32)
        e = dn * gain
        down = grad + spread[rows, 0:1] * (
            e - jnp.mean(e, -1, keepdims=True) - unit * jnp.mean(e * unit, -1, keepdims=True)
        )
        dresid[rows, :] = down
        low = down.astype(bf16)
        dbranch[here, :] = low
        sums[0:1, :] += jnp.sum(low.astype(f32), 0, keepdims=True)
        sums[1:2, :] += jnp.sum(dn * unit, 0, keepdims=True)
        sums[2:3, :] += jnp.sum(dn, 0, keepdims=True)
        sums[3:4, :] += jnp.sum(grad, 0, keepdims=True)
        return carry

    lax.fori_loop(0, 4, back_rows, 0)
    branch_swap.start()
    dattended[own, :] = nt(dbranch[own, :], mixer[own, :]).astype(bf16)
    resid[...] += nn(act[own, :], reduce[...])
    out_swap.wait()
    result[...] = (resid[...] + (out_rx[...].astype(f32) + reduce_bias)).astype(bf16)
    branch_swap.wait()
    dattended[other, :] = nt(dbranch[other, :], mixer[own, :]).astype(bf16)
    emit(tn(attended[...], dbranch[:, right]), 0, [MIXER_AT + 2048 * c])
    emit(tn(att_rx[...], dbranch[:, right]), 1, [MIXER_AT + 2048 * (1 - c)])
    drain(0, [MIXER_AT + 2048 * c])
    drain(1, [MIXER_AT + 2048 * (1 - c)])
    att_swap.wait_send()
    normed_swap.wait_send()
    for copies in stages:
        for copy in copies:
            copy.wait()


def middle(attended, x_own, cot, small, mixer, expand, reduce):
    f32, bf16 = jnp.float32, jnp.bfloat16
    vmem = pl.BlockSpec(memory_space=pltpu.VMEM)
    hbm = pl.BlockSpec(memory_space=pl.ANY)
    count = len(MIDDLE_EARLY)
    early = jax.ShapeDtypeStruct((count, 2, HALF, LANES), bf16)
    return pl.pallas_call(
        middle_kernel,
        out_shape=(
            jax.ShapeDtypeStruct((512, WIDTH), bf16),
            jax.ShapeDtypeStruct((512, WIDTH), f32),
            jax.ShapeDtypeStruct((TOKENS, 512), bf16),
            jax.ShapeDtypeStruct((8, WIDTH), f32),
            jax.ShapeDtypeStruct((4, 512), f32),
            jax.ShapeDtypeStruct((FLAT_ROWS, LANES), bf16),
            early,
            early,
        ),
        in_specs=[vmem] * 9 + [hbm] * 3,
        out_specs=[vmem] * 5 + [hbm] * 3,
        scratch_shapes=[
            pltpu.VMEM((8, WIDTH), f32),
            pltpu.VMEM((WIDTH, WIDTH), bf16),
            pltpu.VMEM((WIDTH, 2048), bf16),
            pltpu.VMEM((2048, WIDTH), bf16),
            pltpu.VMEM((TOKENS, 512), bf16),
            pltpu.VMEM((512, WIDTH), f32),
            pltpu.VMEM((512, WIDTH), f32),
            pltpu.VMEM((512, LANES), f32),
            pltpu.VMEM((TOKENS, WIDTH), bf16),
            pltpu.VMEM((TOKENS, 2048), bf16),
            pltpu.VMEM((TOKENS, 2048), bf16),
            pltpu.VMEM((TOKENS, 2048), bf16),
            pltpu.VMEM((512, WIDTH), f32),
            pltpu.VMEM((512, WIDTH), f32),
            pltpu.VMEM((512, WIDTH), f32),
            pltpu.VMEM((512, WIDTH), bf16),
            pltpu.VMEM((512, WIDTH), bf16),
            pltpu.VMEM((TOKENS, WIDTH), bf16),
            pltpu.VMEM((2, 4096, LANES), bf16),
            pltpu.SemaphoreType.DMA((9,)),
            pltpu.SemaphoreType.DMA((2, 2)),
            pltpu.SemaphoreType.DMA((5,)),
            pltpu.SemaphoreType.DMA((5,)),
            pltpu.SemaphoreType.DMA((2, 4)),
            pltpu.SemaphoreType.DMA((2, 4)),
            pltpu.SemaphoreType.DMA((count, 2, 2)),
            pltpu.SemaphoreType.DMA((count, 2, 2)),
        ],
        compiler_params=pltpu.CompilerParams(
            collective_id=1, has_side_effects=True, vmem_limit_bytes=62 << 20
        ),
        cost_estimate=pl.CostEstimate(flops=30 << 30, bytes_accessed=40 << 20, transcendentals=0),
    )(attended, x_own, cot, *small, mixer, expand, reduce)


UPDATE_ROWS = 616


def owner_table(owners):
    smalls = ((0, 2, 0), (U_JBIAS, U_MIXER, 16), (U_MBIAS, U_EXPAND, 32), (U_EBIAS, U_REDUCE, 56),
              (U_RBIAS, 12300, 88))
    table = []
    for owner in range(owners):
        begin = OWNED_ROWS * owner
        end = begin + OWNED_ROWS
        start = piece_start(owner)
        shift, later = section_shift(begin // 8), section_shift((end - 1) // 8)
        turn = next((8 * u - begin for u in (U_JBIAS, U_MBIAS) if begin < 8 * u < end), OWNED_ROWS)
        row = [begin + 2 * shift - 2 * start, begin + 2 * later - 2 * start, turn, 0, 0, 0, 3 * owner, 0]
        for first, past, at in smalls:
            if 8 * first < end and 8 * past > begin:
                row[3] = at + begin - 8 * first
                row[4] = max(8 * first - begin, 0)
                row[5] = min(8 * past - begin, OWNED_ROWS)
        assert 0 <= row[0] <= row[1] <= 2 * PIECE - 5 * UPDATE_ROWS
        table.append(row)
    return table


def update_kernel(
    table, step_count, learn_rate, master, first, second, own, peer, small, out_hbm, in_hbm,
    new_master, new_first, new_second, small_share, out_copy, in_copy,
    rows, small_rows, held, sem,
):
    f32 = jnp.float32
    i = pl.program_id(0)
    c = lax.axis_index("dp") % 2
    owner = lax.axis_index("dp") * lax.axis_size("group") + lax.axis_index("group")
    place = [table[owner, k] for k in range(7)]
    pairs = ((out_hbm, out_copy), (in_hbm, in_copy))
    fetch = [pltpu.make_async_copy(src, held.at[k], sem.at[k]) for k, (src, _) in enumerate(pairs)]
    give = [pltpu.make_async_copy(held.at[k], dst, sem.at[2 + k]) for k, (_, dst) in enumerate(pairs)]

    @pl.when(i == 0)
    def _():
        for copy in fetch:
            copy.start()
        small_rows[...] = jnp.zeros_like(small_rows)
        small_rows[UPDATE_ROWS : UPDATE_ROWS + LANES, :] = small[...]
        small_share[...] = small_rows[pl.ds(UPDATE_ROWS + place[6], 3), :]

        def weave(k, carry):
            part = pl.ds(pl.multiple_of(112 * k, 16), 112)
            mine, other = own[part, :], peer[part, :]
            even = jnp.where(c == 0, mine, other).reshape(28, 4, LANES)
            odd = jnp.where(c == 0, other, mine).reshape(28, 4, LANES)
            rows[pl.ds(pl.multiple_of(224 * k, 32), 224), :] = jnp.concatenate([even, odd], 1).reshape(
                224, LANES
            )
            return carry

        lax.fori_loop(0, PIECE // 112, weave, 0)

    @pl.when(i == 2)
    def _():
        for copy in fetch:
            copy.wait()
        for copy in give:
            copy.start()

    base = UPDATE_ROWS * i
    k = lax.broadcasted_iota(jnp.int32, (UPDATE_ROWS, LANES), 0) + base
    grad = jnp.where(
        k < place[2],
        rows[pl.ds(place[0] + base, UPDATE_ROWS), :],
        rows[pl.ds(place[1] + base, UPDATE_ROWS), :],
    )
    at = jnp.clip(place[3] + base, -UPDATE_ROWS, LANES) + UPDATE_ROWS
    grad = jnp.where(
        (k >= place[4]) & (k < place[5]), small_rows[pl.ds(at, UPDATE_ROWS), :], grad
    )
    rate = learn_rate[0]
    moment_step = jnp.full((1, LANES), step_count[0].astype(f32))
    fix_one = 1.0 - jnp.exp(moment_step * math.log(beta_first))
    fix_two = 1.0 - jnp.exp(moment_step * math.log(beta_second))
    one = beta_first * first[...] + (1.0 - beta_first) * grad
    two = beta_second * second[...] + (1.0 - beta_second) * grad * grad
    weights = master[...]
    new_first[...] = one
    new_second[...] = two
    new_master[...] = weights - rate * (
        one / fix_one / (jnp.sqrt(two / fix_two) + adam_epsilon) + weight_decay * weights
    )

    @pl.when(i == pl.num_programs(0) - 1)
    def _():
        for copy in give:
            copy.wait()


def update(table, step_count, learn_rate, master, first, second, own, peer, small, output, input_gradient):
    f32 = jnp.float32
    smem = pl.BlockSpec(memory_space=pltpu.SMEM)
    hbm = pl.BlockSpec(memory_space=pl.ANY)
    block = pl.BlockSpec((UPDATE_ROWS, LANES), lambda i: (i, 0))

    def whole(shape):
        return pl.BlockSpec(shape, lambda i: (0, 0))

    flat = jax.ShapeDtypeStruct((OWNED_ROWS, LANES), f32)
    home = jax.ShapeDtypeStruct(output.shape, output.dtype)
    new = pl.pallas_call(
        update_kernel,
        grid=(5,),
        out_shape=(flat, flat, flat, jax.ShapeDtypeStruct((3, LANES), f32), home, home),
        in_specs=[smem, smem, smem] + [block] * 3
        + [whole((PIECE, LANES)), whole((PIECE, LANES)), whole((LANES, LANES))] + [hbm] * 2,
        out_specs=[block] * 3 + [whole((3, LANES))] + [hbm] * 2,
        scratch_shapes=[
            pltpu.VMEM((2 * PIECE, LANES), f32),
            pltpu.VMEM((2 * UPDATE_ROWS + LANES, LANES), f32),
            pltpu.VMEM((2,) + output.shape, output.dtype),
            pltpu.SemaphoreType.DMA((4,)),
        ],
        compiler_params=pltpu.CompilerParams(vmem_limit_bytes=62 << 20),
    )(
        table, step_count, learn_rate, *[whole_array.reshape(OWNED_ROWS, LANES) for whole_array in (master, first, second)],
        own, peer, small, output, input_gradient,
    )
    return [part.reshape(-1) for part in new[:4]] + list(new[4:])


def on_device_chip(
    dp_size, group_size,
    activations, cotangent, segments, padding, step_count, learn_rate,
    gain_before, shift_before, joint_weight, joint_bias, mixer_weight, mixer_bias,
    gain_middle, shift_middle, expand_weight, expand_bias, reduce_weight, reduce_bias,
    master_weights, first_moment, second_moment,
):
    f32, bf16 = jnp.float32, jnp.bfloat16
    dp = lax.axis_index("dp")
    group = lax.axis_index("group")
    c = dp % 2
    slopes = jnp.asarray([2.0 ** (-8.0 * (h + 1) / HEADS) for h in range(HEADS)], f32)
    x_own, cot_all, normed_one, joint, dist, attended, lse = front(
        slopes, activations, cotangent, segments, padding, gain_before, shift_before, joint_bias,
        joint_weight,
    )
    result, dresid, dattended, middle_sums, expand_sums, flat, mid_a, mid_b = middle(
        attended, x_own, cot_all, (mixer_bias, gain_middle, shift_middle, reduce_bias, expand_bias, gain_before),
        mixer_weight, expand_weight, reduce_weight,
    )
    _, own, peer, small_sum, output, input_gradient = rear(
        slopes, joint, attended, dattended, dist, lse, normed_one, joint_weight, x_own, dresid,
        result, middle_sums, expand_sums, mid_a, mid_b, flat,
    )
    table = jnp.asarray(owner_table(dp_size * group_size), jnp.int32)
    new_master, new_first, new_second, small_share, output, input_gradient = update(
        table, step_count, learn_rate, master_weights, first_moment, second_moment, own, peer, small_sum, output,
        input_gradient,
    )
    return (output, input_gradient, new_master, new_first, new_second, small_share)


def on_device(dp_size, group_size, activations, *rest):
    if (dp_size, group_size) == (8, 4) and activations.shape == (2, 256, WIDTH):
        return on_device_chip(dp_size, group_size, activations, *rest)
    return on_device_general(activations, *rest)


def solution(mesh):
    in_specs = (
        P("dp", "group", None),
        P("dp", "group", None),
        P("dp", None),
        P("dp", None),
        P(),
        P(),
        P(),
        P(),
        P(),
        P(),
        P(),
        P(),
        P(),
        P(),
        P(),
        P(),
        P(),
        P(),
        P(("dp", "group")),
        P(("dp", "group")),
        P(("dp", "group")),
    )
    out_specs = (
        P("dp", "group", None),
        P("dp", "group", None),
        P(("dp", "group")),
        P(("dp", "group")),
        P(("dp", "group")),
        P(("dp", "group")),
    )
    return jax.shard_map(
        functools.partial(on_device, mesh.shape["dp"], mesh.shape["group"]), mesh=mesh, in_specs=in_specs, out_specs=out_specs, check_vma=False
    )
```

```python
import functools
import math

import jax
import jax.numpy as jnp
from jax import lax
from jax.experimental import pallas as pl
from jax.experimental.pallas import tpu as pltpu
from jax.sharding import PartitionSpec as P

HEADS = 16
DOC_MOST = 800


beta_first = 0.9
beta_second = 0.95
adam_epsilon = 1e-08
weight_decay = 0.1
norm_epsilon = 1e-05
masked_score = -1e30


def shifted(block, axis, distance):
    devices = range(lax.axis_size(axis))
    route = [(i - distance, i) for i in devices if i - distance in devices]
    return lax.ppermute(block, axis, route)


def standardize(values):
    center = values - jnp.mean(values, -1, keepdims=True)
    spread = lax.rsqrt(jnp.mean(center * center, -1, keepdims=True) + norm_epsilon)
    return (center * spread, spread)


def norm_back(dnormed, normed, spread):
    return spread * (
        dnormed
        - jnp.mean(dnormed, -1, keepdims=True)
        - normed * jnp.mean(dnormed * normed, -1, keepdims=True)
    )


def window_mask(segments, padding, member, hop, block_len):
    places = jnp.arange(block_len, dtype=jnp.int32)
    source = member - hop
    query_place = member * block_len + places
    key_place = source * block_len + places
    start = jnp.maximum(source, 0) * block_len
    seg_query = lax.dynamic_slice_in_dim(segments, member * block_len, block_len, 1)
    seg_key = lax.dynamic_slice_in_dim(segments, start, block_len, 1)
    pad_key = lax.dynamic_slice_in_dim(padding, start, block_len, 1)
    earlier = key_place[None, None, :] <= query_place[None, :, None]
    itself = key_place[None, None, :] == query_place[None, :, None]
    allowed = (
        (seg_query[:, :, None] == seg_key[:, None, :])
        & earlier
        & ((pad_key[:, None, :] == 1) | itself)
        & (source >= 0)
    )
    distance = (query_place[:, None] - key_place[None, :]).astype(jnp.float32)
    return (allowed[:, None], distance)


def piece_scores(query4, key4, slopes, distance, score_scale):
    raw = jnp.einsum("sqhd,skhd->shqk", query4, key4, preferred_element_type=jnp.float32)
    return raw * score_scale - slopes[:, None, None] * distance[None]


def on_device_general(
    activations,
    cotangent,
    segments,
    padding,
    step_count,
    learn_rate,
    gain_before,
    shift_before,
    joint_weight,
    joint_bias,
    mixer_weight,
    mixer_bias,
    gain_middle,
    shift_middle,
    expand_weight,
    expand_bias,
    reduce_weight,
    reduce_bias,
    master_weights,
    first_moment,
    second_moment,
):
    seq_count, block_len, width = activations.shape
    head_size = width // HEADS
    row_count = seq_count * block_len
    shape4 = (seq_count, block_len, HEADS, head_size)
    score_scale = 1.0 / math.sqrt(head_size)
    group_size = lax.axis_size("group")
    member = lax.axis_index("group")
    reach = min((DOC_MOST + block_len - 2) // block_len, group_size - 1)
    slopes = jnp.exp2(-8.0 * (jnp.arange(HEADS, dtype=jnp.float32) + 1.0) / HEADS)
    inputs = activations.reshape(row_count, width).astype(jnp.float32)
    gain_one = gain_before.astype(jnp.float32)
    gain_two = gain_middle.astype(jnp.float32)
    normal_one, spread_one = standardize(inputs)
    normed_one = (normal_one * gain_one + shift_before.astype(jnp.float32)).astype(jnp.bfloat16)
    joint = jnp.dot(normed_one, joint_weight, preferred_element_type=jnp.float32)
    bias_joint = joint_bias.astype(jnp.float32)
    query_rows = (joint[:, :width] + bias_joint[:width]).astype(jnp.bfloat16)
    key_rows = joint[:, width : 2 * width].astype(jnp.bfloat16)
    value_rows = (joint[:, 2 * width :] + bias_joint[width:]).astype(jnp.bfloat16)
    own_piece = jnp.stack([key_rows, value_rows]).reshape(2, seq_count, block_len, width)
    query4 = query_rows.reshape(shape4)
    pieces = [own_piece]
    for hop in range(1, reach + 1):
        pieces.append(shifted(own_piece, "group", hop))
    row_top = jnp.full((seq_count, HEADS, block_len), masked_score, jnp.float32)
    row_total = jnp.zeros((seq_count, HEADS, block_len), jnp.float32)
    for hop in range(reach + 1):
        allowed, distance = window_mask(segments, padding, member, hop, block_len)
        scores = piece_scores(query4, pieces[hop][0].reshape(shape4), slopes, distance, score_scale)
        fresh = jnp.maximum(row_top, jnp.max(jnp.where(allowed, scores, masked_score), -1))
        row_total = row_total * jnp.exp(row_top - fresh) + jnp.sum(
            jnp.exp(jnp.where(allowed, scores - fresh[..., None], masked_score)), -1
        )
        row_top = fresh
    log_total = row_top + jnp.log(row_total)
    attended = jnp.zeros(shape4, jnp.float32)
    for hop in range(reach + 1):
        allowed, distance = window_mask(segments, padding, member, hop, block_len)
        scores = piece_scores(query4, pieces[hop][0].reshape(shape4), slopes, distance, score_scale)
        probs = jnp.exp(jnp.where(allowed, scores - log_total[..., None], masked_score)).astype(
            jnp.bfloat16
        )
        attended = attended + jnp.einsum(
            "shqk,skhd->sqhd",
            probs,
            pieces[hop][1].reshape(shape4),
            preferred_element_type=jnp.float32,
        )
    attended_low = attended.reshape(row_count, width).astype(jnp.bfloat16)
    resid = inputs + (
        jnp.dot(attended_low, mixer_weight, preferred_element_type=jnp.float32)
        + mixer_bias.astype(jnp.float32)
    )
    normal_two, spread_two = standardize(resid)
    normed_two = (normal_two * gain_two + shift_middle.astype(jnp.float32)).astype(jnp.bfloat16)
    hidden = jnp.dot(
        normed_two, expand_weight, preferred_element_type=jnp.float32
    ) + expand_bias.astype(jnp.float32)
    act = jax.nn.gelu(hidden, approximate=True).astype(jnp.bfloat16)
    result = resid + (
        jnp.dot(act, reduce_weight, preferred_element_type=jnp.float32)
        + reduce_bias.astype(jnp.float32)
    )
    output = result.astype(jnp.bfloat16).reshape(seq_count, block_len, width)
    cot_low = cotangent.reshape(row_count, width)
    cot_full = cot_low.astype(jnp.float32)
    reduce_grad = jnp.einsum("tf,td->fd", act, cot_low, preferred_element_type=jnp.float32)
    reduce_bias_grad = jnp.sum(cot_full, 0)
    dact = jnp.einsum("td,fd->tf", cot_low, reduce_weight, preferred_element_type=jnp.float32)
    gelu_pull = jax.vjp(lambda inner: jax.nn.gelu(inner, approximate=True), hidden)[1]
    dhidden = gelu_pull(dact)[0].astype(jnp.bfloat16)
    expand_grad = jnp.einsum("td,tf->df", normed_two, dhidden, preferred_element_type=jnp.float32)
    expand_bias_grad = jnp.sum(dhidden.astype(jnp.float32), 0)
    dnormed_two = jnp.einsum(
        "tf,df->td", dhidden, expand_weight, preferred_element_type=jnp.float32
    )
    gain_middle_grad = jnp.sum(dnormed_two * normal_two, 0)
    shift_middle_grad = jnp.sum(dnormed_two, 0)
    dresid = cot_full + norm_back(dnormed_two * gain_two, normal_two, spread_two)
    dbranch = dresid.astype(jnp.bfloat16)
    mixer_grad = jnp.einsum("td,te->de", attended_low, dbranch, preferred_element_type=jnp.float32)
    mixer_bias_grad = jnp.sum(dbranch.astype(jnp.float32), 0)
    dattended = jnp.einsum(
        "te,de->td", dbranch, mixer_weight, preferred_element_type=jnp.float32
    ).astype(jnp.bfloat16)
    dattended4 = dattended.reshape(shape4)
    row_delta = jnp.einsum("sqhd,sqhd->shq", dattended4.astype(jnp.float32), attended)
    dquery = jnp.zeros(shape4, jnp.float32)
    dkv_own = jnp.zeros((2, seq_count, block_len, width), jnp.float32)
    for hop in range(reach + 1):
        piece = pieces[hop]
        key4 = piece[0].reshape(shape4)
        value4 = piece[1].reshape(shape4)
        allowed, distance = window_mask(segments, padding, member, hop, block_len)
        scores = piece_scores(query4, key4, slopes, distance, score_scale)
        probs = jnp.exp(jnp.where(allowed, scores - log_total[..., None], masked_score))
        dvalue = jnp.einsum(
            "shqk,sqhd->skhd",
            probs.astype(jnp.bfloat16),
            dattended4,
            preferred_element_type=jnp.float32,
        )
        dprobs = jnp.einsum(
            "sqhd,skhd->shqk", dattended4, value4, preferred_element_type=jnp.float32
        )
        dscores = (probs * (dprobs - row_delta[..., None])).astype(jnp.bfloat16)
        dquery = dquery + jnp.einsum(
            "shqk,skhd->sqhd", dscores, key4, preferred_element_type=jnp.float32
        )
        dkey = (
            jnp.einsum("shqk,sqhd->skhd", dscores, query4, preferred_element_type=jnp.float32)
            * score_scale
        )
        returned = jnp.stack([dkey, dvalue]).reshape(2, seq_count, block_len, width)
        if hop == 0:
            dkv_own = returned
        else:
            dkv_own = dkv_own + shifted(returned.astype(jnp.bfloat16), "group", -hop).astype(
                returned.dtype
            )
    dquery_low = (dquery * score_scale).reshape(row_count, width).astype(jnp.bfloat16)
    dkey_low = dkv_own[0].reshape(row_count, width).astype(jnp.bfloat16)
    dvalue_low = dkv_own[1].reshape(row_count, width).astype(jnp.bfloat16)
    djoint = jnp.concatenate([dquery_low, dkey_low, dvalue_low], 1)
    joint_grad = jnp.einsum("td,te->de", normed_one, djoint, preferred_element_type=jnp.float32)
    joint_bias_grad = jnp.concatenate(
        [jnp.sum(dquery_low.astype(jnp.float32), 0), jnp.sum(dvalue_low.astype(jnp.float32), 0)]
    )
    dnormed_one = jnp.einsum("te,de->td", djoint, joint_weight, preferred_element_type=jnp.float32)
    gain_before_grad = jnp.sum(dnormed_one * normal_one, 0)
    shift_before_grad = jnp.sum(dnormed_one, 0)
    dinput = dresid + norm_back(dnormed_one * gain_one, normal_one, spread_one)
    input_gradient = dinput.astype(jnp.bfloat16).reshape(seq_count, block_len, width)
    listing = [
        gain_before_grad,
        shift_before_grad,
        joint_grad,
        joint_bias_grad,
        mixer_grad,
        mixer_bias_grad,
        gain_middle_grad,
        shift_middle_grad,
        expand_grad,
        expand_bias_grad,
        reduce_grad,
        reduce_bias_grad,
    ]
    gradient = jnp.concatenate([single.reshape(-1) for single in listing])
    small_list = [
        gain_before_grad,
        shift_before_grad,
        joint_bias_grad,
        mixer_bias_grad,
        gain_middle_grad,
        shift_middle_grad,
        expand_bias_grad,
        reduce_bias_grad,
    ]
    small_local = jnp.concatenate(small_list)
    share, small_share = (
        lax.psum_scatter(gradient, ("dp", "group"), scatter_dimension=0, tiled=True),
        lax.psum_scatter(small_local, ("dp", "group"), scatter_dimension=0, tiled=True),
    )
    moment_step = step_count[0].astype(jnp.float32)
    rate = learn_rate[0]
    fix_one = 1.0 - jnp.exp(moment_step * math.log(beta_first))
    fix_two = 1.0 - jnp.exp(moment_step * math.log(beta_second))
    updated_first = beta_first * first_moment + (1.0 - beta_first) * share
    updated_second = beta_second * second_moment + (1.0 - beta_second) * share * share
    updated_master = master_weights - rate * (
        updated_first / fix_one / (jnp.sqrt(updated_second / fix_two) + adam_epsilon)
        + weight_decay * master_weights
    )
    return (output, input_gradient, updated_master, updated_first, updated_second, small_share)


WIDTH = 1024
HIDDEN = 4096
TOKENS = 1024
LANES = 128
OWNED = 393600
OWNED_ROWS = OWNED // LANES
PIECE = 1568
HALF = PIECE // 2
JOINT_AT, MIXER_AT, EXPAND_AT, REDUCE_AT = 16, 12320, 16432, 32832
FLAT_ROWS = 49248
U_JOINT, U_JBIAS, U_MIXER, U_MBIAS, U_EXPAND, U_EBIAS, U_REDUCE, U_RBIAS = (
    2, 3074, 3076, 4100, 4103, 8199, 8203, 12299,
)


def section_shift(unit):
    return 8 if unit < U_JBIAS else 16 if unit < U_MBIAS else 20


def piece_start(owner):
    unit = OWNED_ROWS * owner // 8
    return (4 * unit + section_shift(unit)) // 16 * 16


def piece_offset(q, y, x):
    at = [piece_start(4 * q + k) // 16 for k in range(4)]
    row = (
        at[0] * (1 - y) * (1 - x) + at[1] * (1 - y) * x + at[2] * y * (1 - x) + at[3] * y * x
    )
    return pl.multiple_of(row * 16, 16)


MESH_ID = pl.DeviceIdType.MESH


def by_rows(step):
    def one(i, carry):
        step(pl.ds(pl.multiple_of(112 * i, 16), 112))
        return carry

    lax.fori_loop(0, HALF // 112, one, 0)


class Pieces:
    def __init__(self, dp, me, flat, own_a, own_b, rx_a1, rx_b1, rx_a2, rx_b2, acc, load_sem, s2_send, s2_recv):
        self.y, self.x = me // 2, me % 2
        self.x_near = (dp, 2 * self.y + (1 - self.x))
        self.y_near = (dp, 2 * (1 - self.y) + self.x)
        self.flat, self.own_a, self.own_b = flat, own_a, own_b
        self.rx_a1, self.rx_b1, self.rx_a2, self.rx_b2, self.acc = rx_a1, rx_b1, rx_a2, rx_b2, acc
        self.load_sem, self.s2_send, self.s2_recv = load_sem, s2_send, s2_recv

    def loads(self, q, own_slot, ready=None):
        slot = q
        out = []
        for k in range(2):
            for way, (row, own) in enumerate((
                (piece_offset(q, k, self.x), self.own_a),
                (piece_offset(q, self.y, k) + HALF, self.own_b),
            )):
                out.append(pltpu.make_async_copy(
                    self.flat.at[pl.ds(row, HALF)], own.at[own_slot, k], self.load_sem.at[slot, way, k]
                ))
            if ready is not None:
                ready_a, ready_b, at = ready
                for way, (src, dst) in enumerate(((ready_a, self.rx_a1), (ready_b, self.rx_b1))):
                    out.append(pltpu.make_async_copy(
                        src.at[at, k], dst.at[slot, k], self.load_sem.at[slot, 2 + way, k]
                    ))
        return out

    def second(self, slot):
        y, x = self.y, self.x
        return [
            pltpu.make_async_remote_copy(
                src_ref=src, dst_ref=dst.at[slot], send_sem=self.s2_send.at[slot, way],
                recv_sem=self.s2_recv.at[slot, way], device_id=near, device_id_type=MESH_ID,
            )
            for way, (src, dst, near) in enumerate((
                (self.rx_a1.at[slot, 1 - y], self.rx_a2, self.y_near),
                (self.rx_b1.at[slot, 1 - x], self.rx_b2, self.x_near),
            ))
        ]

    def meet(self, slot, own_slot):
        y, x = self.y, self.x
        rx_a1, rx_b1, own_a, own_b, acc = self.rx_a1, self.rx_b1, self.own_a, self.own_b, self.acc

        def away(rows):
            rx_a1[slot, 1 - y, rows] = rx_a1[slot, 1 - y, rows] + own_a[own_slot, 1 - y, rows]
            rx_b1[slot, 1 - x, rows] = rx_b1[slot, 1 - x, rows] + own_b[own_slot, 1 - x, rows]

        by_rows(away)
        for copy in self.second(slot):
            copy.start()

        def kept(rows):
            acc[slot, 0, rows] = rx_a1[slot, y, rows] + own_a[own_slot, y, rows]
            acc[slot, 1, rows] = rx_b1[slot, x, rows] + own_b[own_slot, x, rows]

        by_rows(kept)

    def join(self, slot):
        for copy in self.second(slot):
            copy.wait_recv()
        acc, rx_a2, rx_b2 = self.acc, self.rx_a2, self.rx_b2

        def add(rows):
            acc[slot, 0, rows] = acc[slot, 0, rows] + rx_a2[slot, rows]
            acc[slot, 1, rows] = acc[slot, 1, rows] + rx_b2[slot, rows]

        by_rows(add)


MIDDLE_EARLY = (7, 6, 4)


def nn(a, b):
    return lax.dot_general(a, b, (((1,), (0,)), ((), ())), preferred_element_type=jnp.float32)


def nt(a, b):
    return lax.dot_general(a, b, (((1,), (1,)), ((), ())), preferred_element_type=jnp.float32)


def tn(a, b):
    return lax.dot_general(a, b, (((0,), (0,)), ((), ())), preferred_element_type=jnp.float32)


def head_lanes(value, h):
    lane = lax.broadcasted_iota(jnp.int32, (1, LANES), 1)
    return jnp.where(lane // 64 == h, value, jnp.zeros_like(value))


def plane_devices(dp, me):
    z, c = dp // 2, dp % 2
    near = [(2 * z + 1 - c, me)]
    for d in (1, 2, 3):
        near += [(2 * z, (me + d) % 4), (2 * z + 1, (me + d) % 4)]
    return near


def greet(devices):
    barrier = pltpu.get_barrier_semaphore()
    for near in devices:
        pl.semaphore_signal(barrier, inc=1, device_id=near, device_id_type=MESH_ID)
    pl.semaphore_wait(barrier, len(devices))


class Home:
    def __init__(self, rows, out, dp, me, send_sem, recv_sem):
        z, c = dp // 2, dp % 2
        self.here = c == me // 2
        self.turns = []
        for turn in range(2):
            src = rows.at[pl.ds(256 * turn, 256)]
            dst = out.at[me % 2]
            away = pltpu.make_async_remote_copy(
                src_ref=src, dst_ref=dst, send_sem=send_sem.at[turn], recv_sem=recv_sem.at[me % 2],
                device_id=(2 * z + me // 2, 2 * c + turn), device_id_type=MESH_ID,
            )
            near = pltpu.make_async_copy(src, dst, send_sem.at[turn])
            came = pltpu.make_async_remote_copy(
                src_ref=src, dst_ref=out.at[turn], send_sem=send_sem.at[turn],
                recv_sem=recv_sem.at[turn], device_id=(2 * z + me // 2, 2 * c + turn),
                device_id_type=MESH_ID,
            )
            self.turns.append((away, near, came, self.here & (me % 2 == turn)))

    def start(self):
        for away, near, _, stays in self.turns:
            @pl.when(stays)
            def _():
                near.start()

            @pl.when(jnp.logical_not(stays))
            def _():
                away.start()

    def wait(self):
        for away, near, came, stays in self.turns:
            @pl.when(stays)
            def _():
                near.wait()

            @pl.when(jnp.logical_not(stays))
            def _():
                away.wait_send()
                came.wait_recv()


def first_stage(q, flat, rx_a, rx_b, at, send_sem, recv_sem, dp, me):
    y, x = me // 2, me % 2
    x_near = (dp, 2 * y + (1 - x))
    y_near = (dp, 2 * (1 - y) + x)
    out = []
    for k in range(2):
        for way, (row, rx, near) in enumerate((
            (piece_offset(q, k, 1 - x), rx_a, x_near),
            (piece_offset(q, 1 - y, k) + HALF, rx_b, y_near),
        )):
            out.append(pltpu.make_async_remote_copy(
                src_ref=flat.at[pl.ds(row, HALF)], dst_ref=rx.at[at, k],
                send_sem=send_sem.at[at, way, k], recv_sem=recv_sem.at[at, way, k],
                device_id=near, device_id_type=MESH_ID,
            ))
    return out


def both_heads(value):
    return jnp.concatenate([head_lanes(value, 0), head_lanes(value, 1)], 0)


class Spread:
    def __init__(self, blocks, rows, dp, me, send_sem, recv_sem):
        z, c = dp // 2, dp % 2
        here = c == me // 2
        self.turns = []
        for turn in range(2):
            src = blocks.at[turn]
            dst = rows.at[pl.ds(pl.multiple_of(256 * me, 256), 256)]
            away = pltpu.make_async_remote_copy(
                src_ref=src, dst_ref=dst, send_sem=send_sem.at[turn], recv_sem=recv_sem.at[me % 2],
                device_id=(2 * z + me // 2, 2 * c + turn), device_id_type=MESH_ID,
            )
            near = pltpu.make_async_copy(src, dst, send_sem.at[turn])
            came = pltpu.make_async_remote_copy(
                src_ref=src, dst_ref=rows.at[pl.ds(pl.multiple_of(512 * c + 256 * turn, 256), 256)],
                send_sem=send_sem.at[turn], recv_sem=recv_sem.at[turn],
                device_id=(2 * z + me // 2, 2 * c + turn), device_id_type=MESH_ID,
            )
            self.turns.append((away, near, came, here & (me % 2 == turn)))

    def start(self):
        for away, near, _, stays in self.turns:
            @pl.when(stays)
            def _():
                near.start()

            @pl.when(jnp.logical_not(stays))
            def _():
                away.start()

    def wait_came(self, turn):
        _, near, came, stays = self.turns[turn]

        @pl.when(stays)
        def _():
            near.wait()

        @pl.when(jnp.logical_not(stays))
        def _():
            came.wait_recv()

    def wait_sent(self):
        for away, _, _, stays in self.turns:
            @pl.when(jnp.logical_not(stays))
            def _():
                away.wait_send()


def front_kernel(
    slopes, blocks, cot_blocks, segments, padding, gain_in, shift_in, bias_in, weight_hbm,
    x_out, cot_out, normed_out, joint_out, dist_out, att_out, lse_out,
    x_all, cot_all, normed, joint, weight, dist, att, lse, seg_rx, pad_rx, vectors, columns, s_ref, p_ref, vt_ref, ot_ref,
    weight_sem, out_sem, mark_sem, x_send, x_recv, cot_send, cot_recv, pass_send, pass_recv,
):
    f32, bf16 = jnp.float32, jnp.bfloat16
    dp = lax.axis_index("dp")
    me = lax.axis_index("group")
    c = dp % 2
    core_near = (dp + 1 - 2 * c, me)
    own = pl.ds(pl.multiple_of(512 * c, 512), 512)
    other = pl.ds(pl.multiple_of(512 * (1 - c), 512), 512)

    weights = [
        pltpu.make_async_copy(
            weight_hbm.at[:, pl.ds(pl.multiple_of(1024 * p + 512 * c, 512), 512)],
            weight.at[:, pl.ds(512 * p, 512)], weight_sem.at[p],
        )
        for p in range(3)
    ]
    greet(plane_devices(dp, me))
    x_way = Spread(blocks, x_all, dp, me, x_send, x_recv)
    cot_way = Spread(cot_blocks, cot_all, dp, me, cot_send, cot_recv)
    x_way.start()
    vectors[0:1, :] = gain_in[...].astype(f32).reshape(1, WIDTH)
    vectors[1:2, :] = shift_in[...].astype(f32).reshape(1, WIDTH)
    vectors[2:4, :] = bias_in[...].astype(f32).reshape(2, WIDTH)
    mark_swaps = [
        pltpu.make_async_remote_copy(
            src_ref=src, dst_ref=dst, send_sem=mark_sem.at[0, i], recv_sem=mark_sem.at[1, i],
            device_id=core_near, device_id_type=MESH_ID,
        )
        for i, (src, dst) in enumerate(((segments, seg_rx), (padding, pad_rx)))
    ]
    for copy in mark_swaps:
        copy.start()
    for copy in weights:
        copy.start()

    def hand_over(rows, way, turn):
        at = pl.ds(pl.multiple_of(512 * c + 256 * turn, 256), 256)
        return pltpu.make_async_remote_copy(
            src_ref=rows.at[at], dst_ref=rows.at[at], send_sem=pass_send.at[way, turn],
            recv_sem=pass_recv.at[way, turn], device_id=core_near, device_id_type=MESH_ID,
        )

    for copy in mark_swaps:
        copy.wait()
    odd = me % 2 == 1
    held = c == me // 2

    def row_of(mine, came):
        both = jnp.where(held, mine[...], came[...]).astype(f32)
        return jnp.where(odd, both[1:2], both[0:1])

    seg = row_of(segments, seg_rx)
    pad = row_of(padding, pad_rx)
    kind = lax.broadcasted_iota(jnp.int32, (8, TOKENS), 0)
    columns[...] = jnp.broadcast_to(
        jnp.where(kind == 0, seg, pad).T[:, :8].reshape(TOKENS, 8), (TOKENS, 8)
    )

    def dist_rows(i, carry):
        rows = pl.ds(pl.multiple_of(128 * i, 128), 128)
        key_seg, key_pad = columns[rows, 0:1], columns[rows, 1:2]
        key = (lax.broadcasted_iota(jnp.int32, (128, 1), 0) + 128 * i).astype(f32)
        query = lax.broadcasted_iota(jnp.int32, (128, TOKENS), 1).astype(f32)
        last = jnp.sum(jnp.where(seg <= key_seg, 1.0, 0.0), 1, keepdims=True) - 1.0
        last = jnp.where(key_pad == 1.0, last, key)
        dist[rows, :] = jnp.where((query >= key) & (query <= last), query - key, -masked_score)
        return carry

    lax.fori_loop(0, 8, dist_rows, 0)
    outs = []

    def put(src, dst):
        copy = pltpu.make_async_copy(src, dst, out_sem.at[len(outs)])
        copy.start()
        outs.append(copy)

    put(dist, dist_out)
    gain, shift = vectors[0:1, :], vectors[1:2, :]

    def norm_rows(half):
        def one(i, carry):
            rows = pl.ds(pl.multiple_of(512 * half + 128 * i, 128), 128)
            values = x_all[rows, :].astype(f32)
            center = values - jnp.mean(values, -1, keepdims=True)
            factor = lax.rsqrt(jnp.mean(center * center, -1, keepdims=True) + norm_epsilon)
            normed[rows, :] = (center * factor * gain + shift).astype(bf16)
            return carry

        lax.fori_loop(0, 4, one, 0)
        rows = pl.ds(pl.multiple_of(512 * half, 512), 512)
        lanes = pl.ds(pl.multiple_of(512 * c, 512), 512)
        made = nn(normed[rows, :], weight[...])
        joint[rows, 0:512] = ((made[:, 0:512] + vectors[2:3, lanes]) * 0.125).astype(bf16)
        joint[rows, 512:1024] = made[:, 512:1024].astype(bf16)
        joint[rows, 1024:1536] = (made[:, 1024:1536] + vectors[3:4, lanes]).astype(bf16)

    for turn in range(2):
        x_way.wait_came(turn)
        hand_over(x_all, 0, turn).start()
    x_way.wait_sent()
    cot_way.start()
    put(x_all.at[own], x_out)
    for copy in weights:
        copy.wait()
    norm_rows(c)
    for turn in range(2):
        hand_over(x_all, 0, turn).wait_recv()
    norm_rows(1 - c)
    put(normed, normed_out)
    put(joint, joint_out)

    def pair_step(pair, carry):
        def lanes(block):
            return pl.ds(pl.multiple_of(512 * block + LANES * pair, LANES), LANES)

        vt_ref[...] = joint[:, lanes(2)].astype(f32).T.astype(bf16)
        slope = [slopes[8 * c + 2 * pair + h] for h in range(2)]

        def scores(qb):
            cols = pl.ds(qb * 256, 256)
            queries = both_heads(joint[cols, lanes(0)])
            top = None
            for kb in range(qb + 1):
                rows = pl.ds(kb * 256, 256)
                raw = nt(joint[rows, lanes(1)], queries)
                far = dist[rows, cols]
                parts = [raw[:, 256 * h : 256 * h + 256] - slope[h] * far for h in range(2)]
                for h in range(2):
                    s_ref[qb % 2, rows, 256 * h : 256 * h + 256] = parts[h]
                high = jnp.concatenate([jnp.max(part, 0, keepdims=True) for part in parts], 1)
                top = high if top is None else jnp.maximum(top, high)
            return top

        def weigh(qb, top):
            cols = pl.ds(qb * 256, 256)
            span = pl.ds(0, 256 * (qb + 1))
            total = None
            for kb in range(qb + 1):
                rows = pl.ds(kb * 256, 256)
                p = jnp.exp(s_ref[qb % 2, rows, :] - top)
                more = jnp.sum(p, 0, keepdims=True)
                total = more if total is None else total + more
                p_ref[qb % 2, rows, :] = p.astype(bf16)
            out = nn(vt_ref[:, span], p_ref[qb % 2, span, :]) / total
            ot_ref[0:64, cols] = out[0:64, 0:256]
            ot_ref[64:128, cols] = out[64:128, 256:512]
            row = top + jnp.log(total)
            for h in range(2):
                lse[pair, h : h + 1, cols] = row[:, 256 * h : 256 * h + 256]

        top = scores(0)
        for qb in range(4):
            after = scores(qb + 1) if qb < 3 else None
            weigh(qb, top)
            top = after
        att[:, lanes(0)] = ot_ref[...].T.astype(bf16)

        @pl.when(pair == 2)
        def _():
            for turn in range(2):
                cot_way.wait_came(turn)
                hand_over(cot_all, 1, turn).start()

        return carry

    lax.fori_loop(0, 4, pair_step, 0)
    put(att, att_out)
    put(lse, lse_out)
    for turn in range(2):
        hand_over(cot_all, 1, turn).wait()
        hand_over(x_all, 0, turn).wait_send()
    put(cot_all, cot_out)
    cot_way.wait_sent()
    for copy in outs:
        copy.wait()


def front(slopes, blocks, cot_blocks, segments, padding, gain, shift, bias, weight):
    f32, bf16 = jnp.float32, jnp.bfloat16
    vmem = pl.BlockSpec(memory_space=pltpu.VMEM)
    hbm = pl.BlockSpec(memory_space=pl.ANY)
    return pl.pallas_call(
        front_kernel,
        out_shape=(
            jax.ShapeDtypeStruct((512, WIDTH), bf16),
            jax.ShapeDtypeStruct((TOKENS, WIDTH), bf16),
            jax.ShapeDtypeStruct((TOKENS, WIDTH), bf16),
            jax.ShapeDtypeStruct((TOKENS, 1536), bf16),
            jax.ShapeDtypeStruct((TOKENS, TOKENS), f32),
            jax.ShapeDtypeStruct((TOKENS, 512), bf16),
            jax.ShapeDtypeStruct((4, 2, TOKENS), f32),
        ),
        in_specs=[pl.BlockSpec(memory_space=pltpu.SMEM)] + [hbm] * 2 + [vmem] * 5 + [hbm],
        out_specs=[hbm] * 7,
        scratch_shapes=[
            pltpu.VMEM((TOKENS, WIDTH), bf16),
            pltpu.VMEM((TOKENS, WIDTH), bf16),
            pltpu.VMEM((TOKENS, WIDTH), bf16),
            pltpu.VMEM((TOKENS, 1536), bf16),
            pltpu.VMEM((WIDTH, 1536), bf16),
            pltpu.VMEM((TOKENS, TOKENS), f32),
            pltpu.VMEM((TOKENS, 512), bf16),
            pltpu.VMEM((4, 2, TOKENS), f32),
            pltpu.VMEM((2, TOKENS), jnp.int32),
            pltpu.VMEM((2, TOKENS), jnp.int32),
            pltpu.VMEM((8, WIDTH), f32),
            pltpu.VMEM((TOKENS, 8), f32),
            pltpu.VMEM((2, TOKENS, 512), f32),
            pltpu.VMEM((2, TOKENS, 512), bf16),
            pltpu.VMEM((LANES, TOKENS), bf16),
            pltpu.VMEM((LANES, TOKENS), f32),
            pltpu.SemaphoreType.DMA((3,)),
            pltpu.SemaphoreType.DMA((7,)),
            pltpu.SemaphoreType.DMA((2, 2)),
            pltpu.SemaphoreType.DMA((2,)),
            pltpu.SemaphoreType.DMA((2,)),
            pltpu.SemaphoreType.DMA((2,)),
            pltpu.SemaphoreType.DMA((2,)),
            pltpu.SemaphoreType.DMA((2, 2)),
            pltpu.SemaphoreType.DMA((2, 2)),
        ],
        compiler_params=pltpu.CompilerParams(
            collective_id=0, has_side_effects=True, vmem_limit_bytes=62 << 20
        ),
        cost_estimate=pl.CostEstimate(flops=10 << 30, bytes_accessed=20 << 20, transcendentals=0),
    )(slopes, blocks, cot_blocks, segments, padding, gain, shift, bias, weight)


PLAN = (
    ("greet",), ("i1", 5), ("load",), ("a0",), ("meet", 6), ("meet", 4), ("a1",), ("meet", 7), ("a2",),
    ("join", 4), ("hop", 4, 0), ("i1", 3), ("meet", 5), ("join", 6), ("a3",), ("J",), ("i1", 0),
    ("hop", 4, 1), ("dnp",), ("join", 5), ("dno",), ("i1", 1), ("hop", 6, 0), ("hop", 5, 0), ("meet", 0),
    ("hop", 6, 1), ("ln",), ("fin", 4), ("meet", 1), ("join", 0), ("hop", 5, 1), ("hop", 0, 0), ("join", 7),
    ("i1", 2), ("join", 1), ("meet", 3), ("hop", 0, 1), ("hop", 1, 0), ("hop", 7, 0), ("hop", 7, 1),
    ("hop", 6, 2), ("meet", 2), ("hop", 1, 1), ("join", 3), ("home", "o"), ("hop", 3, 0), ("hop", 0, 2),
    ("fin", 5), ("join", 2), ("hop", 2, 0), ("hop", 1, 2), ("hop", 3, 1), ("hop", 7, 2), ("home", "i"),
    ("hop", 2, 1), ("fin", 3), ("fin", 1), ("fin", 0), ("fin", 7), ("fin", 6), ("fin", 2), ("end",),
)


def rear_kernel(
    slopes, joint_hbm, att_hbm, datt_hbm, dist_hbm, lse, normed_hbm, weight_hbm, x_hbm, dresid_hbm,
    result, mid_sums, expand_sums, mid_a, mid_b, flat_in,
    flat, own_out, peer_out, small_out, output, input_gradient,
    joint, attended, dattended, normed, weight, x_own, dresid,
    dist, p_ref, ds_ref, kt_ref, dqt_ref, dk_acc, dv_acc, delta_ref, djoint, dn_rx, dinput, blocks,
    own_a, own_b, rx_a1, rx_b1, rx_a2, rx_b2, acc, rx_up, rx_dn, parting,
    small_mine, small_rx, small_z,
    dist_sem, block_sem, swap_sem, load_sem, s1_send, s1_recv, s2_send, s2_recv, z_send, z_recv,
    last_sem, sm_send, sm_recv, out_send, out_recv, in_send, in_recv,
):
    f32, bf16 = jnp.float32, jnp.bfloat16
    dp = lax.axis_index("dp")
    me = lax.axis_index("group")
    z, c = dp // 2, dp % 2
    y, x = me // 2, me % 2
    x_near = (dp, 2 * y + (1 - x))
    y_near = (dp, 2 * (1 - y) + x)
    core_near = (2 * z + 1 - c, me)
    own = pl.ds(pl.multiple_of(512 * c, 512), 512)
    other = pl.ds(pl.multiple_of(512 * (1 - c), 512), 512)

    def z_at(d):
        return (2 * d + c, me)

    pieces = Pieces(
        dp, me, flat, own_a, own_b, rx_a1, rx_b1, rx_a2, rx_b2, acc, load_sem, s2_send, s2_recv
    )
    meets = [step[1] for step in PLAN if step[0] == "meet"]
    own_slot = {q: at % 4 for at, q in enumerate(meets)}
    loaded, met = [], []

    def load_ahead(joint_done):
        for q in meets[: len(met) + 4]:
            if q not in loaded and (joint_done or q > 1):
                loaded.append(q)
                start(loads(q))

    def loads(q):
        ready = (mid_a, mid_b, MIDDLE_EARLY.index(q)) if q in MIDDLE_EARLY else None
        return pieces.loads(q, own_slot[q], ready)

    def start(copies):
        for copy in copies:
            copy.start()

    def stage1(q):
        return first_stage(q, flat, rx_a1, rx_b1, q, s1_send, s1_recv, dp, me)

    def hop(q, up, half):
        way = 0 if up else 1
        return pltpu.make_async_remote_copy(
            src_ref=acc.at[q, half], dst_ref=rx_up.at[q - 2, half] if up else rx_dn.at[q, half],
            send_sem=z_send.at[q, way, half], recv_sem=z_recv.at[q, way, half],
            device_id=z_at((z + 1) % 4 if up else (z + 3) % 4), device_id_type=MESH_ID,
        )

    def meet(q):
        for copy in loads(q):
            copy.wait()
        if q not in MIDDLE_EARLY:
            for copy in stage1(q):
                copy.wait_recv()
        pieces.meet(q, own_slot[q])

    def add_came(q, rx, at, half):
        def add(rows):
            acc[q, half, rows] = acc[q, half, rows] + rx[at, half, rows]

        by_rows(add)

    on_way = {(plane, up): [] for plane in range(4) for up in (False, True)}

    def send_on(plane, q, up, half):
        queue = on_way[plane, up]
        if len(queue) >= 2:
            hop(*queue[-2]).wait_send()
        hop(q, up, half).start()
        queue.append((q, up, half))

    def pass_on(q, h):
        aim = q // 2
        if h < aim:
            @pl.when(z == h)
            def _():
                for half in range(2):
                    if h > 0:
                        hop(q, True, half).wait_recv()
                        add_came(q, rx_up, q - 2, half)
                    send_on(h, q, True, half)
        if h < 3 - aim:
            @pl.when(z == 3 - h)
            def _():
                for half in range(2):
                    if h > 0:
                        hop(q, False, half).wait_recv()
                        add_came(q, rx_dn, q, half)
                    send_on(3 - h, q, False, half)

    last = pltpu.make_async_remote_copy(
        src_ref=parting, dst_ref=peer_out, send_sem=last_sem.at[0], recv_sem=last_sem.at[1],
        device_id=core_near, device_id_type=MESH_ID,
    )

    def finish(q):
        aim = q // 2

        @pl.when(z == aim)
        def _():
            mine = c == q % 2
            for k in range(2):
                if aim > 0:
                    hop(q, True, k).wait_recv()
                if aim < 3:
                    hop(q, False, k).wait_recv()

                def add(i, carry):
                    rows = pl.ds(pl.multiple_of(112 * i, 16), 112)
                    place = pl.ds(pl.multiple_of(HALF * k + 112 * i, 16), 112)
                    total = acc[q, k, rows].astype(f32)
                    if aim > 0:
                        total = total + rx_up[q - 2, k, rows].astype(f32)
                    if aim < 3:
                        total = total + rx_dn[q, k, rows].astype(f32)

                    @pl.when(mine)
                    def _():
                        own_out[place] = total

                    @pl.when(jnp.logical_not(mine))
                    def _():
                        parting[place] = total

                    return carry

                lax.fori_loop(0, HALF // 112, add, 0)

            @pl.when(jnp.logical_not(mine))
            def _():
                last.start()

    def small_step(k):
        near = (core_near, x_near, y_near)[k]
        return pltpu.make_async_remote_copy(
            src_ref=small_mine.at[k], dst_ref=small_rx.at[k], send_sem=sm_send.at[k],
            recv_sem=sm_recv.at[k], device_id=near, device_id_type=MESH_ID,
        )

    def small_next(k):
        small_step(k).wait()
        small_mine[k + 1] = small_mine[k] + small_rx[k]
        if k < 2:
            small_step(k + 1).start()

    def small_hop(d):
        return pltpu.make_async_remote_copy(
            src_ref=small_mine.at[3], dst_ref=small_z.at[d - 1], send_sem=sm_send.at[2 + d],
            recv_sem=sm_recv.at[2 + d], device_id=z_at((z + d) % 4), device_id_type=MESH_ID,
        )

    def load(i, src, dst):
        return pltpu.make_async_copy(src, dst, dist_sem.at[i])

    first_loads = [
        load(0, joint_hbm, joint), load(1, att_hbm, attended), load(2, datt_hbm, dattended),
        load(3, dist_hbm, dist),
    ]
    later_loads = [load(4, normed_hbm, normed), load(5, x_hbm, x_own), load(6, dresid_hbm, dresid)]
    for p in range(3):
        later_loads.append(load(
            7 + p, weight_hbm.at[:, pl.ds(pl.multiple_of(1024 * p + 512 * c, 512), 512)],
            weight.at[:, pl.ds(512 * p, 512)],
        ))
    way_out = Home(result, output, dp, me, out_send, out_recv)
    way_in = Home(dinput, input_gradient, dp, me, in_send, in_recv)
    joint_done = []
    small_left = []

    def small_end():
        for d in (1, 2, 3):
            small_hop(d).start()

    def move(step):
        kind, *at = step
        if kind == "i1":
            start(stage1(at[0]))
        elif kind == "meet":
            meet(at[0])
            met.append(at[0])
            load_ahead(bool(joint_done))
        elif kind == "join":
            pieces.join(at[0])
        elif kind == "hop":
            pass_on(*at)
        elif kind == "fin":
            finish(at[0])
        elif kind == "home":
            (way_out if at[0] == "o" else way_in).start()
        else:
            compute[kind]()
        if small_left:
            wait = small_left.pop(0)
            if wait is not None:
                wait()

    names = [step[0] for step in PLAN]
    attention = [names.index(name) for name in ("a0", "a1", "a2", "a3")]

    def go_on(pair):
        for turn in range(3):
            @pl.when(pair == turn)
            def _():
                if turn == 0:
                    start(later_loads)
                for step in PLAN[attention[turn] + 1 : attention[turn + 1]]:
                    move(step)

    def greet_all():
        start(first_loads)
        load_ahead(False)
        greet(plane_devices(dp, me) + [z_at((z + d) % 4) for d in (1, 2, 3)])

    def wait_loads():
        for copy in first_loads:
            copy.wait()

    compute = {"greet": greet_all, "load": wait_loads}
    for step in PLAN[: attention[0]]:
        move(step)


    def pair_step(pair, carry):
        def lanes(block):
            return pl.ds(pl.multiple_of(512 * block + LANES * pair, LANES), LANES)

        here = lanes(0)
        kt_ref[...] = joint[:, lanes(1)].astype(f32).T.astype(bf16)
        product = (attended[:, here].astype(f32) * dattended[:, here].astype(f32)).T
        delta_ref[0:1, :] = jnp.sum(product[:64], 0, keepdims=True)
        delta_ref[1:2, :] = jnp.sum(product[64:], 0, keepdims=True)
        dk_acc[...] = jnp.zeros_like(dk_acc)
        dv_acc[...] = jnp.zeros_like(dv_acc)
        slope = [slopes[8 * c + 2 * pair + h] for h in range(2)]

        def pairs_of(qb):
            cols = pl.ds(qb * 256, 256)
            queries = both_heads(joint[cols, here])
            grads = both_heads(dattended[cols, here])
            for kb in range(qb + 1):
                rows = pl.ds(kb * 256, 256)
                raw = nt(joint[rows, lanes(1)], queries)
                dprobs = nt(joint[rows, lanes(2)], grads)
                far = dist[rows, cols]
                for h in range(2):
                    side = slice(256 * h, 256 * h + 256)
                    p = jnp.exp(raw[:, side] - slope[h] * far - lse[pair, h : h + 1, cols])
                    p_ref[qb % 2, rows, side] = p.astype(bf16)
                    ds_ref[qb % 2, rows, side] = (
                        p * (dprobs[:, side] - delta_ref[h : h + 1, cols])
                    ).astype(bf16)

        def sums_of(qb):
            cols = pl.ds(qb * 256, 256)
            span = pl.ds(0, 256 * (qb + 1))
            dv_acc[span, :] += nn(p_ref[qb % 2, span, :], both_heads(dattended[cols, here]))
            dk_acc[span, :] += nn(ds_ref[qb % 2, span, :], both_heads(joint[cols, here]))
            dq = nn(kt_ref[:, span], ds_ref[qb % 2, span, :])
            dqt_ref[0:64, cols] = dq[0:64, 0:256]
            dqt_ref[64:128, cols] = dq[64:128, 256:512]

        pairs_of(0)
        for qb in range(4):
            if qb < 3:
                pairs_of(qb + 1)
            sums_of(qb)
        djoint[:, lanes(0)] = (dqt_ref[...] * 0.125).T.astype(bf16)
        djoint[:, lanes(1)] = dk_acc[...].astype(bf16)
        djoint[:, lanes(2)] = dv_acc[...].astype(bf16)
        go_on(pair)
        return carry

    lax.fori_loop(0, 4, pair_step, 0)

    def block_copy(slot, i):
        return pltpu.make_async_copy(
            blocks.at[slot], flat.at[pl.ds(JOINT_AT + 3072 * i, 3072)], block_sem.at[slot]
        )

    def joint_gradient():
        for copy in later_loads:
            copy.wait()
        for i in range(4):
            if i >= 2:
                block_copy(i % 2, i - 2).wait()
            block = tn(normed[:, 256 * i : 256 * i + 256], djoint[...]).astype(bf16)
            blocks[i % 2] = block.reshape(3072, LANES)
            block_copy(i % 2, i).start()
        for i in (2, 3):
            block_copy(i % 2, i).wait()
        joint_done.append(True)
        load_ahead(True)

    dn_own, dn_part = dist.at[pl.ds(0, 512)], dist.at[pl.ds(512, 512)]
    dn_swap = pltpu.make_async_remote_copy(
        src_ref=dn_part, dst_ref=dn_rx, send_sem=swap_sem.at[0], recv_sem=swap_sem.at[1],
        device_id=core_near, device_id_type=MESH_ID,
    )

    def norm_part():
        dn_part[...] = nt(djoint[other, :], weight[...])
        dn_swap.start()

    def norm_own():
        dn_own[...] = nt(djoint[own, :], weight[...])
        bias_sums = nn(jnp.ones((8, TOKENS), bf16), djoint[...])
        half = pl.ds(pl.multiple_of(512 * c, 512), 512)
        small_mine[0] = jnp.zeros(small_mine.shape[1:], f32)
        small_mine[0, 2:3, half] = bias_sums[0:1, :512]
        small_mine[0, 3:4, half] = bias_sums[0:1, 1024:]
        small_mine[0, 4:7, :] = mid_sums[0:3, :]
        small_mine[0, 7:11, half] = expand_sums[...]
        small_mine[0, 11:12, :] = mid_sums[3:4, :]

    def norm_back_rows():
        dn_swap.wait()

        def back_rows(i, carry):
            rows = pl.ds(pl.multiple_of(128 * i, 128), 128)
            values = x_own[rows, :].astype(f32)
            center = values - jnp.mean(values, -1, keepdims=True)
            factor = lax.rsqrt(jnp.mean(center * center, -1, keepdims=True) + norm_epsilon)
            unit = center * factor
            dn = dn_own[rows, :] + dn_rx[rows, :]
            e = dn * mid_sums[4:5, :]
            down = dresid[rows, :] + factor * (
                e - jnp.mean(e, -1, keepdims=True) - unit * jnp.mean(e * unit, -1, keepdims=True)
            )
            dinput[rows, :] = down.astype(bf16)
            small_mine[0, 0:1, :] += jnp.sum(dn * unit, 0, keepdims=True)
            small_mine[0, 1:2, :] += jnp.sum(dn, 0, keepdims=True)
            return carry

        lax.fori_loop(0, 4, back_rows, 0)
        small_step(0).start()
        for k in range(3):
            small_left.extend([None, None, functools.partial(small_next, k)])
        small_left.append(small_end)

    def rest_of_small():
        while small_left:
            wait = small_left.pop(0)
            if wait is not None:
                wait()
        for d in (1, 2, 3):
            small_hop(d).wait()

    compute.update(
        J=joint_gradient, dnp=norm_part, dno=norm_own, ln=norm_back_rows, end=rest_of_small
    )
    for step in PLAN[attention[3] + 1 :]:
        move(step)
    small = (small_mine[3] + small_z[1]) + (small_z[0] + small_z[2])
    small_out[...] = small.reshape(small_out.shape)

    last.wait()
    way_out.wait()
    way_in.wait()
    for q in sorted(set(range(8)) - set(MIDDLE_EARLY)):
        for copy in stage1(q):
            copy.wait_send()
    for q in range(8):
        for copy in pieces.second(q):
            copy.wait_send()
    for (plane, _), queue in on_way.items():
        @pl.when(z == plane)
        def _():
            for sent in queue[-2:]:
                hop(*sent).wait_send()


def rear(
    slopes, joint, attended, dattended, dist, lse, normed, weight, x_own, dresid, result,
    mid_sums, expand_sums, mid_a, mid_b, flat,
):
    f32, bf16 = jnp.float32, jnp.bfloat16
    vmem = pl.BlockSpec(memory_space=pltpu.VMEM)
    hbm = pl.BlockSpec(memory_space=pl.ANY)
    home = jax.ShapeDtypeStruct((2, 256, WIDTH), bf16)
    piece = jax.ShapeDtypeStruct((PIECE, LANES), f32)
    return pl.pallas_call(
        rear_kernel,
        out_shape=(
            jax.ShapeDtypeStruct((FLAT_ROWS, LANES), bf16),
            piece,
            piece,
            jax.ShapeDtypeStruct((LANES, LANES), f32),
            home,
            home,
        ),
        in_specs=[pl.BlockSpec(memory_space=pltpu.SMEM)] + [hbm] * 4 + [vmem] + [hbm] * 5
        + [vmem] * 2 + [hbm] * 3,
        out_specs=[hbm] + [vmem] * 3 + [hbm] * 2,
        scratch_shapes=[
            pltpu.VMEM((TOKENS, 1536), bf16),
            pltpu.VMEM((TOKENS, 512), bf16),
            pltpu.VMEM((TOKENS, 512), bf16),
            pltpu.VMEM((TOKENS, WIDTH), bf16),
            pltpu.VMEM((WIDTH, 1536), bf16),
            pltpu.VMEM((512, WIDTH), bf16),
            pltpu.VMEM((512, WIDTH), f32),
            pltpu.VMEM((TOKENS, TOKENS), f32),
            pltpu.VMEM((2, TOKENS, 512), bf16),
            pltpu.VMEM((2, TOKENS, 512), bf16),
            pltpu.VMEM((LANES, TOKENS), bf16),
            pltpu.VMEM((LANES, TOKENS), f32),
            pltpu.VMEM((TOKENS, LANES), f32),
            pltpu.VMEM((TOKENS, LANES), f32),
            pltpu.VMEM((8, TOKENS), f32),
            pltpu.VMEM((TOKENS, 1536), bf16),
            pltpu.VMEM((512, WIDTH), f32),
            pltpu.VMEM((512, WIDTH), bf16),
            pltpu.VMEM((2, 3072, LANES), bf16),
            pltpu.VMEM((4, 2, HALF, LANES), bf16),
            pltpu.VMEM((4, 2, HALF, LANES), bf16),
            pltpu.VMEM((8, 2, HALF, LANES), bf16),
            pltpu.VMEM((8, 2, HALF, LANES), bf16),
            pltpu.VMEM((8, HALF, LANES), bf16),
            pltpu.VMEM((8, HALF, LANES), bf16),
            pltpu.VMEM((8, 2, HALF, LANES), bf16),
            pltpu.VMEM((6, 2, HALF, LANES), bf16),
            pltpu.VMEM((6, 2, HALF, LANES), bf16),
            pltpu.VMEM((PIECE, LANES), f32),
            pltpu.VMEM((4, 16, WIDTH), f32),
            pltpu.VMEM((3, 16, WIDTH), f32),
            pltpu.VMEM((3, 16, WIDTH), f32),
            pltpu.SemaphoreType.DMA((10,)),
            pltpu.SemaphoreType.DMA((2,)),
            pltpu.SemaphoreType.DMA((2,)),
            pltpu.SemaphoreType.DMA((8, 4, 2)),
            pltpu.SemaphoreType.DMA((8, 2, 2)),
            pltpu.SemaphoreType.DMA((8, 2, 2)),
            pltpu.SemaphoreType.DMA((8, 2)),
            pltpu.SemaphoreType.DMA((8, 2)),
            pltpu.SemaphoreType.DMA((8, 2, 2)),
            pltpu.SemaphoreType.DMA((8, 2, 2)),
            pltpu.SemaphoreType.DMA((2,)),
            pltpu.SemaphoreType.DMA((6,)),
            pltpu.SemaphoreType.DMA((6,)),
            pltpu.SemaphoreType.DMA((2,)),
            pltpu.SemaphoreType.DMA((2,)),
            pltpu.SemaphoreType.DMA((2,)),
            pltpu.SemaphoreType.DMA((2,)),
        ],
        input_output_aliases={15: 0},
        compiler_params=pltpu.CompilerParams(
            collective_id=2, has_side_effects=True, vmem_limit_bytes=62 << 20
        ),
        cost_estimate=pl.CostEstimate(flops=30 << 30, bytes_accessed=30 << 20, transcendentals=0),
    )(
        slopes, joint, attended, dattended, dist, lse, normed, weight, x_own, dresid, result,
        mid_sums, expand_sums, mid_a, mid_b, flat,
    )


def middle_kernel(
    attended, x_own, cot, mixer_bias_in, gain_in, shift_in, reduce_bias_in, expand_bias_in, gain_before_in,
    mixer_hbm, expand_hbm, reduce_hbm,
    result, dresid, dattended, sums, expand_sums, flat, rx_a, rx_b,
    vectors, mixer, expand, reduce, att_rx, resid, normal, spread, normed, act, act_rx, dhidden,
    dn_own, dn_part, dn_rx, out_part, out_rx, dbranch, blocks,
    weight_sem, block_sem, send_sem, recv_sem, act_send, act_recv, s1_send, s1_recv,
):
    f32, bf16 = jnp.float32, jnp.bfloat16
    dp = lax.axis_index("dp")
    me = lax.axis_index("group")
    c = dp % 2
    near = (dp + 1 - 2 * c, me)
    own = pl.ds(pl.multiple_of(512 * c, 512), 512)
    other = pl.ds(pl.multiple_of(512 * (1 - c), 512), 512)

    weights = [pltpu.make_async_copy(mixer_hbm, mixer, weight_sem.at[0])]
    for k in range(4):
        part = pl.ds(pl.multiple_of(512 * (2 * k + c), 512), 512)
        weights.append(pltpu.make_async_copy(
            expand_hbm.at[:, part], expand.at[:, pl.ds(512 * k, 512)], weight_sem.at[1 + k]
        ))
    for k in range(4):
        part = pl.ds(pl.multiple_of(512 * (2 * k + c), 512), 512)
        weights.append(pltpu.make_async_copy(
            reduce_hbm.at[part], reduce.at[pl.ds(512 * k, 512)], weight_sem.at[5 + k]
        ))
    for copy in weights:
        copy.start()

    y, x = me // 2, me % 2
    greet([near, (dp, 2 * y + 1 - x), (dp, 2 * (1 - y) + x)])

    def swap(i, src, dst):
        return pltpu.make_async_remote_copy(
            src_ref=src, dst_ref=dst, send_sem=send_sem.at[i], recv_sem=recv_sem.at[i],
            device_id=near, device_id_type=MESH_ID,
        )

    att_swap = swap(0, attended, att_rx)
    normed_swap = swap(1, normed.at[own], normed.at[own])
    dn_swap = swap(2, dn_part, dn_rx)
    out_swap = swap(3, out_part, out_rx)
    branch_swap = swap(4, dbranch.at[own], dbranch.at[own])
    att_swap.start()

    for k, given in enumerate((mixer_bias_in, gain_in, shift_in, reduce_bias_in)):
        vectors[k : k + 1, :] = given[...].astype(f32).reshape(1, WIDTH)
    vectors[4:8, :] = expand_bias_in[...].astype(f32).reshape(4, WIDTH)
    mixer_bias, gain, shift, reduce_bias = (vectors[k : k + 1, :] for k in range(4))

    weights[0].wait()
    resid[...] = nn(attended[own, :], mixer[own, :]) + (x_own[...].astype(f32) + mixer_bias)
    att_swap.wait_recv()
    resid[...] += nn(att_rx[own, :], mixer[other, :])

    def norm_rows(i, carry):
        rows = pl.ds(pl.multiple_of(128 * i, 128), 128)
        here = pl.ds(pl.multiple_of(512 * c + 128 * i, 128), 128)
        values = resid[rows, :]
        center = values - jnp.mean(values, -1, keepdims=True)
        factor = lax.rsqrt(jnp.mean(center * center, -1, keepdims=True) + norm_epsilon)
        unit = center * factor
        normal[rows, :] = unit
        spread[rows, :] = jnp.broadcast_to(factor, (128, LANES))
        normed[here, :] = (unit * gain + shift).astype(bf16)
        return carry

    lax.fori_loop(0, 4, norm_rows, 0)
    normed_swap.start()

    def act_swap(half, k):
        rows = pl.ds(pl.multiple_of(512 * half, 512), 512)
        cols = pl.ds(pl.multiple_of(512 * k, 512), 512)
        return pltpu.make_async_remote_copy(
            src_ref=act.at[rows, cols], dst_ref=act_rx.at[rows, cols],
            send_sem=act_send.at[half, k], recv_sem=act_recv.at[half, k],
            device_id=near, device_id_type=MESH_ID,
        )

    root = math.sqrt(2.0 / math.pi)
    right = pl.ds(pl.multiple_of(512 * c, 512), 512)

    def products(half, k):
        rows = pl.ds(pl.multiple_of(512 * half, 512), 512)
        cols = pl.ds(pl.multiple_of(512 * k, 512), 512)
        u = nn(normed[rows, :], expand[:, cols]) + vectors[pl.ds(4 + k, 1), right]
        return u, nt(cot[rows, :], reduce[cols, :])

    def gelu_block(half, k, first, u, dact):
        rows = pl.ds(pl.multiple_of(512 * half, 512), 512)
        cols = pl.ds(pl.multiple_of(512 * k, 512), 512)
        square = u * u
        t = jnp.tanh(u * (root + (root * 0.044715) * square))
        up = 0.5 + 0.5 * t
        act[rows, cols] = (u * up).astype(bf16)
        slope = up + (0.5 * u) * (1.0 - t * t) * (root + (3.0 * root * 0.044715) * square)
        dh = (dact * slope).astype(bf16)
        dhidden[rows, cols] = dh
        total = jnp.sum(dh.astype(f32), 0, keepdims=True)
        if first:
            expand_sums[pl.ds(k, 1), :] = total
        else:
            expand_sums[pl.ds(k, 1), :] += total
        act_swap(half, k).start()

    def out_copies(slot, places):
        return [
            pltpu.make_async_copy(
                blocks.at[slot, pl.ds(2048 * part, 2048)],
                flat.at[pl.ds(pl.multiple_of(at, 16), 2048)], block_sem.at[slot, part],
            )
            for part, at in enumerate(places)
        ]

    def emit(block, slot, places):
        blocks[slot, : 2048 * len(places)] = block.astype(bf16).reshape(2048 * len(places), LANES)
        for copy in out_copies(slot, places):
            copy.start()

    def drain(slot, places):
        for copy in out_copies(slot, places):
            copy.wait()

    for copy in weights[1:]:
        copy.wait()

    def reduce_places(pair, parity):
        return [REDUCE_AT + 2048 * (2 * (2 * pair + k) + parity) for k in range(2)]

    stages = [
        first_stage(q, flat, rx_a, rx_b, at, s1_send, s1_recv, dp, me)
        for at, q in enumerate(MIDDLE_EARLY)
    ]

    def hidden_pair(turn, carry):
        pair = 1 - turn
        k = [2 * pair, 2 * pair + 1]
        a = products(c, k[0])
        b = products(c, k[1])
        gelu_block(c, k[0], True, *a)

        @pl.when(turn == 0)
        def _():
            normed_swap.wait_recv()

        @pl.when(turn == 1)
        def _():
            drain(0, reduce_places(1, c))
            drain(1, reduce_places(1, 1 - c))
            for copy in stages[0]:
                copy.start()

        a = products(1 - c, k[0])
        gelu_block(c, k[1], True, *b)
        b = products(1 - c, k[1])
        gelu_block(1 - c, k[0], False, *a)
        gelu_block(1 - c, k[1], False, *b)
        left = pl.ds(pl.multiple_of(1024 * pair, 1024), 1024)
        emit(tn(act[:, left], cot[:, right]), 0, reduce_places(pair, c))
        for half in range(2):
            for one in k:
                act_swap(half, one).wait()
        emit(tn(act_rx[:, left], cot[:, right]), 1, reduce_places(pair, 1 - c))
        return carry

    lax.fori_loop(0, 2, hidden_pair, 0)
    drain(0, reduce_places(0, c))
    drain(1, reduce_places(0, 1 - c))
    for copy in stages[1]:
        copy.start()

    def expand_places(i):
        return [EXPAND_AT + 4096 * i, EXPAND_AT + 4096 * i + 2048]

    def expand_step(i, carry):
        block = tn(normed[:, pl.ds(pl.multiple_of(256 * i, 256), 256)], dhidden[...])

        @pl.when(i >= 2)
        def _():
            drain(i % 2, expand_places(i - 2))

        emit(block, i % 2, expand_places(i))
        return carry

    lax.fori_loop(0, 4, expand_step, 0)
    drain(0, expand_places(2))
    drain(1, expand_places(3))
    for copies in stages[2:]:
        for copy in copies:
            copy.start()

    dn_part[...] = nt(dhidden[other, :], expand[...])
    dn_swap.start()
    out_part[...] = nn(act[other, :], reduce[...]).astype(bf16)
    out_swap.start()

    dn_own[...] = nt(dhidden[own, :], expand[...])
    dn_swap.wait()
    sums[...] = jnp.zeros_like(sums)
    sums[4:5, :] = gain_before_in[...].astype(f32).reshape(1, WIDTH)

    def back_rows(i, carry):
        rows = pl.ds(pl.multiple_of(128 * i, 128), 128)
        here = pl.ds(pl.multiple_of(512 * c + 128 * i, 128), 128)
        dn = dn_own[rows, :] + dn_rx[rows, :]
        unit = normal[rows, :]
        grad = cot[here, :].astype(f32)
        e = dn * gain
        down = grad + spread[rows, 0:1] * (
            e - jnp.mean(e, -1, keepdims=True) - unit * jnp.mean(e * unit, -1, keepdims=True)
        )
        dresid[rows, :] = down
        low = down.astype(bf16)
        dbranch[here, :] = low
        sums[0:1, :] += jnp.sum(low.astype(f32), 0, keepdims=True)
        sums[1:2, :] += jnp.sum(dn * unit, 0, keepdims=True)
        sums[2:3, :] += jnp.sum(dn, 0, keepdims=True)
        sums[3:4, :] += jnp.sum(grad, 0, keepdims=True)
        return carry

    lax.fori_loop(0, 4, back_rows, 0)
    branch_swap.start()
    dattended[own, :] = nt(dbranch[own, :], mixer[own, :]).astype(bf16)
    resid[...] += nn(act[own, :], reduce[...])
    out_swap.wait()
    result[...] = (resid[...] + (out_rx[...].astype(f32) + reduce_bias)).astype(bf16)
    branch_swap.wait()
    dattended[other, :] = nt(dbranch[other, :], mixer[own, :]).astype(bf16)
    emit(tn(attended[...], dbranch[:, right]), 0, [MIXER_AT + 2048 * c])
    emit(tn(att_rx[...], dbranch[:, right]), 1, [MIXER_AT + 2048 * (1 - c)])
    drain(0, [MIXER_AT + 2048 * c])
    drain(1, [MIXER_AT + 2048 * (1 - c)])
    att_swap.wait_send()
    normed_swap.wait_send()
    for copies in stages:
        for copy in copies:
            copy.wait()


def middle(attended, x_own, cot, small, mixer, expand, reduce):
    f32, bf16 = jnp.float32, jnp.bfloat16
    vmem = pl.BlockSpec(memory_space=pltpu.VMEM)
    hbm = pl.BlockSpec(memory_space=pl.ANY)
    count = len(MIDDLE_EARLY)
    early = jax.ShapeDtypeStruct((count, 2, HALF, LANES), bf16)
    return pl.pallas_call(
        middle_kernel,
        out_shape=(
            jax.ShapeDtypeStruct((512, WIDTH), bf16),
            jax.ShapeDtypeStruct((512, WIDTH), f32),
            jax.ShapeDtypeStruct((TOKENS, 512), bf16),
            jax.ShapeDtypeStruct((8, WIDTH), f32),
            jax.ShapeDtypeStruct((4, 512), f32),
            jax.ShapeDtypeStruct((FLAT_ROWS, LANES), bf16),
            early,
            early,
        ),
        in_specs=[vmem] * 9 + [hbm] * 3,
        out_specs=[vmem] * 5 + [hbm] * 3,
        scratch_shapes=[
            pltpu.VMEM((8, WIDTH), f32),
            pltpu.VMEM((WIDTH, WIDTH), bf16),
            pltpu.VMEM((WIDTH, 2048), bf16),
            pltpu.VMEM((2048, WIDTH), bf16),
            pltpu.VMEM((TOKENS, 512), bf16),
            pltpu.VMEM((512, WIDTH), f32),
            pltpu.VMEM((512, WIDTH), f32),
            pltpu.VMEM((512, LANES), f32),
            pltpu.VMEM((TOKENS, WIDTH), bf16),
            pltpu.VMEM((TOKENS, 2048), bf16),
            pltpu.VMEM((TOKENS, 2048), bf16),
            pltpu.VMEM((TOKENS, 2048), bf16),
            pltpu.VMEM((512, WIDTH), f32),
            pltpu.VMEM((512, WIDTH), f32),
            pltpu.VMEM((512, WIDTH), f32),
            pltpu.VMEM((512, WIDTH), bf16),
            pltpu.VMEM((512, WIDTH), bf16),
            pltpu.VMEM((TOKENS, WIDTH), bf16),
            pltpu.VMEM((2, 4096, LANES), bf16),
            pltpu.SemaphoreType.DMA((9,)),
            pltpu.SemaphoreType.DMA((2, 2)),
            pltpu.SemaphoreType.DMA((5,)),
            pltpu.SemaphoreType.DMA((5,)),
            pltpu.SemaphoreType.DMA((2, 4)),
            pltpu.SemaphoreType.DMA((2, 4)),
            pltpu.SemaphoreType.DMA((count, 2, 2)),
            pltpu.SemaphoreType.DMA((count, 2, 2)),
        ],
        compiler_params=pltpu.CompilerParams(
            collective_id=1, has_side_effects=True, vmem_limit_bytes=62 << 20
        ),
        cost_estimate=pl.CostEstimate(flops=30 << 30, bytes_accessed=40 << 20, transcendentals=0),
    )(attended, x_own, cot, *small, mixer, expand, reduce)


UPDATE_ROWS = 616


def owner_table(owners):
    smalls = ((0, 2, 0), (U_JBIAS, U_MIXER, 16), (U_MBIAS, U_EXPAND, 32), (U_EBIAS, U_REDUCE, 56),
              (U_RBIAS, 12300, 88))
    table = []
    for owner in range(owners):
        begin = OWNED_ROWS * owner
        end = begin + OWNED_ROWS
        start = piece_start(owner)
        shift, later = section_shift(begin // 8), section_shift((end - 1) // 8)
        turn = next((8 * u - begin for u in (U_JBIAS, U_MBIAS) if begin < 8 * u < end), OWNED_ROWS)
        row = [begin + 2 * shift - 2 * start, begin + 2 * later - 2 * start, turn, 0, 0, 0, 3 * owner, 0]
        for first, past, at in smalls:
            if 8 * first < end and 8 * past > begin:
                row[3] = at + begin - 8 * first
                row[4] = max(8 * first - begin, 0)
                row[5] = min(8 * past - begin, OWNED_ROWS)
        assert 0 <= row[0] <= row[1] <= 2 * PIECE - 5 * UPDATE_ROWS
        table.append(row)
    return table


def update_kernel(
    table, step_count, learn_rate, master, first, second, own, peer, small, out_hbm, in_hbm,
    new_master, new_first, new_second, small_share, out_copy, in_copy,
    rows, small_rows, held, sem,
):
    f32 = jnp.float32
    i = pl.program_id(0)
    c = lax.axis_index("dp") % 2
    owner = lax.axis_index("dp") * lax.axis_size("group") + lax.axis_index("group")
    place = [table[owner, k] for k in range(7)]
    pairs = ((out_hbm, out_copy), (in_hbm, in_copy))
    fetch = [pltpu.make_async_copy(src, held.at[k], sem.at[k]) for k, (src, _) in enumerate(pairs)]
    give = [pltpu.make_async_copy(held.at[k], dst, sem.at[2 + k]) for k, (_, dst) in enumerate(pairs)]

    @pl.when(i == 0)
    def _():
        for copy in fetch:
            copy.start()
        small_rows[...] = jnp.zeros_like(small_rows)
        small_rows[UPDATE_ROWS : UPDATE_ROWS + LANES, :] = small[...]
        small_share[...] = small_rows[pl.ds(UPDATE_ROWS + place[6], 3), :]

        def weave(k, carry):
            part = pl.ds(pl.multiple_of(112 * k, 16), 112)
            mine, other = own[part, :], peer[part, :]
            even = jnp.where(c == 0, mine, other).reshape(28, 4, LANES)
            odd = jnp.where(c == 0, other, mine).reshape(28, 4, LANES)
            rows[pl.ds(pl.multiple_of(224 * k, 32), 224), :] = jnp.concatenate([even, odd], 1).reshape(
                224, LANES
            )
            return carry

        lax.fori_loop(0, PIECE // 112, weave, 0)

    @pl.when(i == 2)
    def _():
        for copy in fetch:
            copy.wait()
        for copy in give:
            copy.start()

    base = UPDATE_ROWS * i
    k = lax.broadcasted_iota(jnp.int32, (UPDATE_ROWS, LANES), 0) + base
    grad = jnp.where(
        k < place[2],
        rows[pl.ds(place[0] + base, UPDATE_ROWS), :],
        rows[pl.ds(place[1] + base, UPDATE_ROWS), :],
    )
    at = jnp.clip(place[3] + base, -UPDATE_ROWS, LANES) + UPDATE_ROWS
    grad = jnp.where(
        (k >= place[4]) & (k < place[5]), small_rows[pl.ds(at, UPDATE_ROWS), :], grad
    )
    rate = learn_rate[0]
    moment_step = jnp.full((1, LANES), step_count[0].astype(f32))
    fix_one = 1.0 - jnp.exp(moment_step * math.log(beta_first))
    fix_two = 1.0 - jnp.exp(moment_step * math.log(beta_second))
    one = beta_first * first[...] + (1.0 - beta_first) * grad
    two = beta_second * second[...] + (1.0 - beta_second) * grad * grad
    weights = master[...]
    new_first[...] = one
    new_second[...] = two
    new_master[...] = weights - rate * (
        one / fix_one / (jnp.sqrt(two / fix_two) + adam_epsilon) + weight_decay * weights
    )

    @pl.when(i == pl.num_programs(0) - 1)
    def _():
        for copy in give:
            copy.wait()


def update(table, step_count, learn_rate, master, first, second, own, peer, small, output, input_gradient):
    f32 = jnp.float32
    smem = pl.BlockSpec(memory_space=pltpu.SMEM)
    hbm = pl.BlockSpec(memory_space=pl.ANY)
    block = pl.BlockSpec((UPDATE_ROWS, LANES), lambda i: (i, 0))

    def whole(shape):
        return pl.BlockSpec(shape, lambda i: (0, 0))

    flat = jax.ShapeDtypeStruct((OWNED_ROWS, LANES), f32)
    home = jax.ShapeDtypeStruct(output.shape, output.dtype)
    new = pl.pallas_call(
        update_kernel,
        grid=(5,),
        out_shape=(flat, flat, flat, jax.ShapeDtypeStruct((3, LANES), f32), home, home),
        in_specs=[smem, smem, smem] + [block] * 3
        + [whole((PIECE, LANES)), whole((PIECE, LANES)), whole((LANES, LANES))] + [hbm] * 2,
        out_specs=[block] * 3 + [whole((3, LANES))] + [hbm] * 2,
        scratch_shapes=[
            pltpu.VMEM((2 * PIECE, LANES), f32),
            pltpu.VMEM((2 * UPDATE_ROWS + LANES, LANES), f32),
            pltpu.VMEM((2,) + output.shape, output.dtype),
            pltpu.SemaphoreType.DMA((4,)),
        ],
        compiler_params=pltpu.CompilerParams(vmem_limit_bytes=62 << 20),
    )(
        table, step_count, learn_rate, *[whole_array.reshape(OWNED_ROWS, LANES) for whole_array in (master, first, second)],
        own, peer, small, output, input_gradient,
    )
    return [part.reshape(-1) for part in new[:4]] + list(new[4:])


def on_device_chip(
    dp_size, group_size,
    activations, cotangent, segments, padding, step_count, learn_rate,
    gain_before, shift_before, joint_weight, joint_bias, mixer_weight, mixer_bias,
    gain_middle, shift_middle, expand_weight, expand_bias, reduce_weight, reduce_bias,
    master_weights, first_moment, second_moment,
):
    f32, bf16 = jnp.float32, jnp.bfloat16
    dp = lax.axis_index("dp")
    group = lax.axis_index("group")
    c = dp % 2
    slopes = jnp.asarray([2.0 ** (-8.0 * (h + 1) / HEADS) for h in range(HEADS)], f32)
    x_own, cot_all, normed_one, joint, dist, attended, lse = front(
        slopes, activations, cotangent, segments, padding, gain_before, shift_before, joint_bias,
        joint_weight,
    )
    result, dresid, dattended, middle_sums, expand_sums, flat, mid_a, mid_b = middle(
        attended, x_own, cot_all, (mixer_bias, gain_middle, shift_middle, reduce_bias, expand_bias, gain_before),
        mixer_weight, expand_weight, reduce_weight,
    )
    _, own, peer, small_sum, output, input_gradient = rear(
        slopes, joint, attended, dattended, dist, lse, normed_one, joint_weight, x_own, dresid,
        result, middle_sums, expand_sums, mid_a, mid_b, flat,
    )
    table = jnp.asarray(owner_table(dp_size * group_size), jnp.int32)
    new_master, new_first, new_second, small_share, output, input_gradient = update(
        table, step_count, learn_rate, master_weights, first_moment, second_moment, own, peer, small_sum, output,
        input_gradient,
    )
    return (output, input_gradient, new_master, new_first, new_second, small_share)


def on_device(dp_size, group_size, activations, *rest):
    if (dp_size, group_size) == (8, 4) and activations.shape == (2, 256, WIDTH):
        return on_device_chip(dp_size, group_size, activations, *rest)
    return on_device_general(activations, *rest)


def solution(mesh):
    in_specs = (
        P("dp", "group", None),
        P("dp", "group", None),
        P("dp", None),
        P("dp", None),
        P(),
        P(),
        P(),
        P(),
        P(),
        P(),
        P(),
        P(),
        P(),
        P(),
        P(),
        P(),
        P(),
        P(),
        P(("dp", "group")),
        P(("dp", "group")),
        P(("dp", "group")),
    )
    out_specs = (
        P("dp", "group", None),
        P("dp", "group", None),
        P(("dp", "group")),
        P(("dp", "group")),
        P(("dp", "group")),
        P(("dp", "group")),
    )
    return jax.shard_map(
        functools.partial(on_device, mesh.shape["dp"], mesh.shape["group"]), mesh=mesh, in_specs=in_specs, out_specs=out_specs, check_vma=False
    )
```
